32 devices in a mesh: dp: 2 (over x), ctx: 4 (over y, core), tp: 4 (over z).
Axes of the slice: x: 2, y: 2, z: 4, core: 2. Of those that a mesh axis runs over, the one named last changes fastest.
Arguments:
- tokens: bfloat16 [12, 1024, 768], P('dp', 'ctx'), may hold values from -6 to 6
- segments: int32 [12, 1024], P('dp', 'ctx'), may hold values from 0 to 15, never falling along the last dimension, each value on 1 to 512 neighbouring positions
- w_qkv: bfloat16 [768, 3, 768], P(('dp', 'ctx'), None, 'tp'), may hold values from -0.21875 to 0.21875
- q_bias: float32 [768], P('tp'), may hold values from -3 to 3
- v_bias: float32 [768], P('tp'), may hold values from -3 to 3
- w_out: bfloat16 [768, 768], P(('dp', 'ctx'), 'tp'), may hold values from -0.875 to 0.875
- out_bias: float32 [768], replicated, may hold values from -3 to 3
- gain_one: float32 [768], replicated, may hold values from 0.25 to 1.75
- shift_one: float32 [768], replicated, may hold values from -2 to 2
- w_in: bfloat16 [768, 3072], P(('dp', 'ctx'), 'tp'), may hold values from -0.21875 to 0.21875
- in_bias: float32 [3072], P('tp'), may hold values from -3 to 3
- w_back: bfloat16 [768, 3072], P(('dp', 'ctx'), 'tp'), may hold values from -0.15625 to 0.15625
- back_bias: float32 [768], replicated, may hold values from -3 to 3
- gain_two: float32 [768], replicated, may hold values from 0.25 to 1.75
- shift_two: float32 [768], replicated, may hold values from -2 to 2
- cotangent: bfloat16 [12, 1024, 768], P('dp', 'ctx'), may hold values from -6 to 6
Outputs:
- output: bfloat16 [12, 1024, 768], P('dp', 'ctx')
- d_tokens: float32 [12, 1024, 768], P('dp', 'ctx')
- d_w_qkv: float32 [768, 3, 768], P(('dp', 'ctx'), None, 'tp')
- d_q_bias: float32 [768], P('tp')
- d_v_bias: float32 [768], P('tp')
- d_w_out: float32 [768, 768], P(('dp', 'ctx'), 'tp')
- d_out_bias: float32 [768], replicated
- d_gain_one: float32 [768], replicated
- d_shift_one: float32 [768], replicated
- d_w_in: float32 [768, 3072], P(('dp', 'ctx'), 'tp')
- d_in_bias: float32 [3072], P('tp')
- d_w_back: float32 [768, 3072], P(('dp', 'ctx'), 'tp')
- d_back_bias: float32 [768], replicated
- d_gain_two: float32 [768], replicated
- d_shift_two: float32 [768], replicated
The draws below stay inside these ranges and needn't reach their ends.
Inputs may be any that keep to these rules, and one draw needn't show every extreme that they name: `segments`: within one sequence segment numbers never fall; each of the 16 numbers covers 1 to 512 consecutive positions, one exactly 512.
All inputs are finite; a program needn't handle non-finite values.
Results may differ from the reference program's by a relative error of at most 0.013.
The reference program's roundings to bfloat16 on the way count: a program that leaves them out, or rounds other values in their place, can miss the bound.
Values may be sent and summed in bfloat16 or wider, within the bound.
A program may use at most 128 MiB of HBM per device.

```python
import math
import jax
import jax.numpy as jnp
import numpy as np
from jax import lax

D = 768
HEADS = 12
FF = 3072
HEAD = 64
LENGTH = 1024
SEGS = 16
MOST = 512
SEQS = 12


def level_of(rng, dims, shards, low, top_value):
    factor_of, own = 1.0, jax.random.fold_in(rng, 6)
    for position, shards_of in shards:
        heights = jnp.exp(jax.random.uniform(jax.random.fold_in(own, position), (shards_of,), jnp.float32, low / len(shards), top_value / len(shards)))
        factor_of = factor_of * jnp.repeat(heights, dims[position] // shards_of).reshape([-1 if axis == position else 1 for axis in range(len(dims))])
    return factor_of


def profile(amount, total, limit, skew):
    loads = [(1 << 20) // math.isqrt(grade ** skew) + 1 for grade in range(2, amount + 1)]
    surplus, holding = total - limit - (amount - 1), [1] * (amount - 1)
    while surplus > 0:
        movable = [i for i in range(amount - 1) if holding[i] < limit]
        whole, budget = sum([loads[i] for i in movable]), surplus
        for i in movable:
            addition = min(limit - holding[i], max(1, budget * loads[i] // whole), surplus)
            holding[i] = holding[i] + addition
            surplus = surplus - addition
    return np.array([limit] + holding)


def uneven_parts(key, number_of, total, most, lean):
    if number_of == 2:
        one = jax.random.randint(key, (), max(1, total - most), min(most, total - 1) + 1)
        return jnp.stack([one, total - one])
    sizes = jnp.asarray(profile(number_of, total, most, lean), jnp.int32)
    twos = (number_of - 1) // 2
    giver, taker = sizes[1:1 + 2 * twos:2], sizes[2:2 + 2 * twos:2]
    room = jnp.minimum(giver - 1, most - taker)
    moved = jax.random.randint(jax.random.fold_in(key, 1), (twos,), 0, 1 << 20) % (room + 1)
    sizes = sizes.at[1:1 + 2 * twos:2].set(giver - moved).at[2:2 + 2 * twos:2].set(taker + moved)
    return sizes[jax.random.permutation(jax.random.fold_in(key, 2), number_of)]


def scatter_about(rng, dims, width, reach, pieces=(), dtype=jnp.bfloat16):
    values = jax.random.normal(rng, dims, jnp.float32) * width
    if len(pieces) > 0:
        values = level_of(rng, dims, pieces, -0.22, 0.18) * values
    return jnp.clip(values, min=-reach, max=reach).astype(dtype)


def setup_inputs(seed: int = 0) -> dict:
    seeds = jax.random.split(jax.random.key(seed), 17)
    return {
        "tokens": scatter_about(seeds[0], (SEQS, LENGTH, D), 1.0, 6.0, ((0, 2), (1, 4))),
        "segments": jax.vmap(lambda own: jnp.searchsorted(jnp.cumsum(uneven_parts(own, SEGS, LENGTH, MOST, 3)), jnp.arange(LENGTH), side="right"))(jax.random.split(seeds[1], SEQS)).reshape((SEQS, LENGTH)).astype(jnp.int32),
        "w_qkv": scatter_about(seeds[2], (D, 3, D), D ** -0.5, 0.21875, ((0, 8), (2, 4))),
        "q_bias": scatter_about(seeds[3], (D,), 0.5, 3.0, ((0, 4),), jnp.float32),
        "v_bias": scatter_about(seeds[4], (D,), 0.5, 3.0, ((0, 4),), jnp.float32),
        "w_out": scatter_about(seeds[5], (D, D), (D // 16) ** -0.5, 0.875, ((0, 8), (1, 4))),
        "out_bias": scatter_about(seeds[6], (D,), 0.5, 3.0, (), jnp.float32),
        "gain_one": jnp.clip(1.0 + 0.15 * jax.random.normal(seeds[7], (D,), jnp.float32), 0.25, 1.75),
        "shift_one": scatter_about(seeds[8], (D,), 0.3, 2.0, (), jnp.float32),
        "w_in": scatter_about(seeds[9], (D, FF), D ** -0.5, 0.21875, ((0, 8), (1, 4))),
        "in_bias": scatter_about(seeds[10], (FF,), 0.5, 3.0, ((0, 4),), jnp.float32),
        "w_back": scatter_about(seeds[11], (D, FF), (FF // 2) ** -0.5, 0.15625, ((0, 8), (1, 4))),
        "back_bias": scatter_about(seeds[12], (D,), 0.5, 3.0, (), jnp.float32),
        "gain_two": jnp.clip(1.0 + 0.15 * jax.random.normal(seeds[13], (D,), jnp.float32), 0.25, 1.75),
        "shift_two": scatter_about(seeds[14], (D,), 0.3, 2.0, (), jnp.float32),
        "cotangent": scatter_about(seeds[15], (SEQS, LENGTH, D), 1.0, 6.0, ((0, 2), (1, 4))),
    }


@jax.custom_vjp
def low(v):
    return lax.optimization_barrier(v.astype(jnp.bfloat16)).astype(jnp.float32)

@jax.custom_vjp
def low_back(v):
    return v

def low_keep(v):
    return (low(v), None)

def low_pass(kept, grad):
    return (grad,)

def back_keep(v):
    return (v, None)

def back_low(kept, grad):
    return (low(grad),)
low.defvjp(low_keep, low_pass)
low_back.defvjp(back_keep, back_low)
highest = lax.Precision.HIGHEST

def layer_norm(value, gain, shift):
    mean = lax.optimization_barrier(jnp.mean(value, -1, keepdims=True))
    centered = value - mean
    var = lax.optimization_barrier(jnp.mean(centered * centered, -1, keepdims=True))
    return centered * lax.rsqrt(var + 1e-12) * gain + shift

def forward(x, seg, w_qkv, q_bias, v_bias, w_out, out_bias, gain_one, shift_one, w_in, in_bias, w_back, back_bias, gain_two, shift_two):
    length = x.shape[0]
    projected = jnp.einsum('td,dcf->tcf', x, w_qkv, precision=highest)
    query = low(low_back(projected[:, 0]) + q_bias)
    key = low(low_back(projected[:, 1]))
    value = low(low_back(projected[:, 2]) + v_bias)
    q_heads = query.reshape(length, HEADS, HEAD)
    k_heads = key.reshape(length, HEADS, HEAD)
    v_heads = value.reshape(length, HEADS, HEAD)
    raw = low_back(jnp.einsum('qhe,khe->hqk', q_heads, k_heads, precision=highest))
    same = seg[:, None] == seg[None, :]
    scores = jnp.where(same[None], raw * (1.0 / math.sqrt(HEAD)), -1e+30)
    peak = lax.optimization_barrier(jnp.max(scores, -1, keepdims=True))
    expo = jnp.exp(scores - peak)
    probs = expo / lax.optimization_barrier(jnp.sum(expo, -1, keepdims=True))
    probs_low = low(probs)
    context = jnp.einsum('hqk,khe->qhe', probs_low, v_heads, precision=highest).reshape(length, D)
    context = low(low_back(context))
    attended = low_back(jnp.dot(context, w_out.T, precision=highest)) + out_bias
    normed = layer_norm(x + attended, gain_one, shift_one)
    inner = low_back(jnp.dot(low(normed), w_in, precision=highest)) + in_bias
    active = low(jax.nn.gelu(inner, approximate=False))
    branch = low_back(jnp.dot(active, w_back.T, precision=highest)) + back_bias
    return layer_norm(normed + branch, gain_two, shift_two)

def reference(tokens, segments, w_qkv, q_bias, v_bias, w_out, out_bias, gain_one, shift_one, w_in, in_bias, w_back, back_bias, gain_two, shift_two, cotangent):
    params = tuple((a.astype(jnp.float32) for a in (w_qkv, q_bias, v_bias, w_out, out_bias, gain_one, shift_one, w_in, in_bias, w_back, back_bias, gain_two, shift_two)))

    def step(carry, item):
        x, seg, grad_out = item

        def local(xx, *weights):
            return forward(xx, seg, *weights)
        result, pull = jax.vjp(local, x.astype(jnp.float32), *params)
        grads = pull(grad_out.astype(jnp.float32))
        summed = tuple((c + g for c, g in zip(carry, grads[1:])))
        return (summed, (result.astype(jnp.bfloat16), grads[0]))
    start = tuple((jnp.zeros(p.shape, jnp.float32) for p in params))
    sums, (output, d_tokens) = lax.scan(step, start, (tokens, segments, cotangent))
    return (output, d_tokens, sums[0], sums[1], sums[2], sums[3], sums[4], sums[5], sums[6], sums[7], sums[8], sums[9], sums[10], sums[11], sums[12])
```

```python
import functools
import math

import jax
import jax.numpy as jnp
from jax import lax
from jax.experimental import pallas as pl
from jax.experimental.pallas import tpu as pltpu
from jax.sharding import PartitionSpec as P

HEAD = 64
NEG = -1e30
BF = jnp.bfloat16
F32 = jnp.float32
ALL = ("dp", "ctx", "tp")


def norm_parts(value):
    mean = jnp.mean(value, -1, keepdims=True)
    centered = value - mean
    rstd = lax.rsqrt(jnp.mean(centered * centered, -1, keepdims=True) + 1e-12)
    return (centered * rstd, rstd)


def norm_back(grad, normal, rstd, gain):
    d_gain = jnp.sum(grad * normal, 0)
    d_shift = jnp.sum(grad, 0)
    scaled = grad * gain
    d_value = rstd * (
        scaled
        - jnp.mean(scaled, -1, keepdims=True)
        - normal * jnp.mean(scaled * normal, -1, keepdims=True)
    )
    return (d_value, d_gain, d_shift)


def gelu_slope(inner):
    return 0.5 * (1.0 + lax.erf(inner / math.sqrt(2.0))) + inner * jnp.exp(
        -0.5 * inner * inner
    ) / math.sqrt(2.0 * math.pi)


def swap_with(value, axis, size, mask):
    return lax.ppermute(value, axis, [(i, i ^ mask) for i in range(size)])


def in_order(parts, me, axis=0):
    shape = list(parts[0].shape)
    shape.insert(axis, len(parts))
    out = jnp.zeros(tuple(shape), parts[0].dtype)
    for k, part in enumerate(parts):
        out = lax.dynamic_update_index_in_dim(out, part, me ^ k, axis)
    return out


def gather_axis(value, axis, size, me):
    parts = [value] + [swap_with(value, axis, size, k) for k in range(1, size)]
    return in_order(parts, me)


def exchange_axis(blocks, axis, size, me):
    parts = [lax.dynamic_index_in_dim(blocks, me, 0, keepdims=False)]
    for k in range(1, size):
        parts.append(
            swap_with(lax.dynamic_index_in_dim(blocks, me ^ k, 0, keepdims=False), axis, size, k)
        )
    return parts


def gather_weight(shard, sizes, me):
    nd, nc, nt = sizes
    d, c, z = me
    zset = gather_axis(shard, "tp", nt, z)
    if nd != 2:
        full = lax.all_gather(zset, ("dp", "ctx"), axis=1, tiled=False)
        return full
    half = nt // 2
    px = swap_with(zset, "dp", nd, 1)
    py = swap_with(zset, "ctx", nc, 2)
    pd = jnp.concatenate(
        [swap_with(px[:half], "ctx", nc, 2), swap_with(py[half:], "dp", nd, 1)], 0
    )
    own = [zset, px, py, pd]
    other = [swap_with(v, "ctx", nc, 1) for v in own]
    row = d * nc + c
    out = jnp.zeros((nt, nd * nc) + shard.shape, shard.dtype)
    for core, group in ((0, own), (1, other)):
        for k, part in enumerate(group):
            at = row ^ (core + (nc if k in (1, 3) else 0) + (2 if k in (2, 3) else 0))
            out = lax.dynamic_update_index_in_dim(out, part, at, 1)
    return out


def add_low(a, b):
    return (a.astype(F32) + b.astype(F32)).astype(BF)


def scatter_weight(grad, sizes, me):
    nd, nc, nt = sizes
    d, c, z = me
    if nd != 2:
        part = lax.psum_scatter(
            grad.astype(F32), ("dp", "ctx"), scatter_dimension=1, tiled=False
        ).astype(BF)
    else:
        rows, cols = grad.shape[2:]
        view = grad.reshape(nt, nd, nc // 2, 2, rows, cols)
        core = c % 2
        y = c // 2
        keep = lax.dynamic_index_in_dim(view, core, 3, keepdims=False)
        send = lax.dynamic_index_in_dim(view, 1 - core, 3, keepdims=False)
        a = add_low(keep, swap_with(send, "ctx", nc, 1))
        half = nt // 2
        one, two = a[:half], a[half:]
        r1 = swap_with(lax.dynamic_index_in_dim(one, 1 - d, 1, keepdims=False), "dp", nd, 1)
        r2 = swap_with(lax.dynamic_index_in_dim(two, 1 - y, 2, keepdims=False), "ctx", nc, 2)
        one = add_low(lax.dynamic_index_in_dim(one, d, 1, keepdims=False), r1)
        two = add_low(lax.dynamic_index_in_dim(two, y, 2, keepdims=False), r2)
        r1 = swap_with(lax.dynamic_index_in_dim(one, 1 - y, 1, keepdims=False), "ctx", nc, 2)
        r2 = swap_with(lax.dynamic_index_in_dim(two, 1 - d, 1, keepdims=False), "dp", nd, 1)
        one = add_low(lax.dynamic_index_in_dim(one, y, 1, keepdims=False), r1)
        two = add_low(lax.dynamic_index_in_dim(two, d, 1, keepdims=False), r2)
        part = jnp.concatenate([one, two], 0)
    parts = exchange_axis(part, "tp", nt, z)
    return sum(p.astype(F32) for p in parts)


def transpose_ctx_tp(value, n):
    pairs = [(a * n + b, b * n + a) for a in range(n) for b in range(n)]
    return lax.ppermute(value, ("ctx", "tp"), pairs)


def pair_perm(value, sizes, kd, kt):
    nd, _, nt = sizes
    pairs = [
        (a * nt + b, (a ^ kd) * nt + (b ^ kt)) for a in range(nd) for b in range(nt)
    ]
    return lax.ppermute(value, ("dp", "tp"), pairs)


def gather_heads(shard, sizes, me):
    nd, nc, nt = sizes
    d, c, z = me
    mine = transpose_ctx_tp(shard, nc)
    if nd != 2:
        return lax.all_gather(mine, ("dp", "tp"), axis=0, tiled=True)
    out = jnp.zeros((nd * nt,) + shard.shape, shard.dtype)
    for kd in range(nd):
        for kt in range(nt):
            part = pair_perm(mine, sizes, kd, kt) if kd or kt else mine
            out = lax.dynamic_update_index_in_dim(out, part, (d ^ kd) * nt + (z ^ kt), 0)
    return out.reshape((nd * nt * shard.shape[0],) + shard.shape[1:])


def scatter_heads(grad, sizes, me):
    nd, nc, nt = sizes
    d, c, z = me
    blocks = grad.reshape((nd * nt, grad.shape[0] // (nd * nt)) + grad.shape[1:])
    if nd != 2:
        total = lax.psum_scatter(
            blocks.astype(F32), ("dp", "tp"), scatter_dimension=0, tiled=False
        )
    else:
        total = 0.0
        for kd in range(nd):
            for kt in range(nt):
                block = lax.dynamic_index_in_dim(
                    blocks, (d ^ kd) * nt + (z ^ kt), 0, keepdims=False
                )
                if kd or kt:
                    block = pair_perm(block, sizes, kd, kt)
                total = total + block.astype(F32)
    return transpose_ctx_tp(total, nc)


def sum_all(value, sizes):
    nd, nc, nt = sizes
    if nd != 2:
        return lax.psum(value, ALL)
    for axis, size, mask in (
        ("ctx", nc, 1),
        ("ctx", nc, 2),
        ("dp", nd, 1),
        ("tp", nt, 1),
        ("tp", nt, 2),
    ):
        value = value + swap_with(value, axis, size, mask)
    return value


def block_rows(qb, half, ln):
    hl = ln // 2
    whole = qb < 4
    b = jnp.where(whole, qb, qb - 4)
    r0 = jnp.where(whole, 2 * ln * b, (4 * b + 1) * ln + hl * half)
    r1 = jnp.where(whole, r0 + hl, r0 + 2 * ln)
    o0 = jnp.where(whole, 3 * hl * b, 6 * hl * b + ln)
    o1 = jnp.where(whole, o0 + hl, o0 + 3 * hl)
    seq = jnp.where(whole, 0, 1)
    m = lambda v: pl.multiple_of(v, 128)
    return m(r0), m(r1), m(o0), m(o1), seq


def two(ref, r0, r1, hl, cols):
    return jnp.concatenate([ref[pl.ds(r0, hl), cols], ref[pl.ds(r1, hl), cols]], 0)


def two_lanes(ref, rows, r0, r1, hl):
    return jnp.concatenate([ref[rows, pl.ds(r0, hl)], ref[rows, pl.ds(r1, hl)]], 1)


def dot_nt(a, b):
    return lax.dot_general(a, b, (((1,), (1,)), ((), ())), preferred_element_type=F32)


def dot_nn(a, b):
    return lax.dot_general(a, b, (((1,), (0,)), ((), ())), preferred_element_type=F32)


def fill_transposed(kv, kvt, ln, nc, heads):
    @pl.loop(0, nc)
    def _(j):
        for seq in range(2):
            rows = pl.ds(pl.multiple_of((2 * j + seq) * ln, ln), ln)
            for h in range(heads):
                kvt[seq * heads + h, :, pl.ds(pl.multiple_of(j * ln, ln), ln)] = kv[
                    rows, 128 * h : 128 * h + 128
                ].T


def attend_kernel(heads, ln, nc, info, q_ref, kv, seg_col, seg_row, out, lse, ctx_t, s_scr, kvt, acc):
    half = info[12]
    hl = ln // 2
    fill_transposed(kv, kvt, ln, nc, heads)

    @pl.loop(0, 6)
    def _(qb):
        r0, r1, o0, o1, seq = block_rows(qb, half, ln)
        lo, hi = info[qb], info[6 + qb]
        sq = two_lanes(seg_row, slice(0, 1), r0, r1, hl)
        q = [two(q_ref, r0, r1, hl, slice(128 * h, 128 * h + 128)) for h in range(heads)]

        def score(j, peaks):
            rows = pl.ds(pl.multiple_of((2 * j + seq) * ln, ln), ln)
            same = seg_col[rows, :] == sq
            new = []
            for h in range(heads):
                s = dot_nt(kv[rows, 128 * h : 128 * h + 128], q[h])
                s = jnp.where(same, s, NEG)
                s_scr[h, pl.ds(pl.multiple_of(j * ln, ln), ln), :] = s
                new.append(jnp.maximum(peaks[h], jnp.max(s, 0, keepdims=True)))
            return tuple(new)

        peaks = lax.fori_loop(
            lo, hi, score, tuple(jnp.full((1, ln), NEG, F32) for _ in range(heads))
        )
        acc[...] = jnp.zeros_like(acc)

        def collect(j, sums):
            keys = pl.ds(pl.multiple_of(j * ln, ln), ln)
            new = []
            for h in range(heads):
                p = jnp.exp(s_scr[h, keys, :] - peaks[h])
                new.append(sums[h] + jnp.sum(p, 0, keepdims=True))
                acc[h] += dot_nn(kvt[seq * heads + h, :, keys], p.astype(BF))
            return tuple(new)

        sums = lax.fori_loop(
            lo, hi, collect, tuple(jnp.zeros((1, ln), F32) for _ in range(heads))
        )
        whole = []
        for h in range(heads):
            one = acc[h, HEAD:, :] / sums[h]
            whole.append(one)
            line = peaks[h] + jnp.log(sums[h])
            for part, at in ((0, o0), (hl, o1)):
                ctx_t[HEAD * h : HEAD * h + HEAD, pl.ds(at, hl)] = one[:, part : part + hl]
                lse[h : h + 1, pl.ds(at, hl)] = line[:, part : part + hl]
        turned = jnp.concatenate(whole, 0).T.astype(BF)
        out[pl.ds(o0, hl), :] = turned[:hl]
        out[pl.ds(o1, hl), :] = turned[hl:]


def attend(info, q_ref, kv, seg_col, seg_row, heads, ln, nc):
    rows = 3 * ln // 2 * nc
    vm = pl.BlockSpec(memory_space=pltpu.VMEM)
    return pl.pallas_call(
        functools.partial(attend_kernel, heads, ln, nc),
        out_shape=(
            jax.ShapeDtypeStruct((rows, heads * HEAD), BF),
            jax.ShapeDtypeStruct((8, rows), F32),
            jax.ShapeDtypeStruct((heads * HEAD, rows), F32),
        ),
        in_specs=[pl.BlockSpec(memory_space=pltpu.SMEM), vm, vm, vm, vm],
        out_specs=(vm, vm, vm),
        scratch_shapes=[
            pltpu.VMEM((heads, nc * ln, ln), F32),
            pltpu.VMEM((2 * heads, 128, nc * ln), BF),
            pltpu.VMEM((heads, 128, ln), F32),
        ],
        compiler_params=pltpu.CompilerParams(vmem_limit_bytes=32 << 20),
        cost_estimate=pl.CostEstimate(
            flops=8 * heads * rows * nc * ln * 128,
            bytes_accessed=8 << 20,
            transcendentals=heads * rows * nc * ln,
        ),
        name="attend",
    )(info, q_ref, kv, seg_col, seg_row)


def attend_back_kernel(
    heads, ln, nc, info, q_ref, kv, d_out, seg_col, seg_row, lse, ctx_t, d_q, d_kv, d_bias, dkv, kvt, dqt
):
    half = info[12]
    hl = ln // 2
    fill_transposed(kv, kvt, ln, nc, heads)
    dkv[...] = jnp.zeros_like(dkv)
    d_bias[...] = jnp.zeros_like(d_bias)

    @pl.loop(0, nc)
    def _(c):
        rows = pl.ds(pl.multiple_of((2 * c + 1) * ln, ln), ln)
        d_q[rows, :] = jnp.zeros((ln, heads * HEAD), BF)

    @pl.loop(0, 6)
    def _(qb):
        r0, r1, o0, o1, seq = block_rows(qb, half, ln)
        lo, hi = info[qb], info[6 + qb]
        sq = two_lanes(seg_row, slice(0, 1), r0, r1, hl)
        q, do, line, delta = [], [], [], []
        for h in range(heads):
            q.append(two(q_ref, r0, r1, hl, slice(128 * h, 128 * h + 128)))
            do.append(two(d_out, o0, o1, hl, slice(128 * h, 128 * h + 128)))
            line.append(two_lanes(lse, slice(h, h + 1), o0, o1, hl))
            turned = do[h].astype(F32).T[HEAD:, :]
            kept = two_lanes(ctx_t, slice(HEAD * h, HEAD * h + HEAD), o0, o1, hl)
            delta.append(jnp.sum(turned * kept, 0, keepdims=True))
        dqt[...] = jnp.zeros_like(dqt)

        @pl.loop(lo, hi)
        def _(j):
            rows = pl.ds(pl.multiple_of((2 * j + seq) * ln, ln), ln)
            keys = pl.ds(pl.multiple_of(j * ln, ln), ln)
            same = seg_col[rows, :] == sq
            for h in range(heads):
                kvh = kv[rows, 128 * h : 128 * h + 128]
                p = jnp.where(same, jnp.exp(dot_nt(kvh, q[h]) - line[h]), 0.0)
                ds = (p * (dot_nt(kvh, do[h]) - delta[h])).astype(BF)
                dkv[rows, 128 * h : 128 * h + 128] += dot_nn(ds, q[h]) + dot_nn(
                    p.astype(BF), do[h]
                )
                dqt[h] += dot_nn(kvt[seq * heads + h, :, keys], ds)

        turned = jnp.concatenate([dqt[h, :HEAD, :] for h in range(heads)], 0).T * 0.125
        d_bias[0:1, heads * 128 :] += jnp.sum(turned, 0, keepdims=True)
        low = turned.astype(BF)
        d_q[pl.ds(r0, hl), :] = low[:hl]
        d_q[pl.ds(r1, hl), :] = low[hl:]

    @pl.loop(0, 2 * nc)
    def _(c):
        rows = pl.ds(pl.multiple_of(c * ln, ln), ln)
        for h in range(heads):
            got = dkv[rows, 128 * h : 128 * h + 128]
            d_bias[0:1, 128 * h : 128 * h + 128] += jnp.sum(got, 0, keepdims=True)
            d_kv[rows, 128 * h : 128 * h + 128] = got.astype(BF)


def attend_back(info, q_ref, kv, d_out, seg_col, seg_row, lse, ctx_t, heads, ln, nc):
    rows = 3 * ln // 2 * nc
    vm = pl.BlockSpec(memory_space=pltpu.VMEM)
    return pl.pallas_call(
        functools.partial(attend_back_kernel, heads, ln, nc),
        out_shape=(
            jax.ShapeDtypeStruct((2 * nc * ln, heads * HEAD), BF),
            jax.ShapeDtypeStruct((2 * nc * ln, heads * 128), BF),
            jax.ShapeDtypeStruct((8, heads * (HEAD + 128)), F32),
        ),
        in_specs=[pl.BlockSpec(memory_space=pltpu.SMEM)] + [vm] * 7,
        out_specs=(vm, vm, vm),
        scratch_shapes=[
            pltpu.VMEM((2 * nc * ln, heads * 128), F32),
            pltpu.VMEM((2 * heads, 128, nc * ln), BF),
            pltpu.VMEM((heads, 128, ln), F32),
        ],
        compiler_params=pltpu.CompilerParams(vmem_limit_bytes=40 << 20),
        cost_estimate=pl.CostEstimate(
            flops=20 * heads * rows * nc * ln * 128,
            bytes_accessed=14 << 20,
            transcendentals=heads * rows * nc * ln,
        ),
        name="attend_back",
    )(info, q_ref, kv, d_out, seg_col, seg_row, lse, ctx_t)


MESH = pl.DeviceIdType.MESH


class Copies:
    def __init__(self, send, recv):
        self.send, self.recv, self.open = send, recv, []

    def make(self, i, src, dst, device):
        return pltpu.make_async_remote_copy(
            src_ref=src,
            dst_ref=dst,
            send_sem=self.send.at[i],
            recv_sem=self.recv.at[i],
            device_id=device,
            device_id_type=MESH,
        )

    def start(self, i, src, dst, device):
        copy = self.make(i, src, dst, device)
        copy.start()
        self.open.append(copy)

    def arrived(self, i, dst, device):
        self.make(i, dst, dst, device).wait_recv()

    def sent(self):
        for copy in self.open:
            copy.wait_send()
        self.open = []


def forward_kernel(
    heads,
    ln,
    tok2,
    seg2,
    w_head,
    b_head,
    b_unit,
    w_o,
    w_i,
    w_b,
    ctx_all,
    x_out,
    q_out,
    kv_out,
    wh_out,
    o_full,
    i_full,
    b_full,
    bu_full,
    lse,
    ctx_t,
    seg,
    x2,
    wh,
    bh,
    q_scr,
    kv,
    s_scr,
    kvt,
    acc,
    segc,
    segr,
    context,
    send,
    recv,
    local,
):
    d, c, z = (lax.axis_index(n) for n in ALL)
    nc = 4
    hl = ln // 2
    own = ln + hl
    half = z % 2
    wr = w_i.shape[0]
    units = w_i.shape[1]
    row = d * nc + c
    rc = Copies(send, recv)
    at_c = lambda k: (d, c ^ k, z)
    at_x = (1 - d, c, z)
    at_xz = lambda kd, kt: (d ^ kd, c, z ^ kt)
    across = (d, z, c)
    pairs = [(kd, kt) for kd in range(2) for kt in range(4) if kd or kt]

    barrier = pltpu.get_barrier_semaphore()
    everyone = [at_c(k) for k in (1, 2, 3)] + [at_xz(*p) for p in pairs]
    for device in everyone:
        pl.semaphore_signal(barrier, inc=1, device_id=device, device_id_type=MESH)

    @pl.when(c != z)
    def _():
        pl.semaphore_signal(barrier, inc=1, device_id=across, device_id_type=MESH)

    pl.semaphore_wait(barrier, len(everyone) + jnp.where(c != z, 1, 0))

    number = iter(range(100))
    locals_ = []

    def copy_here(src, dst):
        copy = pltpu.make_async_copy(src, dst, local.at[len(locals_)])
        copy.start()
        locals_.append(copy)
        return copy

    n_ty, n_tc, n_tf = next(number), next(number), next(number)
    tok_at = lambda i: x2.at[pl.ds(2 * i, 2)]
    rc.start(n_ty, tok2, tok_at(c), at_c(2))
    n_wa, n_ba = next(number), next(number)
    wh_at = lambda r: wh.at[pl.ds(pl.multiple_of(r * wr, wr), wr)]

    def across_copies():
        return (
            rc.make(n_wa, w_head, wh_at(row), across),
            rc.make(n_ba, b_head, bh, across),
        )

    @pl.when(c != z)
    def _():
        for copy in across_copies():
            copy.start()

    mine = copy_here(tok2, tok_at(c))
    here = [
        pltpu.make_async_copy(w_head, wh_at(row), local.at[30]),
        pltpu.make_async_copy(b_head, bh, local.at[31]),
    ]

    @pl.when(c == z)
    def _():
        for copy in here:
            copy.start()

    rc.start(n_tc, tok2, tok_at(c), at_c(1))
    n_seg = [next(number) for _ in range(3)]
    for k in (1, 2, 3):
        rc.start(n_seg[k - 1], seg2, seg.at[c], at_c(k))
    seg_here = copy_here(seg2, seg.at[c])
    bu_here = copy_here(b_unit, bu_full.at[z])
    i_at = lambda r, t: i_full.at[r, :, pl.ds(pl.multiple_of(t * units, 128), units)]
    b_at = lambda r, t: b_full.at[r, :, pl.ds(pl.multiple_of(t * units, 128), units)]
    o_at = lambda r, t: o_full.at[t, r]
    w_here = [
        copy_here(w_o, o_at(row, z)),
        copy_here(w_i, i_at(row, z)),
        copy_here(w_b, b_at(row, z)),
    ]

    row_w = d * nc + z

    @pl.when(c != z)
    def _():
        for copy in across_copies():
            copy.wait_recv()

    @pl.when(c == z)
    def _():
        for copy in here:
            copy.wait()

    n_wx = [next(number) for _ in pairs]
    for i, p in zip(n_wx, pairs):
        rc.start(i, wh_at(row_w), wh_at(row_w), at_xz(*p))

    n_bu = [next(number) for _ in range(3)]
    n_z = [[next(number) for _ in range(3)] for _ in range(3)]
    full_at = (o_at, i_at, b_at)
    for k in (1, 2, 3):
        rc.start(n_bu[k - 1], b_unit, bu_full.at[z], at_xz(0, k))
    for w, src in enumerate((w_o, w_i, w_b)):
        for k in (1, 2, 3):
            rc.start(n_z[w][k - 1], src, full_at[w](row, z), at_xz(0, k))

    rc.arrived(n_ty, tok_at(c ^ 2), at_c(2))
    rc.start(n_tf, tok_at(c ^ 2), tok_at(c ^ 2), at_c(1))
    for k in (1, 2, 3):
        rc.arrived(n_seg[k - 1], seg.at[c ^ k], at_c(k))
    seg_here.wait()
    q_scr[...] = jnp.zeros_like(q_scr)
    for i in range(nc):
        for s in range(2):
            line = seg[i, s : s + 1, :].astype(F32)
            segr[2 * i + s, 0:1, :] = line
            segc[2 * i + s] = jnp.broadcast_to(line, (128, ln)).T
    for i, (kd, kt) in zip(n_wx, pairs):
        rc.arrived(i, wh_at((d ^ kd) * nc + (z ^ kt)), at_xz(kd, kt))
    mine.wait()
    rc.arrived(n_tc, tok_at(c ^ 1), at_c(1))
    rc.arrived(n_tf, tok_at(c ^ 3), at_c(1))
    x_here = copy_here(x2, x_out)
    wh_here = copy_here(wh, wh_out)
    wide = heads * 128

    @pl.loop(0, 2 * nc)
    def _(i):
        x = x2[i]
        rows = pl.ds(pl.multiple_of(i * ln, ln), ln)
        got = (dot_nn(x, wh[:, :wide]) + bh[0:1, :wide]).astype(BF)
        kv[rows, :] = got
        qp = ((dot_nn(x, wh[:, wide:]) + bh[0:1, wide:]).astype(BF).astype(F32) * 0.125).astype(BF)
        for h in range(heads):
            q_scr[rows, 128 * h : 128 * h + HEAD] = qp[:, HEAD * h : HEAD * h + HEAD]

    q_here = copy_here(q_scr, q_out)
    kv_here = copy_here(kv, kv_out)

    @pl.loop(0, nc)
    def _(j):
        for s in range(2):
            rows = pl.ds(pl.multiple_of((2 * j + s) * ln, ln), ln)
            for h in range(heads):
                kvt[s * heads + h, :, pl.ds(pl.multiple_of(j * ln, ln), ln)] = kv[
                    rows, 128 * h : 128 * h + 128
                ].T

    groups = ((0, 1), (2,))
    row_at = (lambda r: o_full.at[:, r], lambda r: i_full.at[r], lambda r: b_full.at[r])
    hw = wr // 2
    low_at = (
        lambda r: o_full.at[:, r, pl.ds(0, hw)],
        lambda r: i_full.at[r, pl.ds(0, hw)],
        lambda r: b_full.at[r, pl.ds(0, hw)],
    )
    high_at = (
        lambda r: o_full.at[:, r, pl.ds(hw, hw)],
        lambda r: i_full.at[r, pl.ds(hw, hw)],
        lambda r: b_full.at[r, pl.ds(hw, hw)],
    )
    n_x, n_y, n_d1, n_d2 = ([next(number) for _ in range(3)] for _ in range(4))
    n_c = [[next(number) for _ in range(4)] for _ in range(3)]

    def stage_plane(w):
        w_here[w].wait()
        for k in (1, 2, 3):
            rc.arrived(n_z[w][k - 1], full_at[w](row, z ^ k), at_xz(0, k))
        rc.start(n_x[w], row_at[w](row), row_at[w](row), at_x)
        rc.start(n_y[w], row_at[w](row), row_at[w](row), at_c(2))
        rc.start(n_c[w][0], row_at[w](row), row_at[w](row), at_c(1))

    row_x, row_y, row_d = row ^ 4, row ^ 2, row ^ 6

    def stage_corner(w):
        rc.arrived(n_x[w], row_at[w](row_x), at_x)
        rc.start(n_d1[w], low_at[w](row_x), low_at[w](row_x), at_c(2))
        rc.start(n_c[w][1], row_at[w](row_x), row_at[w](row_x), at_c(1))
        rc.arrived(n_y[w], row_at[w](row_y), at_c(2))
        rc.start(n_d2[w], high_at[w](row_y), high_at[w](row_y), at_x)
        rc.start(n_c[w][2], row_at[w](row_y), row_at[w](row_y), at_c(1))

    def stage_core(w):
        rc.arrived(n_d1[w], low_at[w](row_d), at_c(2))
        rc.arrived(n_d2[w], high_at[w](row_d), at_x)
        rc.start(n_c[w][3], row_at[w](row_d), row_at[w](row_d), at_c(1))

    def stage_end(w):
        for i, r in zip(n_c[w], (row, row_x, row_y, row_d)):
            rc.arrived(i, row_at[w](r ^ 1), at_c(1))

    def block(qb):
        r0, r1, o0, o1, seq = block_rows(qb, half, ln)
        b0 = jnp.where(qb < 4, qb, 2 * (qb - 4))
        b1 = jnp.where(qb < 4, qb, 2 * (qb - 4) + 1)
        s0 = pl.multiple_of(jnp.where(qb < 4, 0, hl * half), 128)
        s1 = pl.multiple_of(jnp.where(qb < 4, hl, hl * half), 128)
        sq = jnp.concatenate(
            [
                segr[2 * b0 + seq, 0:1, pl.ds(s0, hl)],
                segr[2 * b1 + seq, 0:1, pl.ds(s1, hl)],
            ],
            1,
        )
        q = [two(q_scr, r0, r1, hl, slice(128 * h, 128 * h + 128)) for h in range(heads)]

        def score(j, peaks):
            rows = pl.ds(pl.multiple_of((2 * j + seq) * ln, ln), ln)
            key_seg = segc[2 * j + seq]
            same = jnp.concatenate([key_seg, key_seg], 1) == sq
            new = []
            for h in range(heads):
                s = dot_nt(kv[rows, 128 * h : 128 * h + 128], q[h])
                s = jnp.where(same, s, NEG)
                s_scr[h, pl.ds(pl.multiple_of(j * ln, ln), ln), :] = s
                new.append(jnp.maximum(peaks[h], jnp.max(s, 0, keepdims=True)))
            return tuple(new)

        peaks = lax.fori_loop(
            0, nc, score, tuple(jnp.full((1, ln), NEG, F32) for _ in range(heads))
        )
        acc[...] = jnp.zeros_like(acc)

        def collect(j, sums):
            keys = pl.ds(pl.multiple_of(j * ln, ln), ln)
            new = []
            for h in range(heads):
                p = jnp.exp(s_scr[h, keys, :] - peaks[h])
                new.append(sums[h] + jnp.sum(p, 0, keepdims=True))
                acc[h] += dot_nn(kvt[seq * heads + h, :, keys], p.astype(BF))
            return tuple(new)

        sums = lax.fori_loop(
            0, nc, collect, tuple(jnp.zeros((1, ln), F32) for _ in range(heads))
        )
        whole = []
        for h in range(heads):
            one = acc[h, HEAD:, :] / sums[h]
            whole.append(one)
            line = peaks[h] + jnp.log(sums[h])
            for part, at in ((0, o0), (hl, o1)):
                ctx_t[HEAD * h : HEAD * h + HEAD, pl.ds(at, hl)] = one[:, part : part + hl]
                lse[h : h + 1, pl.ds(at, hl)] = line[:, part : part + hl]
        turned = jnp.concatenate(whole, 0).T.astype(BF)
        context[pl.ds(o0, hl), :] = turned[:hl]
        context[pl.ds(o1, hl), :] = turned[hl:]

    stage_plane(0)
    stage_plane(1)
    pl.loop(0, 2)(block)
    stage_plane(2)
    pl.loop(2, 4)(block)
    stage_corner(0)
    stage_corner(1)
    pl.loop(4, 6)(block)

    n_ctx = [next(number) for _ in range(3)]
    ctx_at = lambda i: context.at[pl.ds(pl.multiple_of(i * own, 128), own)]
    for k in (1, 2, 3):
        rc.start(n_ctx[k - 1], ctx_at(c ^ k), ctx_all.at[c], at_c(k))
    ctx_here = copy_here(ctx_at(c), ctx_all.at[c])
    stage_corner(2)
    stage_core(0)
    stage_core(1)
    for k in (1, 2, 3):
        rc.arrived(n_ctx[k - 1], ctx_all.at[c ^ k], at_c(k))
        rc.arrived(n_bu[k - 1], bu_full.at[z ^ k], at_xz(0, k))
    stage_core(2)
    for w in range(3):
        stage_end(w)
    for copy in (bu_here, x_here, wh_here, q_here, kv_here, ctx_here):
        copy.wait()
    rc.sent()

    @pl.when(c != z)
    def _():
        for copy in across_copies():
            copy.wait_send()


def forward(tok2, seg2, w_head, b_head, b_unit, w_o, w_i, w_b, heads):
    ln, width = tok2.shape[1:]
    wr, units = w_i.shape
    group = w_o.shape[1]
    nc, nt, nr = 4, 4, 8
    rows = 3 * ln // 2 * nc
    hb = pl.BlockSpec(memory_space=pl.ANY)
    vm = pl.BlockSpec(memory_space=pltpu.VMEM)
    sds = jax.ShapeDtypeStruct
    return pl.pallas_call(
        functools.partial(forward_kernel, heads, ln),
        out_shape=(
            sds((nc, 3 * ln // 2, group), BF),
            sds((2 * nc, ln, width), BF),
            sds((2 * nc * ln, heads * 128), BF),
            sds((2 * nc * ln, heads * 128), BF),
            sds((nr * wr, 3 * group), BF),
            sds((nt, nr, wr, group), BF),
            sds((nr, wr, nt * units), BF),
            sds((nr, wr, nt * units), BF),
            sds((nt, 8, units), F32),
            sds((8, rows), F32),
            sds((group, rows), F32),
            sds((nc, 8, ln), jnp.int32),
        ),
        in_specs=[hb] * 8,
        out_specs=(hb,) * 9 + (vm,) * 3,
        scratch_shapes=[
            pltpu.VMEM((2 * nc, ln, width), BF),
            pltpu.VMEM((nr * wr, 3 * group), BF),
            pltpu.VMEM((8, 3 * group), F32),
            pltpu.VMEM((2 * nc * ln, heads * 128), BF),
            pltpu.VMEM((2 * nc * ln, heads * 128), BF),
            pltpu.VMEM((heads, nc * ln, ln), F32),
            pltpu.VMEM((2 * heads, 128, nc * ln), BF),
            pltpu.VMEM((heads, 128, ln), F32),
            pltpu.VMEM((2 * nc, ln, 128), F32),
            pltpu.VMEM((2 * nc, 8, ln), F32),
            pltpu.VMEM((rows, group), BF),
            pltpu.SemaphoreType.DMA((80,)),
            pltpu.SemaphoreType.DMA((80,)),
            pltpu.SemaphoreType.DMA((32,)),
        ],
        compiler_params=pltpu.CompilerParams(
            vmem_limit_bytes=40 << 20, collective_id=0, has_side_effects=True
        ),
        name="forward",
    )(tok2, seg2, w_head, b_head, b_unit, w_o, w_i, w_b)


def head_order(kinds, heads):
    lead = kinds[0].shape[:-1]
    q, k, v = (a.reshape(lead + (heads, HEAD)) for a in kinds)
    kv = jnp.concatenate([k, v], -1).reshape(lead + (heads * 2 * HEAD,))
    return jnp.concatenate([kv, q.reshape(lead + (heads * HEAD,))], -1)


def head_kinds(value, heads):
    lead = value.shape[:-1]
    kv = value[..., : heads * 2 * HEAD].reshape(lead + (heads, 2, HEAD))
    flat = lambda a: a.reshape(lead + (heads * HEAD,))
    return value[..., heads * 2 * HEAD :], flat(kv[..., 0, :]), flat(kv[..., 1, :])


def forward_plain(sizes, me, tok2, seg2, w_head, b_head, b_unit, w_o, w_i, w_b, heads):
    nd, nc, nt = sizes
    d, c, z = me
    ln, width = tok2.shape[1:]
    hl = ln // 2
    half = z % 2
    group = w_o.shape[1]
    seg_all = gather_axis(seg2, "ctx", nc, c)
    x2 = gather_axis(tok2, "ctx", nc, c).reshape(2 * nc, ln, width)
    wh = gather_heads(w_head, sizes, me)
    bh = transpose_ctx_tp(b_head, nc)[0]
    b_all = gather_axis(b_unit, "tp", nt, z)
    gather = lambda w: lax.all_gather(
        lax.all_gather(w, "tp", axis=1, tiled=True), ("dp", "ctx"), axis=0, tiled=True
    )
    o_full = jnp.transpose(gather(w_o).reshape(width, nt, group), (1, 0, 2))
    proj = (jnp.dot(x2.reshape(-1, width), wh, preferred_element_type=F32) + bh).astype(BF)
    kv = proj[:, : 2 * group]
    q = (proj[:, 2 * group :].astype(F32) * 0.125).astype(BF).reshape(-1, heads, HEAD)
    q = jnp.concatenate([q, jnp.zeros_like(q)], -1).reshape(-1, heads * 128)
    info, seg_col, seg_row = key_blocks(seg_all, half, ln, nc)
    context, lse, ctx_t = attend(info, q, kv, seg_col, seg_row, heads, ln, nc)
    ctx_all = in_order(exchange_axis(context.reshape(nc, ln + hl, group), "ctx", nc, c), c)
    return (
        ctx_all,
        x2,
        q,
        kv,
        wh,
        o_full,
        gather(w_i),
        gather(w_b),
        b_all,
        lse,
        ctx_t,
        seg_all,
    )


def key_blocks(seg_all, half, ln, nc):
    hl = ln // 2
    seg2 = seg_all[:, :2]
    flat = jnp.transpose(seg2, (1, 0, 2)).reshape(2, nc * ln)
    first = jnp.concatenate([seg2[:, 0, 0], jnp.take(seg2[0::2, 1], half * hl, axis=1)])
    last = jnp.concatenate([seg2[:, 0, -1], jnp.take(seg2[1::2, 1], half * hl + hl - 1, axis=1)])
    of = jnp.concatenate(
        [
            jnp.broadcast_to(flat[:1], (nc, nc * ln)),
            jnp.broadcast_to(flat[1:], (nc // 2, nc * ln)),
        ],
        0,
    )
    lo = jnp.sum(of < first[:, None], 1) // ln
    hi = (jnp.sum(of <= last[:, None], 1) + ln - 1) // ln
    info = jnp.concatenate([lo, hi, half[None]]).astype(jnp.int32)
    seg_flat = seg2.reshape(2 * nc * ln)
    return info, seg_flat[:, None], seg_flat[None, :]


def per_device(
    sizes,
    tokens,
    segments,
    w_qkv,
    q_bias,
    v_bias,
    w_out,
    out_bias,
    gain_one,
    shift_one,
    w_in,
    in_bias,
    w_back,
    back_bias,
    gain_two,
    shift_two,
    cotangent,
):
    nd, nc, nt = sizes
    seqs, ln, width = tokens.shape
    hl = ln // 2
    group = w_out.shape[1]
    heads = group // HEAD
    units = w_in.shape[1]
    wr = w_in.shape[0]
    d, c, z = (lax.axis_index(n) for n in ALL)
    me = (d, c, z)
    whole_of = lambda t: (3 * t + 1) // 2
    shared_of = lambda t: 1 + 3 * (t // 2)
    half_of = lambda t: t % 2
    sf, sh, half = whole_of(z), shared_of(z), half_of(z)

    def own_rows(a):
        one = lax.dynamic_index_in_dim(a, sf, 0, keepdims=False)
        two_ = lax.dynamic_index_in_dim(a, sh, 0, keepdims=False)
        return jnp.concatenate([one, lax.dynamic_slice_in_dim(two_, half * hl, hl, 0)], 0)

    def own_pair(a):
        return jnp.stack(
            [
                lax.dynamic_index_in_dim(a, sf, 0, keepdims=False),
                lax.dynamic_index_in_dim(a, sh, 0, keepdims=False),
            ],
            0,
        )

    tok2 = own_pair(tokens)
    seg2 = jnp.concatenate([own_pair(segments), jnp.zeros((6, ln), jnp.int32)], 0)
    w_head = head_order([w_qkv[:, i] for i in range(3)], heads)
    b_head = head_order([q_bias, jnp.zeros_like(q_bias), v_bias], heads)
    b_head = jnp.broadcast_to(b_head[None], (8, 3 * group))
    b_unit = jnp.broadcast_to(in_bias[None], (8, units))
    args = (tok2, seg2, w_head, b_head, b_unit, w_out, w_in, w_back, heads)
    got = forward(*args) if sizes == (2, 4, 4) else forward_plain(sizes, me, *args)
    ctx_all, x2, q, kv, wh, w_o, w_i, w_b, b_in, lse, ctx_t, seg_all = got
    x2 = x2.reshape(2 * nc * ln, width)
    w_o = w_o.reshape(nt, width, group)
    w_i = w_i.reshape(width, nt * units)
    w_b = w_b.reshape(width, nt * units)
    b_in = b_in[:, 0].reshape(nt * units)
    info, seg_col, seg_row = key_blocks(seg_all, half, ln, nc)
    own = ln + hl

    x_own = own_rows(tokens).astype(F32)
    attended = jnp.einsum("gtf,gdf->td", ctx_all, w_o, preferred_element_type=F32) + out_bias
    normal_one, rstd_one = norm_parts(x_own + attended)
    normed = normal_one * gain_one + shift_one
    normed_low = normed.astype(BF)
    inner = jnp.dot(normed_low, w_i, preferred_element_type=F32) + b_in
    active = jax.nn.gelu(inner, approximate=False).astype(BF)
    branch = jnp.einsum("tf,df->td", active, w_b, preferred_element_type=F32)
    second = normed + branch + back_bias
    normal_two, rstd_two = norm_parts(second)
    out_low = (normal_two * gain_two + shift_two).astype(BF)

    def spread_rows(rows_low, dtype):
        out = jnp.zeros((seqs, ln, width), dtype)
        parts = [rows_low] + [swap_with(rows_low, "tp", nt, k) for k in range(1, nt)]
        for k, part in enumerate(parts):
            t = z ^ k
            part = part.astype(dtype)
            out = lax.dynamic_update_slice(out, part[None, :ln], (whole_of(t), 0, 0))
            out = lax.dynamic_update_slice(
                out, part[None, ln:], (shared_of(t), half_of(t) * hl, 0)
            )
        return out

    d_second, d_gain_two, d_shift_two = norm_back(
        own_rows(cotangent).astype(F32), normal_two, rstd_two, gain_two
    )
    d_second_low = d_second.astype(BF)
    d_back_bias = jnp.sum(d_second, 0)
    d_w_back = jnp.einsum("td,tf->df", d_second_low, active, preferred_element_type=F32)
    d_active = jnp.dot(d_second_low, w_b, preferred_element_type=F32)
    d_inner = d_active * gelu_slope(inner)
    d_in_bias = jnp.sum(d_inner, 0)
    d_inner_low = d_inner.astype(BF)
    d_w_in = jnp.einsum("td,tf->df", normed_low, d_inner_low, preferred_element_type=F32)
    d_normed = jnp.einsum("tf,df->td", d_inner_low, w_i, preferred_element_type=F32) + d_second
    d_first, d_gain_one, d_shift_one = norm_back(d_normed, normal_one, rstd_one, gain_one)
    d_first_low = d_first.astype(BF)
    d_out_bias = jnp.sum(d_first, 0)
    d_w_out = jnp.einsum("td,gtf->gdf", d_first_low, ctx_all, preferred_element_type=F32)
    d_ctx = jnp.einsum("td,gdf->gtf", d_first_low, w_o, preferred_element_type=F32).astype(BF)
    d_ctx = in_order(exchange_axis(d_ctx, "ctx", nc, c), c).reshape(nc * own, heads, HEAD)
    d_ctx = jnp.concatenate([jnp.zeros_like(d_ctx), d_ctx], -1).reshape(nc * own, heads * 128)

    nr = nd * nc
    by_unit = lambda g: jnp.transpose(g.astype(BF).reshape(nr, wr, nt, units), (2, 0, 1, 3))
    g_back = scatter_weight(by_unit(d_w_back), sizes, me)
    g_in = scatter_weight(by_unit(d_w_in), sizes, me)
    g_out = scatter_weight(d_w_out.astype(BF).reshape(nt, nr, wr, group), sizes, me)
    output = spread_rows(out_low, BF)
    small = sum_all(
        jnp.concatenate(
            [
                jnp.stack(
                    [d_out_bias, d_gain_one, d_shift_one, d_back_bias, d_gain_two, d_shift_two]
                ).reshape(-1),
                d_in_bias.reshape(-1),
            ]
        ),
        sizes,
    )

    d_q, d_kv, d_bias = attend_back(
        info, q, kv, d_ctx, seg_col, seg_row, lse, ctx_t, heads, ln, nc
    )
    d_proj = jnp.concatenate([d_kv, d_q], -1)
    part = jnp.einsum("tf,df->td", d_proj, wh, preferred_element_type=F32).astype(BF)
    part = part.reshape(nc // 2, 2, 2, ln, width)
    core, y = c % 2, c // 2
    part = add_low(
        lax.dynamic_index_in_dim(part, core, 1, keepdims=False),
        swap_with(lax.dynamic_index_in_dim(part, 1 - core, 1, keepdims=False), "ctx", nc, 1),
    )
    part = add_low(
        lax.dynamic_index_in_dim(part, y, 0, keepdims=False),
        swap_with(lax.dynamic_index_in_dim(part, 1 - y, 0, keepdims=False), "ctx", nc, 2),
    )
    shared = part[1].reshape(2, hl, width)
    shared = lax.dynamic_index_in_dim(shared, half, 0, keepdims=False).astype(F32) + swap_with(
        lax.dynamic_index_in_dim(shared, 1 - half, 0, keepdims=False), "tp", nt, 1
    ).astype(F32)
    d_own = (jnp.concatenate([part[0].astype(F32), shared], 0) + d_first).astype(BF)
    d_tokens = spread_rows(d_own, F32)

    d_wh = jnp.einsum("td,tf->df", x2, d_proj, preferred_element_type=F32).astype(BF)
    g_qkv = jnp.stack(head_kinds(scatter_heads(d_wh, sizes, me), heads), 1)
    d_qb, _, d_vb = head_kinds(d_bias[0], heads)
    qv = jnp.concatenate([d_qb, d_vb])
    slots = lax.dynamic_update_index_in_dim(jnp.zeros((nc, 2 * group), F32), qv, c, 0)
    slots = sum_all(slots, sizes)
    qv = lax.dynamic_index_in_dim(slots, z, 0, keepdims=False)
    wide = small[: 6 * width].reshape(6, width)
    g_in_bias = lax.dynamic_index_in_dim(
        small[6 * width :].reshape(nt, units), z, 0, keepdims=False
    )
    return (
        output,
        d_tokens,
        g_qkv,
        qv[:group],
        qv[group:],
        g_out,
        wide[0],
        wide[1],
        wide[2],
        g_in,
        g_in_bias,
        g_back,
        wide[3],
        wide[4],
        wide[5],
    )


def solution(mesh):
    sizes = tuple(mesh.shape[n] for n in ALL)
    rows = P(("dp", "ctx"), "tp")
    return jax.shard_map(
        functools.partial(per_device, sizes),
        mesh=mesh,
        in_specs=(
            P("dp", "ctx", None),
            P("dp", "ctx"),
            P(("dp", "ctx"), None, "tp"),
            P("tp"),
            P("tp"),
            rows,
            P(),
            P(),
            P(),
            rows,
            P("tp"),
            rows,
            P(),
            P(),
            P(),
            P("dp", "ctx", None),
        ),
        out_specs=(
            P("dp", "ctx", None),
            P("dp", "ctx", None),
            P(("dp", "ctx"), None, "tp"),
            P("tp"),
            P("tp"),
            rows,
            P(),
            P(),
            P(),
            rows,
            P("tp"),
            rows,
            P(),
            P(),
            P(),
        ),
        check_vma=False,
    )
```

```python
import functools
import math

import jax
import jax.numpy as jnp
from jax import lax
from jax.experimental import pallas as pl
from jax.experimental.pallas import tpu as pltpu
from jax.sharding import PartitionSpec as P

HEAD = 64
NEG = -1e30
BF = jnp.bfloat16
F32 = jnp.float32
ALL = ("dp", "ctx", "tp")


def norm_parts(value):
    mean = jnp.mean(value, -1, keepdims=True)
    centered = value - mean
    rstd = lax.rsqrt(jnp.mean(centered * centered, -1, keepdims=True) + 1e-12)
    return (centered * rstd, rstd)


def norm_back(grad, normal, rstd, gain):
    d_gain = jnp.sum(grad * normal, 0)
    d_shift = jnp.sum(grad, 0)
    scaled = grad * gain
    d_value = rstd * (
        scaled
        - jnp.mean(scaled, -1, keepdims=True)
        - normal * jnp.mean(scaled * normal, -1, keepdims=True)
    )
    return (d_value, d_gain, d_shift)


def gelu_slope(inner):
    return 0.5 * (1.0 + lax.erf(inner / math.sqrt(2.0))) + inner * jnp.exp(
        -0.5 * inner * inner
    ) / math.sqrt(2.0 * math.pi)


def swap_with(value, axis, size, mask):
    return lax.ppermute(value, axis, [(i, i ^ mask) for i in range(size)])


def in_order(parts, me, axis=0):
    shape = list(parts[0].shape)
    shape.insert(axis, len(parts))
    out = jnp.zeros(tuple(shape), parts[0].dtype)
    for k, part in enumerate(parts):
        out = lax.dynamic_update_index_in_dim(out, part, me ^ k, axis)
    return out


def gather_axis(value, axis, size, me):
    parts = [value] + [swap_with(value, axis, size, k) for k in range(1, size)]
    return in_order(parts, me)


def exchange_axis(blocks, axis, size, me):
    parts = [lax.dynamic_index_in_dim(blocks, me, 0, keepdims=False)]
    for k in range(1, size):
        parts.append(
            swap_with(lax.dynamic_index_in_dim(blocks, me ^ k, 0, keepdims=False), axis, size, k)
        )
    return parts


def scatter_weight(grad, sizes, me):
    nd, nc, nt = sizes
    part = lax.psum_scatter(
        grad.astype(F32), ("dp", "ctx"), scatter_dimension=1, tiled=False
    ).astype(BF)
    parts = exchange_axis(part, "tp", nt, me[2])
    return sum(p.astype(F32) for p in parts)


def transpose_ctx_tp(value, n):
    pairs = [(a * n + b, b * n + a) for a in range(n) for b in range(n)]
    return lax.ppermute(value, ("ctx", "tp"), pairs)


def gather_heads(shard, sizes, me):
    mine = transpose_ctx_tp(shard, sizes[1])
    return lax.all_gather(mine, ("dp", "tp"), axis=0, tiled=True)


def scatter_heads(grad, sizes, me):
    nd, nc, nt = sizes
    blocks = grad.reshape((nd * nt, grad.shape[0] // (nd * nt)) + grad.shape[1:])
    total = lax.psum_scatter(
        blocks.astype(F32), ("dp", "tp"), scatter_dimension=0, tiled=False
    )
    return transpose_ctx_tp(total, nc)


def block_rows(qb, half, ln):
    hl = ln // 2
    whole = qb < 4
    b = jnp.where(whole, qb, qb - 4)
    r0 = jnp.where(whole, 2 * ln * b, (4 * b + 1) * ln + hl * half)
    r1 = jnp.where(whole, r0 + hl, r0 + 2 * ln)
    o0 = jnp.where(whole, 3 * hl * b, 6 * hl * b + ln)
    o1 = jnp.where(whole, o0 + hl, o0 + 3 * hl)
    seq = jnp.where(whole, 0, 1)
    m = lambda v: pl.multiple_of(v, 128)
    return m(r0), m(r1), m(o0), m(o1), seq


def two(ref, r0, r1, hl, cols):
    return jnp.concatenate([ref[pl.ds(r0, hl), cols], ref[pl.ds(r1, hl), cols]], 0)


def two_lanes(ref, rows, r0, r1, hl):
    return jnp.concatenate([ref[rows, pl.ds(r0, hl)], ref[rows, pl.ds(r1, hl)]], 1)


def dot_nt(a, b):
    return lax.dot_general(a, b, (((1,), (1,)), ((), ())), preferred_element_type=F32)


def dot_nn(a, b):
    return lax.dot_general(a, b, (((1,), (0,)), ((), ())), preferred_element_type=F32)


def fill_transposed(kv, kvt, ln, nc, heads):
    @pl.loop(0, nc)
    def _(j):
        for seq in range(2):
            rows = pl.ds(pl.multiple_of((2 * j + seq) * ln, ln), ln)
            for h in range(heads):
                kvt[seq * heads + h, :, pl.ds(pl.multiple_of(j * ln, ln), ln)] = kv[
                    rows, 128 * h : 128 * h + 128
                ].T


def attend_kernel(heads, ln, nc, info, q_ref, kv, seg_col, seg_row, out, lse, ctx_t, s_scr, kvt, acc):
    half = info[12]
    hl = ln // 2
    fill_transposed(kv, kvt, ln, nc, heads)

    @pl.loop(0, 6)
    def _(qb):
        r0, r1, o0, o1, seq = block_rows(qb, half, ln)
        lo, hi = info[qb], info[6 + qb]
        sq = two_lanes(seg_row, slice(0, 1), r0, r1, hl)
        q = [two(q_ref, r0, r1, hl, slice(128 * h, 128 * h + 128)) for h in range(heads)]

        def score(j, peaks):
            rows = pl.ds(pl.multiple_of((2 * j + seq) * ln, ln), ln)
            same = seg_col[rows, :] == sq
            new = []
            for h in range(heads):
                s = dot_nt(kv[rows, 128 * h : 128 * h + 128], q[h])
                s = jnp.where(same, s, NEG)
                s_scr[h, pl.ds(pl.multiple_of(j * ln, ln), ln), :] = s
                new.append(jnp.maximum(peaks[h], jnp.max(s, 0, keepdims=True)))
            return tuple(new)

        peaks = lax.fori_loop(
            lo, hi, score, tuple(jnp.full((1, ln), NEG, F32) for _ in range(heads))
        )
        acc[...] = jnp.zeros_like(acc)

        def collect(j, sums):
            keys = pl.ds(pl.multiple_of(j * ln, ln), ln)
            new = []
            for h in range(heads):
                p = jnp.exp(s_scr[h, keys, :] - peaks[h])
                new.append(sums[h] + jnp.sum(p, 0, keepdims=True))
                acc[h] += dot_nn(kvt[seq * heads + h, :, keys], p.astype(BF))
            return tuple(new)

        sums = lax.fori_loop(
            lo, hi, collect, tuple(jnp.zeros((1, ln), F32) for _ in range(heads))
        )
        whole = []
        for h in range(heads):
            one = acc[h, HEAD:, :] / sums[h]
            whole.append(one)
            line = peaks[h] + jnp.log(sums[h])
            for part, at in ((0, o0), (hl, o1)):
                ctx_t[HEAD * h : HEAD * h + HEAD, pl.ds(at, hl)] = one[:, part : part + hl]
                lse[h : h + 1, pl.ds(at, hl)] = line[:, part : part + hl]
        turned = jnp.concatenate(whole, 0).T.astype(BF)
        out[pl.ds(o0, hl), :] = turned[:hl]
        out[pl.ds(o1, hl), :] = turned[hl:]


def attend(info, q_ref, kv, seg_col, seg_row, heads, ln, nc):
    rows = 3 * ln // 2 * nc
    vm = pl.BlockSpec(memory_space=pltpu.VMEM)
    return pl.pallas_call(
        functools.partial(attend_kernel, heads, ln, nc),
        out_shape=(
            jax.ShapeDtypeStruct((rows, heads * HEAD), BF),
            jax.ShapeDtypeStruct((8, rows), F32),
            jax.ShapeDtypeStruct((heads * HEAD, rows), F32),
        ),
        in_specs=[pl.BlockSpec(memory_space=pltpu.SMEM), vm, vm, vm, vm],
        out_specs=(vm, vm, vm),
        scratch_shapes=[
            pltpu.VMEM((heads, nc * ln, ln), F32),
            pltpu.VMEM((2 * heads, 128, nc * ln), BF),
            pltpu.VMEM((heads, 128, ln), F32),
        ],
        compiler_params=pltpu.CompilerParams(vmem_limit_bytes=32 << 20),
        cost_estimate=pl.CostEstimate(
            flops=8 * heads * rows * nc * ln * 128,
            bytes_accessed=8 << 20,
            transcendentals=heads * rows * nc * ln,
        ),
        name="attend",
    )(info, q_ref, kv, seg_col, seg_row)


def attend_back_kernel(
    heads, ln, nc, info, q_ref, kv, d_out, seg_col, seg_row, lse, ctx_t, d_q, d_kv, d_bias, dkv, kvt, dqt
):
    half = info[12]
    hl = ln // 2
    fill_transposed(kv, kvt, ln, nc, heads)
    dkv[...] = jnp.zeros_like(dkv)
    d_bias[...] = jnp.zeros_like(d_bias)

    @pl.loop(0, nc)
    def _(c):
        rows = pl.ds(pl.multiple_of((2 * c + 1) * ln, ln), ln)
        d_q[rows, :] = jnp.zeros((ln, heads * HEAD), BF)

    @pl.loop(0, 6)
    def _(qb):
        r0, r1, o0, o1, seq = block_rows(qb, half, ln)
        lo, hi = info[qb], info[6 + qb]
        sq = two_lanes(seg_row, slice(0, 1), r0, r1, hl)
        q, do, line, delta = [], [], [], []
        for h in range(heads):
            q.append(two(q_ref, r0, r1, hl, slice(128 * h, 128 * h + 128)))
            do.append(two(d_out, o0, o1, hl, slice(128 * h, 128 * h + 128)))
            line.append(two_lanes(lse, slice(h, h + 1), o0, o1, hl))
            turned = do[h].astype(F32).T[HEAD:, :]
            kept = two_lanes(ctx_t, slice(HEAD * h, HEAD * h + HEAD), o0, o1, hl)
            delta.append(jnp.sum(turned * kept, 0, keepdims=True))
        dqt[...] = jnp.zeros_like(dqt)

        @pl.loop(lo, hi)
        def _(j):
            rows = pl.ds(pl.multiple_of((2 * j + seq) * ln, ln), ln)
            keys = pl.ds(pl.multiple_of(j * ln, ln), ln)
            same = seg_col[rows, :] == sq
            for h in range(heads):
                kvh = kv[rows, 128 * h : 128 * h + 128]
                p = jnp.where(same, jnp.exp(dot_nt(kvh, q[h]) - line[h]), 0.0)
                ds = (p * (dot_nt(kvh, do[h]) - delta[h])).astype(BF)
                dkv[rows, 128 * h : 128 * h + 128] += dot_nn(ds, q[h]) + dot_nn(
                    p.astype(BF), do[h]
                )
                dqt[h] += dot_nn(kvt[seq * heads + h, :, keys], ds)

        turned = jnp.concatenate([dqt[h, :HEAD, :] for h in range(heads)], 0).T * 0.125
        d_bias[0:1, heads * 128 :] += jnp.sum(turned, 0, keepdims=True)
        low = turned.astype(BF)
        d_q[pl.ds(r0, hl), :] = low[:hl]
        d_q[pl.ds(r1, hl), :] = low[hl:]

    @pl.loop(0, 2 * nc)
    def _(c):
        rows = pl.ds(pl.multiple_of(c * ln, ln), ln)
        for h in range(heads):
            got = dkv[rows, 128 * h : 128 * h + 128]
            d_bias[0:1, 128 * h : 128 * h + 128] += jnp.sum(got, 0, keepdims=True)
            d_kv[rows, 128 * h : 128 * h + 128] = got.astype(BF)


def attend_back(info, q_ref, kv, d_out, seg_col, seg_row, lse, ctx_t, heads, ln, nc):
    rows = 3 * ln // 2 * nc
    vm = pl.BlockSpec(memory_space=pltpu.VMEM)
    return pl.pallas_call(
        functools.partial(attend_back_kernel, heads, ln, nc),
        out_shape=(
            jax.ShapeDtypeStruct((2 * nc * ln, heads * HEAD), BF),
            jax.ShapeDtypeStruct((2 * nc * ln, heads * 128), BF),
            jax.ShapeDtypeStruct((8, heads * (HEAD + 128)), F32),
        ),
        in_specs=[pl.BlockSpec(memory_space=pltpu.SMEM)] + [vm] * 7,
        out_specs=(vm, vm, vm),
        scratch_shapes=[
            pltpu.VMEM((2 * nc * ln, heads * 128), F32),
            pltpu.VMEM((2 * heads, 128, nc * ln), BF),
            pltpu.VMEM((heads, 128, ln), F32),
        ],
        compiler_params=pltpu.CompilerParams(vmem_limit_bytes=40 << 20),
        cost_estimate=pl.CostEstimate(
            flops=20 * heads * rows * nc * ln * 128,
            bytes_accessed=14 << 20,
            transcendentals=heads * rows * nc * ln,
        ),
        name="attend_back",
    )(info, q_ref, kv, d_out, seg_col, seg_row, lse, ctx_t)


MESH = pl.DeviceIdType.MESH


class Copies:
    def __init__(self, send, recv):
        self.send, self.recv, self.open = send, recv, []

    def make(self, i, src, dst, device):
        return pltpu.make_async_remote_copy(
            src_ref=src,
            dst_ref=dst,
            send_sem=self.send.at[i],
            recv_sem=self.recv.at[i],
            device_id=device,
            device_id_type=MESH,
        )

    def start(self, i, parts, when=None):
        if when is None:
            self.make(i, *parts()).start()
        else:

            @pl.when(when())
            def _():
                self.make(i, *parts()).start()

        self.open.append((i, parts, when))

    def arrived(self, i, dst, device):
        self.make(i, dst, dst, device).wait_recv()

    def sent(self):
        for i, parts, when in self.open:
            if when is None:
                self.make(i, *parts()).wait_send()
            else:

                @pl.when(when())
                def _():
                    self.make(i, *parts()).wait_send()


def forward_kernel(
    heads,
    ln,
    tok2,
    seg2,
    w_head,
    b_head,
    b_unit,
    w_o,
    w_i,
    w_b,
    ctx_all,
    xt_out,
    q_out,
    kv_out,
    wh_out,
    o_full,
    i_full,
    b_full,
    bu_full,
    lse,
    ctx_t,
    seg,
    x2,
    xt,
    wh,
    bh,
    q_scr,
    kv,
    s_scr,
    kvt,
    acc,
    segc,
    segr,
    context,
    send,
    recv,
    local,
):
    d, c, z = (lax.axis_index(n) for n in ALL)
    nc = 4
    hl = ln // 2
    own = ln + hl
    half = z % 2
    wr = w_i.shape[0]
    units = w_i.shape[1]
    row = d * nc + c
    rc = Copies(send, recv)
    at_c = lambda k: (d, c ^ k, z)
    at_x = (1 - d, c, z)
    at_xz = lambda kd, kt: (d ^ kd, c, z ^ kt)
    across = (d, z, c)
    pairs = [(kd, kt) for kd in range(2) for kt in range(4) if kd or kt]

    barrier = pltpu.get_barrier_semaphore()
    everyone = [at_c(k) for k in (1, 2, 3)] + [at_xz(*p) for p in pairs]
    for device in everyone:
        pl.semaphore_signal(barrier, inc=1, device_id=device, device_id_type=MESH)

    @pl.when(c != z)
    def _():
        pl.semaphore_signal(barrier, inc=1, device_id=across, device_id_type=MESH)

    pl.semaphore_wait(barrier, len(everyone) + jnp.where(c != z, 1, 0))

    number = iter(range(100))
    locals_ = []

    def copy_here(src, dst):
        copy = pltpu.make_async_copy(src, dst, local.at[len(locals_)])
        copy.start()
        locals_.append(copy)
        return copy

    n_ty, n_tc, n_tf = next(number), next(number), next(number)
    tok_at = lambda i: x2.at[pl.ds(2 * i, 2)]
    rc.start(n_ty, lambda: (tok2, tok_at(c), at_c(2)))
    n_wa, n_ba = next(number), next(number)
    wh_at = lambda r: wh.at[pl.ds(pl.multiple_of(r * wr, wr), wr)]

    def across_copies():
        return (
            rc.make(n_wa, w_head, wh_at(row), across),
            rc.make(n_ba, b_head, bh, across),
        )

    @pl.when(c != z)
    def _():
        for copy in across_copies():
            copy.start()

    mine = copy_here(tok2, tok_at(c))
    here = [
        pltpu.make_async_copy(w_head, wh_at(row), local.at[30]),
        pltpu.make_async_copy(b_head, bh, local.at[31]),
    ]

    @pl.when(c == z)
    def _():
        for copy in here:
            copy.start()

    rc.start(n_tc, lambda: (tok2, tok_at(c), at_c(1)))
    n_seg = [next(number) for _ in range(3)]
    for k in (1, 2, 3):
        rc.start(n_seg[k - 1], lambda k=k: (seg2, seg.at[c], at_c(k)))
    seg_here = copy_here(seg2, seg.at[c])
    bu_here = copy_here(b_unit, bu_full.at[z])
    i_at = lambda r, t: i_full.at[r, :, pl.ds(pl.multiple_of(t * units, 128), units)]
    b_at = lambda r, t: b_full.at[r, :, pl.ds(pl.multiple_of(t * units, 128), units)]
    o_at = lambda r, t: o_full.at[t, r]
    w_here = [
        copy_here(w_o, o_at(row, z)),
        copy_here(w_i, i_at(row, z)),
        copy_here(w_b, b_at(row, z)),
    ]

    row_w = d * nc + z

    @pl.when(c != z)
    def _():
        for copy in across_copies():
            copy.wait_recv()

    @pl.when(c == z)
    def _():
        for copy in here:
            copy.wait()

    n_wx = [next(number) for _ in pairs]
    for i, p in zip(n_wx, pairs):
        rc.start(i, lambda p=p: (wh_at(row_w), wh_at(row_w), at_xz(*p)))

    n_bu = [next(number) for _ in range(3)]
    n_z = [[next(number) for _ in range(3)] for _ in range(3)]
    full_at = (o_at, i_at, b_at)
    for k in (1, 2, 3):
        rc.start(n_bu[k - 1], lambda k=k: (b_unit, bu_full.at[z], at_xz(0, k)))
    for w, src in enumerate((w_o, w_i, w_b)):
        for k in (1, 2, 3):
            rc.start(n_z[w][k - 1], lambda k=k, w=w, src=src: (src, full_at[w](row, z), at_xz(0, k)))

    rc.arrived(n_ty, tok_at(c ^ 2), at_c(2))
    rc.start(n_tf, lambda: (tok_at(c ^ 2), tok_at(c ^ 2), at_c(1)))
    for k in (1, 2, 3):
        rc.arrived(n_seg[k - 1], seg.at[c ^ k], at_c(k))
    seg_here.wait()
    q_scr[...] = jnp.zeros_like(q_scr)
    for i in range(nc):
        for s in range(2):
            line = seg[i, s : s + 1, :].astype(F32)
            segr[2 * i + s, 0:1, :] = line
            segc[2 * i + s] = jnp.broadcast_to(line, (128, ln)).T
    for i, (kd, kt) in zip(n_wx, pairs):
        rc.arrived(i, wh_at((d ^ kd) * nc + (z ^ kt)), at_xz(kd, kt))
    mine.wait()
    rc.arrived(n_tc, tok_at(c ^ 1), at_c(1))
    rc.arrived(n_tf, tok_at(c ^ 3), at_c(1))
    wh_here = copy_here(wh, wh_out)
    wide = heads * 128

    @pl.loop(0, 2 * nc)
    def _(i):
        x = x2[i]
        rows = pl.ds(pl.multiple_of(i * ln, ln), ln)
        xt[:, rows] = x.T
        got = (dot_nn(x, wh[:, :wide]) + bh[0:1, :wide]).astype(BF)
        kv[rows, :] = got
        qp = ((dot_nn(x, wh[:, wide:]) + bh[0:1, wide:]).astype(BF).astype(F32) * 0.125).astype(BF)
        for h in range(heads):
            q_scr[rows, 128 * h : 128 * h + HEAD] = qp[:, HEAD * h : HEAD * h + HEAD]

    x_here = copy_here(xt, xt_out)
    q_here = copy_here(q_scr, q_out)
    kv_here = copy_here(kv, kv_out)

    @pl.loop(0, nc)
    def _(j):
        for s in range(2):
            rows = pl.ds(pl.multiple_of((2 * j + s) * ln, ln), ln)
            for h in range(heads):
                kvt[s * heads + h, :, pl.ds(pl.multiple_of(j * ln, ln), ln)] = kv[
                    rows, 128 * h : 128 * h + 128
                ].T

    groups = ((0, 1), (2,))
    row_at = (lambda r: o_full.at[:, r], lambda r: i_full.at[r], lambda r: b_full.at[r])
    hw = wr // 2
    low_at = (
        lambda r: o_full.at[:, r, pl.ds(0, hw)],
        lambda r: i_full.at[r, pl.ds(0, hw)],
        lambda r: b_full.at[r, pl.ds(0, hw)],
    )
    high_at = (
        lambda r: o_full.at[:, r, pl.ds(hw, hw)],
        lambda r: i_full.at[r, pl.ds(hw, hw)],
        lambda r: b_full.at[r, pl.ds(hw, hw)],
    )
    n_x, n_y, n_d1, n_d2 = ([next(number) for _ in range(3)] for _ in range(4))
    n_c = [[next(number) for _ in range(4)] for _ in range(3)]

    def stage_plane(w):
        w_here[w].wait()
        for k in (1, 2, 3):
            rc.arrived(n_z[w][k - 1], full_at[w](row, z ^ k), at_xz(0, k))
        rc.start(n_x[w], lambda w=w: (row_at[w](row), row_at[w](row), at_x))
        rc.start(n_y[w], lambda w=w: (row_at[w](row), row_at[w](row), at_c(2)))
        rc.start(n_c[w][0], lambda w=w: (row_at[w](row), row_at[w](row), at_c(1)))

    row_x, row_y, row_d = row ^ 4, row ^ 2, row ^ 6

    def stage_corner(w):
        rc.arrived(n_x[w], row_at[w](row_x), at_x)
        rc.start(n_d1[w], lambda w=w: (low_at[w](row_x), low_at[w](row_x), at_c(2)))
        rc.start(n_c[w][1], lambda w=w: (row_at[w](row_x), row_at[w](row_x), at_c(1)))
        rc.arrived(n_y[w], row_at[w](row_y), at_c(2))
        rc.start(n_d2[w], lambda w=w: (high_at[w](row_y), high_at[w](row_y), at_x))
        rc.start(n_c[w][2], lambda w=w: (row_at[w](row_y), row_at[w](row_y), at_c(1)))

    def stage_core(w):
        rc.arrived(n_d1[w], low_at[w](row_d), at_c(2))
        rc.arrived(n_d2[w], high_at[w](row_d), at_x)
        rc.start(n_c[w][3], lambda w=w: (row_at[w](row_d), row_at[w](row_d), at_c(1)))

    def stage_end(w):
        for i, r in zip(n_c[w], (row, row_x, row_y, row_d)):
            rc.arrived(i, row_at[w](r ^ 1), at_c(1))

    def block(qb):
        r0, r1, o0, o1, seq = block_rows(qb, half, ln)
        b0 = jnp.where(qb < 4, qb, 2 * (qb - 4))
        b1 = jnp.where(qb < 4, qb, 2 * (qb - 4) + 1)
        s0 = pl.multiple_of(jnp.where(qb < 4, 0, hl * half), 128)
        s1 = pl.multiple_of(jnp.where(qb < 4, hl, hl * half), 128)
        sq = jnp.concatenate(
            [
                segr[2 * b0 + seq, 0:1, pl.ds(s0, hl)],
                segr[2 * b1 + seq, 0:1, pl.ds(s1, hl)],
            ],
            1,
        )
        q = [two(q_scr, r0, r1, hl, slice(128 * h, 128 * h + 128)) for h in range(heads)]

        def score(j, peaks):
            rows = pl.ds(pl.multiple_of((2 * j + seq) * ln, ln), ln)
            key_seg = segc[2 * j + seq]
            same = jnp.concatenate([key_seg, key_seg], 1) == sq
            new = []
            for h in range(heads):
                s = dot_nt(kv[rows, 128 * h : 128 * h + 128], q[h])
                s = jnp.where(same, s, NEG)
                s_scr[h, pl.ds(pl.multiple_of(j * ln, ln), ln), :] = s
                new.append(jnp.maximum(peaks[h], jnp.max(s, 0, keepdims=True)))
            return tuple(new)

        peaks = lax.fori_loop(
            0, nc, score, tuple(jnp.full((1, ln), NEG, F32) for _ in range(heads))
        )
        acc[...] = jnp.zeros_like(acc)

        def collect(j, sums):
            keys = pl.ds(pl.multiple_of(j * ln, ln), ln)
            new = []
            for h in range(heads):
                p = jnp.exp(s_scr[h, keys, :] - peaks[h])
                new.append(sums[h] + jnp.sum(p, 0, keepdims=True))
                acc[h] += dot_nn(kvt[seq * heads + h, :, keys], p.astype(BF))
            return tuple(new)

        sums = lax.fori_loop(
            0, nc, collect, tuple(jnp.zeros((1, ln), F32) for _ in range(heads))
        )
        whole = []
        for h in range(heads):
            one = acc[h, HEAD:, :] / sums[h]
            whole.append(one)
            line = peaks[h] + jnp.log(sums[h])
            for part, at in ((0, o0), (hl, o1)):
                ctx_t[HEAD * h : HEAD * h + HEAD, pl.ds(at, hl)] = one[:, part : part + hl]
                lse[h : h + 1, pl.ds(at, hl)] = line[:, part : part + hl]
        turned = jnp.concatenate(whole, 0).T.astype(BF)
        context[pl.ds(o0, hl), :] = turned[:hl]
        context[pl.ds(o1, hl), :] = turned[hl:]

    stage_plane(0)
    stage_plane(1)

    @pl.loop(0, 6)
    def _(qb):
        block(qb)

        @pl.when(qb == 1)
        def _():
            stage_plane(2)

        @pl.when(qb == 3)
        def _():
            stage_corner(0)
            stage_corner(1)

    n_ctx = [next(number) for _ in range(3)]
    ctx_at = lambda i: context.at[pl.ds(pl.multiple_of(i * own, 128), own)]
    for k in (1, 2, 3):
        rc.start(n_ctx[k - 1], lambda k=k: (ctx_at(c ^ k), ctx_all.at[c], at_c(k)))
    ctx_here = copy_here(ctx_at(c), ctx_all.at[c])
    stage_corner(2)
    stage_core(0)
    stage_core(1)
    for k in (1, 2, 3):
        rc.arrived(n_ctx[k - 1], ctx_all.at[c ^ k], at_c(k))
        rc.arrived(n_bu[k - 1], bu_full.at[z ^ k], at_xz(0, k))
    stage_core(2)
    for w in range(3):
        stage_end(w)
    for copy in (bu_here, x_here, wh_here, q_here, kv_here, ctx_here):
        copy.wait()
    rc.sent()

    @pl.when(c != z)
    def _():
        for copy in across_copies():
            copy.wait_send()


def forward(tok2, seg2, w_head, b_head, b_unit, w_o, w_i, w_b, heads):
    ln, width = tok2.shape[1:]
    wr, units = w_i.shape
    group = w_o.shape[1]
    nc, nt, nr = 4, 4, 8
    rows = 3 * ln // 2 * nc
    hb = pl.BlockSpec(memory_space=pl.ANY)
    vm = pl.BlockSpec(memory_space=pltpu.VMEM)
    sds = jax.ShapeDtypeStruct
    return pl.pallas_call(
        functools.partial(forward_kernel, heads, ln),
        out_shape=(
            sds((nc, 3 * ln // 2, group), BF),
            sds((width, 2 * nc * ln), BF),
            sds((2 * nc * ln, heads * 128), BF),
            sds((2 * nc * ln, heads * 128), BF),
            sds((nr * wr, 3 * group), BF),
            sds((nt, nr, wr, group), BF),
            sds((nr, wr, nt * units), BF),
            sds((nr, wr, nt * units), BF),
            sds((nt, 8, units), F32),
            sds((8, rows), F32),
            sds((group, rows), F32),
            sds((nc, 8, ln), jnp.int32),
        ),
        in_specs=[hb] * 8,
        out_specs=(hb,) * 9 + (vm,) * 3,
        scratch_shapes=[
            pltpu.VMEM((2 * nc, ln, width), BF),
            pltpu.VMEM((width, 2 * nc * ln), BF),
            pltpu.VMEM((nr * wr, 3 * group), BF),
            pltpu.VMEM((8, 3 * group), F32),
            pltpu.VMEM((2 * nc * ln, heads * 128), BF),
            pltpu.VMEM((2 * nc * ln, heads * 128), BF),
            pltpu.VMEM((heads, nc * ln, ln), F32),
            pltpu.VMEM((2 * heads, 128, nc * ln), BF),
            pltpu.VMEM((heads, 128, ln), F32),
            pltpu.VMEM((2 * nc, ln, 128), F32),
            pltpu.VMEM((2 * nc, 8, ln), F32),
            pltpu.VMEM((rows, group), BF),
            pltpu.SemaphoreType.DMA((80,)),
            pltpu.SemaphoreType.DMA((80,)),
            pltpu.SemaphoreType.DMA((32,)),
        ],
        compiler_params=pltpu.CompilerParams(
            vmem_limit_bytes=40 << 20, collective_id=0, has_side_effects=True
        ),
        name="forward",
    )(tok2, seg2, w_head, b_head, b_unit, w_o, w_i, w_b)


def add_into(dst, other, rows):
    @pl.loop(0, rows // 16)
    def _(i):
        at = pl.ds(pl.multiple_of(i * 16, 16), 16)
        for a, b in zip(dst, other):
            a[at, :] = (a[at, :].astype(F32) + b[at, :].astype(F32)).astype(a.dtype)


def backward_kernel(
    heads,
    ln,
    d_ctx,
    g_b,
    g_i,
    g_o,
    out_low,
    d_first,
    small_in,
    q_in,
    kv_in,
    xt_in,
    wh_in,
    lse,
    ctx_t,
    seg,
    output,
    d_tokens,
    gf_b,
    gf_i,
    gf_o,
    gf_h,
    small,
    bias,
    q_scr,
    kv,
    xt,
    wh,
    d_got,
    d_o,
    kvt,
    dkv,
    dqt,
    d_proj,
    segc,
    segr,
    part,
    got_c,
    got_y,
    got_z,
    send_y,
    send_z,
    mine,
    done,
    o_b,
    o_i,
    o_o,
    r_b,
    r_i,
    r_o,
    x_b,
    x_i,
    x_o,
    y_b,
    y_i,
    y_o,
    z_b,
    z_i,
    z_o,
    acc_h,
    o_h,
    x_h,
    z_h,
    send_h,
    small_got,
    bias_sum,
    bias_got,
    h_got,
    bias_fin,
    send,
    recv,
    local,
):
    d, c, z = (lax.axis_index(n) for n in ALL)
    nc = 4
    hl = ln // 2
    own = ln + hl
    half = z % 2
    core, y = c % 2, c // 2
    wr = gf_b.shape[0]
    units = gf_b.shape[1]
    width = out_low.shape[1]
    wide = heads * 128
    rc = Copies(send, recv)
    at_c = lambda k: (d, c ^ k, z)
    at_x = (1 - d, c, z)
    at_z = lambda k: (d, c, z ^ k)
    across = (d, z, c)

    barrier = pltpu.get_barrier_semaphore()
    everyone = [at_c(k) for k in (1, 2, 3)] + [at_z(k) for k in (1, 2, 3)] + [at_x]
    for device in everyone:
        pl.semaphore_signal(barrier, inc=1, device_id=device, device_id_type=MESH)

    @pl.when(c != z)
    def _():
        pl.semaphore_signal(barrier, inc=1, device_id=across, device_id_type=MESH)

    pl.semaphore_wait(barrier, len(everyone) + jnp.where(c != z, 1, 0))

    number = iter(range(200))
    local_number = iter(range(40))

    def copy_here(src, dst):
        copy = pltpu.make_async_copy(src, dst, local.at[next(local_number)])
        copy.start()
        return copy

    flat = lambda ref: (lambda xy, h: (ref.at[xy, :, pl.ds(1536 * h, 1536)],))
    weights = []
    for own_b, got_b, x_buf, y_buf, z_buf, grad, final, is_o in (
        (o_b, r_b, x_b, y_b, z_b, g_b, gf_b, False),
        (o_i, r_i, x_i, y_i, z_i, g_i, gf_i, False),
        (o_o, r_o, x_o, y_o, z_o, g_o, gf_o, True),
    ):
        n = [next(number) for _ in range(12)]
        weights.append((own_b, got_b, x_buf, y_buf, z_buf, grad, final, is_o, n))
    half_units = 2 * units

    def of_core(w, which):
        grad, is_o = w[5], w[7]
        return grad.at[:, :, which] if is_o else grad.at[:, which]

    def part_of(w, xy, h):
        if w[7]:
            return w[0].at[pl.ds(2 * h, 2), xy]
        return w[0].at[xy, :, pl.ds(half_units * h, half_units)]

    def views(w, xy, h):
        if w[7]:
            return [w[0].at[2 * h, xy], w[0].at[2 * h + 1, xy]]
        return [w[0].at[xy, :, pl.ds(half_units * h, half_units)]]

    def buf_views(w, ref, i):
        return [ref.at[i, 0], ref.at[i, 1]] if w[7] else [ref.at[i]]

    def unit_at(w, t):
        xy = 2 * d + y
        if w[7]:
            return w[0].at[t, xy]
        return w[0].at[xy, :, pl.ds(pl.multiple_of(t * units, 128), units)]

    w_here = [copy_here(of_core(w, core), w[0]) for w in weights]
    blk = lambda x_, y_: 2 * x_ + y_

    def w_core_send(w):
        rc.start(w[8][0], lambda: (of_core(w, 1 - core), w[1], at_c(1)))

    def w_core_add(i):
        w = weights[i]
        w_here[i].wait()
        rc.arrived(w[8][0], w[1], at_c(1))

        @pl.loop(0, 4)
        def _(xy):
            if w[7]:
                add_into([w[0].at[t, xy] for t in range(4)], [w[1].at[t, xy] for t in range(4)], wr)
            else:
                add_into([w[0].at[xy]], [w[1].at[xy]], wr)

        n = w[8]
        for j in range(2):
            rc.start(n[1 + j], lambda j=j: (part_of(w, blk(1 - d, j), 0), w[2].at[j], at_x))
            rc.start(n[3 + j], lambda j=j: (part_of(w, blk(j, 1 - y), 1), w[3].at[j], at_c(2)))

    def w_plane(i):
        w = weights[i]
        n = w[8]
        for j in range(2):
            rc.arrived(n[1 + j], w[2].at[j], at_x)
        for j in range(2):
            add_into(views(w, blk(d, j), 0), buf_views(w, w[2], j), wr)
        rc.start(n[5], lambda: (part_of(w, blk(d, 1 - y), 0), w[3].at[2], at_c(2)))
        for j in range(2):
            rc.arrived(n[3 + j], w[3].at[j], at_c(2))
        for j in range(2):
            add_into(views(w, blk(j, y), 1), buf_views(w, w[3], j), wr)
        rc.start(n[6], lambda: (part_of(w, blk(1 - d, y), 1), w[2].at[2], at_x))

    def w_corner(i):
        w = weights[i]
        n = w[8]
        rc.arrived(n[5], w[3].at[2], at_c(2))
        add_into(views(w, blk(d, y), 0), buf_views(w, w[3], 2), wr)
        rc.arrived(n[6], w[2].at[2], at_x)
        add_into(views(w, blk(d, y), 1), buf_views(w, w[2], 2), wr)
        rc.start(n[7], lambda: (unit_at(w, z ^ 1), w[4].at[0], at_z(1)))
        rc.start(n[8], lambda: (unit_at(w, z ^ 3), w[4].at[1], at_z(1)))

    def w_line(i):
        w = weights[i]
        n = w[8]
        rc.arrived(n[8], w[4].at[1], at_z(1))
        add_into([unit_at(w, z ^ 2)], [w[4].at[1]], wr)
        rc.start(n[9], lambda: (unit_at(w, z ^ 2), w[4].at[2], at_z(2)))
        rc.arrived(n[7], w[4].at[0], at_z(1))
        add_into([unit_at(w, z)], [w[4].at[0]], wr)

    def w_end(i):
        w = weights[i]
        rc.arrived(w[8][9], w[4].at[2], at_z(2))
        w[6][...] = unit_at(w, z)[...].astype(F32) + w[4].at[2][...].astype(F32)

    whole_of = lambda t: (3 * t + 1) // 2
    shared_of = lambda t: 1 + 3 * (t // 2)

    class Line:
        def __init__(self, at):
            self.at = at
            self.left = [next(number) for _ in range(3)]
            self.right = [next(number) for _ in range(3)]

        def begin(self, src):
            rc.start(self.left[0], lambda: (src, self.at(z), (d, c, z + 1)), lambda: z < 3)
            rc.start(self.right[0], lambda: (src, self.at(z), (d, c, z - 1)), lambda: z > 0)

        def step(self, j):
            from_left, from_right = z - j, z + j

            @pl.when(z >= j)
            def _():
                rc.arrived(self.left[j - 1], self.at(from_left), (d, c, z - 1))

            if j < 3:
                rc.start(
                    self.left[j],
                    lambda: (self.at(z - j), self.at(z - j), (d, c, z + 1)),
                    lambda: (z >= j) & (z < 3),
                )

            @pl.when(z + j <= 3)
            def _():
                rc.arrived(self.right[j - 1], self.at(from_right), (d, c, z + 1))

            if j < 3:
                rc.start(
                    self.right[j],
                    lambda: (self.at(z + j), self.at(z + j), (d, c, z - 1)),
                    lambda: (z + j <= 3) & (z > 0),
                )

    whole_rows = lambda ref, a, n: (lambda t: ref.at[whole_of(t), pl.ds(a, n)])
    shared_rows = lambda ref: (
        lambda t: ref.at[shared_of(t), pl.ds(pl.multiple_of((t % 2) * hl, 128), hl)]
    )
    out_lines = [Line(whole_rows(output, 0, ln)), Line(shared_rows(output))]
    tok_lines = [
        Line(whole_rows(d_tokens, 0, hl)),
        Line(whole_rows(d_tokens, hl, hl)),
        Line(shared_rows(d_tokens)),
    ]

    n_ctx = [next(number) for _ in range(3)]
    for k in (1, 2, 3):
        rc.start(n_ctx[k - 1], lambda k=k: (d_ctx.at[c ^ k], d_got.at[c], at_c(k)))
    ctx_here = copy_here(d_ctx.at[c], d_got.at[c])
    for w in weights:
        w_core_send(w)
    kv_here = copy_here(kv_in, kv)
    q_here = copy_here(q_in, q_scr)
    n_small = [next(number) for _ in range(5)]
    small_to = (at_c(1), at_c(2), at_x, at_z(1), at_z(2))
    small[...] = small_in[...]

    def small_send(i):
        rc.start(n_small[i], lambda: (small_got.at[i, 1], small_got.at[i, 0], small_to[i]))

    def small_step(i):
        rc.arrived(n_small[i], small_got.at[i, 0], small_to[i])
        small[...] += small_got[i, 0]
        if i < 4:
            small_got[i + 1, 1] = small[...]
            small_send(i + 1)

    small_got[0, 1] = small_in[...]
    small_send(0)
    wh_here = copy_here(wh_in, wh)
    xt_here = copy_here(xt_in, xt)
    out_lines[0].begin(out_low.at[pl.ds(0, ln)])
    out_lines[1].begin(out_low.at[pl.ds(ln, hl)])
    out_here = [
        copy_here(out_low.at[pl.ds(0, ln)], out_lines[0].at(z)),
        copy_here(out_low.at[pl.ds(ln, hl)], out_lines[1].at(z)),
    ]

    for i in range(nc):
        for s in range(2):
            line = seg[i, s : s + 1, :].astype(F32)
            segr[2 * i + s, 0:1, :] = line
            segc[2 * i + s] = jnp.broadcast_to(line, (128, ln)).T
    dkv[...] = jnp.zeros_like(dkv)
    d_o[...] = jnp.zeros_like(d_o)
    d_proj[...] = jnp.zeros_like(d_proj)
    bias_sum[...] = jnp.zeros_like(bias_sum)
    kv_here.wait()

    @pl.loop(0, nc)
    def _(j):
        for s in range(2):
            rows = pl.ds(pl.multiple_of((2 * j + s) * ln, ln), ln)
            for h in range(heads):
                kvt[s * heads + h, :, pl.ds(pl.multiple_of(j * ln, ln), ln)] = kv[
                    rows, 128 * h : 128 * h + 128
                ].T

    w_core_add(0)
    small_step(0)
    for k in (1, 2, 3):
        rc.arrived(n_ctx[k - 1], d_got.at[c ^ k], at_c(k))
    ctx_here.wait()

    @pl.loop(0, nc)
    def _(i):
        rows = pl.ds(pl.multiple_of(i * own, 128), own)
        for h in range(heads):
            d_o[rows, 128 * h + HEAD : 128 * h + 128] = d_got[i, :, HEAD * h : HEAD * h + HEAD]

    q_here.wait()
    w_core_add(1)
    w_core_add(2)
    small_step(1)

    def block(qb):
        r0, r1, o0, o1, seq = block_rows(qb, half, ln)
        b0 = jnp.where(qb < 4, qb, 2 * (qb - 4))
        b1 = jnp.where(qb < 4, qb, 2 * (qb - 4) + 1)
        s0 = pl.multiple_of(jnp.where(qb < 4, 0, hl * half), 128)
        s1 = pl.multiple_of(jnp.where(qb < 4, hl, hl * half), 128)
        sq = jnp.concatenate(
            [
                segr[2 * b0 + seq, 0:1, pl.ds(s0, hl)],
                segr[2 * b1 + seq, 0:1, pl.ds(s1, hl)],
            ],
            1,
        )
        q, do, line, delta = [], [], [], []
        for h in range(heads):
            q.append(two(q_scr, r0, r1, hl, slice(128 * h, 128 * h + 128)))
            do.append(two(d_o, o0, o1, hl, slice(128 * h, 128 * h + 128)))
            line.append(two_lanes(lse, slice(h, h + 1), o0, o1, hl))
            turned = do[h].astype(F32).T[HEAD:, :]
            kept = two_lanes(ctx_t, slice(HEAD * h, HEAD * h + HEAD), o0, o1, hl)
            delta.append(jnp.sum(turned * kept, 0, keepdims=True))
        dqt[...] = jnp.zeros_like(dqt)

        @pl.loop(0, nc)
        def _(j):
            rows = pl.ds(pl.multiple_of((2 * j + seq) * ln, ln), ln)
            keys = pl.ds(pl.multiple_of(j * ln, ln), ln)
            key_seg = segc[2 * j + seq]
            same = jnp.concatenate([key_seg, key_seg], 1) == sq
            for h in range(heads):
                kvh = kv[rows, 128 * h : 128 * h + 128]
                p = jnp.where(same, jnp.exp(dot_nt(kvh, q[h]) - line[h]), 0.0)
                ds = (p * (dot_nt(kvh, do[h]) - delta[h])).astype(BF)
                dkv[rows, 128 * h : 128 * h + 128] += dot_nn(ds, q[h]) + dot_nn(
                    p.astype(BF), do[h]
                )
                dqt[h] += dot_nn(kvt[seq * heads + h, :, keys], ds)

        turned = jnp.concatenate([dqt[h, :HEAD, :] for h in range(heads)], 0).T * 0.125
        bias_sum[0:1, wide:] += jnp.sum(turned, 0, keepdims=True)
        low = turned.astype(BF)
        d_proj[pl.ds(r0, hl), wide:] = low[:hl]
        d_proj[pl.ds(r1, hl), wide:] = low[hl:]

    n_tc = [[next(number), next(number)] for _ in range(2)]
    n_ty = [[next(number), next(number)] for _ in range(2)]
    n_tz = next(number)

    def rows_of(cb, s):
        rows = pl.ds(pl.multiple_of((2 * cb + s) * ln, ln), ln)
        got = dkv[rows, :]
        bias_sum[0:1, :wide] += jnp.sum(got, 0, keepdims=True)
        d_proj[rows, :wide] = got.astype(BF)
        part[cb, s] = dot_nt(d_proj[rows, :], wh[...]).astype(BF)

    def t_partial(s):
        rows_of(c ^ 3, s)
        rc.start(n_tc[s][0], lambda: (part.at[c ^ 3, s], got_c.at[s, 0], at_c(1)))
        rows_of(c ^ 1, s)
        rc.start(n_tc[s][1], lambda: (part.at[c ^ 1, s], got_c.at[s, 1], at_c(1)))
        rows_of(c ^ 2, s)
        rows_of(c, s)

    def t_core(s):
        rc.arrived(n_tc[s][0], got_c.at[s, 0], at_c(1))
        for k in range(2):
            at = slice(k * hl, k * hl + hl)
            send_y[s, at] = (part[c ^ 2, s, at].astype(F32) + got_c[s, 0, at].astype(F32)).astype(BF)
            rc.start(
                n_ty[s][k],
                lambda k=k: (
                    send_y.at[s, pl.ds(k * hl, hl)],
                    got_y.at[s, pl.ds(k * hl, hl)],
                    at_c(2),
                ),
            )
        rc.arrived(n_tc[s][1], got_c.at[s, 1], at_c(1))
        mine[s] = part[c, s].astype(F32) + got_c[s, 1].astype(F32)

    def t_shared():
        for k in range(2):
            rc.arrived(n_ty[1][k], got_y.at[1, pl.ds(k * hl, hl)], at_c(2))
        mine[1] += got_y[1].astype(F32)
        send_z[...] = mine[1, pl.ds(pl.multiple_of((1 - half) * hl, 128), hl)].astype(BF)
        rc.start(n_tz, lambda: (send_z, got_z, at_z(1)))

    def t_shared_end():
        rc.arrived(n_tz, got_z, at_z(1))
        mine_half = mine[1, pl.ds(pl.multiple_of(half * hl, 128), hl)]
        done[ln:, :] = (mine_half + got_z[...].astype(F32) + d_first[ln:, :]).astype(BF)
        tok_lines[2].begin(done.at[pl.ds(ln, hl)])

    def t_whole(k):
        at = slice(k * hl, k * hl + hl)
        rc.arrived(n_ty[0][k], got_y.at[0, pl.ds(k * hl, hl)], at_c(2))
        done[at, :] = (mine[0, at] + got_y[0, at].astype(F32) + d_first[at, :]).astype(BF)
        tok_lines[k].begin(done.at[pl.ds(k * hl, hl)])

    n_h = [next(number) for _ in range(8)]

    def h_partial():
        @pl.loop(0, 2 * nc)
        def _(i):
            rows = pl.ds(pl.multiple_of(i * ln, ln), ln)
            acc_h[...] += dot_nn(xt[:, rows], d_proj[rows, :])

        o_h[...] = acc_h[...].astype(BF)
        rows_x = lambda x_: pl.ds(pl.multiple_of(x_ * 4 * wr, wr), 4 * wr)
        rc.start(n_h[0], lambda: (o_h.at[rows_x(1 - d)], x_h, at_x))

    h_at = lambda t: o_h.at[pl.ds(pl.multiple_of((4 * d + t) * wr, wr), wr)]

    def h_plane():
        rc.arrived(n_h[0], x_h, at_x)
        add_into([o_h.at[pl.ds(pl.multiple_of(d * 4 * wr, wr), 4 * wr)]], [x_h], 4 * wr)
        rc.start(n_h[1], lambda: (h_at(z ^ 3), z_h.at[1], at_z(1)))
        rc.start(n_h[2], lambda: (h_at(z ^ 1), z_h.at[0], at_z(1)))

    def h_line():
        rc.arrived(n_h[1], z_h.at[1], at_z(1))
        add_into([h_at(z ^ 2)], [z_h.at[1]], wr)
        rc.start(n_h[3], lambda: (h_at(z ^ 2), z_h.at[2], at_z(2)))
        rc.arrived(n_h[2], z_h.at[0], at_z(1))
        add_into([h_at(z)], [z_h.at[0]], wr)

    def h_end():
        rc.arrived(n_h[3], z_h.at[2], at_z(2))
        send_h[...] = h_at(z)[...].astype(F32) + z_h[2].astype(F32)
        rc.start(n_h[4], lambda: (send_h, h_got, across), lambda: c != z)

        @pl.when(c == z)
        def _():
            h_got[...] = send_h[...]

    n_bias = [next(number) for _ in range(4)]
    bias_to = (at_x, at_z(1), at_z(2))

    def bias_send(i):
        bias_got[i, 1] = bias_sum[...]
        rc.start(n_bias[i], lambda: (bias_got.at[i, 1], bias_got.at[i, 0], bias_to[i]))

    def bias_step(i):
        rc.arrived(n_bias[i], bias_got.at[i, 0], bias_to[i])
        bias_sum[...] += bias_got[i, 0]
        if i < 2:
            bias_send(i + 1)
            return
        rc.start(n_bias[3], lambda: (bias_sum, bias_fin, across), lambda: c != z)

        @pl.when(c == z)
        def _():
            bias_fin[...] = bias_sum[...]

    wh_here.wait()

    @pl.loop(0, 6)
    def _(i):
        block(jnp.where(i < 2, i + 4, i - 2))

        @pl.when(i == 1)
        def _():
            t_partial(1)
            w_plane(0)
            for line in out_lines:
                line.step(1)
            small_step(2)
            t_core(1)

        @pl.when(i == 3)
        def _():
            w_plane(1)
            w_plane(2)
            small_step(3)
            for line in out_lines:
                line.step(2)
            t_shared()

        @pl.when(i == 4)
        def _():
            w_corner(0)
            small_step(4)
            t_shared_end()

    t_partial(0)
    t_core(0)
    bias_send(0)
    acc_h[...] = jnp.zeros_like(acc_h)
    xt_here.wait()
    h_partial()
    w_corner(1)
    w_corner(2)
    t_whole(0)
    t_whole(1)
    for line in out_lines:
        line.step(3)
    tok_lines[2].step(1)
    h_plane()
    bias_step(0)
    w_line(0)
    tok_lines[0].step(1)
    tok_lines[1].step(1)
    tok_lines[2].step(2)
    w_line(1)
    w_line(2)
    bias_step(1)
    h_line()
    tok_lines[0].step(2)
    tok_lines[1].step(2)
    bias_step(2)
    h_end()
    w_end(0)
    w_end(1)
    w_end(2)
    tok_here = [
        copy_here(done.at[pl.ds(0, hl)], tok_lines[0].at(z)),
        copy_here(done.at[pl.ds(hl, hl)], tok_lines[1].at(z)),
        copy_here(done.at[pl.ds(ln, hl)], tok_lines[2].at(z)),
    ]
    for line in tok_lines:
        line.step(3)

    @pl.when(c != z)
    def _():
        rc.arrived(n_h[4], h_got, across)
        rc.arrived(n_bias[3], bias_fin, across)

    gf_h[...] = h_got[...]
    bias[...] = bias_fin[...]

    for copy in out_here + tok_here:
        copy.wait()
    rc.sent()


def backward(d_ctx, g_b, g_i, g_o, out_low, d_first, small, q, kv, xt, wh, lse, ctx_t, seg, heads, seqs):
    nc, own, group = d_ctx.shape
    ln = own * 2 // 3
    hl = ln // 2
    width = out_low.shape[1]
    wr, all_units = g_b.shape[2:]
    units = all_units // 4
    hb = pl.BlockSpec(memory_space=pl.ANY)
    vm = pl.BlockSpec(memory_space=pltpu.VMEM)
    sds = jax.ShapeDtypeStruct
    v = pltpu.VMEM
    rows = nc * own
    n2 = 2 * nc * ln
    return pl.pallas_call(
        functools.partial(backward_kernel, heads, ln),
        out_shape=(
            sds((seqs, ln, width), BF),
            sds((seqs, ln, width), BF),
            sds((wr, units), F32),
            sds((wr, units), F32),
            sds((wr, group), F32),
            sds((wr, 3 * group), F32),
            sds(small.shape, F32),
            sds((8, 3 * group), F32),
        ),
        in_specs=[hb] * 5 + [vm, vm] + [hb] * 4 + [vm] * 3,
        out_specs=(hb, hb) + (vm,) * 6,
        scratch_shapes=[
            v((n2, heads * 128), BF),
            v((n2, heads * 128), BF),
            v((width, n2), BF),
            v((width, 3 * group), BF),
            v((nc, own, group), BF),
            v((rows, heads * 128), BF),
            v((2 * heads, 128, nc * ln), BF),
            v((n2, heads * 128), F32),
            v((heads, 128, ln), F32),
            v((n2, 3 * group), BF),
            v((2 * nc, ln, 128), F32),
            v((2 * nc, 8, ln), F32),
            v((nc, 2, ln, width), BF),
            v((2, 2, ln, width), BF),
            v((2, ln, width), BF),
            v((hl, width), BF),
            v((2, ln, width), BF),
            v((hl, width), BF),
            v((2, ln, width), F32),
            v((own, width), BF),
            v((4, wr, all_units), BF),
            v((4, wr, all_units), BF),
            v((4, 4, wr, group), BF),
            v((4, wr, all_units), BF),
            v((4, wr, all_units), BF),
            v((4, 4, wr, group), BF),
            v((3, wr, 2 * units), BF),
            v((3, wr, 2 * units), BF),
            v((3, 2, wr, group), BF),
            v((3, wr, 2 * units), BF),
            v((3, wr, 2 * units), BF),
            v((3, 2, wr, group), BF),
            v((3, wr, units), BF),
            v((3, wr, units), BF),
            v((3, wr, group), BF),
            v((width, 3 * group), F32),
            v((width, 3 * group), BF),
            v((4 * wr, 3 * group), BF),
            v((3, wr, 3 * group), BF),
            v((wr, 3 * group), F32),
            v((5, 2) + small.shape, F32),
            v((8, 3 * group), F32),
            v((3, 2, 8, 3 * group), F32),
            v((wr, 3 * group), F32),
            v((8, 3 * group), F32),
            pltpu.SemaphoreType.DMA((130,)),
            pltpu.SemaphoreType.DMA((130,)),
            pltpu.SemaphoreType.DMA((40,)),
        ],
        compiler_params=pltpu.CompilerParams(
            vmem_limit_bytes=58 << 20, collective_id=1, has_side_effects=True
        ),
        name="backward",
    )(d_ctx, g_b, g_i, g_o, out_low, d_first, small, q, kv, xt, wh, lse, ctx_t, seg)


def head_order(kinds, heads):
    lead = kinds[0].shape[:-1]
    q, k, v = (a.reshape(lead + (heads, HEAD)) for a in kinds)
    kv = jnp.concatenate([k, v], -1).reshape(lead + (heads * 2 * HEAD,))
    return jnp.concatenate([kv, q.reshape(lead + (heads * HEAD,))], -1)


def head_kinds(value, heads):
    lead = value.shape[:-1]
    kv = value[..., : heads * 2 * HEAD].reshape(lead + (heads, 2, HEAD))
    flat = lambda a: a.reshape(lead + (heads * HEAD,))
    return value[..., heads * 2 * HEAD :], flat(kv[..., 0, :]), flat(kv[..., 1, :])


def forward_plain(sizes, me, tok2, seg2, w_head, b_head, b_unit, w_o, w_i, w_b, heads):
    nd, nc, nt = sizes
    d, c, z = me
    ln, width = tok2.shape[1:]
    hl = ln // 2
    half = z % 2
    group = w_o.shape[1]
    seg_all = gather_axis(seg2, "ctx", nc, c)
    x2 = gather_axis(tok2, "ctx", nc, c).reshape(2 * nc, ln, width)
    wh = gather_heads(w_head, sizes, me)
    bh = transpose_ctx_tp(b_head, nc)[0]
    b_all = gather_axis(b_unit, "tp", nt, z)
    gather = lambda w: lax.all_gather(
        lax.all_gather(w, "tp", axis=1, tiled=True), ("dp", "ctx"), axis=0, tiled=True
    )
    o_full = jnp.transpose(gather(w_o).reshape(width, nt, group), (1, 0, 2))
    proj = (jnp.dot(x2.reshape(-1, width), wh, preferred_element_type=F32) + bh).astype(BF)
    kv = proj[:, : 2 * group]
    q = (proj[:, 2 * group :].astype(F32) * 0.125).astype(BF).reshape(-1, heads, HEAD)
    q = jnp.concatenate([q, jnp.zeros_like(q)], -1).reshape(-1, heads * 128)
    info, seg_col, seg_row = key_blocks(seg_all, half, ln, nc)
    context, lse, ctx_t = attend(info, q, kv, seg_col, seg_row, heads, ln, nc)
    ctx_all = in_order(exchange_axis(context.reshape(nc, ln + hl, group), "ctx", nc, c), c)
    return (
        ctx_all,
        x2.reshape(-1, width).T,
        q,
        kv,
        wh,
        o_full,
        gather(w_i),
        gather(w_b),
        b_all,
        lse,
        ctx_t,
        seg_all,
    )


def key_blocks(seg_all, half, ln, nc):
    hl = ln // 2
    seg2 = seg_all[:, :2]
    flat = jnp.transpose(seg2, (1, 0, 2)).reshape(2, nc * ln)
    first = jnp.concatenate([seg2[:, 0, 0], jnp.take(seg2[0::2, 1], half * hl, axis=1)])
    last = jnp.concatenate([seg2[:, 0, -1], jnp.take(seg2[1::2, 1], half * hl + hl - 1, axis=1)])
    of = jnp.concatenate(
        [
            jnp.broadcast_to(flat[:1], (nc, nc * ln)),
            jnp.broadcast_to(flat[1:], (nc // 2, nc * ln)),
        ],
        0,
    )
    lo = jnp.sum(of < first[:, None], 1) // ln
    hi = (jnp.sum(of <= last[:, None], 1) + ln - 1) // ln
    info = jnp.concatenate([lo, hi, half[None]]).astype(jnp.int32)
    seg_flat = seg2.reshape(2 * nc * ln)
    return info, seg_flat[:, None], seg_flat[None, :]


def backward_plain(
    sizes, me, d_ctx, low, out_low, d_first, small, q, kv, xt, wh, lse, ctx_t, seg_all, heads, seqs
):
    nd, nc, nt = sizes
    d, c, z = me
    own, group = d_ctx.shape[1:]
    ln = own * 2 // 3
    hl = ln // 2
    half = z % 2
    width = out_low.shape[1]
    units = low[0].shape[1] // nt
    nr = nd * nc
    wr = width // nr
    info, seg_col, seg_row = key_blocks(seg_all, half, ln, nc)

    def spread_rows(rows_low, dtype):
        out = jnp.zeros((seqs, ln, width), dtype)
        parts = [rows_low] + [swap_with(rows_low, "tp", nt, k) for k in range(1, nt)]
        for k, part in enumerate(parts):
            t = z ^ k
            part = part.astype(dtype)
            out = lax.dynamic_update_slice(out, part[None, :ln], ((3 * t + 1) // 2, 0, 0))
            out = lax.dynamic_update_slice(
                out, part[None, ln:], (1 + 3 * (t // 2), (t % 2) * hl, 0)
            )
        return out

    by_unit = lambda g: jnp.transpose(g.reshape(nr, wr, nt, units), (2, 0, 1, 3))
    g_back = scatter_weight(by_unit(low[0]), sizes, me)
    g_in = scatter_weight(by_unit(low[1]), sizes, me)
    g_out = scatter_weight(low[2].reshape(nt, nr, wr, group), sizes, me)
    output = spread_rows(out_low, BF)
    small = lax.psum(small, ALL)
    d_ctx = in_order(exchange_axis(d_ctx, "ctx", nc, c), c).reshape(nc * own, heads, HEAD)
    d_ctx = jnp.concatenate([jnp.zeros_like(d_ctx), d_ctx], -1).reshape(nc * own, heads * 128)
    d_q, d_kv, d_bias = attend_back(
        info, q, kv, d_ctx, seg_col, seg_row, lse, ctx_t, heads, ln, nc
    )
    d_proj = jnp.concatenate([d_kv, d_q], -1)
    part = jnp.einsum("tf,df->td", d_proj, wh, preferred_element_type=F32)
    part = lax.psum_scatter(
        part.reshape(nc, 2 * ln, width), "ctx", scatter_dimension=0, tiled=False
    ).reshape(2, ln, width)
    shared = part[1].reshape(2, hl, width)
    shared = lax.dynamic_index_in_dim(shared, half, 0, keepdims=False) + swap_with(
        lax.dynamic_index_in_dim(shared, 1 - half, 0, keepdims=False), "tp", nt, 1
    )
    d_own = (jnp.concatenate([part[0], shared], 0) + d_first).astype(BF)
    d_tokens = spread_rows(d_own, F32)
    g_h = scatter_heads(jnp.dot(xt, d_proj, preferred_element_type=F32).astype(BF), sizes, me)
    slots = jnp.zeros((nc,) + d_bias[0].shape, F32)
    slots = lax.psum(lax.dynamic_update_index_in_dim(slots, d_bias[0], c, 0), ALL)
    d_bias = lax.dynamic_index_in_dim(slots, z, 0, keepdims=False)
    return output, d_tokens, g_back, g_in, g_out, g_h, small, d_bias


def per_device(
    sizes,
    tokens,
    segments,
    w_qkv,
    q_bias,
    v_bias,
    w_out,
    out_bias,
    gain_one,
    shift_one,
    w_in,
    in_bias,
    w_back,
    back_bias,
    gain_two,
    shift_two,
    cotangent,
):
    nd, nc, nt = sizes
    seqs, ln, width = tokens.shape
    hl = ln // 2
    group = w_out.shape[1]
    heads = group // HEAD
    units = w_in.shape[1]
    wr = w_in.shape[0]
    d, c, z = (lax.axis_index(n) for n in ALL)
    me = (d, c, z)
    whole_of = lambda t: (3 * t + 1) // 2
    shared_of = lambda t: 1 + 3 * (t // 2)
    half_of = lambda t: t % 2
    sf, sh, half = whole_of(z), shared_of(z), half_of(z)

    def own_rows(a):
        one = lax.dynamic_index_in_dim(a, sf, 0, keepdims=False)
        two_ = lax.dynamic_index_in_dim(a, sh, 0, keepdims=False)
        return jnp.concatenate([one, lax.dynamic_slice_in_dim(two_, half * hl, hl, 0)], 0)

    def own_pair(a):
        return jnp.stack(
            [
                lax.dynamic_index_in_dim(a, sf, 0, keepdims=False),
                lax.dynamic_index_in_dim(a, sh, 0, keepdims=False),
            ],
            0,
        )

    tok2 = own_pair(tokens)
    seg2 = jnp.concatenate([own_pair(segments), jnp.zeros((6, ln), jnp.int32)], 0)
    w_head = head_order([w_qkv[:, i] for i in range(3)], heads)
    b_head = head_order([q_bias, jnp.zeros_like(q_bias), v_bias], heads)
    b_head = jnp.broadcast_to(b_head[None], (8, 3 * group))
    b_unit = jnp.broadcast_to(in_bias[None], (8, units))
    args = (tok2, seg2, w_head, b_head, b_unit, w_out, w_in, w_back, heads)
    got = forward(*args) if sizes == (2, 4, 4) else forward_plain(sizes, me, *args)
    ctx_all, xt, q, kv, wh, w_o, w_i, w_b, b_in, lse, ctx_t, seg_all = got
    w_o = w_o.reshape(nt, width, group)
    w_i = w_i.reshape(width, nt * units)
    w_b = w_b.reshape(width, nt * units)
    b_in = b_in[:, 0].reshape(nt * units)
    own = ln + hl

    x_own = own_rows(tokens).astype(F32)
    attended = jnp.einsum("gtf,gdf->td", ctx_all, w_o, preferred_element_type=F32) + out_bias
    normal_one, rstd_one = norm_parts(x_own + attended)
    normed = normal_one * gain_one + shift_one
    normed_low = normed.astype(BF)
    inner = jnp.dot(normed_low, w_i, preferred_element_type=F32) + b_in
    active = jax.nn.gelu(inner, approximate=False).astype(BF)
    branch = jnp.einsum("tf,df->td", active, w_b, preferred_element_type=F32)
    second = normed + branch + back_bias
    normal_two, rstd_two = norm_parts(second)
    out_low = (normal_two * gain_two + shift_two).astype(BF)

    d_second, d_gain_two, d_shift_two = norm_back(
        own_rows(cotangent).astype(F32), normal_two, rstd_two, gain_two
    )
    d_second_low = d_second.astype(BF)
    d_back_bias = jnp.sum(d_second, 0)
    d_w_back = jnp.einsum("td,tf->df", d_second_low, active, preferred_element_type=F32)
    d_active = jnp.dot(d_second_low, w_b, preferred_element_type=F32)
    d_inner = d_active * gelu_slope(inner)
    d_in_bias = jnp.sum(d_inner, 0)
    d_inner_low = d_inner.astype(BF)
    d_w_in = jnp.einsum("td,tf->df", normed_low, d_inner_low, preferred_element_type=F32)
    d_normed = jnp.einsum("tf,df->td", d_inner_low, w_i, preferred_element_type=F32) + d_second
    d_first, d_gain_one, d_shift_one = norm_back(d_normed, normal_one, rstd_one, gain_one)
    d_first_low = d_first.astype(BF)
    d_out_bias = jnp.sum(d_first, 0)
    d_w_out = jnp.einsum("td,gtf->gdf", d_first_low, ctx_all, preferred_element_type=F32)
    d_ctx = jnp.einsum("td,gdf->gtf", d_first_low, w_o, preferred_element_type=F32).astype(BF)
    small = jnp.concatenate(
        [d_out_bias, d_gain_one, d_shift_one, d_back_bias, d_gain_two, d_shift_two, d_in_bias]
    )
    low = (d_w_back.astype(BF), d_w_in.astype(BF), d_w_out.astype(BF))
    if sizes == (2, 4, 4):
        small = jnp.concatenate([small, jnp.zeros((-small.shape[0] % 1024,), F32)])
        output, d_tokens, g_back, g_in, g_out, g_h, small, d_bias = backward(
            d_ctx,
            low[0].reshape(4, 2, wr, nt * units),
            low[1].reshape(4, 2, wr, nt * units),
            low[2].reshape(nt, 4, 2, wr, group),
            out_low,
            d_first,
            small.reshape(-1, 128),
            q,
            kv,
            xt,
            wh,
            lse,
            ctx_t,
            seg_all,
            heads,
            seqs,
        )
        d_tokens = d_tokens.astype(F32)
        small = small.reshape(-1)
        d_bias = d_bias[0]
    else:
        output, d_tokens, g_back, g_in, g_out, g_h, small, d_bias = backward_plain(
            sizes, me, d_ctx, low, out_low, d_first, small, q, kv, xt, wh, lse, ctx_t, seg_all, heads, seqs
        )
    g_qkv = jnp.stack(head_kinds(g_h, heads), 1)
    d_qb, _, d_vb = head_kinds(d_bias, heads)
    qv = jnp.concatenate([d_qb, d_vb])
    wide = small[: 6 * width].reshape(6, width)
    g_in_bias = lax.dynamic_index_in_dim(
        small[6 * width : 6 * width + nt * units].reshape(nt, units), z, 0, keepdims=False
    )
    return (
        output,
        d_tokens,
        g_qkv,
        qv[:group],
        qv[group:],
        g_out,
        wide[0],
        wide[1],
        wide[2],
        g_in,
        g_in_bias,
        g_back,
        wide[3],
        wide[4],
        wide[5],
    )


def solution(mesh):
    sizes = tuple(mesh.shape[n] for n in ALL)
    rows = P(("dp", "ctx"), "tp")
    return jax.shard_map(
        functools.partial(per_device, sizes),
        mesh=mesh,
        in_specs=(
            P("dp", "ctx", None),
            P("dp", "ctx"),
            P(("dp", "ctx"), None, "tp"),
            P("tp"),
            P("tp"),
            rows,
            P(),
            P(),
            P(),
            rows,
            P("tp"),
            rows,
            P(),
            P(),
            P(),
            P("dp", "ctx", None),
        ),
        out_specs=(
            P("dp", "ctx", None),
            P("dp", "ctx", None),
            P(("dp", "ctx"), None, "tp"),
            P("tp"),
            P("tp"),
            rows,
            P(),
            P(),
            P(),
            rows,
            P("tp"),
            rows,
            P(),
            P(),
            P(),
        ),
        check_vma=False,
    )
```

```python
import functools
import math

import jax
import jax.numpy as jnp
from jax import lax
from jax.experimental import pallas as pl
from jax.experimental.pallas import tpu as pltpu
from jax.sharding import PartitionSpec as P

HEAD = 64
NEG = -1e30
BF = jnp.bfloat16
F32 = jnp.float32
ALL = ("dp", "ctx", "tp")


def norm_parts(value):
    mean = jnp.mean(value, -1, keepdims=True)
    centered = value - mean
    rstd = lax.rsqrt(jnp.mean(centered * centered, -1, keepdims=True) + 1e-12)
    return (centered * rstd, rstd)


def norm_back(grad, normal, rstd, gain):
    d_gain = jnp.sum(grad * normal, 0)
    d_shift = jnp.sum(grad, 0)
    scaled = grad * gain
    d_value = rstd * (
        scaled
        - jnp.mean(scaled, -1, keepdims=True)
        - normal * jnp.mean(scaled * normal, -1, keepdims=True)
    )
    return (d_value, d_gain, d_shift)


def gelu_slope(inner):
    return 0.5 * (1.0 + lax.erf(inner / math.sqrt(2.0))) + inner * jnp.exp(
        -0.5 * inner * inner
    ) / math.sqrt(2.0 * math.pi)


def swap_with(value, axis, size, mask):
    return lax.ppermute(value, axis, [(i, i ^ mask) for i in range(size)])


def in_order(parts, me, axis=0):
    shape = list(parts[0].shape)
    shape.insert(axis, len(parts))
    out = jnp.zeros(tuple(shape), parts[0].dtype)
    for k, part in enumerate(parts):
        out = lax.dynamic_update_index_in_dim(out, part, me ^ k, axis)
    return out


def gather_axis(value, axis, size, me):
    parts = [value] + [swap_with(value, axis, size, k) for k in range(1, size)]
    return in_order(parts, me)


def exchange_axis(blocks, axis, size, me):
    parts = [lax.dynamic_index_in_dim(blocks, me, 0, keepdims=False)]
    for k in range(1, size):
        parts.append(
            swap_with(lax.dynamic_index_in_dim(blocks, me ^ k, 0, keepdims=False), axis, size, k)
        )
    return parts


def scatter_weight(grad, sizes, me):
    nd, nc, nt = sizes
    part = lax.psum_scatter(
        grad.astype(F32), ("dp", "ctx"), scatter_dimension=1, tiled=False
    ).astype(BF)
    parts = exchange_axis(part, "tp", nt, me[2])
    return sum(p.astype(F32) for p in parts)


def transpose_ctx_tp(value, n):
    pairs = [(a * n + b, b * n + a) for a in range(n) for b in range(n)]
    return lax.ppermute(value, ("ctx", "tp"), pairs)


def gather_heads(shard, sizes, me):
    mine = transpose_ctx_tp(shard, sizes[1])
    return lax.all_gather(mine, ("dp", "tp"), axis=0, tiled=True)


def scatter_heads(grad, sizes, me):
    nd, nc, nt = sizes
    blocks = grad.reshape((nd * nt, grad.shape[0] // (nd * nt)) + grad.shape[1:])
    total = lax.psum_scatter(
        blocks.astype(F32), ("dp", "tp"), scatter_dimension=0, tiled=False
    )
    return transpose_ctx_tp(total, nc)


def block_rows(qb, half, ln):
    hl = ln // 2
    whole = qb < 4
    b = jnp.where(whole, qb, qb - 4)
    r0 = jnp.where(whole, 2 * ln * b, (4 * b + 1) * ln + hl * half)
    r1 = jnp.where(whole, r0 + hl, r0 + 2 * ln)
    o0 = jnp.where(whole, 3 * hl * b, 6 * hl * b + ln)
    o1 = jnp.where(whole, o0 + hl, o0 + 3 * hl)
    seq = jnp.where(whole, 0, 1)
    m = lambda v: pl.multiple_of(v, 128)
    return m(r0), m(r1), m(o0), m(o1), seq


def two(ref, r0, r1, hl, cols):
    return jnp.concatenate([ref[pl.ds(r0, hl), cols], ref[pl.ds(r1, hl), cols]], 0)


def two_lanes(ref, rows, r0, r1, hl):
    return jnp.concatenate([ref[rows, pl.ds(r0, hl)], ref[rows, pl.ds(r1, hl)]], 1)


def dot_nt(a, b):
    return lax.dot_general(a, b, (((1,), (1,)), ((), ())), preferred_element_type=F32)


def dot_nn(a, b):
    return lax.dot_general(a, b, (((1,), (0,)), ((), ())), preferred_element_type=F32)


def fill_transposed(kv, kvt, ln, nc, heads):
    @pl.loop(0, nc)
    def _(j):
        for seq in range(2):
            rows = pl.ds(pl.multiple_of((2 * j + seq) * ln, ln), ln)
            for h in range(heads):
                kvt[seq * heads + h, :, pl.ds(pl.multiple_of(j * ln, ln), ln)] = kv[
                    rows, 128 * h : 128 * h + 128
                ].T


def attend_kernel(heads, ln, nc, info, q_ref, kv, seg_col, seg_row, out, lse, ctx_t, s_scr, kvt, acc):
    half = info[12]
    hl = ln // 2
    fill_transposed(kv, kvt, ln, nc, heads)

    @pl.loop(0, 6)
    def _(qb):
        r0, r1, o0, o1, seq = block_rows(qb, half, ln)
        lo, hi = info[qb], info[6 + qb]
        sq = two_lanes(seg_row, slice(0, 1), r0, r1, hl)
        q = [two(q_ref, r0, r1, hl, slice(128 * h, 128 * h + 128)) for h in range(heads)]

        def score(j, peaks):
            rows = pl.ds(pl.multiple_of((2 * j + seq) * ln, ln), ln)
            same = seg_col[rows, :] == sq
            new = []
            for h in range(heads):
                s = dot_nt(kv[rows, 128 * h : 128 * h + 128], q[h])
                s = jnp.where(same, s, NEG)
                s_scr[h, pl.ds(pl.multiple_of(j * ln, ln), ln), :] = s
                new.append(jnp.maximum(peaks[h], jnp.max(s, 0, keepdims=True)))
            return tuple(new)

        peaks = lax.fori_loop(
            lo, hi, score, tuple(jnp.full((1, ln), NEG, F32) for _ in range(heads))
        )
        acc[...] = jnp.zeros_like(acc)

        def collect(j, sums):
            keys = pl.ds(pl.multiple_of(j * ln, ln), ln)
            new = []
            for h in range(heads):
                p = jnp.exp(s_scr[h, keys, :] - peaks[h])
                new.append(sums[h] + jnp.sum(p, 0, keepdims=True))
                acc[h] += dot_nn(kvt[seq * heads + h, :, keys], p.astype(BF))
            return tuple(new)

        sums = lax.fori_loop(
            lo, hi, collect, tuple(jnp.zeros((1, ln), F32) for _ in range(heads))
        )
        whole = []
        for h in range(heads):
            one = acc[h, HEAD:, :] / sums[h]
            whole.append(one)
            line = peaks[h] + jnp.log(sums[h])
            for part, at in ((0, o0), (hl, o1)):
                ctx_t[HEAD * h : HEAD * h + HEAD, pl.ds(at, hl)] = one[:, part : part + hl]
                lse[h : h + 1, pl.ds(at, hl)] = line[:, part : part + hl]
        turned = jnp.concatenate(whole, 0).T.astype(BF)
        out[pl.ds(o0, hl), :] = turned[:hl]
        out[pl.ds(o1, hl), :] = turned[hl:]


def attend(info, q_ref, kv, seg_col, seg_row, heads, ln, nc):
    rows = 3 * ln // 2 * nc
    vm = pl.BlockSpec(memory_space=pltpu.VMEM)
    return pl.pallas_call(
        functools.partial(attend_kernel, heads, ln, nc),
        out_shape=(
            jax.ShapeDtypeStruct((rows, heads * HEAD), BF),
            jax.ShapeDtypeStruct((8, rows), F32),
            jax.ShapeDtypeStruct((heads * HEAD, rows), F32),
        ),
        in_specs=[pl.BlockSpec(memory_space=pltpu.SMEM), vm, vm, vm, vm],
        out_specs=(vm, vm, vm),
        scratch_shapes=[
            pltpu.VMEM((heads, nc * ln, ln), F32),
            pltpu.VMEM((2 * heads, 128, nc * ln), BF),
            pltpu.VMEM((heads, 128, ln), F32),
        ],
        compiler_params=pltpu.CompilerParams(vmem_limit_bytes=32 << 20),
        cost_estimate=pl.CostEstimate(
            flops=8 * heads * rows * nc * ln * 128,
            bytes_accessed=8 << 20,
            transcendentals=heads * rows * nc * ln,
        ),
        name="attend",
    )(info, q_ref, kv, seg_col, seg_row)


def attend_back_kernel(
    heads, ln, nc, info, q_ref, kv, d_out, seg_col, seg_row, lse, ctx_t, d_q, d_kv, d_bias, dkv, kvt, dqt
):
    half = info[12]
    hl = ln // 2
    fill_transposed(kv, kvt, ln, nc, heads)
    dkv[...] = jnp.zeros_like(dkv)
    d_bias[...] = jnp.zeros_like(d_bias)

    @pl.loop(0, nc)
    def _(c):
        rows = pl.ds(pl.multiple_of((2 * c + 1) * ln, ln), ln)
        d_q[rows, :] = jnp.zeros((ln, heads * HEAD), BF)

    @pl.loop(0, 6)
    def _(qb):
        r0, r1, o0, o1, seq = block_rows(qb, half, ln)
        lo, hi = info[qb], info[6 + qb]
        sq = two_lanes(seg_row, slice(0, 1), r0, r1, hl)
        q, do, line, delta = [], [], [], []
        for h in range(heads):
            q.append(two(q_ref, r0, r1, hl, slice(128 * h, 128 * h + 128)))
            do.append(two(d_out, o0, o1, hl, slice(128 * h, 128 * h + 128)))
            line.append(two_lanes(lse, slice(h, h + 1), o0, o1, hl))
            turned = do[h].astype(F32).T[HEAD:, :]
            kept = two_lanes(ctx_t, slice(HEAD * h, HEAD * h + HEAD), o0, o1, hl)
            delta.append(jnp.sum(turned * kept, 0, keepdims=True))
        dqt[...] = jnp.zeros_like(dqt)

        @pl.loop(lo, hi)
        def _(j):
            rows = pl.ds(pl.multiple_of((2 * j + seq) * ln, ln), ln)
            keys = pl.ds(pl.multiple_of(j * ln, ln), ln)
            same = seg_col[rows, :] == sq
            for h in range(heads):
                kvh = kv[rows, 128 * h : 128 * h + 128]
                p = jnp.where(same, jnp.exp(dot_nt(kvh, q[h]) - line[h]), 0.0)
                ds = (p * (dot_nt(kvh, do[h]) - delta[h])).astype(BF)
                dkv[rows, 128 * h : 128 * h + 128] += dot_nn(ds, q[h]) + dot_nn(
                    p.astype(BF), do[h]
                )
                dqt[h] += dot_nn(kvt[seq * heads + h, :, keys], ds)

        turned = jnp.concatenate([dqt[h, :HEAD, :] for h in range(heads)], 0).T * 0.125
        d_bias[0:1, heads * 128 :] += jnp.sum(turned, 0, keepdims=True)
        low = turned.astype(BF)
        d_q[pl.ds(r0, hl), :] = low[:hl]
        d_q[pl.ds(r1, hl), :] = low[hl:]

    @pl.loop(0, 2 * nc)
    def _(c):
        rows = pl.ds(pl.multiple_of(c * ln, ln), ln)
        for h in range(heads):
            got = dkv[rows, 128 * h : 128 * h + 128]
            d_bias[0:1, 128 * h : 128 * h + 128] += jnp.sum(got, 0, keepdims=True)
            d_kv[rows, 128 * h : 128 * h + 128] = got.astype(BF)


def attend_back(info, q_ref, kv, d_out, seg_col, seg_row, lse, ctx_t, heads, ln, nc):
    rows = 3 * ln // 2 * nc
    vm = pl.BlockSpec(memory_space=pltpu.VMEM)
    return pl.pallas_call(
        functools.partial(attend_back_kernel, heads, ln, nc),
        out_shape=(
            jax.ShapeDtypeStruct((2 * nc * ln, heads * HEAD), BF),
            jax.ShapeDtypeStruct((2 * nc * ln, heads * 128), BF),
            jax.ShapeDtypeStruct((8, heads * (HEAD + 128)), F32),
        ),
        in_specs=[pl.BlockSpec(memory_space=pltpu.SMEM)] + [vm] * 7,
        out_specs=(vm, vm, vm),
        scratch_shapes=[
            pltpu.VMEM((2 * nc * ln, heads * 128), F32),
            pltpu.VMEM((2 * heads, 128, nc * ln), BF),
            pltpu.VMEM((heads, 128, ln), F32),
        ],
        compiler_params=pltpu.CompilerParams(vmem_limit_bytes=40 << 20),
        cost_estimate=pl.CostEstimate(
            flops=20 * heads * rows * nc * ln * 128,
            bytes_accessed=14 << 20,
            transcendentals=heads * rows * nc * ln,
        ),
        name="attend_back",
    )(info, q_ref, kv, d_out, seg_col, seg_row, lse, ctx_t)


MESH = pl.DeviceIdType.MESH


class Copies:
    def __init__(self, send, recv):
        self.send, self.recv, self.open = send, recv, []

    def make(self, i, src, dst, device, sent=None):
        return pltpu.make_async_remote_copy(
            src_ref=src,
            dst_ref=dst,
            send_sem=self.send.at[i if sent is None else sent],
            recv_sem=self.recv.at[i],
            device_id=device,
            device_id_type=MESH,
        )

    def start(self, i, parts, when=None, sent=None):
        number = (lambda: i) if not callable(i) else i

        def go(wait):
            copy = self.make(number(), *parts(), sent=sent)
            copy.wait_send() if wait else copy.start()

        self.run(go, when, False)
        self.open.append((go, when))

    def run(self, go, when, wait):
        if when is None:
            go(wait)
        else:

            @pl.when(when())
            def _():
                go(wait)

    def arrived(self, i, dst, device):
        self.make(i, dst, dst, device).wait_recv()

    def all_sent(self):
        for go, when in self.open:
            self.run(go, when, True)


def line_order(z, i):
    if i == 0:
        return z
    if i == 1:
        return jnp.where(z == 0, 1, z - 1)
    if i == 2:
        return jnp.where(z == 0, 2, jnp.where(z == 3, 1, z + 1))
    return jnp.where(z < 2, 3, 0)


def forward_kernel(
    heads,
    ln,
    tok2,
    seg2,
    w_head,
    b_head,
    b_unit,
    w_o,
    w_i,
    w_b,
    ctx_all,
    xt_out,
    q_out,
    kv_out,
    wh_out,
    o_full,
    w_full,
    bu_full,
    lse,
    ctx_t,
    seg,
    x2,
    xt,
    wh,
    bh,
    q_scr,
    kv,
    s_scr,
    kvt,
    acc,
    segc,
    segr,
    context,
    send,
    recv,
    local,
):
    d, c, z = (lax.axis_index(n) for n in ALL)
    nc = 4
    hl = ln // 2
    own = ln + hl
    half = z % 2
    wr = w_i.shape[0]
    units = w_i.shape[1]
    row = d * nc + c
    row_x, row_y, row_d = row ^ 4, row ^ 2, row ^ 6
    rc = Copies(send, recv)
    at_c = lambda k: (d, c ^ k, z)
    at_x = (1 - d, c, z)
    to_c = lambda k: (lambda: at_c(k))
    to_x = lambda: at_x
    at_z = lambda k: (d, c, z ^ k)
    across = (d, z, c)
    order = [line_order(z, i) for i in range(4)]
    number = iter(range(0, 400))
    four = lambda: [next(number) for _ in range(4)][0]
    local_number = iter(range(32))

    def copy_here(src, dst):
        copy = pltpu.make_async_copy(src, dst, local.at[next(local_number)])
        copy.start()
        return copy

    t_cols = lambda t: pl.ds(pl.multiple_of(t * units, 128), units)
    w_at = lambda r, t: w_full.at[:, r, :, t_cols(t)]
    o_at = lambda r, t: o_full.at[t, r]
    wh_at = lambda r: wh.at[pl.ds(pl.multiple_of(r * wr, wr), wr)]
    tok_at = lambda i: x2.at[pl.ds(2 * i, 2)]
    w_here = [
        copy_here(w_i, w_full.at[0, row, :, t_cols(z)]),
        copy_here(w_b, w_full.at[1, row, :, t_cols(z)]),
        copy_here(w_o, o_at(row, z)),
    ]
    mine = copy_here(tok2, tok_at(c))
    seg_here = copy_here(seg2, seg.at[c])
    bu_here = copy_here(b_unit, bu_full.at[z])
    here_sem = [local.at[next(local_number)] for _ in range(2)]
    here = [
        pltpu.make_async_copy(w_head, wh_at(row), here_sem[0]),
        pltpu.make_async_copy(b_head, bh, here_sem[1]),
    ]

    @pl.when(c == z)
    def _():
        for copy in here:
            copy.start()

    barrier = pltpu.get_barrier_semaphore()
    everyone = [at_c(k) for k in (1, 2, 3)] + [at_z(k) for k in (1, 2, 3)] + [at_x]
    for device in everyone:
        pl.semaphore_signal(barrier, inc=1, device_id=device, device_id_type=MESH)

    @pl.when(c != z)
    def _():
        pl.semaphore_signal(barrier, inc=1, device_id=across, device_id_type=MESH)

    pl.semaphore_wait(barrier, len(everyone) + jnp.where(c != z, 1, 0))

    n_ty, n_tc, n_tf, n_wa, n_ba = (next(number) for _ in range(5))
    rc.start(n_ty, lambda: (tok2, tok_at(c), at_c(2)))
    not_here = lambda: c != z
    rc.start(n_wa, lambda: (w_head, wh_at(row), across), not_here)
    rc.start(n_ba, lambda: (b_head, bh, across), not_here)
    rc.start(n_tc, lambda: (tok2, tok_at(c), at_c(1)))
    n_seg = four()
    for k in (1, 2, 3):
        rc.start(n_seg + k, lambda k=k: (seg2, seg.at[c], at_c(k)))

    class Line:
        def __init__(self, at):
            self.at = at
            self.n = [next(number) for _ in range(5)][0]

        def begin(self):
            own_ = lambda: self.at(z)
            rc.start(
                lambda: self.n + z,
                lambda: (own_(), own_(), (d, c, z + 1)),
                lambda: z < 3,
                self.n + 3,
            )
            rc.start(
                lambda: self.n + z,
                lambda: (own_(), own_(), (d, c, z - 1)),
                lambda: z > 0,
                self.n + 4,
            )

        def step(self, i):
            t = lambda: order[i]
            rc.arrived(self.n + t(), self.at(t()), (d, c, z))
            rc.start(
                lambda: self.n + t(),
                lambda: (
                    self.at(t()),
                    self.at(t()),
                    (d, c, jnp.where(t() < z, z + 1, z - 1)),
                ),
                lambda: jnp.where(t() < z, z < 3, z > 0),
                self.n + i - 1,
            )

    head_line = Line(lambda t: wh_at(d * nc + t))
    lines = (Line(lambda t: w_at(row, t)), Line(lambda t: o_at(row, t)))
    full_at = (w_at, o_at)
    n_hx = four()
    n_x, n_y, n_d = ([four(), four()] for _ in range(3))
    n_c = [[four(), four()] for _ in range(4)]

    def pass_on(n, i, r, device):
        t = lambda: order[i]
        for w in range(2):
            rc.start(
                lambda w=w: n[w] + t(),
                lambda w=w: (full_at[w](r, t()), full_at[w](r, t()), device()),
                None,
                n[w] + i,
            )

    def came(n, i, r, device):
        t = order[i]
        for w in range(2):
            rc.arrived(n[w] + t, full_at[w](r, t), device)

    def head_x(i):
        t = lambda: order[i]
        at = lambda: wh_at(d * nc + t())
        rc.start(lambda: n_hx + t(), lambda: (at(), at(), at_x), None, n_hx + i)

    def dense_step(i, chips):
        for line in lines:
            line.step(i)
        pass_on(n_x, i, row, to_x)
        if chips:
            dense_y(i)

    def dense_y(i):
        pass_on(n_y, i, row, to_c(2))
        pass_on(n_c[0], i, row, to_c(1))

    def from_x(i):
        came(n_x, i, row_x, at_x)
        if i >= 3:
            pass_on(n_d, i, row_x, to_c(2))
        pass_on(n_c[1], i, row_x, to_c(1))

    def from_y(i):
        came(n_y, i, row_y, at_c(2))
        if i < 3:
            pass_on(n_d, i, row_y, to_x)
        pass_on(n_c[2], i, row_y, to_c(1))

    def from_corner(i):
        came(n_d, i, row_d, at_x)
        pass_on(n_c[3], i, row_d, to_c(1))

    for copy in w_here:
        copy.wait()
    for line in lines:
        line.begin()
    pass_on(n_x, 0, row, to_x)
    pass_on(n_y, 0, row, to_c(2))
    pass_on(n_c[0], 0, row, to_c(1))
    n_bu = four()
    for k in (1, 2, 3):
        rc.start(n_bu + k, lambda k=k: (b_unit, bu_full.at[z], at_z(k)))

    @pl.when(c != z)
    def _():
        rc.arrived(n_wa, wh_at(d * nc + z), across)
        rc.arrived(n_ba, bh, across)

    @pl.when(c == z)
    def _():
        for copy in here:
            copy.wait()

    head_line.begin()
    head_x(0)
    q_scr[...] = jnp.zeros_like(q_scr)
    head_line.step(1)
    head_x(1)
    dense_step(1, True)
    head_line.step(2)
    head_x(2)
    head_line.step(3)
    head_x(3)
    for k in (1, 2, 3):
        rc.arrived(n_seg + k, seg.at[c ^ k], at_c(k))
    seg_here.wait()
    for i in range(nc):
        for s in range(2):
            line = seg[i, s : s + 1, :].astype(F32)
            segr[2 * i + s, 0:1, :] = line
            segc[2 * i + s] = jnp.broadcast_to(line, (128, ln)).T
    rc.arrived(n_ty, tok_at(c ^ 2), at_c(2))
    rc.start(n_tf, lambda: (tok_at(c ^ 2), tok_at(c ^ 2), at_c(1)))
    dense_step(2, True)
    for t in range(4):
        rc.arrived(n_hx + t, wh_at((1 - d) * nc + t), at_x)
    mine.wait()
    rc.arrived(n_tc, tok_at(c ^ 1), at_c(1))
    rc.arrived(n_tf, tok_at(c ^ 3), at_c(1))
    wh_here = copy_here(wh, wh_out)
    wide = heads * 128

    @pl.loop(0, 2 * nc)
    def _(i):
        x = x2[i]
        rows = pl.ds(pl.multiple_of(i * ln, ln), ln)
        xt[:, rows] = x.T
        got = (dot_nn(x, wh[:, :wide]) + bh[0:1, :wide]).astype(BF)
        kv[rows, :] = got
        qp = ((dot_nn(x, wh[:, wide:]) + bh[0:1, wide:]).astype(BF).astype(F32) * 0.125).astype(BF)
        for h in range(heads):
            q_scr[rows, 128 * h : 128 * h + HEAD] = qp[:, HEAD * h : HEAD * h + HEAD]

    x_here = copy_here(xt, xt_out)
    q_here = copy_here(q_scr, q_out)
    kv_here = copy_here(kv, kv_out)
    dense_step(3, True)
    from_x(0)

    @pl.loop(0, nc)
    def _(j):
        for s in range(2):
            rows = pl.ds(pl.multiple_of((2 * j + s) * ln, ln), ln)
            for h in range(heads):
                kvt[s * heads + h, :, pl.ds(pl.multiple_of(j * ln, ln), ln)] = kv[
                    rows, 128 * h : 128 * h + 128
                ].T

    from_x(1)

    def block(qb):
        r0, r1, o0, o1, seq = block_rows(qb, half, ln)
        b0 = jnp.where(qb < 4, qb, 2 * (qb - 4))
        b1 = jnp.where(qb < 4, qb, 2 * (qb - 4) + 1)
        s0 = pl.multiple_of(jnp.where(qb < 4, 0, hl * half), 128)
        s1 = pl.multiple_of(jnp.where(qb < 4, hl, hl * half), 128)
        sq = jnp.concatenate(
            [
                segr[2 * b0 + seq, 0:1, pl.ds(s0, hl)],
                segr[2 * b1 + seq, 0:1, pl.ds(s1, hl)],
            ],
            1,
        )
        q = [two(q_scr, r0, r1, hl, slice(128 * h, 128 * h + 128)) for h in range(heads)]

        def score(j, peaks):
            rows = pl.ds(pl.multiple_of((2 * j + seq) * ln, ln), ln)
            key_seg = segc[2 * j + seq]
            same = jnp.concatenate([key_seg, key_seg], 1) == sq
            new = []
            for h in range(heads):
                s = dot_nt(kv[rows, 128 * h : 128 * h + 128], q[h])
                s = jnp.where(same, s, NEG)
                s_scr[h, pl.ds(pl.multiple_of(j * ln, ln), ln), :] = s
                new.append(jnp.maximum(peaks[h], jnp.max(s, 0, keepdims=True)))
            return tuple(new)

        peaks = lax.fori_loop(
            0, nc, score, tuple(jnp.full((1, ln), NEG, F32) for _ in range(heads))
        )
        acc[...] = jnp.zeros_like(acc)

        def collect(j, sums):
            keys = pl.ds(pl.multiple_of(j * ln, ln), ln)
            new = []
            for h in range(heads):
                p = jnp.exp(s_scr[h, keys, :] - peaks[h])
                new.append(sums[h] + jnp.sum(p, 0, keepdims=True))
                acc[h] += dot_nn(kvt[seq * heads + h, :, keys], p.astype(BF))
            return tuple(new)

        sums = lax.fori_loop(
            0, nc, collect, tuple(jnp.zeros((1, ln), F32) for _ in range(heads))
        )
        whole = []
        for h in range(heads):
            one = acc[h, HEAD:, :] / sums[h]
            whole.append(one)
            line = peaks[h] + jnp.log(sums[h])
            for part, at in ((0, o0), (hl, o1)):
                ctx_t[HEAD * h : HEAD * h + HEAD, pl.ds(at, hl)] = one[:, part : part + hl]
                lse[h : h + 1, pl.ds(at, hl)] = line[:, part : part + hl]
        turned = jnp.concatenate(whole, 0).T.astype(BF)
        context[pl.ds(o0, hl), :] = turned[:hl]
        context[pl.ds(o1, hl), :] = turned[hl:]

    @pl.loop(0, 6)
    def _(qb):
        block(qb)

        @pl.when(qb == 1)
        def _():
            from_y(0)

        @pl.when(qb == 3)
        def _():
            from_x(2)
            from_y(1)

    n_ctx = four()
    ctx_at = lambda i: context.at[pl.ds(pl.multiple_of(i * own, 128), own)]
    for k in (1, 2, 3):
        rc.start(n_ctx + k, lambda k=k: (ctx_at(c ^ k), ctx_all.at[c], at_c(k)))
    ctx_here = copy_here(ctx_at(c), ctx_all.at[c])
    from_x(3)
    from_y(2)
    from_corner(0)
    from_corner(1)
    for k in (1, 2, 3):
        rc.arrived(n_ctx + k, ctx_all.at[c ^ k], at_c(k))
        rc.arrived(n_bu + k, bu_full.at[z ^ k], at_z(k))
    from_y(3)
    from_corner(2)
    from_corner(3)
    for n, r in zip(n_c, (row, row_x, row_y, row_d)):
        for i in range(4):
            came(n, i, r ^ 1, at_c(1))
    for copy in (bu_here, x_here, wh_here, q_here, kv_here, ctx_here):
        copy.wait()
    rc.all_sent()


def forward(tok2, seg2, w_head, b_head, b_unit, w_o, w_i, w_b, heads):
    ln, width = tok2.shape[1:]
    wr, units = w_i.shape
    group = w_o.shape[1]
    nc, nt, nr = 4, 4, 8
    rows = 3 * ln // 2 * nc
    hb = pl.BlockSpec(memory_space=pl.ANY)
    vm = pl.BlockSpec(memory_space=pltpu.VMEM)
    sds = jax.ShapeDtypeStruct
    return pl.pallas_call(
        functools.partial(forward_kernel, heads, ln),
        out_shape=(
            sds((nc, 3 * ln // 2, group), BF),
            sds((width, 2 * nc * ln), BF),
            sds((2 * nc * ln, heads * 128), BF),
            sds((2 * nc * ln, heads * 128), BF),
            sds((nr * wr, 3 * group), BF),
            sds((nt, nr, wr, group), BF),
            sds((2, nr, wr, nt * units), BF),
            sds((nt, 8, units), F32),
            sds((8, rows), F32),
            sds((group, rows), F32),
            sds((nc, 8, ln), jnp.int32),
        ),
        in_specs=[hb] * 8,
        out_specs=(hb,) * 8 + (vm,) * 3,
        scratch_shapes=[
            pltpu.VMEM((2 * nc, ln, width), BF),
            pltpu.VMEM((width, 2 * nc * ln), BF),
            pltpu.VMEM((nr * wr, 3 * group), BF),
            pltpu.VMEM((8, 3 * group), F32),
            pltpu.VMEM((2 * nc * ln, heads * 128), BF),
            pltpu.VMEM((2 * nc * ln, heads * 128), BF),
            pltpu.VMEM((heads, nc * ln, ln), F32),
            pltpu.VMEM((2 * heads, 128, nc * ln), BF),
            pltpu.VMEM((heads, 128, ln), F32),
            pltpu.VMEM((2 * nc, ln, 128), F32),
            pltpu.VMEM((2 * nc, 8, ln), F32),
            pltpu.VMEM((rows, group), BF),
            pltpu.SemaphoreType.DMA((120,)),
            pltpu.SemaphoreType.DMA((120,)),
            pltpu.SemaphoreType.DMA((32,)),
        ],
        compiler_params=pltpu.CompilerParams(
            vmem_limit_bytes=40 << 20, collective_id=0, has_side_effects=True
        ),
        name="forward",
    )(tok2, seg2, w_head, b_head, b_unit, w_o, w_i, w_b)


def add_into(dst, other, rows):
    @pl.loop(0, rows // 16)
    def _(i):
        at = pl.ds(pl.multiple_of(i * 16, 16), 16)
        for a, b in zip(dst, other):
            a[at, :] = (a[at, :].astype(F32) + b[at, :].astype(F32)).astype(a.dtype)


def backward_kernel(
    heads,
    ln,
    d_ctx,
    g_b,
    g_i,
    g_o,
    out_low,
    d_first,
    small_in,
    q_in,
    kv_in,
    xt_in,
    wh_in,
    lse,
    ctx_t,
    seg,
    output,
    d_tokens,
    gf_b,
    gf_i,
    gf_o,
    gf_h,
    small,
    bias,
    q_scr,
    kv,
    xt,
    wh,
    d_got,
    d_o,
    kvt,
    dkv,
    dqt,
    d_proj,
    segc,
    segr,
    part,
    got_c,
    got_y,
    got_z,
    send_y,
    send_z,
    mine,
    done,
    o_b,
    o_i,
    o_o,
    r_b,
    r_i,
    r_o,
    x_b,
    x_i,
    x_o,
    y_b,
    y_i,
    y_o,
    z_b,
    z_i,
    z_o,
    acc_h,
    o_h,
    x_h,
    z_h,
    send_h,
    small_got,
    bias_sum,
    bias_got,
    h_got,
    bias_fin,
    send,
    recv,
    local,
):
    d, c, z = (lax.axis_index(n) for n in ALL)
    nc = 4
    hl = ln // 2
    own = ln + hl
    half = z % 2
    core, y = c % 2, c // 2
    wr = gf_b.shape[0]
    units = gf_b.shape[1]
    width = out_low.shape[1]
    wide = heads * 128
    rc = Copies(send, recv)
    at_c = lambda k: (d, c ^ k, z)
    at_x = (1 - d, c, z)
    at_z = lambda k: (d, c, z ^ k)
    across = (d, z, c)

    barrier = pltpu.get_barrier_semaphore()
    everyone = [at_c(k) for k in (1, 2, 3)] + [at_z(k) for k in (1, 2, 3)] + [at_x]
    for device in everyone:
        pl.semaphore_signal(barrier, inc=1, device_id=device, device_id_type=MESH)

    @pl.when(c != z)
    def _():
        pl.semaphore_signal(barrier, inc=1, device_id=across, device_id_type=MESH)

    pl.semaphore_wait(barrier, len(everyone) + jnp.where(c != z, 1, 0))

    number = iter(range(200))
    local_number = iter(range(40))

    def copy_here(src, dst):
        copy = pltpu.make_async_copy(src, dst, local.at[next(local_number)])
        copy.start()
        return copy

    flat = lambda ref: (lambda xy, h: (ref.at[xy, :, pl.ds(1536 * h, 1536)],))
    weights = []
    for own_b, got_b, x_buf, y_buf, z_buf, grad, final, is_o in (
        (o_b, r_b, x_b, y_b, z_b, g_b, gf_b, False),
        (o_i, r_i, x_i, y_i, z_i, g_i, gf_i, False),
        (o_o, r_o, x_o, y_o, z_o, g_o, gf_o, True),
    ):
        n = [next(number) for _ in range(12)]
        weights.append((own_b, got_b, x_buf, y_buf, z_buf, grad, final, is_o, n))
    half_units = 2 * units

    def of_core(w, which):
        grad, is_o = w[5], w[7]
        return grad.at[:, :, which] if is_o else grad.at[:, which]

    def part_of(w, xy, h):
        if w[7]:
            return w[0].at[pl.ds(2 * h, 2), xy]
        return w[0].at[xy, :, pl.ds(half_units * h, half_units)]

    def views(w, xy, h):
        if w[7]:
            return [w[0].at[2 * h, xy], w[0].at[2 * h + 1, xy]]
        return [w[0].at[xy, :, pl.ds(half_units * h, half_units)]]

    def buf_views(w, ref, i):
        return [ref.at[i, 0], ref.at[i, 1]] if w[7] else [ref.at[i]]

    def unit_at(w, t):
        xy = 2 * d + y
        if w[7]:
            return w[0].at[t, xy]
        return w[0].at[xy, :, pl.ds(pl.multiple_of(t * units, 128), units)]

    w_here = [copy_here(of_core(w, core), w[0]) for w in weights]
    blk = lambda x_, y_: 2 * x_ + y_

    def w_core_send(w):
        rc.start(w[8][0], lambda: (of_core(w, 1 - core), w[1], at_c(1)))

    def w_core_add(i):
        w = weights[i]
        w_here[i].wait()
        rc.arrived(w[8][0], w[1], at_c(1))

        @pl.loop(0, 4)
        def _(xy):
            if w[7]:
                add_into([w[0].at[t, xy] for t in range(4)], [w[1].at[t, xy] for t in range(4)], wr)
            else:
                add_into([w[0].at[xy]], [w[1].at[xy]], wr)

        n = w[8]
        for j in range(2):
            rc.start(n[1 + j], lambda j=j: (part_of(w, blk(1 - d, j), 0), w[2].at[j], at_x))
            rc.start(n[3 + j], lambda j=j: (part_of(w, blk(j, 1 - y), 1), w[3].at[j], at_c(2)))

    def w_plane(i):
        w = weights[i]
        n = w[8]
        for j in range(2):
            rc.arrived(n[1 + j], w[2].at[j], at_x)
        for j in range(2):
            add_into(views(w, blk(d, j), 0), buf_views(w, w[2], j), wr)
        rc.start(n[5], lambda: (part_of(w, blk(d, 1 - y), 0), w[3].at[2], at_c(2)))
        for j in range(2):
            rc.arrived(n[3 + j], w[3].at[j], at_c(2))
        for j in range(2):
            add_into(views(w, blk(j, y), 1), buf_views(w, w[3], j), wr)
        rc.start(n[6], lambda: (part_of(w, blk(1 - d, y), 1), w[2].at[2], at_x))

    def w_corner(i):
        w = weights[i]
        n = w[8]
        rc.arrived(n[5], w[3].at[2], at_c(2))
        add_into(views(w, blk(d, y), 0), buf_views(w, w[3], 2), wr)
        rc.arrived(n[6], w[2].at[2], at_x)
        add_into(views(w, blk(d, y), 1), buf_views(w, w[2], 2), wr)
        rc.start(n[7], lambda: (unit_at(w, z ^ 1), w[4].at[0], at_z(1)))
        rc.start(n[8], lambda: (unit_at(w, z ^ 3), w[4].at[1], at_z(1)))

    def w_line(i):
        w = weights[i]
        n = w[8]
        rc.arrived(n[8], w[4].at[1], at_z(1))
        add_into([unit_at(w, z ^ 2)], [w[4].at[1]], wr)
        rc.start(n[9], lambda: (unit_at(w, z ^ 2), w[4].at[2], at_z(2)))
        rc.arrived(n[7], w[4].at[0], at_z(1))
        add_into([unit_at(w, z)], [w[4].at[0]], wr)

    def w_end(i):
        w = weights[i]
        rc.arrived(w[8][9], w[4].at[2], at_z(2))
        w[6][...] = unit_at(w, z)[...].astype(F32) + w[4].at[2][...].astype(F32)

    whole_of = lambda t: (3 * t + 1) // 2
    shared_of = lambda t: 1 + 3 * (t // 2)

    class Line:
        def __init__(self, at):
            self.at = at
            self.left = [next(number) for _ in range(3)]
            self.right = [next(number) for _ in range(3)]

        def begin(self, src):
            rc.start(self.left[0], lambda: (src, self.at(z), (d, c, z + 1)), lambda: z < 3)
            rc.start(self.right[0], lambda: (src, self.at(z), (d, c, z - 1)), lambda: z > 0)

        def step(self, j):
            from_left, from_right = z - j, z + j

            @pl.when(z >= j)
            def _():
                rc.arrived(self.left[j - 1], self.at(from_left), (d, c, z - 1))

            if j < 3:
                rc.start(
                    self.left[j],
                    lambda: (self.at(z - j), self.at(z - j), (d, c, z + 1)),
                    lambda: (z >= j) & (z < 3),
                )

            @pl.when(z + j <= 3)
            def _():
                rc.arrived(self.right[j - 1], self.at(from_right), (d, c, z + 1))

            if j < 3:
                rc.start(
                    self.right[j],
                    lambda: (self.at(z + j), self.at(z + j), (d, c, z - 1)),
                    lambda: (z + j <= 3) & (z > 0),
                )

    whole_rows = lambda ref, a, n: (lambda t: ref.at[whole_of(t), pl.ds(a, n)])
    shared_rows = lambda ref: (
        lambda t: ref.at[shared_of(t), pl.ds(pl.multiple_of((t % 2) * hl, 128), hl)]
    )
    out_lines = [Line(whole_rows(output, 0, ln)), Line(shared_rows(output))]
    tok_lines = [
        Line(whole_rows(d_tokens, 0, hl)),
        Line(whole_rows(d_tokens, hl, hl)),
        Line(shared_rows(d_tokens)),
    ]

    n_ctx = [next(number) for _ in range(3)]
    for k in (1, 2, 3):
        rc.start(n_ctx[k - 1], lambda k=k: (d_ctx.at[c ^ k], d_got.at[c], at_c(k)))
    ctx_here = copy_here(d_ctx.at[c], d_got.at[c])
    for w in weights:
        w_core_send(w)
    kv_here = copy_here(kv_in, kv)
    q_here = copy_here(q_in, q_scr)
    n_small = [next(number) for _ in range(5)]
    small_to = (at_c(1), at_c(2), at_x, at_z(1), at_z(2))
    small[...] = small_in[...]

    def small_send(i):
        rc.start(n_small[i], lambda: (small_got.at[i, 1], small_got.at[i, 0], small_to[i]))

    def small_step(i):
        rc.arrived(n_small[i], small_got.at[i, 0], small_to[i])
        small[...] += small_got[i, 0]
        if i < 4:
            small_got[i + 1, 1] = small[...]
            small_send(i + 1)

    small_got[0, 1] = small_in[...]
    small_send(0)
    wh_here = copy_here(wh_in, wh)
    xt_here = copy_here(xt_in, xt)
    out_lines[0].begin(out_low.at[pl.ds(0, ln)])
    out_lines[1].begin(out_low.at[pl.ds(ln, hl)])
    out_here = [
        copy_here(out_low.at[pl.ds(0, ln)], out_lines[0].at(z)),
        copy_here(out_low.at[pl.ds(ln, hl)], out_lines[1].at(z)),
    ]

    for i in range(nc):
        for s in range(2):
            line = seg[i, s : s + 1, :].astype(F32)
            segr[2 * i + s, 0:1, :] = line
            segc[2 * i + s] = jnp.broadcast_to(line, (128, ln)).T
    dkv[...] = jnp.zeros_like(dkv)
    d_o[...] = jnp.zeros_like(d_o)
    d_proj[...] = jnp.zeros_like(d_proj)
    bias_sum[...] = jnp.zeros_like(bias_sum)
    kv_here.wait()

    @pl.loop(0, nc)
    def _(j):
        for s in range(2):
            rows = pl.ds(pl.multiple_of((2 * j + s) * ln, ln), ln)
            for h in range(heads):
                kvt[s * heads + h, :, pl.ds(pl.multiple_of(j * ln, ln), ln)] = kv[
                    rows, 128 * h : 128 * h + 128
                ].T

    w_core_add(0)
    small_step(0)
    for k in (1, 2, 3):
        rc.arrived(n_ctx[k - 1], d_got.at[c ^ k], at_c(k))
    ctx_here.wait()

    @pl.loop(0, nc)
    def _(i):
        rows = pl.ds(pl.multiple_of(i * own, 128), own)
        for h in range(heads):
            d_o[rows, 128 * h + HEAD : 128 * h + 128] = d_got[i, :, HEAD * h : HEAD * h + HEAD]

    q_here.wait()
    w_core_add(1)

    def block(qb):
        r0, r1, o0, o1, seq = block_rows(qb, half, ln)
        b0 = jnp.where(qb < 4, qb, 2 * (qb - 4))
        b1 = jnp.where(qb < 4, qb, 2 * (qb - 4) + 1)
        s0 = pl.multiple_of(jnp.where(qb < 4, 0, hl * half), 128)
        s1 = pl.multiple_of(jnp.where(qb < 4, hl, hl * half), 128)
        sq = jnp.concatenate(
            [
                segr[2 * b0 + seq, 0:1, pl.ds(s0, hl)],
                segr[2 * b1 + seq, 0:1, pl.ds(s1, hl)],
            ],
            1,
        )
        q, do, line, delta = [], [], [], []
        for h in range(heads):
            q.append(two(q_scr, r0, r1, hl, slice(128 * h, 128 * h + 128)))
            do.append(two(d_o, o0, o1, hl, slice(128 * h, 128 * h + 128)))
            line.append(two_lanes(lse, slice(h, h + 1), o0, o1, hl))
            turned = do[h].astype(F32).T[HEAD:, :]
            kept = two_lanes(ctx_t, slice(HEAD * h, HEAD * h + HEAD), o0, o1, hl)
            delta.append(jnp.sum(turned * kept, 0, keepdims=True))
        dqt[...] = jnp.zeros_like(dqt)

        @pl.loop(0, nc)
        def _(j):
            rows = pl.ds(pl.multiple_of((2 * j + seq) * ln, ln), ln)
            keys = pl.ds(pl.multiple_of(j * ln, ln), ln)
            key_seg = segc[2 * j + seq]
            same = jnp.concatenate([key_seg, key_seg], 1) == sq
            for h in range(heads):
                kvh = kv[rows, 128 * h : 128 * h + 128]
                p = jnp.where(same, jnp.exp(dot_nt(kvh, q[h]) - line[h]), 0.0)
                ds = (p * (dot_nt(kvh, do[h]) - delta[h])).astype(BF)
                dkv[rows, 128 * h : 128 * h + 128] += dot_nn(ds, q[h]) + dot_nn(
                    p.astype(BF), do[h]
                )
                dqt[h] += dot_nn(kvt[seq * heads + h, :, keys], ds)

        turned = jnp.concatenate([dqt[h, :HEAD, :] for h in range(heads)], 0).T * 0.125
        bias_sum[0:1, wide:] += jnp.sum(turned, 0, keepdims=True)
        low = turned.astype(BF)
        d_proj[pl.ds(r0, hl), wide:] = low[:hl]
        d_proj[pl.ds(r1, hl), wide:] = low[hl:]

    n_tc = [[next(number), next(number)] for _ in range(2)]
    n_ty = [[next(number), next(number)] for _ in range(2)]
    n_tz = next(number)

    def rows_of(cb, s):
        rows = pl.ds(pl.multiple_of((2 * cb + s) * ln, ln), ln)
        got = dkv[rows, :]
        bias_sum[0:1, :wide] += jnp.sum(got, 0, keepdims=True)
        d_proj[rows, :wide] = got.astype(BF)
        part[cb, s] = dot_nt(d_proj[rows, :], wh[...]).astype(BF)

    def t_partial(s):
        rows_of(c ^ 3, s)
        rc.start(n_tc[s][0], lambda: (part.at[c ^ 3, s], got_c.at[s, 0], at_c(1)))
        rows_of(c ^ 1, s)
        rc.start(n_tc[s][1], lambda: (part.at[c ^ 1, s], got_c.at[s, 1], at_c(1)))
        rows_of(c ^ 2, s)
        rows_of(c, s)

    def t_core(s):
        rc.arrived(n_tc[s][0], got_c.at[s, 0], at_c(1))
        for k in range(2):
            at = slice(k * hl, k * hl + hl)
            send_y[s, at] = (part[c ^ 2, s, at].astype(F32) + got_c[s, 0, at].astype(F32)).astype(BF)
            rc.start(
                n_ty[s][k],
                lambda k=k: (
                    send_y.at[s, pl.ds(k * hl, hl)],
                    got_y.at[s, pl.ds(k * hl, hl)],
                    at_c(2),
                ),
            )
        rc.arrived(n_tc[s][1], got_c.at[s, 1], at_c(1))
        mine[s] = part[c, s].astype(F32) + got_c[s, 1].astype(F32)

    def t_shared():
        for k in range(2):
            rc.arrived(n_ty[1][k], got_y.at[1, pl.ds(k * hl, hl)], at_c(2))
        mine[1] += got_y[1].astype(F32)
        send_z[...] = mine[1, pl.ds(pl.multiple_of((1 - half) * hl, 128), hl)].astype(BF)
        rc.start(n_tz, lambda: (send_z, got_z, at_z(1)))

    def t_shared_end():
        rc.arrived(n_tz, got_z, at_z(1))
        mine_half = mine[1, pl.ds(pl.multiple_of(half * hl, 128), hl)]
        done[ln:, :] = (mine_half + got_z[...].astype(F32) + d_first[ln:, :]).astype(BF)
        tok_lines[2].begin(done.at[pl.ds(ln, hl)])

    def t_whole(k):
        at = slice(k * hl, k * hl + hl)
        rc.arrived(n_ty[0][k], got_y.at[0, pl.ds(k * hl, hl)], at_c(2))
        done[at, :] = (mine[0, at] + got_y[0, at].astype(F32) + d_first[at, :]).astype(BF)
        tok_lines[k].begin(done.at[pl.ds(k * hl, hl)])

    n_h = [next(number) for _ in range(8)]

    def h_partial(seq):
        @pl.loop(0, nc)
        def _(i):
            rows = pl.ds(pl.multiple_of((2 * i + seq) * ln, ln), ln)
            acc_h[...] += dot_nn(xt[:, rows], d_proj[rows, :])

    def h_send():
        o_h[...] = acc_h[...].astype(BF)
        rows_x = lambda x_: pl.ds(pl.multiple_of(x_ * 4 * wr, wr), 4 * wr)
        rc.start(n_h[0], lambda: (o_h.at[rows_x(1 - d)], x_h, at_x))

    h_at = lambda t: o_h.at[pl.ds(pl.multiple_of((4 * d + t) * wr, wr), wr)]

    def h_plane():
        rc.arrived(n_h[0], x_h, at_x)
        add_into([o_h.at[pl.ds(pl.multiple_of(d * 4 * wr, wr), 4 * wr)]], [x_h], 4 * wr)
        rc.start(n_h[1], lambda: (h_at(z ^ 3), z_h.at[1], at_z(1)))
        rc.start(n_h[2], lambda: (h_at(z ^ 1), z_h.at[0], at_z(1)))

    def h_line():
        rc.arrived(n_h[1], z_h.at[1], at_z(1))
        add_into([h_at(z ^ 2)], [z_h.at[1]], wr)
        rc.start(n_h[3], lambda: (h_at(z ^ 2), z_h.at[2], at_z(2)))
        rc.arrived(n_h[2], z_h.at[0], at_z(1))
        add_into([h_at(z)], [z_h.at[0]], wr)

    def h_end():
        rc.arrived(n_h[3], z_h.at[2], at_z(2))
        send_h[...] = h_at(z)[...].astype(F32) + z_h[2].astype(F32)
        rc.start(n_h[4], lambda: (send_h, h_got, across), lambda: c != z)

        @pl.when(c == z)
        def _():
            h_got[...] = send_h[...]

    n_bias = [next(number) for _ in range(4)]
    bias_to = (at_x, at_z(1), at_z(2))

    def bias_send(i):
        bias_got[i, 1] = bias_sum[...]
        rc.start(n_bias[i], lambda: (bias_got.at[i, 1], bias_got.at[i, 0], bias_to[i]))

    def bias_step(i):
        rc.arrived(n_bias[i], bias_got.at[i, 0], bias_to[i])
        bias_sum[...] += bias_got[i, 0]
        if i < 2:
            bias_send(i + 1)
            return
        rc.start(n_bias[3], lambda: (bias_sum, bias_fin, across), lambda: c != z)

        @pl.when(c == z)
        def _():
            bias_fin[...] = bias_sum[...]

    wh_here.wait()
    xt_here.wait()
    acc_h[...] = jnp.zeros_like(acc_h)

    @pl.loop(0, 6)
    def _(i):
        block(jnp.where(i < 2, i + 4, i - 2))

        @pl.when(i == 0)
        def _():
            w_core_add(2)

        @pl.when(i == 1)
        def _():
            t_partial(1)
            h_partial(1)
            small_step(1)
            for line in out_lines:
                line.step(1)

        @pl.when(i == 2)
        def _():
            w_plane(0)
            t_core(1)

        @pl.when(i == 3)
        def _():
            small_step(2)

        @pl.when(i == 4)
        def _():
            w_corner(0)
            small_step(3)
            for line in out_lines:
                line.step(2)

    t_partial(0)
    h_partial(0)
    h_send()
    bias_send(0)
    t_core(0)
    t_shared()
    w_plane(1)
    small_step(4)
    t_whole(0)
    t_whole(1)
    w_plane(2)
    t_shared_end()
    bias_step(0)
    h_plane()
    w_line(0)
    tok_lines[0].step(1)
    tok_lines[1].step(1)
    tok_lines[2].step(1)
    w_corner(1)
    bias_step(1)
    w_corner(2)
    tok_lines[0].step(2)
    tok_lines[1].step(2)
    tok_lines[2].step(2)
    h_line()
    bias_step(2)
    w_line(1)
    w_line(2)
    h_end()
    for line in out_lines:
        line.step(3)
    w_end(0)
    w_end(1)
    w_end(2)
    tok_here = [
        copy_here(done.at[pl.ds(0, hl)], tok_lines[0].at(z)),
        copy_here(done.at[pl.ds(hl, hl)], tok_lines[1].at(z)),
        copy_here(done.at[pl.ds(ln, hl)], tok_lines[2].at(z)),
    ]
    for line in tok_lines:
        line.step(3)

    @pl.when(c != z)
    def _():
        rc.arrived(n_h[4], h_got, across)
        rc.arrived(n_bias[3], bias_fin, across)

    gf_h[...] = h_got[...]
    bias[...] = bias_fin[...]

    for copy in out_here + tok_here:
        copy.wait()
    rc.all_sent()


def backward(d_ctx, g_b, g_i, g_o, out_low, d_first, small, q, kv, xt, wh, lse, ctx_t, seg, heads, seqs):
    nc, own, group = d_ctx.shape
    ln = own * 2 // 3
    hl = ln // 2
    width = out_low.shape[1]
    wr, all_units = g_b.shape[2:]
    units = all_units // 4
    hb = pl.BlockSpec(memory_space=pl.ANY)
    vm = pl.BlockSpec(memory_space=pltpu.VMEM)
    sds = jax.ShapeDtypeStruct
    v = pltpu.VMEM
    rows = nc * own
    n2 = 2 * nc * ln
    return pl.pallas_call(
        functools.partial(backward_kernel, heads, ln),
        out_shape=(
            sds((seqs, ln, width), BF),
            sds((seqs, ln, width), BF),
            sds((wr, units), F32),
            sds((wr, units), F32),
            sds((wr, group), F32),
            sds((wr, 3 * group), F32),
            sds(small.shape, F32),
            sds((8, 3 * group), F32),
        ),
        in_specs=[hb] * 5 + [vm, vm] + [hb] * 4 + [vm] * 3,
        out_specs=(hb, hb) + (vm,) * 6,
        scratch_shapes=[
            v((n2, heads * 128), BF),
            v((n2, heads * 128), BF),
            v((width, n2), BF),
            v((width, 3 * group), BF),
            v((nc, own, group), BF),
            v((rows, heads * 128), BF),
            v((2 * heads, 128, nc * ln), BF),
            v((n2, heads * 128), F32),
            v((heads, 128, ln), F32),
            v((n2, 3 * group), BF),
            v((2 * nc, ln, 128), F32),
            v((2 * nc, 8, ln), F32),
            v((nc, 2, ln, width), BF),
            v((2, 2, ln, width), BF),
            v((2, ln, width), BF),
            v((hl, width), BF),
            v((2, ln, width), BF),
            v((hl, width), BF),
            v((2, ln, width), F32),
            v((own, width), BF),
            v((4, wr, all_units), BF),
            v((4, wr, all_units), BF),
            v((4, 4, wr, group), BF),
            v((4, wr, all_units), BF),
            v((4, wr, all_units), BF),
            v((4, 4, wr, group), BF),
            v((3, wr, 2 * units), BF),
            v((3, wr, 2 * units), BF),
            v((3, 2, wr, group), BF),
            v((3, wr, 2 * units), BF),
            v((3, wr, 2 * units), BF),
            v((3, 2, wr, group), BF),
            v((3, wr, units), BF),
            v((3, wr, units), BF),
            v((3, wr, group), BF),
            v((width, 3 * group), F32),
            v((width, 3 * group), BF),
            v((4 * wr, 3 * group), BF),
            v((3, wr, 3 * group), BF),
            v((wr, 3 * group), F32),
            v((5, 2) + small.shape, F32),
            v((8, 3 * group), F32),
            v((3, 2, 8, 3 * group), F32),
            v((wr, 3 * group), F32),
            v((8, 3 * group), F32),
            pltpu.SemaphoreType.DMA((130,)),
            pltpu.SemaphoreType.DMA((130,)),
            pltpu.SemaphoreType.DMA((40,)),
        ],
        compiler_params=pltpu.CompilerParams(
            vmem_limit_bytes=58 << 20, collective_id=1, has_side_effects=True
        ),
        name="backward",
    )(d_ctx, g_b, g_i, g_o, out_low, d_first, small, q, kv, xt, wh, lse, ctx_t, seg)


def head_order(kinds, heads):
    lead = kinds[0].shape[:-1]
    q, k, v = (a.reshape(lead + (heads, HEAD)) for a in kinds)
    kv = jnp.concatenate([k, v], -1).reshape(lead + (heads * 2 * HEAD,))
    return jnp.concatenate([kv, q.reshape(lead + (heads * HEAD,))], -1)


def head_kinds(value, heads):
    lead = value.shape[:-1]
    kv = value[..., : heads * 2 * HEAD].reshape(lead + (heads, 2, HEAD))
    flat = lambda a: a.reshape(lead + (heads * HEAD,))
    return value[..., heads * 2 * HEAD :], flat(kv[..., 0, :]), flat(kv[..., 1, :])


def forward_plain(sizes, me, tok2, seg2, w_head, b_head, b_unit, w_o, w_i, w_b, heads):
    nd, nc, nt = sizes
    d, c, z = me
    ln, width = tok2.shape[1:]
    hl = ln // 2
    half = z % 2
    group = w_o.shape[1]
    seg_all = gather_axis(seg2, "ctx", nc, c)
    x2 = gather_axis(tok2, "ctx", nc, c).reshape(2 * nc, ln, width)
    wh = gather_heads(w_head, sizes, me)
    bh = transpose_ctx_tp(b_head, nc)[0]
    b_all = gather_axis(b_unit, "tp", nt, z)
    gather = lambda w: lax.all_gather(
        lax.all_gather(w, "tp", axis=1, tiled=True), ("dp", "ctx"), axis=0, tiled=True
    )
    o_full = jnp.transpose(gather(w_o).reshape(width, nt, group), (1, 0, 2))
    proj = (jnp.dot(x2.reshape(-1, width), wh, preferred_element_type=F32) + bh).astype(BF)
    kv = proj[:, : 2 * group]
    q = (proj[:, 2 * group :].astype(F32) * 0.125).astype(BF).reshape(-1, heads, HEAD)
    q = jnp.concatenate([q, jnp.zeros_like(q)], -1).reshape(-1, heads * 128)
    info, seg_col, seg_row = key_blocks(seg_all, half, ln, nc)
    context, lse, ctx_t = attend(info, q, kv, seg_col, seg_row, heads, ln, nc)
    ctx_all = in_order(exchange_axis(context.reshape(nc, ln + hl, group), "ctx", nc, c), c)
    return (
        ctx_all,
        x2.reshape(-1, width).T,
        q,
        kv,
        wh,
        o_full,
        jnp.stack([gather(w_i), gather(w_b)]),
        b_all,
        lse,
        ctx_t,
        seg_all,
    )


def key_blocks(seg_all, half, ln, nc):
    hl = ln // 2
    seg2 = seg_all[:, :2]
    flat = jnp.transpose(seg2, (1, 0, 2)).reshape(2, nc * ln)
    first = jnp.concatenate([seg2[:, 0, 0], jnp.take(seg2[0::2, 1], half * hl, axis=1)])
    last = jnp.concatenate([seg2[:, 0, -1], jnp.take(seg2[1::2, 1], half * hl + hl - 1, axis=1)])
    of = jnp.concatenate(
        [
            jnp.broadcast_to(flat[:1], (nc, nc * ln)),
            jnp.broadcast_to(flat[1:], (nc // 2, nc * ln)),
        ],
        0,
    )
    lo = jnp.sum(of < first[:, None], 1) // ln
    hi = (jnp.sum(of <= last[:, None], 1) + ln - 1) // ln
    info = jnp.concatenate([lo, hi, half[None]]).astype(jnp.int32)
    seg_flat = seg2.reshape(2 * nc * ln)
    return info, seg_flat[:, None], seg_flat[None, :]


def backward_plain(
    sizes, me, d_ctx, low, out_low, d_first, small, q, kv, xt, wh, lse, ctx_t, seg_all, heads, seqs
):
    nd, nc, nt = sizes
    d, c, z = me
    own, group = d_ctx.shape[1:]
    ln = own * 2 // 3
    hl = ln // 2
    half = z % 2
    width = out_low.shape[1]
    units = low[0].shape[1] // nt
    nr = nd * nc
    wr = width // nr
    info, seg_col, seg_row = key_blocks(seg_all, half, ln, nc)

    def spread_rows(rows_low, dtype):
        out = jnp.zeros((seqs, ln, width), dtype)
        parts = [rows_low] + [swap_with(rows_low, "tp", nt, k) for k in range(1, nt)]
        for k, part in enumerate(parts):
            t = z ^ k
            part = part.astype(dtype)
            out = lax.dynamic_update_slice(out, part[None, :ln], ((3 * t + 1) // 2, 0, 0))
            out = lax.dynamic_update_slice(
                out, part[None, ln:], (1 + 3 * (t // 2), (t % 2) * hl, 0)
            )
        return out

    by_unit = lambda g: jnp.transpose(g.reshape(nr, wr, nt, units), (2, 0, 1, 3))
    g_back = scatter_weight(by_unit(low[0]), sizes, me)
    g_in = scatter_weight(by_unit(low[1]), sizes, me)
    g_out = scatter_weight(low[2].reshape(nt, nr, wr, group), sizes, me)
    output = spread_rows(out_low, BF)
    small = lax.psum(small, ALL)
    d_ctx = in_order(exchange_axis(d_ctx, "ctx", nc, c), c).reshape(nc * own, heads, HEAD)
    d_ctx = jnp.concatenate([jnp.zeros_like(d_ctx), d_ctx], -1).reshape(nc * own, heads * 128)
    d_q, d_kv, d_bias = attend_back(
        info, q, kv, d_ctx, seg_col, seg_row, lse, ctx_t, heads, ln, nc
    )
    d_proj = jnp.concatenate([d_kv, d_q], -1)
    part = jnp.einsum("tf,df->td", d_proj, wh, preferred_element_type=F32)
    part = lax.psum_scatter(
        part.reshape(nc, 2 * ln, width), "ctx", scatter_dimension=0, tiled=False
    ).reshape(2, ln, width)
    shared = part[1].reshape(2, hl, width)
    shared = lax.dynamic_index_in_dim(shared, half, 0, keepdims=False) + swap_with(
        lax.dynamic_index_in_dim(shared, 1 - half, 0, keepdims=False), "tp", nt, 1
    )
    d_own = (jnp.concatenate([part[0], shared], 0) + d_first).astype(BF)
    d_tokens = spread_rows(d_own, F32)
    g_h = scatter_heads(jnp.dot(xt, d_proj, preferred_element_type=F32).astype(BF), sizes, me)
    slots = jnp.zeros((nc,) + d_bias[0].shape, F32)
    slots = lax.psum(lax.dynamic_update_index_in_dim(slots, d_bias[0], c, 0), ALL)
    d_bias = lax.dynamic_index_in_dim(slots, z, 0, keepdims=False)
    return output, d_tokens, g_back, g_in, g_out, g_h, small, d_bias


def per_device(
    sizes,
    tokens,
    segments,
    w_qkv,
    q_bias,
    v_bias,
    w_out,
    out_bias,
    gain_one,
    shift_one,
    w_in,
    in_bias,
    w_back,
    back_bias,
    gain_two,
    shift_two,
    cotangent,
):
    nd, nc, nt = sizes
    seqs, ln, width = tokens.shape
    hl = ln // 2
    group = w_out.shape[1]
    heads = group // HEAD
    units = w_in.shape[1]
    wr = w_in.shape[0]
    d, c, z = (lax.axis_index(n) for n in ALL)
    me = (d, c, z)
    whole_of = lambda t: (3 * t + 1) // 2
    shared_of = lambda t: 1 + 3 * (t // 2)
    half_of = lambda t: t % 2
    sf, sh, half = whole_of(z), shared_of(z), half_of(z)

    def own_rows(a):
        one = lax.dynamic_index_in_dim(a, sf, 0, keepdims=False)
        two_ = lax.dynamic_index_in_dim(a, sh, 0, keepdims=False)
        return jnp.concatenate([one, lax.dynamic_slice_in_dim(two_, half * hl, hl, 0)], 0)

    def own_pair(a):
        return jnp.stack(
            [
                lax.dynamic_index_in_dim(a, sf, 0, keepdims=False),
                lax.dynamic_index_in_dim(a, sh, 0, keepdims=False),
            ],
            0,
        )

    tok2 = own_pair(tokens)
    seg2 = jnp.concatenate([own_pair(segments), jnp.zeros((6, ln), jnp.int32)], 0)
    w_head = head_order([w_qkv[:, i] for i in range(3)], heads)
    b_head = head_order([q_bias, jnp.zeros_like(q_bias), v_bias], heads)
    b_head = jnp.broadcast_to(b_head[None], (8, 3 * group))
    b_unit = jnp.broadcast_to(in_bias[None], (8, units))
    args = (tok2, seg2, w_head, b_head, b_unit, w_out, w_in, w_back, heads)
    got = forward(*args) if sizes == (2, 4, 4) else forward_plain(sizes, me, *args)
    ctx_all, xt, q, kv, wh, w_o, w_ib, b_in, lse, ctx_t, seg_all = got
    w_o = w_o.reshape(nt, width, group)
    w_ib = w_ib.reshape(2, width, nt * units)
    w_i, w_b = w_ib[0], w_ib[1]
    b_in = b_in[:, 0].reshape(nt * units)
    own = ln + hl

    x_own = own_rows(tokens).astype(F32)
    attended = jnp.einsum("gtf,gdf->td", ctx_all, w_o, preferred_element_type=F32) + out_bias
    normal_one, rstd_one = norm_parts(x_own + attended)
    normed = normal_one * gain_one + shift_one
    normed_low = normed.astype(BF)
    inner = jnp.dot(normed_low, w_i, preferred_element_type=F32) + b_in
    active = jax.nn.gelu(inner, approximate=False).astype(BF)
    branch = jnp.einsum("tf,df->td", active, w_b, preferred_element_type=F32)
    second = normed + branch + back_bias
    normal_two, rstd_two = norm_parts(second)
    out_low = (normal_two * gain_two + shift_two).astype(BF)

    d_second, d_gain_two, d_shift_two = norm_back(
        own_rows(cotangent).astype(F32), normal_two, rstd_two, gain_two
    )
    d_second_low = d_second.astype(BF)
    d_back_bias = jnp.sum(d_second, 0)
    d_w_back = jnp.einsum("td,tf->df", d_second_low, active, preferred_element_type=F32)
    d_active = jnp.dot(d_second_low, w_b, preferred_element_type=F32)
    d_inner = d_active * gelu_slope(inner)
    d_in_bias = jnp.sum(d_inner, 0)
    d_inner_low = d_inner.astype(BF)
    d_w_in = jnp.einsum("td,tf->df", normed_low, d_inner_low, preferred_element_type=F32)
    d_normed = jnp.einsum("tf,df->td", d_inner_low, w_i, preferred_element_type=F32) + d_second
    d_first, d_gain_one, d_shift_one = norm_back(d_normed, normal_one, rstd_one, gain_one)
    d_first_low = d_first.astype(BF)
    d_out_bias = jnp.sum(d_first, 0)
    d_w_out = jnp.einsum("td,gtf->gdf", d_first_low, ctx_all, preferred_element_type=F32)
    d_ctx = jnp.einsum("td,gdf->gtf", d_first_low, w_o, preferred_element_type=F32).astype(BF)
    small = jnp.concatenate(
        [d_out_bias, d_gain_one, d_shift_one, d_back_bias, d_gain_two, d_shift_two, d_in_bias]
    )
    low = (d_w_back.astype(BF), d_w_in.astype(BF), d_w_out.astype(BF))
    if sizes == (2, 4, 4):
        small = jnp.concatenate([small, jnp.zeros((-small.shape[0] % 1024,), F32)])
        output, d_tokens, g_back, g_in, g_out, g_h, small, d_bias = backward(
            d_ctx,
            low[0].reshape(4, 2, wr, nt * units),
            low[1].reshape(4, 2, wr, nt * units),
            low[2].reshape(nt, 4, 2, wr, group),
            out_low,
            d_first,
            small.reshape(-1, 128),
            q,
            kv,
            xt,
            wh,
            lse,
            ctx_t,
            seg_all,
            heads,
            seqs,
        )
        d_tokens = d_tokens.astype(F32)
        small = small.reshape(-1)
        d_bias = d_bias[0]
    else:
        output, d_tokens, g_back, g_in, g_out, g_h, small, d_bias = backward_plain(
            sizes, me, d_ctx, low, out_low, d_first, small, q, kv, xt, wh, lse, ctx_t, seg_all, heads, seqs
        )
    g_qkv = jnp.stack(head_kinds(g_h, heads), 1)
    d_qb, _, d_vb = head_kinds(d_bias, heads)
    qv = jnp.concatenate([d_qb, d_vb])
    wide = small[: 6 * width].reshape(6, width)
    g_in_bias = lax.dynamic_index_in_dim(
        small[6 * width : 6 * width + nt * units].reshape(nt, units), z, 0, keepdims=False
    )
    return (
        output,
        d_tokens,
        g_qkv,
        qv[:group],
        qv[group:],
        g_out,
        wide[0],
        wide[1],
        wide[2],
        g_in,
        g_in_bias,
        g_back,
        wide[3],
        wide[4],
        wide[5],
    )


def solution(mesh):
    sizes = tuple(mesh.shape[n] for n in ALL)
    rows = P(("dp", "ctx"), "tp")
    return jax.shard_map(
        functools.partial(per_device, sizes),
        mesh=mesh,
        in_specs=(
            P("dp", "ctx", None),
            P("dp", "ctx"),
            P(("dp", "ctx"), None, "tp"),
            P("tp"),
            P("tp"),
            rows,
            P(),
            P(),
            P(),
            rows,
            P("tp"),
            rows,
            P(),
            P(),
            P(),
            P("dp", "ctx", None),
        ),
        out_specs=(
            P("dp", "ctx", None),
            P("dp", "ctx", None),
            P(("dp", "ctx"), None, "tp"),
            P("tp"),
            P("tp"),
            rows,
            P(),
            P(),
            P(),
            rows,
            P("tp"),
            rows,
            P(),
            P(),
            P(),
        ),
        check_vma=False,
    )
```

```python
import functools
import math

import jax
import jax.numpy as jnp
from jax import lax
from jax.experimental import pallas as pl
from jax.experimental.pallas import tpu as pltpu
from jax.sharding import PartitionSpec as P

HEAD = 64
NEG = -1e30
BF = jnp.bfloat16
F32 = jnp.float32
ALL = ("dp", "ctx", "tp")


def norm_parts(value):
    mean = jnp.mean(value, -1, keepdims=True)
    centered = value - mean
    rstd = lax.rsqrt(jnp.mean(centered * centered, -1, keepdims=True) + 1e-12)
    return (centered * rstd, rstd)


def norm_back(grad, normal, rstd, gain):
    d_gain = jnp.sum(grad * normal, 0)
    d_shift = jnp.sum(grad, 0)
    scaled = grad * gain
    d_value = rstd * (
        scaled
        - jnp.mean(scaled, -1, keepdims=True)
        - normal * jnp.mean(scaled * normal, -1, keepdims=True)
    )
    return (d_value, d_gain, d_shift)


def gelu_slope(inner):
    return 0.5 * (1.0 + lax.erf(inner / math.sqrt(2.0))) + inner * jnp.exp(
        -0.5 * inner * inner
    ) / math.sqrt(2.0 * math.pi)


def swap_with(value, axis, size, mask):
    return lax.ppermute(value, axis, [(i, i ^ mask) for i in range(size)])


def in_order(parts, me, axis=0):
    shape = list(parts[0].shape)
    shape.insert(axis, len(parts))
    out = jnp.zeros(tuple(shape), parts[0].dtype)
    for k, part in enumerate(parts):
        out = lax.dynamic_update_index_in_dim(out, part, me ^ k, axis)
    return out


def gather_axis(value, axis, size, me):
    parts = [value] + [swap_with(value, axis, size, k) for k in range(1, size)]
    return in_order(parts, me)


def exchange_axis(blocks, axis, size, me):
    parts = [lax.dynamic_index_in_dim(blocks, me, 0, keepdims=False)]
    for k in range(1, size):
        parts.append(
            swap_with(lax.dynamic_index_in_dim(blocks, me ^ k, 0, keepdims=False), axis, size, k)
        )
    return parts


def scatter_weight(grad, sizes, me):
    nd, nc, nt = sizes
    part = lax.psum_scatter(
        grad.astype(F32), ("dp", "ctx"), scatter_dimension=1, tiled=False
    ).astype(BF)
    parts = exchange_axis(part, "tp", nt, me[2])
    return sum(p.astype(F32) for p in parts)


def transpose_ctx_tp(value, n):
    pairs = [(a * n + b, b * n + a) for a in range(n) for b in range(n)]
    return lax.ppermute(value, ("ctx", "tp"), pairs)


def gather_heads(shard, sizes, me):
    mine = transpose_ctx_tp(shard, sizes[1])
    return lax.all_gather(mine, ("dp", "tp"), axis=0, tiled=True)


def scatter_heads(grad, sizes, me):
    nd, nc, nt = sizes
    blocks = grad.reshape((nd * nt, grad.shape[0] // (nd * nt)) + grad.shape[1:])
    total = lax.psum_scatter(
        blocks.astype(F32), ("dp", "tp"), scatter_dimension=0, tiled=False
    )
    return transpose_ctx_tp(total, nc)


def block_rows(qb, half, ln):
    hl = ln // 2
    whole = qb < 4
    b = jnp.where(whole, qb, qb - 4)
    r0 = jnp.where(whole, 2 * ln * b, (4 * b + 1) * ln + hl * half)
    r1 = jnp.where(whole, r0 + hl, r0 + 2 * ln)
    o0 = jnp.where(whole, 3 * hl * b, 6 * hl * b + ln)
    o1 = jnp.where(whole, o0 + hl, o0 + 3 * hl)
    seq = jnp.where(whole, 0, 1)
    m = lambda v: pl.multiple_of(v, 128)
    return m(r0), m(r1), m(o0), m(o1), seq


def two(ref, r0, r1, hl, cols):
    return jnp.concatenate([ref[pl.ds(r0, hl), cols], ref[pl.ds(r1, hl), cols]], 0)


def two_lanes(ref, rows, r0, r1, hl):
    return jnp.concatenate([ref[rows, pl.ds(r0, hl)], ref[rows, pl.ds(r1, hl)]], 1)


def dot_nt(a, b):
    return lax.dot_general(a, b, (((1,), (1,)), ((), ())), preferred_element_type=F32)


def dot_nn(a, b):
    return lax.dot_general(a, b, (((1,), (0,)), ((), ())), preferred_element_type=F32)


def fill_transposed(kv, kvt, ln, nc, heads):
    @pl.loop(0, nc)
    def _(j):
        for seq in range(2):
            rows = pl.ds(pl.multiple_of((2 * j + seq) * ln, ln), ln)
            for h in range(heads):
                kvt[seq * heads + h, :, pl.ds(pl.multiple_of(j * ln, ln), ln)] = kv[
                    rows, 128 * h : 128 * h + 128
                ].T


def attend_kernel(heads, ln, nc, info, q_ref, kv, seg_col, seg_row, out, lse, ctx_t, s_scr, kvt, acc):
    half = info[12]
    hl = ln // 2
    fill_transposed(kv, kvt, ln, nc, heads)

    @pl.loop(0, 6)
    def _(qb):
        r0, r1, o0, o1, seq = block_rows(qb, half, ln)
        lo, hi = info[qb], info[6 + qb]
        sq = two_lanes(seg_row, slice(0, 1), r0, r1, hl)
        q = [two(q_ref, r0, r1, hl, slice(128 * h, 128 * h + 128)) for h in range(heads)]

        def score(j, peaks):
            rows = pl.ds(pl.multiple_of((2 * j + seq) * ln, ln), ln)
            same = seg_col[rows, :] == sq
            new = []
            for h in range(heads):
                s = dot_nt(kv[rows, 128 * h : 128 * h + 128], q[h])
                s = jnp.where(same, s, NEG)
                s_scr[h, pl.ds(pl.multiple_of(j * ln, ln), ln), :] = s
                new.append(jnp.maximum(peaks[h], jnp.max(s, 0, keepdims=True)))
            return tuple(new)

        peaks = lax.fori_loop(
            lo, hi, score, tuple(jnp.full((1, ln), NEG, F32) for _ in range(heads))
        )
        acc[...] = jnp.zeros_like(acc)

        def collect(j, sums):
            keys = pl.ds(pl.multiple_of(j * ln, ln), ln)
            new = []
            for h in range(heads):
                p = jnp.exp(s_scr[h, keys, :] - peaks[h])
                new.append(sums[h] + jnp.sum(p, 0, keepdims=True))
                acc[h] += dot_nn(kvt[seq * heads + h, :, keys], p.astype(BF))
            return tuple(new)

        sums = lax.fori_loop(
            lo, hi, collect, tuple(jnp.zeros((1, ln), F32) for _ in range(heads))
        )
        whole = []
        for h in range(heads):
            one = acc[h, HEAD:, :] / sums[h]
            whole.append(one)
            line = peaks[h] + jnp.log(sums[h])
            for part, at in ((0, o0), (hl, o1)):
                ctx_t[HEAD * h : HEAD * h + HEAD, pl.ds(at, hl)] = one[:, part : part + hl]
                lse[h : h + 1, pl.ds(at, hl)] = line[:, part : part + hl]
        turned = jnp.concatenate(whole, 0).T.astype(BF)
        out[pl.ds(o0, hl), :] = turned[:hl]
        out[pl.ds(o1, hl), :] = turned[hl:]


def attend(info, q_ref, kv, seg_col, seg_row, heads, ln, nc):
    rows = 3 * ln // 2 * nc
    vm = pl.BlockSpec(memory_space=pltpu.VMEM)
    return pl.pallas_call(
        functools.partial(attend_kernel, heads, ln, nc),
        out_shape=(
            jax.ShapeDtypeStruct((rows, heads * HEAD), BF),
            jax.ShapeDtypeStruct((8, rows), F32),
            jax.ShapeDtypeStruct((heads * HEAD, rows), F32),
        ),
        in_specs=[pl.BlockSpec(memory_space=pltpu.SMEM), vm, vm, vm, vm],
        out_specs=(vm, vm, vm),
        scratch_shapes=[
            pltpu.VMEM((heads, nc * ln, ln), F32),
            pltpu.VMEM((2 * heads, 128, nc * ln), BF),
            pltpu.VMEM((heads, 128, ln), F32),
        ],
        compiler_params=pltpu.CompilerParams(vmem_limit_bytes=32 << 20),
        cost_estimate=pl.CostEstimate(
            flops=8 * heads * rows * nc * ln * 128,
            bytes_accessed=8 << 20,
            transcendentals=heads * rows * nc * ln,
        ),
        name="attend",
    )(info, q_ref, kv, seg_col, seg_row)


def attend_back_kernel(
    heads, ln, nc, info, q_ref, kv, d_out, seg_col, seg_row, lse, ctx_t, d_q, d_kv, d_bias, dkv, kvt, dqt
):
    half = info[12]
    hl = ln // 2
    fill_transposed(kv, kvt, ln, nc, heads)
    dkv[...] = jnp.zeros_like(dkv)
    d_bias[...] = jnp.zeros_like(d_bias)

    @pl.loop(0, nc)
    def _(c):
        rows = pl.ds(pl.multiple_of((2 * c + 1) * ln, ln), ln)
        d_q[rows, :] = jnp.zeros((ln, heads * HEAD), BF)

    @pl.loop(0, 6)
    def _(qb):
        r0, r1, o0, o1, seq = block_rows(qb, half, ln)
        lo, hi = info[qb], info[6 + qb]
        sq = two_lanes(seg_row, slice(0, 1), r0, r1, hl)
        q, do, line, delta = [], [], [], []
        for h in range(heads):
            q.append(two(q_ref, r0, r1, hl, slice(128 * h, 128 * h + 128)))
            do.append(two(d_out, o0, o1, hl, slice(128 * h, 128 * h + 128)))
            line.append(two_lanes(lse, slice(h, h + 1), o0, o1, hl))
            turned = do[h].astype(F32).T[HEAD:, :]
            kept = two_lanes(ctx_t, slice(HEAD * h, HEAD * h + HEAD), o0, o1, hl)
            delta.append(jnp.sum(turned * kept, 0, keepdims=True))
        dqt[...] = jnp.zeros_like(dqt)

        @pl.loop(lo, hi)
        def _(j):
            rows = pl.ds(pl.multiple_of((2 * j + seq) * ln, ln), ln)
            keys = pl.ds(pl.multiple_of(j * ln, ln), ln)
            same = seg_col[rows, :] == sq
            for h in range(heads):
                kvh = kv[rows, 128 * h : 128 * h + 128]
                p = jnp.where(same, jnp.exp(dot_nt(kvh, q[h]) - line[h]), 0.0)
                ds = (p * (dot_nt(kvh, do[h]) - delta[h])).astype(BF)
                dkv[rows, 128 * h : 128 * h + 128] += dot_nn(ds, q[h]) + dot_nn(
                    p.astype(BF), do[h]
                )
                dqt[h] += dot_nn(kvt[seq * heads + h, :, keys], ds)

        turned = jnp.concatenate([dqt[h, :HEAD, :] for h in range(heads)], 0).T * 0.125
        d_bias[0:1, heads * 128 :] += jnp.sum(turned, 0, keepdims=True)
        low = turned.astype(BF)
        d_q[pl.ds(r0, hl), :] = low[:hl]
        d_q[pl.ds(r1, hl), :] = low[hl:]

    @pl.loop(0, 2 * nc)
    def _(c):
        rows = pl.ds(pl.multiple_of(c * ln, ln), ln)
        for h in range(heads):
            got = dkv[rows, 128 * h : 128 * h + 128]
            d_bias[0:1, 128 * h : 128 * h + 128] += jnp.sum(got, 0, keepdims=True)
            d_kv[rows, 128 * h : 128 * h + 128] = got.astype(BF)


def attend_back(info, q_ref, kv, d_out, seg_col, seg_row, lse, ctx_t, heads, ln, nc):
    rows = 3 * ln // 2 * nc
    vm = pl.BlockSpec(memory_space=pltpu.VMEM)
    return pl.pallas_call(
        functools.partial(attend_back_kernel, heads, ln, nc),
        out_shape=(
            jax.ShapeDtypeStruct((2 * nc * ln, heads * HEAD), BF),
            jax.ShapeDtypeStruct((2 * nc * ln, heads * 128), BF),
            jax.ShapeDtypeStruct((8, heads * (HEAD + 128)), F32),
        ),
        in_specs=[pl.BlockSpec(memory_space=pltpu.SMEM)] + [vm] * 7,
        out_specs=(vm, vm, vm),
        scratch_shapes=[
            pltpu.VMEM((2 * nc * ln, heads * 128), F32),
            pltpu.VMEM((2 * heads, 128, nc * ln), BF),
            pltpu.VMEM((heads, 128, ln), F32),
        ],
        compiler_params=pltpu.CompilerParams(vmem_limit_bytes=40 << 20),
        cost_estimate=pl.CostEstimate(
            flops=20 * heads * rows * nc * ln * 128,
            bytes_accessed=14 << 20,
            transcendentals=heads * rows * nc * ln,
        ),
        name="attend_back",
    )(info, q_ref, kv, d_out, seg_col, seg_row, lse, ctx_t)


MESH = pl.DeviceIdType.MESH


class Copies:
    def __init__(self, send, recv):
        self.send, self.recv, self.open = send, recv, []

    def make(self, i, src, dst, device, sent=None):
        return pltpu.make_async_remote_copy(
            src_ref=src,
            dst_ref=dst,
            send_sem=self.send.at[i if sent is None else sent],
            recv_sem=self.recv.at[i],
            device_id=device,
            device_id_type=MESH,
        )

    def start(self, i, parts, when=None, sent=None):
        number = (lambda: i) if not callable(i) else i

        def go(wait):
            copy = self.make(number(), *parts(), sent=sent)
            copy.wait_send() if wait else copy.start()

        self.run(go, when, False)
        self.open.append((go, when))

    def run(self, go, when, wait):
        if when is None:
            go(wait)
        else:

            @pl.when(when())
            def _():
                go(wait)

    def arrived(self, i, dst, device):
        self.make(i, dst, dst, device).wait_recv()

    def all_sent(self):
        for go, when in self.open:
            self.run(go, when, True)


def line_order(z, i):
    if i == 0:
        return z
    if i == 1:
        return jnp.where(z == 0, 1, z - 1)
    if i == 2:
        return jnp.where(z == 0, 2, jnp.where(z == 3, 1, z + 1))
    return jnp.where(z < 2, 3, 0)


def forward_kernel(
    heads,
    ln,
    tok2,
    seg2,
    w_head,
    b_head,
    b_unit,
    w_o,
    w_i,
    w_b,
    ctx_all,
    xt_out,
    q_out,
    kv_out,
    wh_out,
    o_full,
    w_full,
    bu_full,
    lse,
    ctx_t,
    seg,
    x2,
    xt,
    wh,
    bh,
    q_scr,
    kv,
    s_scr,
    kvt,
    acc,
    segc,
    segr,
    context,
    w_src,
    o_src,
    send,
    recv,
    local,
):
    d, c, z = (lax.axis_index(n) for n in ALL)
    nc = 4
    hl = ln // 2
    own = ln + hl
    half = z % 2
    wr = w_i.shape[0]
    units = w_i.shape[1]
    row = d * nc + c
    row_x, row_y, row_d = row ^ 4, row ^ 2, row ^ 6
    rc = Copies(send, recv)
    at_c = lambda k: (d, c ^ k, z)
    at_x = (1 - d, c, z)
    to_c = lambda k: (lambda: at_c(k))
    to_x = lambda: at_x
    at_z = lambda k: (d, c, z ^ k)
    across = (d, z, c)
    order = [line_order(z, i) for i in range(4)]
    number = iter(range(0, 400))
    four = lambda: [next(number) for _ in range(4)][0]
    local_number = iter(range(32))

    def copy_here(src, dst):
        copy = pltpu.make_async_copy(src, dst, local.at[next(local_number)])
        copy.start()
        return copy

    t_cols = lambda t: pl.ds(pl.multiple_of(t * units, 128), units)
    w_at = lambda r, t: w_full.at[:, r, :, t_cols(t)]
    o_at = lambda r, t: o_full.at[t, r]
    wh_at = lambda r: wh.at[pl.ds(pl.multiple_of(r * wr, wr), wr)]
    tok_at = lambda i: x2.at[pl.ds(2 * i, 2)]
    w_here = [copy_here(w_i, w_src.at[0]), copy_here(w_b, w_src.at[1]), copy_here(w_o, o_src)]
    mine = copy_here(tok2, tok_at(c))
    seg_here = copy_here(seg2, seg.at[c])
    bu_here = copy_here(b_unit, bu_full.at[z])
    here_sem = [local.at[next(local_number)] for _ in range(2)]
    here = [
        pltpu.make_async_copy(w_head, wh_at(row), here_sem[0]),
        pltpu.make_async_copy(b_head, bh, here_sem[1]),
    ]

    @pl.when(c == z)
    def _():
        for copy in here:
            copy.start()

    barrier = pltpu.get_barrier_semaphore()
    everyone = [at_c(k) for k in (1, 2, 3)] + [at_z(k) for k in (1, 2, 3)] + [at_x]
    for device in everyone:
        pl.semaphore_signal(barrier, inc=1, device_id=device, device_id_type=MESH)

    @pl.when(c != z)
    def _():
        pl.semaphore_signal(barrier, inc=1, device_id=across, device_id_type=MESH)

    pl.semaphore_wait(barrier, len(everyone) + jnp.where(c != z, 1, 0))

    n_ty, n_tc, n_tf, n_wa, n_ba = (next(number) for _ in range(5))
    not_here = lambda: c != z
    rc.start(n_wa, lambda: (w_head, wh_at(row), across), not_here)
    rc.start(n_ba, lambda: (b_head, bh, across), not_here)
    rc.start(n_ty, lambda: (tok2, tok_at(c), at_c(2)))
    rc.start(n_tc, lambda: (tok2, tok_at(c), at_c(1)))
    n_seg = four()
    for k in (1, 2, 3):
        rc.start(n_seg + k, lambda k=k: (seg2, seg.at[c], at_c(k)))

    class Line:
        def __init__(self, at):
            self.at = at
            self.n = [next(number) for _ in range(5)][0]

        def begin(self, src):
            rc.start(
                lambda: self.n + z,
                lambda: (src, self.at(z), (d, c, z + 1)),
                lambda: z < 3,
                self.n + 3,
            )
            rc.start(
                lambda: self.n + z,
                lambda: (src, self.at(z), (d, c, z - 1)),
                lambda: z > 0,
                self.n + 4,
            )

        def step(self, i):
            t = lambda: order[i]
            rc.arrived(self.n + t(), self.at(t()), (d, c, z))
            rc.start(
                lambda: self.n + t(),
                lambda: (
                    self.at(t()),
                    self.at(t()),
                    (d, c, jnp.where(t() < z, z + 1, z - 1)),
                ),
                lambda: jnp.where(t() < z, z < 3, z > 0),
                self.n + i - 1,
            )

    n_hz = four()
    lines = (Line(lambda t: w_at(row, t)), Line(lambda t: o_at(row, t)))
    full_at = (w_at, o_at)
    sources = (w_src, o_src)
    n_hx = four()
    n_x, n_y, n_d = ([four(), four()] for _ in range(3))
    n_c = [[four(), four()] for _ in range(4)]

    def pass_on(n, i, r, device, first=False):
        t = lambda: order[i]
        for w in range(2):
            rc.start(
                lambda w=w: n[w] + t(),
                lambda w=w: (
                    sources[w] if first and i == 0 else full_at[w](r, t()),
                    full_at[w](r, t()),
                    device(),
                ),
                None,
                n[w] + i,
            )

    def came(n, i, r, device):
        t = order[i]
        for w in range(2):
            rc.arrived(n[w] + t, full_at[w](r, t), device)

    def dense_step(i, chips):
        for line in lines:
            line.step(i)
        pass_on(n_x, i, row, to_x, True)
        if chips:
            dense_y(i)

    def dense_y(i):
        pass_on(n_y, i, row, to_c(2), True)
        pass_on(n_c[0], i, row, to_c(1), True)

    def from_x(i):
        came(n_x, i, row_x, at_x)
        if i >= 3:
            pass_on(n_d, i, row_x, to_c(2))
        pass_on(n_c[1], i, row_x, to_c(1))

    def from_y(i):
        came(n_y, i, row_y, at_c(2))
        if i < 3:
            pass_on(n_d, i, row_y, to_x)
        pass_on(n_c[2], i, row_y, to_c(1))

    def from_corner(i):
        came(n_d, i, row_d, at_x)
        pass_on(n_c[3], i, row_d, to_c(1))

    for copy in w_here:
        copy.wait()
    pass_on(n_x, 0, row, to_x, True)
    pass_on(n_y, 0, row, to_c(2), True)
    pass_on(n_c[0], 0, row, to_c(1), True)
    own_here = [copy_here(w_src, w_at(row, z)), copy_here(o_src, o_at(row, z))]
    n_bu = four()
    for k in (1, 2, 3):
        rc.start(n_bu + k, lambda k=k: (b_unit, bu_full.at[z], at_z(k)))

    @pl.when(c != z)
    def _():
        rc.arrived(n_wa, wh_at(d * nc + z), across)
        rc.arrived(n_ba, bh, across)

    @pl.when(c == z)
    def _():
        for copy in here:
            copy.wait()

    head_at = lambda t: wh_at(d * nc + t)
    for k in (1, 2, 3):
        rc.start(n_hz + k, lambda k=k: (head_at(z), head_at(z), at_z(k)))
    rc.start(n_hx, lambda: (head_at(z), head_at(z), at_x))
    for line, src in zip(lines, sources):
        line.begin(src)
    q_scr[...] = jnp.zeros_like(q_scr)
    for k in (1, 2, 3):
        rc.arrived(n_hz + k, head_at(z ^ k), at_z(k))
        rc.start(n_hx + k, lambda k=k: (head_at(z ^ k), head_at(z ^ k), at_x))
    dense_step(1, True)
    for k in (1, 2, 3):
        rc.arrived(n_seg + k, seg.at[c ^ k], at_c(k))
    seg_here.wait()
    for i in range(nc):
        for s in range(2):
            line = seg[i, s : s + 1, :].astype(F32)
            segr[2 * i + s, 0:1, :] = line
            segc[2 * i + s] = jnp.broadcast_to(line, (128, ln)).T
    rc.arrived(n_ty, tok_at(c ^ 2), at_c(2))
    rc.start(n_tf, lambda: (tok_at(c ^ 2), tok_at(c ^ 2), at_c(1)))
    dense_step(2, True)
    for t in range(4):
        rc.arrived(n_hx + t, wh_at((1 - d) * nc + (z ^ t)), at_x)
    mine.wait()
    rc.arrived(n_tc, tok_at(c ^ 1), at_c(1))
    rc.arrived(n_tf, tok_at(c ^ 3), at_c(1))
    wh_here = copy_here(wh, wh_out)
    wide = heads * 128

    @pl.loop(0, 2 * nc)
    def _(i):
        x = x2[i]
        rows = pl.ds(pl.multiple_of(i * ln, ln), ln)
        xt[:, rows] = x.T
        got = (dot_nn(x, wh[:, :wide]) + bh[0:1, :wide]).astype(BF)
        kv[rows, :] = got
        qp = ((dot_nn(x, wh[:, wide:]) + bh[0:1, wide:]).astype(BF).astype(F32) * 0.125).astype(BF)
        for h in range(heads):
            q_scr[rows, 128 * h : 128 * h + HEAD] = qp[:, HEAD * h : HEAD * h + HEAD]

    x_here = copy_here(xt, xt_out)
    q_here = copy_here(q_scr, q_out)
    kv_here = copy_here(kv, kv_out)
    dense_step(3, True)
    from_x(0)

    @pl.loop(0, nc)
    def _(j):
        for s in range(2):
            rows = pl.ds(pl.multiple_of((2 * j + s) * ln, ln), ln)
            for h in range(heads):
                kvt[s * heads + h, :, pl.ds(pl.multiple_of(j * ln, ln), ln)] = kv[
                    rows, 128 * h : 128 * h + 128
                ].T

    from_x(1)

    def block(qb):
        r0, r1, o0, o1, seq = block_rows(qb, half, ln)
        b0 = jnp.where(qb < 4, qb, 2 * (qb - 4))
        b1 = jnp.where(qb < 4, qb, 2 * (qb - 4) + 1)
        s0 = pl.multiple_of(jnp.where(qb < 4, 0, hl * half), 128)
        s1 = pl.multiple_of(jnp.where(qb < 4, hl, hl * half), 128)
        sq = jnp.concatenate(
            [
                segr[2 * b0 + seq, 0:1, pl.ds(s0, hl)],
                segr[2 * b1 + seq, 0:1, pl.ds(s1, hl)],
            ],
            1,
        )
        q = [two(q_scr, r0, r1, hl, slice(128 * h, 128 * h + 128)) for h in range(heads)]

        def score(j, peaks):
            rows = pl.ds(pl.multiple_of((2 * j + seq) * ln, ln), ln)
            key_seg = segc[2 * j + seq]
            same = jnp.concatenate([key_seg, key_seg], 1) == sq
            new = []
            for h in range(heads):
                s = dot_nt(kv[rows, 128 * h : 128 * h + 128], q[h])
                s = jnp.where(same, s, NEG)
                s_scr[h, pl.ds(pl.multiple_of(j * ln, ln), ln), :] = s
                new.append(jnp.maximum(peaks[h], jnp.max(s, 0, keepdims=True)))
            return tuple(new)

        peaks = lax.fori_loop(
            0, nc, score, tuple(jnp.full((1, ln), NEG, F32) for _ in range(heads))
        )
        acc[...] = jnp.zeros_like(acc)

        def collect(j, sums):
            keys = pl.ds(pl.multiple_of(j * ln, ln), ln)
            new = []
            for h in range(heads):
                p = jnp.exp(s_scr[h, keys, :] - peaks[h])
                new.append(sums[h] + jnp.sum(p, 0, keepdims=True))
                acc[h] += dot_nn(kvt[seq * heads + h, :, keys], p.astype(BF))
            return tuple(new)

        sums = lax.fori_loop(
            0, nc, collect, tuple(jnp.zeros((1, ln), F32) for _ in range(heads))
        )
        whole = []
        for h in range(heads):
            one = acc[h, HEAD:, :] / sums[h]
            whole.append(one)
            line = peaks[h] + jnp.log(sums[h])
            for part, at in ((0, o0), (hl, o1)):
                ctx_t[HEAD * h : HEAD * h + HEAD, pl.ds(at, hl)] = one[:, part : part + hl]
                lse[h : h + 1, pl.ds(at, hl)] = line[:, part : part + hl]
        turned = jnp.concatenate(whole, 0).T.astype(BF)
        context[pl.ds(o0, hl), :] = turned[:hl]
        context[pl.ds(o1, hl), :] = turned[hl:]

    @pl.loop(0, 6)
    def _(qb):
        block(qb)

        @pl.when(qb == 1)
        def _():
            from_y(0)

        @pl.when(qb == 3)
        def _():
            from_x(2)
            from_y(1)

    n_ctx = four()
    ctx_at = lambda i: context.at[pl.ds(pl.multiple_of(i * own, 128), own)]
    for k in (1, 2, 3):
        rc.start(n_ctx + k, lambda k=k: (ctx_at(c ^ k), ctx_all.at[c], at_c(k)))
    ctx_here = copy_here(ctx_at(c), ctx_all.at[c])
    from_x(3)
    from_y(2)
    from_corner(0)
    from_corner(1)
    for k in (1, 2, 3):
        rc.arrived(n_ctx + k, ctx_all.at[c ^ k], at_c(k))
        rc.arrived(n_bu + k, bu_full.at[z ^ k], at_z(k))
    from_y(3)
    from_corner(2)
    from_corner(3)
    for n, r in zip(n_c, (row, row_x, row_y, row_d)):
        for i in range(4):
            came(n, i, r ^ 1, at_c(1))
    for copy in own_here + [bu_here, x_here, wh_here, q_here, kv_here, ctx_here]:
        copy.wait()
    rc.all_sent()


def forward(tok2, seg2, w_head, b_head, b_unit, w_o, w_i, w_b, heads):
    ln, width = tok2.shape[1:]
    wr, units = w_i.shape
    group = w_o.shape[1]
    nc, nt, nr = 4, 4, 8
    rows = 3 * ln // 2 * nc
    hb = pl.BlockSpec(memory_space=pltpu.HBM)
    vm = pl.BlockSpec(memory_space=pltpu.VMEM)
    sds = jax.ShapeDtypeStruct
    return pl.pallas_call(
        functools.partial(forward_kernel, heads, ln),
        out_shape=(
            sds((nc, 3 * ln // 2, group), BF),
            sds((width, 2 * nc * ln), BF),
            sds((2 * nc * ln, heads * 128), BF),
            sds((2 * nc * ln, heads * 128), BF),
            sds((nr * wr, 3 * group), BF),
            sds((nt, nr, wr, group), BF),
            sds((2, nr, wr, nt * units), BF),
            sds((nt, 8, units), F32),
            sds((8, rows), F32),
            sds((group, rows), F32),
            sds((nc, 8, ln), jnp.int32),
        ),
        in_specs=[hb] * 4 + [vm] + [hb] * 3,
        out_specs=(hb,) * 8 + (vm,) * 3,
        scratch_shapes=[
            pltpu.VMEM((2 * nc, ln, width), BF),
            pltpu.VMEM((width, 2 * nc * ln), BF),
            pltpu.VMEM((nr * wr, 3 * group), BF),
            pltpu.VMEM((8, 3 * group), F32),
            pltpu.VMEM((2 * nc * ln, heads * 128), BF),
            pltpu.VMEM((2 * nc * ln, heads * 128), BF),
            pltpu.VMEM((heads, nc * ln, ln), F32),
            pltpu.VMEM((2 * heads, 128, nc * ln), BF),
            pltpu.VMEM((heads, 128, ln), F32),
            pltpu.VMEM((2 * nc, ln, 128), F32),
            pltpu.VMEM((2 * nc, 8, ln), F32),
            pltpu.VMEM((rows, group), BF),
            pltpu.VMEM((2, wr, units), BF),
            pltpu.VMEM((wr, group), BF),
            pltpu.SemaphoreType.DMA((120,)),
            pltpu.SemaphoreType.DMA((120,)),
            pltpu.SemaphoreType.DMA((32,)),
        ],
        compiler_params=pltpu.CompilerParams(
            vmem_limit_bytes=60 << 20, collective_id=0, has_side_effects=True
        ),
        name="forward",
    )(tok2, seg2, w_head, b_head, b_unit, w_o, w_i, w_b)


def middle_kernel(
    ln,
    tokens,
    cotangent,
    ctx_all,
    w_o,
    w_ib,
    b_in,
    vectors,
    d_ctx,
    g_b,
    g_i,
    g_o,
    out_low,
    d_first,
    small,
    x_own,
    c_own,
    w_v,
    ctx_v,
    w_ov,
    n_one,
    r_one,
    normed,
    low,
    low_t,
    tmp,
    acc,
    active,
    slope,
    n_two,
    d_sec,
    d_low,
    gb_v,
    gi_v,
    w_sem,
    g_sem,
    sem,
):
    z = lax.axis_index("tp")
    hl = ln // 2
    own = ln + hl
    blocks, _, group = ctx_all.shape
    width = x_own.shape[1]
    units = w_v.shape[2] // 4
    step = 32
    out_bias, gain_one, shift_one, back_bias, gain_two, shift_two = (
        vectors.at[pl.ds(i, 1)] for i in range(6)
    )
    half_rows = pl.ds(pl.multiple_of((z % 2) * hl, 128), hl)
    first_rows = []
    for i, (src, dst) in enumerate(((tokens, x_own), (cotangent, c_own))):
        for j, (a, b) in enumerate(
            (
                (src.at[(3 * z + 1) // 2], dst.at[pl.ds(0, ln)]),
                (src.at[1 + 3 * (z // 2), half_rows], dst.at[pl.ds(ln, hl)]),
            )
        ):
            first_rows.append(pltpu.make_async_copy(a, b, sem.at[2 * i + j]))
    first_rows.append(pltpu.make_async_copy(ctx_all, ctx_v, sem.at[4]))
    first_rows.append(pltpu.make_async_copy(w_o, w_ov, sem.at[5]))
    for copy in first_rows:
        copy.start()
    t_cols = lambda t: pl.ds(pl.multiple_of(t * units, 128), units)

    def weight(which, t):
        return pltpu.make_async_copy(
            w_ib.at[which, :, t_cols(t)], w_v.at[which, :, t_cols(t)], w_sem.at[which, t]
        )

    for t in range(4):
        for which in range(2):
            weight(which, t).start()
    for copy in first_rows:
        copy.wait()

    def chunks(body):
        @pl.loop(0, own // step)
        def _(i):
            body(pl.ds(pl.multiple_of(i * step, step), step))

    mean = lambda v: jnp.mean(v, -1, keepdims=True)
    add = lambda i, v: small.__setitem__(
        (slice(i, i + 1), slice(None)), small[i : i + 1, :] + jnp.sum(v, 0, keepdims=True)
    )
    small[...] = jnp.zeros_like(small)

    tmp[...] = dot_nt(ctx_v[0], w_ov[0])
    for g in range(1, blocks):
        tmp[...] += dot_nt(ctx_v[g], w_ov[g])

    def norm_one(r):
        value = x_own[r, :].astype(F32) + (tmp[r, :] + out_bias[...])
        centered = value - mean(value)
        rstd = lax.rsqrt(mean(centered * centered) + 1e-12)
        normal = centered * rstd
        n_one[r, :] = normal
        r_one[r, :] = jnp.broadcast_to(rstd, (step, 128))
        got = normal * gain_one[...] + shift_one[...]
        normed[r, :] = got
        low[r, :] = got.astype(BF)
        acc[r, :] = got + back_bias[...]

    chunks(norm_one)
    low_t[...] = low[...].T

    @pl.loop(0, 4)
    def _(t):
        weight(0, t).wait()
        weight(1, t).wait()
        tmp[...] = dot_nn(low[...], w_v[0, :, t_cols(t)]) + b_in[pl.ds(t, 1), 0, :]

        def gelu(r):
            u = tmp[r, :]
            cdf = 0.5 * (1.0 + lax.erf(u * math.sqrt(0.5)))
            active[r, t_cols(t)] = (u * cdf).astype(BF)
            slope[r, t_cols(t)] = cdf + u * jnp.exp(-0.5 * u * u) * (
                1.0 / math.sqrt(2.0 * math.pi)
            )

        chunks(gelu)
        acc[...] += dot_nt(active[:, t_cols(t)], w_v[1, :, t_cols(t)])

    def norm_two(r):
        value = acc[r, :]
        centered = value - mean(value)
        rstd = lax.rsqrt(mean(centered * centered) + 1e-12)
        normal = centered * rstd
        out_low[r, :] = (normal * gain_two[...] + shift_two[...]).astype(BF)
        grad = c_own[r, :].astype(F32)
        add(4, grad * normal)
        add(5, grad)
        scaled = grad * gain_two[...]
        got = rstd * (scaled - mean(scaled) - normal * mean(scaled * normal))
        d_sec[r, :] = got
        add(3, got)
        d_low[r, :] = got.astype(BF)
        acc[r, :] = got

    chunks(norm_two)
    n_two[...] = d_low[...].T

    @pl.loop(0, 4)
    def _(t):
        gb_v[:, t_cols(t)] = dot_nn(n_two[...], active[:, t_cols(t)]).astype(BF)
        pltpu.make_async_copy(gb_v.at[:, t_cols(t)], g_b.at[:, t_cols(t)], g_sem.at[0, t]).start()
        tmp[...] = dot_nn(d_low[...], w_v[1, :, t_cols(t)])

        def inner_back(r):
            got = tmp[r, :] * slope[r, t_cols(t)]
            at = pl.ds(6 + t, 1)
            small[at, :] += jnp.sum(got, 0, keepdims=True)
            active[r, t_cols(t)] = got.astype(BF)

        chunks(inner_back)
        gi_v[:, t_cols(t)] = dot_nn(low_t[...], active[:, t_cols(t)]).astype(BF)
        pltpu.make_async_copy(gi_v.at[:, t_cols(t)], g_i.at[:, t_cols(t)], g_sem.at[1, t]).start()
        acc[...] += dot_nt(active[:, t_cols(t)], w_v[0, :, t_cols(t)])

    def norm_one_back(r):
        grad = acc[r, :]
        normal = n_one[r, :]
        add(1, grad * normal)
        add(2, grad)
        scaled = grad * gain_one[...]
        got = r_one[r, 0:1] * (scaled - mean(scaled) - normal * mean(scaled * normal))
        d_first[r, :] = got
        add(0, got)
        d_low[r, :] = got.astype(BF)

    chunks(norm_one_back)
    n_two[...] = d_low[...].T
    for g in range(blocks):
        d_ctx[g] = dot_nn(d_low[...], w_ov[g]).astype(BF)
        g_o[g] = dot_nn(n_two[...], ctx_v[g]).astype(BF)
    for t in range(4):
        pltpu.make_async_copy(gb_v.at[:, t_cols(t)], g_b.at[:, t_cols(t)], g_sem.at[0, t]).wait()
        pltpu.make_async_copy(gi_v.at[:, t_cols(t)], g_i.at[:, t_cols(t)], g_sem.at[1, t]).wait()


def middle(tokens, cotangent, ctx_all, w_o, w_ib, b_in, vectors):
    blocks, own, group = ctx_all.shape
    ln, width = tokens.shape[1:]
    all_units = w_ib.shape[2]
    hb = pl.BlockSpec(memory_space=pltpu.HBM)
    vm = pl.BlockSpec(memory_space=pltpu.VMEM)
    sds = jax.ShapeDtypeStruct
    v = pltpu.VMEM
    return pl.pallas_call(
        functools.partial(middle_kernel, ln),
        out_shape=(
            sds((blocks, own, group), BF),
            sds((width, all_units), BF),
            sds((width, all_units), BF),
            sds((blocks, width, group), BF),
            sds((own, width), BF),
            sds((own, width), F32),
            sds((16, width), F32),
        ),
        in_specs=[hb] * 5 + [vm] * 2,
        out_specs=(vm, hb, hb, vm, vm, vm, vm),
        scratch_shapes=[
            v((own, width), BF),
            v((own, width), BF),
            v((2, width, all_units), BF),
            v((blocks, own, group), BF),
            v((blocks, width, group), BF),
            v((own, width), F32),
            v((own, 128), F32),
            v((own, width), F32),
            v((own, width), BF),
            v((width, own), BF),
            v((own, width), F32),
            v((own, width), F32),
            v((own, all_units), BF),
            v((own, all_units), F32),
            v((width, own), BF),
            v((own, width), F32),
            v((own, width), BF),
            v((width, all_units), BF),
            v((width, all_units), BF),
            pltpu.SemaphoreType.DMA((2, 4)),
            pltpu.SemaphoreType.DMA((2, 4)),
            pltpu.SemaphoreType.DMA((6,)),
        ],
        compiler_params=pltpu.CompilerParams(vmem_limit_bytes=60 << 20),
        cost_estimate=pl.CostEstimate(
            flops=2 * own * width * (6 * all_units + 3 * width),
            bytes_accessed=24 << 20,
            transcendentals=2 * own * all_units,
        ),
        name="middle",
    )(tokens, cotangent, ctx_all, w_o, w_ib, b_in, vectors)


def add_into(dst, other, rows):
    @pl.loop(0, rows // 16)
    def _(i):
        at = pl.ds(pl.multiple_of(i * 16, 16), 16)
        for a, b in zip(dst, other):
            a[at, :] = (a[at, :].astype(F32) + b[at, :].astype(F32)).astype(a.dtype)


def backward_kernel(
    heads,
    ln,
    d_ctx,
    g_b,
    g_i,
    g_o,
    out_low,
    d_first,
    small_in,
    q_in,
    kv_in,
    xt_in,
    wh_in,
    lse,
    ctx_t,
    seg,
    output,
    d_tokens,
    gf_b,
    gf_i,
    gf_o,
    gf_h,
    small,
    bias,
    q_scr,
    kv,
    xt,
    wh,
    d_got,
    d_o,
    kvt,
    dkv,
    dqt,
    d_proj,
    segc,
    segr,
    part,
    got_c,
    got_y,
    got_z,
    send_y,
    send_z,
    mine,
    done,
    o_b,
    o_i,
    o_o,
    r_b,
    r_i,
    r_o,
    x_b,
    x_i,
    x_o,
    y_b,
    y_i,
    y_o,
    z_b,
    z_i,
    z_o,
    acc_h,
    o_h,
    x_h,
    z_h,
    send_h,
    small_got,
    bias_sum,
    bias_got,
    h_got,
    bias_fin,
    send,
    recv,
    local,
):
    d, c, z = (lax.axis_index(n) for n in ALL)
    nc = 4
    hl = ln // 2
    own = ln + hl
    half = z % 2
    core, y = c % 2, c // 2
    wr = gf_b.shape[0]
    units = gf_b.shape[1]
    width = out_low.shape[1]
    wide = heads * 128
    rc = Copies(send, recv)
    at_c = lambda k: (d, c ^ k, z)
    at_x = (1 - d, c, z)
    at_z = lambda k: (d, c, z ^ k)
    across = (d, z, c)

    barrier = pltpu.get_barrier_semaphore()
    everyone = [at_c(k) for k in (1, 2, 3)] + [at_z(k) for k in (1, 2, 3)] + [at_x]
    for device in everyone:
        pl.semaphore_signal(barrier, inc=1, device_id=device, device_id_type=MESH)

    @pl.when(c != z)
    def _():
        pl.semaphore_signal(barrier, inc=1, device_id=across, device_id_type=MESH)

    pl.semaphore_wait(barrier, len(everyone) + jnp.where(c != z, 1, 0))

    number = iter(range(200))
    local_number = iter(range(40))

    def copy_here(src, dst):
        copy = pltpu.make_async_copy(src, dst, local.at[next(local_number)])
        copy.start()
        return copy

    flat = lambda ref: (lambda xy, h: (ref.at[xy, :, pl.ds(1536 * h, 1536)],))
    weights = []
    for own_b, got_b, x_buf, y_buf, z_buf, grad, final, is_o in (
        (o_b, r_b, x_b, y_b, z_b, g_b, gf_b, False),
        (o_i, r_i, x_i, y_i, z_i, g_i, gf_i, False),
        (o_o, r_o, x_o, y_o, z_o, g_o, gf_o, True),
    ):
        n = [next(number) for _ in range(12)]
        weights.append((own_b, got_b, x_buf, y_buf, z_buf, grad, final, is_o, n))
    half_units = 2 * units

    def of_core(w, which):
        grad, is_o = w[5], w[7]
        return grad.at[:, :, which] if is_o else grad.at[:, which]

    def part_of(w, xy, h):
        if w[7]:
            return w[0].at[pl.ds(2 * h, 2), xy]
        return w[0].at[xy, :, pl.ds(half_units * h, half_units)]

    def views(w, xy, h):
        if w[7]:
            return [w[0].at[2 * h, xy], w[0].at[2 * h + 1, xy]]
        return [w[0].at[xy, :, pl.ds(half_units * h, half_units)]]

    def buf_views(w, ref, i):
        return [ref.at[i, 0], ref.at[i, 1]] if w[7] else [ref.at[i]]

    def unit_at(w, t):
        xy = 2 * d + y
        if w[7]:
            return w[0].at[t, xy]
        return w[0].at[xy, :, pl.ds(pl.multiple_of(t * units, 128), units)]

    w_here = [copy_here(of_core(w, core), w[0]) for w in weights]
    blk = lambda x_, y_: 2 * x_ + y_

    def w_core_send(w):
        rc.start(w[8][0], lambda: (of_core(w, 1 - core), w[1], at_c(1)))

    def w_core_add(i):
        w = weights[i]
        w_here[i].wait()
        rc.arrived(w[8][0], w[1], at_c(1))

        @pl.loop(0, 4)
        def _(xy):
            if w[7]:
                add_into([w[0].at[t, xy] for t in range(4)], [w[1].at[t, xy] for t in range(4)], wr)
            else:
                add_into([w[0].at[xy]], [w[1].at[xy]], wr)

        n = w[8]
        for j in range(2):
            rc.start(n[1 + j], lambda j=j: (part_of(w, blk(1 - d, j), 0), w[2].at[j], at_x))
            rc.start(n[3 + j], lambda j=j: (part_of(w, blk(j, 1 - y), 1), w[3].at[j], at_c(2)))

    def w_plane(i):
        w = weights[i]
        n = w[8]
        for j in range(2):
            rc.arrived(n[1 + j], w[2].at[j], at_x)
        for j in range(2):
            add_into(views(w, blk(d, j), 0), buf_views(w, w[2], j), wr)
        rc.start(n[5], lambda: (part_of(w, blk(d, 1 - y), 0), w[3].at[2], at_c(2)))
        for j in range(2):
            rc.arrived(n[3 + j], w[3].at[j], at_c(2))
        for j in range(2):
            add_into(views(w, blk(j, y), 1), buf_views(w, w[3], j), wr)
        rc.start(n[6], lambda: (part_of(w, blk(1 - d, y), 1), w[2].at[2], at_x))

    def w_corner(i):
        w = weights[i]
        n = w[8]
        rc.arrived(n[5], w[3].at[2], at_c(2))
        add_into(views(w, blk(d, y), 0), buf_views(w, w[3], 2), wr)
        rc.arrived(n[6], w[2].at[2], at_x)
        add_into(views(w, blk(d, y), 1), buf_views(w, w[2], 2), wr)
        for t in (0, 1, 2):
            chain_send(w, t, 3)
        for t in (3, 2, 1):
            chain_send(w, t, 0)

    def chain_send(w, t, at):
        to = at + 1 if t > at else at - 1
        slot = 4 if to == t and t > at else t
        n = w[8]
        rc.start(
            n[7 + slot],
            lambda: (unit_at(w, t), w[4].at[slot], (d, c, to)),
            lambda: z == at,
            n[7 + t],
        )

    def chain_pass(w, t, at):
        @pl.when(z == at)
        def _():
            rc.arrived(w[8][7 + t], w[4].at[t], at_x)
            add_into([unit_at(w, t)], [w[4].at[t]], wr)

        chain_send(w, t, at)

    def w_line(i):
        w = weights[i]
        for t in (0, 1):
            chain_pass(w, t, 2)
        for t in (3, 2):
            chain_pass(w, t, 1)

    def w_next(i):
        w = weights[i]
        chain_pass(w, 3, 2)
        chain_pass(w, 0, 1)

    def w_end(i):
        w = weights[i]
        for t in range(4):

            @pl.when(z == t)
            def _():
                if t < 3:
                    rc.arrived(w[8][7 + t], w[4].at[t], at_x)
                if t > 0:
                    rc.arrived(w[8][11], w[4].at[4], at_x)

        total = unit_at(w, z)[...].astype(F32) + w[4].at[z][...].astype(F32)
        w[6][...] = total + w[4].at[4][...].astype(F32)

    whole_of = lambda t: (3 * t + 1) // 2
    shared_of = lambda t: 1 + 3 * (t // 2)

    class Line:
        def __init__(self, at):
            self.at = at
            self.left = [next(number) for _ in range(3)]
            self.right = [next(number) for _ in range(3)]

        def begin(self, src):
            rc.start(self.left[0], lambda: (src, self.at(z), (d, c, z + 1)), lambda: z < 3)
            rc.start(self.right[0], lambda: (src, self.at(z), (d, c, z - 1)), lambda: z > 0)

        def step(self, j):
            from_left, from_right = z - j, z + j

            @pl.when(z >= j)
            def _():
                rc.arrived(self.left[j - 1], self.at(from_left), (d, c, z - 1))

            if j < 3:
                rc.start(
                    self.left[j],
                    lambda: (self.at(z - j), self.at(z - j), (d, c, z + 1)),
                    lambda: (z >= j) & (z < 3),
                )

            @pl.when(z + j <= 3)
            def _():
                rc.arrived(self.right[j - 1], self.at(from_right), (d, c, z + 1))

            if j < 3:
                rc.start(
                    self.right[j],
                    lambda: (self.at(z + j), self.at(z + j), (d, c, z - 1)),
                    lambda: (z + j <= 3) & (z > 0),
                )

    whole_rows = lambda ref, a, n: (lambda t: ref.at[whole_of(t), pl.ds(a, n)])
    shared_rows = lambda ref: (
        lambda t: ref.at[shared_of(t), pl.ds(pl.multiple_of((t % 2) * hl, 128), hl)]
    )
    out_lines = [Line(whole_rows(output, 0, ln)), Line(shared_rows(output))]
    tok_lines = [
        Line(whole_rows(d_tokens, 0, hl)),
        Line(whole_rows(d_tokens, hl, hl)),
        Line(shared_rows(d_tokens)),
    ]

    n_ctx = [next(number) for _ in range(3)]
    for k in (1, 2, 3):
        rc.start(n_ctx[k - 1], lambda k=k: (d_ctx.at[c ^ k], d_got.at[c], at_c(k)))
    ctx_here = copy_here(d_ctx.at[c], d_got.at[c])
    kv_here = copy_here(kv_in, kv)
    q_here = copy_here(q_in, q_scr)
    n_small = [next(number) for _ in range(5)]
    small_to = (at_c(1), at_c(2), at_x, at_z(1), at_z(2))
    small[...] = small_in[...]

    def small_send(i):
        rc.start(n_small[i], lambda: (small_got.at[i, 1], small_got.at[i, 0], small_to[i]))

    def small_step(i):
        rc.arrived(n_small[i], small_got.at[i, 0], small_to[i])
        small[...] += small_got[i, 0]
        if i < 4:
            small_got[i + 1, 1] = small[...]
            small_send(i + 1)

    small_got[0, 1] = small_in[...]
    wh_here = copy_here(wh_in, wh)
    xt_here = copy_here(xt_in, xt)
    out_here = [
        copy_here(out_low.at[pl.ds(0, ln)], out_lines[0].at(z)),
        copy_here(out_low.at[pl.ds(ln, hl)], out_lines[1].at(z)),
    ]

    def block(qb):
        r0, r1, o0, o1, seq = block_rows(qb, half, ln)
        b0 = jnp.where(qb < 4, qb, 2 * (qb - 4))
        b1 = jnp.where(qb < 4, qb, 2 * (qb - 4) + 1)
        s0 = pl.multiple_of(jnp.where(qb < 4, 0, hl * half), 128)
        s1 = pl.multiple_of(jnp.where(qb < 4, hl, hl * half), 128)
        sq = jnp.concatenate(
            [
                segr[2 * b0 + seq, 0:1, pl.ds(s0, hl)],
                segr[2 * b1 + seq, 0:1, pl.ds(s1, hl)],
            ],
            1,
        )
        q, do, line, delta = [], [], [], []
        for h in range(heads):
            q.append(two(q_scr, r0, r1, hl, slice(128 * h, 128 * h + 128)))
            do.append(two(d_o, o0, o1, hl, slice(128 * h, 128 * h + 128)))
            line.append(two_lanes(lse, slice(h, h + 1), o0, o1, hl))
            turned = do[h].astype(F32).T[HEAD:, :]
            kept = two_lanes(ctx_t, slice(HEAD * h, HEAD * h + HEAD), o0, o1, hl)
            delta.append(jnp.sum(turned * kept, 0, keepdims=True))
        dqt[...] = jnp.zeros_like(dqt)

        @pl.loop(0, nc)
        def _(j):
            rows = pl.ds(pl.multiple_of((2 * j + seq) * ln, ln), ln)
            keys = pl.ds(pl.multiple_of(j * ln, ln), ln)
            key_seg = segc[2 * j + seq]
            same = jnp.concatenate([key_seg, key_seg], 1) == sq
            for h in range(heads):
                kvh = kv[rows, 128 * h : 128 * h + 128]
                p = jnp.where(same, jnp.exp(dot_nt(kvh, q[h]) - line[h]), 0.0)
                ds = (p * (dot_nt(kvh, do[h]) - delta[h])).astype(BF)
                dkv[rows, 128 * h : 128 * h + 128] += dot_nn(ds, q[h]) + dot_nn(
                    p.astype(BF), do[h]
                )
                dqt[h] += dot_nn(kvt[seq * heads + h, :, keys], ds)

        turned = jnp.concatenate([dqt[h, :HEAD, :] for h in range(heads)], 0).T * 0.125
        bias_sum[0:1, wide:] += jnp.sum(turned, 0, keepdims=True)
        low = turned.astype(BF)
        d_proj[pl.ds(r0, hl), wide:] = low[:hl]
        d_proj[pl.ds(r1, hl), wide:] = low[hl:]

    n_tc = [[next(number), next(number)] for _ in range(2)]
    n_ty = [[next(number), next(number)] for _ in range(2)]
    n_tz = next(number)

    def rows_of(cb, s):
        rows = pl.ds(pl.multiple_of((2 * cb + s) * ln, ln), ln)
        got = dkv[rows, :]
        bias_sum[0:1, :wide] += jnp.sum(got, 0, keepdims=True)
        d_proj[rows, :wide] = got.astype(BF)
        part[cb, s] = dot_nt(d_proj[rows, :], wh[...]).astype(BF)

    def t_partial(s):
        rows_of(c ^ 3, s)
        rc.start(n_tc[s][0], lambda: (part.at[c ^ 3, s], got_c.at[s, 0], at_c(1)))
        rows_of(c ^ 1, s)
        rc.start(n_tc[s][1], lambda: (part.at[c ^ 1, s], got_c.at[s, 1], at_c(1)))
        rows_of(c ^ 2, s)
        rows_of(c, s)

    def t_core(s):
        rc.arrived(n_tc[s][0], got_c.at[s, 0], at_c(1))
        for k in range(2):
            at = slice(k * hl, k * hl + hl)
            send_y[s, at] = (part[c ^ 2, s, at].astype(F32) + got_c[s, 0, at].astype(F32)).astype(BF)
            rc.start(
                n_ty[s][k],
                lambda k=k: (
                    send_y.at[s, pl.ds(k * hl, hl)],
                    got_y.at[s, pl.ds(k * hl, hl)],
                    at_c(2),
                ),
            )
        rc.arrived(n_tc[s][1], got_c.at[s, 1], at_c(1))
        mine[s] = part[c, s].astype(F32) + got_c[s, 1].astype(F32)

    def t_shared():
        for k in range(2):
            rc.arrived(n_ty[1][k], got_y.at[1, pl.ds(k * hl, hl)], at_c(2))
        mine[1] += got_y[1].astype(F32)
        send_z[...] = mine[1, pl.ds(pl.multiple_of((1 - half) * hl, 128), hl)].astype(BF)
        rc.start(n_tz, lambda: (send_z, got_z, at_z(1)))

    def t_shared_end():
        rc.arrived(n_tz, got_z, at_z(1))
        mine_half = mine[1, pl.ds(pl.multiple_of(half * hl, 128), hl)]
        done[ln:, :] = (mine_half + got_z[...].astype(F32) + d_first[ln:, :]).astype(BF)
        tok_lines[2].begin(done.at[pl.ds(ln, hl)])

    def t_whole(k):
        at = slice(k * hl, k * hl + hl)
        rc.arrived(n_ty[0][k], got_y.at[0, pl.ds(k * hl, hl)], at_c(2))
        done[at, :] = (mine[0, at] + got_y[0, at].astype(F32) + d_first[at, :]).astype(BF)
        tok_lines[k].begin(done.at[pl.ds(k * hl, hl)])

    n_h = [next(number) for _ in range(8)]

    def h_partial(seq):
        @pl.loop(0, nc)
        def _(i):
            rows = pl.ds(pl.multiple_of((2 * i + seq) * ln, ln), ln)
            acc_h[...] += dot_nn(xt[:, rows], d_proj[rows, :])

    def h_send():
        o_h[...] = acc_h[...].astype(BF)
        rows_x = lambda x_: pl.ds(pl.multiple_of(x_ * 4 * wr, wr), 4 * wr)
        rc.start(n_h[0], lambda: (o_h.at[rows_x(1 - d)], x_h, at_x))

    h_at = lambda t: o_h.at[pl.ds(pl.multiple_of((4 * d + t) * wr, wr), wr)]

    def h_plane():
        rc.arrived(n_h[0], x_h, at_x)
        add_into([o_h.at[pl.ds(pl.multiple_of(d * 4 * wr, wr), 4 * wr)]], [x_h], 4 * wr)
        rc.start(n_h[1], lambda: (h_at(z ^ 3), z_h.at[1], at_z(1)))
        rc.start(n_h[2], lambda: (h_at(z ^ 1), z_h.at[0], at_z(1)))

    def h_line():
        rc.arrived(n_h[1], z_h.at[1], at_z(1))
        add_into([h_at(z ^ 2)], [z_h.at[1]], wr)
        rc.start(n_h[3], lambda: (h_at(z ^ 2), z_h.at[2], at_z(2)))
        rc.arrived(n_h[2], z_h.at[0], at_z(1))
        add_into([h_at(z)], [z_h.at[0]], wr)

    def h_end():
        rc.arrived(n_h[3], z_h.at[2], at_z(2))
        send_h[...] = h_at(z)[...].astype(F32) + z_h[2].astype(F32)
        rc.start(n_h[4], lambda: (send_h, h_got, across), lambda: c != z)

        @pl.when(c == z)
        def _():
            h_got[...] = send_h[...]

    n_bias = [next(number) for _ in range(4)]
    bias_to = (at_x, at_z(1), at_z(2))

    def bias_send(i):
        bias_got[i, 1] = bias_sum[...]
        rc.start(n_bias[i], lambda: (bias_got.at[i, 1], bias_got.at[i, 0], bias_to[i]))

    def bias_step(i):
        rc.arrived(n_bias[i], bias_got.at[i, 0], bias_to[i])
        bias_sum[...] += bias_got[i, 0]
        if i < 2:
            bias_send(i + 1)
            return
        rc.start(n_bias[3], lambda: (bias_sum, bias_fin, across), lambda: c != z)

        @pl.when(c == z)
        def _():
            bias_fin[...] = bias_sum[...]

    for w in weights:

        @pl.when(z == 0)
        def _():
            w[4][4] = jnp.zeros_like(w[4][4])

        @pl.when(z == 3)
        def _():
            w[4][3] = jnp.zeros_like(w[4][3])

    def get_ctx():
        for k in (1, 2, 3):
            rc.arrived(n_ctx[k - 1], d_got.at[c ^ k], at_c(k))
        ctx_here.wait()

        @pl.loop(0, nc)
        def _(i):
            rows = pl.ds(pl.multiple_of(i * own, 128), own)
            for h in range(heads):
                d_o[rows, 128 * h + HEAD : 128 * h + 128] = d_got[
                    i, :, HEAD * h : HEAD * h + HEAD
                ]

        q_here.wait()
        wh_here.wait()
        xt_here.wait()

    def out_begin():
        out_lines[0].begin(out_low.at[pl.ds(0, ln)])
        out_lines[1].begin(out_low.at[pl.ds(ln, hl)])

    out_begin()
    w_core_send(weights[0])
    w_core_send(weights[2])
    for i in range(nc):
        for s in range(2):
            line = seg[i, s : s + 1, :].astype(F32)
            segr[2 * i + s, 0:1, :] = line
            segc[2 * i + s] = jnp.broadcast_to(line, (128, ln)).T
    dkv[...] = jnp.zeros_like(dkv)
    d_o[...] = jnp.zeros_like(d_o)
    d_proj[...] = jnp.zeros_like(d_proj)
    bias_sum[...] = jnp.zeros_like(bias_sum)
    acc_h[...] = jnp.zeros_like(acc_h)
    kv_here.wait()

    @pl.loop(0, nc)
    def _(j):
        for s in range(2):
            rows = pl.ds(pl.multiple_of((2 * j + s) * ln, ln), ln)
            for h in range(heads):
                kvt[s * heads + h, :, pl.ds(pl.multiple_of(j * ln, ln), ln)] = kv[
                    rows, 128 * h : 128 * h + 128
                ].T

    small_send(0)
    w_core_add(0)
    get_ctx()

    @pl.loop(0, 6)
    def _(i):
        block(jnp.where(i == 0, 0, jnp.where(i == 1, 1, jnp.where(i == 2, 2, jnp.where(i == 3, 3, jnp.where(i == 4, 4, 5))))))

        @pl.when(i == 0)
        def _():
            w_core_send(weights[1])
            small_step(0)
            w_core_add(2)
            out_lines[0].step(1)
            out_lines[1].step(1)

        @pl.when(i == 3)
        def _():
            t_partial(0)
            out_lines[0].step(2)
            out_lines[1].step(2)
            t_core(0)
            w_plane(2)

    t_whole(0)
    h_partial(0)
    t_whole(1)
    w_plane(0)
    t_partial(1)
    w_corner(2)
    t_core(1)
    small_step(1)
    bias_send(0)
    w_core_add(1)
    tok_lines[0].step(1)
    w_corner(0)
    w_line(2)
    small_step(2)
    bias_step(0)
    tok_lines[1].step(1)
    h_partial(1)
    out_lines[0].step(3)
    out_lines[1].step(3)
    tok_lines[0].step(2)
    t_shared()
    bias_step(1)
    h_send()
    t_shared_end()
    tok_lines[1].step(2)
    w_plane(1)
    tok_lines[0].step(3)
    w_line(0)
    h_plane()
    tok_lines[2].step(1)
    w_next(0)
    bias_step(2)
    h_line()
    small_step(3)
    w_next(2)
    w_corner(1)
    w_end(2)
    w_end(0)
    h_end()
    tok_lines[2].step(2)
    w_line(1)
    w_next(1)
    tok_lines[1].step(3)
    tok_lines[2].step(3)
    small_step(4)
    w_end(1)
    tok_here = [
        copy_here(done.at[pl.ds(0, hl)], tok_lines[0].at(z)),
        copy_here(done.at[pl.ds(hl, hl)], tok_lines[1].at(z)),
        copy_here(done.at[pl.ds(ln, hl)], tok_lines[2].at(z)),
    ]

    @pl.when(c != z)
    def _():
        rc.arrived(n_h[4], h_got, across)
        rc.arrived(n_bias[3], bias_fin, across)

    gf_h[...] = h_got[...]
    bias[...] = bias_fin[...]

    for copy in out_here + tok_here:
        copy.wait()
    rc.all_sent()


def backward(d_ctx, g_b, g_i, g_o, out_low, d_first, small, q, kv, xt, wh, lse, ctx_t, seg, heads, seqs):
    nc, own, group = d_ctx.shape
    ln = own * 2 // 3
    hl = ln // 2
    width = out_low.shape[1]
    wr, all_units = g_b.shape[2:]
    units = all_units // 4
    hb = pl.BlockSpec(memory_space=pltpu.HBM)
    vm = pl.BlockSpec(memory_space=pltpu.VMEM)
    sds = jax.ShapeDtypeStruct
    v = pltpu.VMEM
    rows = nc * own
    n2 = 2 * nc * ln
    return pl.pallas_call(
        functools.partial(backward_kernel, heads, ln),
        out_shape=(
            sds((seqs, ln, width), BF),
            sds((seqs, ln, width), BF),
            sds((wr, units), F32),
            sds((wr, units), F32),
            sds((wr, group), F32),
            sds((wr, 3 * group), F32),
            sds(small.shape, F32),
            sds((8, 3 * group), F32),
        ),
        in_specs=[hb] * 4 + [vm] * 3 + [hb] * 4 + [vm] * 3,
        out_specs=(hb, hb) + (vm,) * 6,
        scratch_shapes=[
            v((n2, heads * 128), BF),
            v((n2, heads * 128), BF),
            v((width, n2), BF),
            v((width, 3 * group), BF),
            v((nc, own, group), BF),
            v((rows, heads * 128), BF),
            v((2 * heads, 128, nc * ln), BF),
            v((n2, heads * 128), F32),
            v((heads, 128, ln), F32),
            v((n2, 3 * group), BF),
            v((2 * nc, ln, 128), F32),
            v((2 * nc, 8, ln), F32),
            v((nc, 2, ln, width), BF),
            v((2, 2, ln, width), BF),
            v((2, ln, width), BF),
            v((hl, width), BF),
            v((2, ln, width), BF),
            v((hl, width), BF),
            v((2, ln, width), F32),
            v((own, width), BF),
            v((4, wr, all_units), BF),
            v((4, wr, all_units), BF),
            v((4, 4, wr, group), BF),
            v((4, wr, all_units), BF),
            v((4, wr, all_units), BF),
            v((4, 4, wr, group), BF),
            v((3, wr, 2 * units), BF),
            v((3, wr, 2 * units), BF),
            v((3, 2, wr, group), BF),
            v((3, wr, 2 * units), BF),
            v((3, wr, 2 * units), BF),
            v((3, 2, wr, group), BF),
            v((5, wr, units), BF),
            v((5, wr, units), BF),
            v((5, wr, group), BF),
            v((width, 3 * group), F32),
            v((width, 3 * group), BF),
            v((4 * wr, 3 * group), BF),
            v((3, wr, 3 * group), BF),
            v((wr, 3 * group), F32),
            v((5, 2) + small.shape, F32),
            v((8, 3 * group), F32),
            v((3, 2, 8, 3 * group), F32),
            v((wr, 3 * group), F32),
            v((8, 3 * group), F32),
            pltpu.SemaphoreType.DMA((130,)),
            pltpu.SemaphoreType.DMA((130,)),
            pltpu.SemaphoreType.DMA((40,)),
        ],
        compiler_params=pltpu.CompilerParams(
            vmem_limit_bytes=60 << 20, collective_id=1, has_side_effects=True
        ),
        name="backward",
    )(d_ctx, g_b, g_i, g_o, out_low, d_first, small, q, kv, xt, wh, lse, ctx_t, seg)


def finish_kernel(
    heads, tok_in, out_in, g_b, g_i, g_o, g_h, small, bias,
    tok, out, gb, gi, go, gh, gq, gv, w0, w1, w2, in_b, w3, w4, w5,
):
    tok[...] = tok_in[...].astype(F32)
    out[...] = out_in[...]
    z = lax.axis_index("tp")
    wide = heads * 128

    @pl.when(pl.program_id(0) == 0)
    def _():
        gb[...] = g_b[...]
        gi[...] = g_i[...]
        go[...] = g_o[...]
        pick = lambda ref, rows, at: jnp.concatenate(
            [ref[rows, 128 * h + at : 128 * h + at + HEAD] for h in range(heads)], -1
        )
        gh[:, 0, :] = g_h[:, wide:]
        gh[:, 1, :] = pick(g_h, slice(None), 0)
        gh[:, 2, :] = pick(g_h, slice(None), HEAD)
        gq[...] = bias[0, wide:]
        gv[...] = pick(bias, 0, HEAD)
        for i, ref in ((0, w0), (1, w1), (2, w2), (3, w3), (4, w4), (5, w5)):
            ref[...] = small[i, :]
        in_b[...] = small[pl.ds(6 + z, 1), :].reshape(in_b.shape)


def finish(d_tokens, output, g_b, g_i, g_o, g_h, small, d_bias, heads):
    seqs, ln, width = d_tokens.shape
    wr, units = g_b.shape
    group = g_o.shape[1]
    one = lambda: pl.BlockSpec((1, ln, width), lambda i: (i, 0, 0))
    whole = lambda shape: pl.BlockSpec(shape, lambda i: (0,) * len(shape))
    sds = jax.ShapeDtypeStruct
    rest = [
        (wr, units), (wr, units), (wr, group), (wr, 3, group), (group,), (group,),
        (width,), (width,), (width,), (units,), (width,), (width,), (width,),
    ]
    return pl.pallas_call(
        functools.partial(finish_kernel, heads),
        grid=(seqs,),
        out_shape=[sds(d_tokens.shape, F32), sds(output.shape, BF)] + [sds(s, F32) for s in rest],
        in_specs=[one(), one()]
        + [whole(a.shape) for a in (g_b, g_i, g_o, g_h, small, d_bias)],
        out_specs=[one(), one()] + [whole(s) for s in rest],
        compiler_params=pltpu.CompilerParams(vmem_limit_bytes=60 << 20),
        name="finish",
    )(d_tokens, output, g_b, g_i, g_o, g_h, small, d_bias)


def head_order(kinds, heads):
    lead = kinds[0].shape[:-1]
    q, k, v = (a.reshape(lead + (heads, HEAD)) for a in kinds)
    kv = jnp.concatenate([k, v], -1).reshape(lead + (heads * 2 * HEAD,))
    return jnp.concatenate([kv, q.reshape(lead + (heads * HEAD,))], -1)


def forward_plain(sizes, me, tok2, seg2, w_head, b_head, b_unit, w_o, w_i, w_b, heads):
    nd, nc, nt = sizes
    d, c, z = me
    ln, width = tok2.shape[1:]
    hl = ln // 2
    half = z % 2
    group = w_o.shape[1]
    seg_all = gather_axis(seg2, "ctx", nc, c)
    x2 = gather_axis(tok2, "ctx", nc, c).reshape(2 * nc, ln, width)
    wh = gather_heads(w_head, sizes, me)
    bh = transpose_ctx_tp(b_head, nc)[0]
    b_all = gather_axis(b_unit, "tp", nt, z)
    gather = lambda w: lax.all_gather(
        lax.all_gather(w, "tp", axis=1, tiled=True), ("dp", "ctx"), axis=0, tiled=True
    )
    o_full = jnp.transpose(gather(w_o).reshape(width, nt, group), (1, 0, 2))
    proj = (jnp.dot(x2.reshape(-1, width), wh, preferred_element_type=F32) + bh).astype(BF)
    kv = proj[:, : 2 * group]
    q = (proj[:, 2 * group :].astype(F32) * 0.125).astype(BF).reshape(-1, heads, HEAD)
    q = jnp.concatenate([q, jnp.zeros_like(q)], -1).reshape(-1, heads * 128)
    info, seg_col, seg_row = key_blocks(seg_all, half, ln, nc)
    context, lse, ctx_t = attend(info, q, kv, seg_col, seg_row, heads, ln, nc)
    ctx_all = in_order(exchange_axis(context.reshape(nc, ln + hl, group), "ctx", nc, c), c)
    return (
        ctx_all,
        x2.reshape(-1, width).T,
        q,
        kv,
        wh,
        o_full,
        jnp.stack([gather(w_i), gather(w_b)]),
        b_all,
        lse,
        ctx_t,
        seg_all,
    )


def key_blocks(seg_all, half, ln, nc):
    hl = ln // 2
    seg2 = seg_all[:, :2]
    flat = jnp.transpose(seg2, (1, 0, 2)).reshape(2, nc * ln)
    first = jnp.concatenate([seg2[:, 0, 0], jnp.take(seg2[0::2, 1], half * hl, axis=1)])
    last = jnp.concatenate([seg2[:, 0, -1], jnp.take(seg2[1::2, 1], half * hl + hl - 1, axis=1)])
    of = jnp.concatenate(
        [
            jnp.broadcast_to(flat[:1], (nc, nc * ln)),
            jnp.broadcast_to(flat[1:], (nc // 2, nc * ln)),
        ],
        0,
    )
    lo = jnp.sum(of < first[:, None], 1) // ln
    hi = (jnp.sum(of <= last[:, None], 1) + ln - 1) // ln
    info = jnp.concatenate([lo, hi, half[None]]).astype(jnp.int32)
    seg_flat = seg2.reshape(2 * nc * ln)
    return info, seg_flat[:, None], seg_flat[None, :]


def backward_plain(
    sizes, me, d_ctx, low, out_low, d_first, small, q, kv, xt, wh, lse, ctx_t, seg_all, heads, seqs
):
    nd, nc, nt = sizes
    d, c, z = me
    own, group = d_ctx.shape[1:]
    ln = own * 2 // 3
    hl = ln // 2
    half = z % 2
    width = out_low.shape[1]
    units = low[0].shape[1] // nt
    nr = nd * nc
    wr = width // nr
    info, seg_col, seg_row = key_blocks(seg_all, half, ln, nc)

    def spread_rows(rows_low, dtype):
        out = jnp.zeros((seqs, ln, width), dtype)
        parts = [rows_low] + [swap_with(rows_low, "tp", nt, k) for k in range(1, nt)]
        for k, part in enumerate(parts):
            t = z ^ k
            part = part.astype(dtype)
            out = lax.dynamic_update_slice(out, part[None, :ln], ((3 * t + 1) // 2, 0, 0))
            out = lax.dynamic_update_slice(
                out, part[None, ln:], (1 + 3 * (t // 2), (t % 2) * hl, 0)
            )
        return out

    by_unit = lambda g: jnp.transpose(g.reshape(nr, wr, nt, units), (2, 0, 1, 3))
    g_back = scatter_weight(by_unit(low[0]), sizes, me)
    g_in = scatter_weight(by_unit(low[1]), sizes, me)
    g_out = scatter_weight(low[2].reshape(nt, nr, wr, group), sizes, me)
    output = spread_rows(out_low, BF)
    small = lax.psum(small, ALL)
    d_ctx = in_order(exchange_axis(d_ctx, "ctx", nc, c), c).reshape(nc * own, heads, HEAD)
    d_ctx = jnp.concatenate([jnp.zeros_like(d_ctx), d_ctx], -1).reshape(nc * own, heads * 128)
    d_q, d_kv, d_bias = attend_back(
        info, q, kv, d_ctx, seg_col, seg_row, lse, ctx_t, heads, ln, nc
    )
    d_proj = jnp.concatenate([d_kv, d_q], -1)
    part = jnp.einsum("tf,df->td", d_proj, wh, preferred_element_type=F32)
    part = lax.psum_scatter(
        part.reshape(nc, 2 * ln, width), "ctx", scatter_dimension=0, tiled=False
    ).reshape(2, ln, width)
    shared = part[1].reshape(2, hl, width)
    shared = lax.dynamic_index_in_dim(shared, half, 0, keepdims=False) + swap_with(
        lax.dynamic_index_in_dim(shared, 1 - half, 0, keepdims=False), "tp", nt, 1
    )
    d_own = (jnp.concatenate([part[0], shared], 0) + d_first).astype(BF)
    d_tokens = spread_rows(d_own, BF)
    g_h = scatter_heads(jnp.dot(xt, d_proj, preferred_element_type=F32).astype(BF), sizes, me)
    slots = jnp.zeros((nc,) + d_bias[0].shape, F32)
    slots = lax.psum(lax.dynamic_update_index_in_dim(slots, d_bias[0], c, 0), ALL)
    d_bias = lax.dynamic_index_in_dim(slots, z, 0, keepdims=False)
    d_bias = jnp.broadcast_to(d_bias[None], (8,) + d_bias.shape)
    return output, d_tokens, g_back, g_in, g_out, g_h, small, d_bias


def per_device(
    sizes,
    tokens,
    segments,
    w_qkv,
    q_bias,
    v_bias,
    w_out,
    out_bias,
    gain_one,
    shift_one,
    w_in,
    in_bias,
    w_back,
    back_bias,
    gain_two,
    shift_two,
    cotangent,
):
    nd, nc, nt = sizes
    seqs, ln, width = tokens.shape
    group = w_out.shape[1]
    heads = group // HEAD
    units = w_in.shape[1]
    wr = w_in.shape[0]
    d, c, z = (lax.axis_index(n) for n in ALL)
    me = (d, c, z)
    whole_of = lambda t: (3 * t + 1) // 2
    shared_of = lambda t: 1 + 3 * (t // 2)
    half_of = lambda t: t % 2
    sf, sh, half = whole_of(z), shared_of(z), half_of(z)

    def own_pair(a):
        return jnp.stack(
            [
                lax.dynamic_index_in_dim(a, sf, 0, keepdims=False),
                lax.dynamic_index_in_dim(a, sh, 0, keepdims=False),
            ],
            0,
        )

    tok2 = own_pair(tokens)
    seg2 = jnp.concatenate([own_pair(segments), jnp.zeros((6, ln), jnp.int32)], 0)
    w_head = head_order([w_qkv[:, i] for i in range(3)], heads)
    b_head = head_order([q_bias, jnp.zeros_like(q_bias), v_bias], heads)
    b_head = jnp.broadcast_to(b_head[None], (8, 3 * group))
    b_unit = jnp.broadcast_to(in_bias[None], (8, units))
    args = (tok2, seg2, w_head, b_head, b_unit, w_out, w_in, w_back, heads)
    got = forward(*args) if sizes == (2, 4, 4) else forward_plain(sizes, me, *args)
    ctx_all, xt, q, kv, wh, w_o, w_ib, b_in, lse, ctx_t, seg_all = got
    w_o = w_o.reshape(nt, width, group)
    w_ib = w_ib.reshape(2, width, nt * units)
    vectors = jnp.stack([out_bias, gain_one, shift_one, back_bias, gain_two, shift_two])
    d_ctx, g_b, g_i, g_o, out_low, d_first, small = middle(
        tokens, cotangent, ctx_all, w_o, w_ib, b_in, vectors
    )
    low = (g_b, g_i, g_o)
    if sizes == (2, 4, 4):
        output, d_tokens, g_back, g_in, g_out, g_h, small, d_bias = backward(
            d_ctx,
            low[0].reshape(4, 2, wr, nt * units),
            low[1].reshape(4, 2, wr, nt * units),
            low[2].reshape(nt, 4, 2, wr, group),
            out_low,
            d_first,
            small,
            q,
            kv,
            xt,
            wh,
            lse,
            ctx_t,
            seg_all,
            heads,
            seqs,
        )
    else:
        output, d_tokens, g_back, g_in, g_out, g_h, small, d_bias = backward_plain(
            sizes, me, d_ctx, low, out_low, d_first, small, q, kv, xt, wh, lse, ctx_t, seg_all, heads, seqs
        )
    d_tokens, output, g_b, g_i, g_o, g_h, d_qb, d_vb, w0, w1, w2, d_in, w3, w4, w5 = finish(
        d_tokens, output, g_back, g_in, g_out, g_h, small, d_bias, heads
    )
    return (output, d_tokens, g_h, d_qb, d_vb, g_o, w0, w1, w2, g_i, d_in, g_b, w3, w4, w5)


def solution(mesh):
    sizes = tuple(mesh.shape[n] for n in ALL)
    rows = P(("dp", "ctx"), "tp")
    return jax.shard_map(
        functools.partial(per_device, sizes),
        mesh=mesh,
        in_specs=(
            P("dp", "ctx", None),
            P("dp", "ctx"),
            P(("dp", "ctx"), None, "tp"),
            P("tp"),
            P("tp"),
            rows,
            P(),
            P(),
            P(),
            rows,
            P("tp"),
            rows,
            P(),
            P(),
            P(),
            P("dp", "ctx", None),
        ),
        out_specs=(
            P("dp", "ctx", None),
            P("dp", "ctx", None),
            P(("dp", "ctx"), None, "tp"),
            P("tp"),
            P("tp"),
            rows,
            P(),
            P(),
            P(),
            rows,
            P("tp"),
            rows,
            P(),
            P(),
            P(),
        ),
        check_vma=False,
    )
```

```python
import functools
import math

import jax
import jax.numpy as jnp
from jax import lax
from jax.experimental import pallas as pl
from jax.experimental.pallas import tpu as pltpu
from jax.sharding import PartitionSpec as P

HEAD = 64
NEG = -1e30
BF = jnp.bfloat16
F32 = jnp.float32
ALL = ("dp", "ctx", "tp")


def norm_parts(value):
    mean = jnp.mean(value, -1, keepdims=True)
    centered = value - mean
    rstd = lax.rsqrt(jnp.mean(centered * centered, -1, keepdims=True) + 1e-12)
    return (centered * rstd, rstd)


def norm_back(grad, normal, rstd, gain):
    d_gain = jnp.sum(grad * normal, 0)
    d_shift = jnp.sum(grad, 0)
    scaled = grad * gain
    d_value = rstd * (
        scaled
        - jnp.mean(scaled, -1, keepdims=True)
        - normal * jnp.mean(scaled * normal, -1, keepdims=True)
    )
    return (d_value, d_gain, d_shift)


def gelu_slope(inner):
    return 0.5 * (1.0 + lax.erf(inner / math.sqrt(2.0))) + inner * jnp.exp(
        -0.5 * inner * inner
    ) / math.sqrt(2.0 * math.pi)


def swap_with(value, axis, size, mask):
    return lax.ppermute(value, axis, [(i, i ^ mask) for i in range(size)])


def in_order(parts, me, axis=0):
    shape = list(parts[0].shape)
    shape.insert(axis, len(parts))
    out = jnp.zeros(tuple(shape), parts[0].dtype)
    for k, part in enumerate(parts):
        out = lax.dynamic_update_index_in_dim(out, part, me ^ k, axis)
    return out


def gather_axis(value, axis, size, me):
    parts = [value] + [swap_with(value, axis, size, k) for k in range(1, size)]
    return in_order(parts, me)


def exchange_axis(blocks, axis, size, me):
    parts = [lax.dynamic_index_in_dim(blocks, me, 0, keepdims=False)]
    for k in range(1, size):
        parts.append(
            swap_with(lax.dynamic_index_in_dim(blocks, me ^ k, 0, keepdims=False), axis, size, k)
        )
    return parts


def scatter_weight(grad, sizes, me):
    nd, nc, nt = sizes
    part = lax.psum_scatter(
        grad.astype(F32), ("dp", "ctx"), scatter_dimension=1, tiled=False
    ).astype(BF)
    parts = exchange_axis(part, "tp", nt, me[2])
    return sum(p.astype(F32) for p in parts)


def transpose_ctx_tp(value, n):
    pairs = [(a * n + b, b * n + a) for a in range(n) for b in range(n)]
    return lax.ppermute(value, ("ctx", "tp"), pairs)


def gather_heads(shard, sizes, me):
    mine = transpose_ctx_tp(shard, sizes[1])
    return lax.all_gather(mine, ("dp", "tp"), axis=0, tiled=True)


def scatter_heads(grad, sizes, me):
    nd, nc, nt = sizes
    blocks = grad.reshape((nd * nt, grad.shape[0] // (nd * nt)) + grad.shape[1:])
    total = lax.psum_scatter(
        blocks.astype(F32), ("dp", "tp"), scatter_dimension=0, tiled=False
    )
    return transpose_ctx_tp(total, nc)


def block_rows(qb, half, ln):
    hl = ln // 2
    whole = qb < 4
    b = jnp.where(whole, qb, qb - 4)
    r0 = jnp.where(whole, 2 * ln * b, (4 * b + 1) * ln + hl * half)
    r1 = jnp.where(whole, r0 + hl, r0 + 2 * ln)
    o0 = jnp.where(whole, 3 * hl * b, 6 * hl * b + ln)
    o1 = jnp.where(whole, o0 + hl, o0 + 3 * hl)
    seq = jnp.where(whole, 0, 1)
    m = lambda v: pl.multiple_of(v, 128)
    return m(r0), m(r1), m(o0), m(o1), seq


def two(ref, r0, r1, hl, cols):
    return jnp.concatenate([ref[pl.ds(r0, hl), cols], ref[pl.ds(r1, hl), cols]], 0)


def two_lanes(ref, rows, r0, r1, hl):
    return jnp.concatenate([ref[rows, pl.ds(r0, hl)], ref[rows, pl.ds(r1, hl)]], 1)


def dot_nt(a, b):
    return lax.dot_general(a, b, (((1,), (1,)), ((), ())), preferred_element_type=F32)


def dot_nn(a, b):
    return lax.dot_general(a, b, (((1,), (0,)), ((), ())), preferred_element_type=F32)


def fill_transposed(kv, kvt, ln, nc, heads):
    @pl.loop(0, nc)
    def _(j):
        for seq in range(2):
            rows = pl.ds(pl.multiple_of((2 * j + seq) * ln, ln), ln)
            for h in range(heads):
                kvt[seq * heads + h, :, pl.ds(pl.multiple_of(j * ln, ln), ln)] = kv[
                    rows, 128 * h : 128 * h + 128
                ].T


def attend_kernel(heads, ln, nc, info, q_ref, kv, seg_col, seg_row, out, lse, ctx_t, s_scr, kvt, acc):
    half = info[12]
    hl = ln // 2
    fill_transposed(kv, kvt, ln, nc, heads)

    @pl.loop(0, 6)
    def _(qb):
        r0, r1, o0, o1, seq = block_rows(qb, half, ln)
        lo, hi = info[qb], info[6 + qb]
        sq = two_lanes(seg_row, slice(0, 1), r0, r1, hl)
        q = [two(q_ref, r0, r1, hl, slice(128 * h, 128 * h + 128)) for h in range(heads)]

        def score(j, peaks):
            rows = pl.ds(pl.multiple_of((2 * j + seq) * ln, ln), ln)
            same = seg_col[rows, :] == sq
            new = []
            for h in range(heads):
                s = dot_nt(kv[rows, 128 * h : 128 * h + 128], q[h])
                s = jnp.where(same, s, NEG)
                s_scr[h, pl.ds(pl.multiple_of(j * ln, ln), ln), :] = s
                new.append(jnp.maximum(peaks[h], jnp.max(s, 0, keepdims=True)))
            return tuple(new)

        peaks = lax.fori_loop(
            lo, hi, score, tuple(jnp.full((1, ln), NEG, F32) for _ in range(heads))
        )
        acc[...] = jnp.zeros_like(acc)

        def collect(j, sums):
            keys = pl.ds(pl.multiple_of(j * ln, ln), ln)
            new = []
            for h in range(heads):
                p = jnp.exp(s_scr[h, keys, :] - peaks[h])
                new.append(sums[h] + jnp.sum(p, 0, keepdims=True))
                acc[h] += dot_nn(kvt[seq * heads + h, :, keys], p.astype(BF))
            return tuple(new)

        sums = lax.fori_loop(
            lo, hi, collect, tuple(jnp.zeros((1, ln), F32) for _ in range(heads))
        )
        whole = []
        for h in range(heads):
            one = acc[h, HEAD:, :] / sums[h]
            whole.append(one)
            line = peaks[h] + jnp.log(sums[h])
            for part, at in ((0, o0), (hl, o1)):
                ctx_t[HEAD * h : HEAD * h + HEAD, pl.ds(at, hl)] = one[:, part : part + hl]
                lse[h : h + 1, pl.ds(at, hl)] = line[:, part : part + hl]
        turned = jnp.concatenate(whole, 0).T.astype(BF)
        out[pl.ds(o0, hl), :] = turned[:hl]
        out[pl.ds(o1, hl), :] = turned[hl:]


def attend(info, q_ref, kv, seg_col, seg_row, heads, ln, nc):
    rows = 3 * ln // 2 * nc
    vm = pl.BlockSpec(memory_space=pltpu.VMEM)
    return pl.pallas_call(
        functools.partial(attend_kernel, heads, ln, nc),
        out_shape=(
            jax.ShapeDtypeStruct((rows, heads * HEAD), BF),
            jax.ShapeDtypeStruct((8, rows), F32),
            jax.ShapeDtypeStruct((heads * HEAD, rows), F32),
        ),
        in_specs=[pl.BlockSpec(memory_space=pltpu.SMEM), vm, vm, vm, vm],
        out_specs=(vm, vm, vm),
        scratch_shapes=[
            pltpu.VMEM((heads, nc * ln, ln), F32),
            pltpu.VMEM((2 * heads, 128, nc * ln), BF),
            pltpu.VMEM((heads, 128, ln), F32),
        ],
        compiler_params=pltpu.CompilerParams(vmem_limit_bytes=32 << 20),
        cost_estimate=pl.CostEstimate(
            flops=8 * heads * rows * nc * ln * 128,
            bytes_accessed=8 << 20,
            transcendentals=heads * rows * nc * ln,
        ),
        name="attend",
    )(info, q_ref, kv, seg_col, seg_row)


def attend_back_kernel(
    heads, ln, nc, info, q_ref, kv, d_out, seg_col, seg_row, lse, ctx_t, d_q, d_kv, d_bias, dkv, kvt, dqt
):
    half = info[12]
    hl = ln // 2
    fill_transposed(kv, kvt, ln, nc, heads)
    dkv[...] = jnp.zeros_like(dkv)
    d_bias[...] = jnp.zeros_like(d_bias)

    @pl.loop(0, nc)
    def _(c):
        rows = pl.ds(pl.multiple_of((2 * c + 1) * ln, ln), ln)
        d_q[rows, :] = jnp.zeros((ln, heads * HEAD), BF)

    @pl.loop(0, 6)
    def _(qb):
        r0, r1, o0, o1, seq = block_rows(qb, half, ln)
        lo, hi = info[qb], info[6 + qb]
        sq = two_lanes(seg_row, slice(0, 1), r0, r1, hl)
        q, do, line, delta = [], [], [], []
        for h in range(heads):
            q.append(two(q_ref, r0, r1, hl, slice(128 * h, 128 * h + 128)))
            do.append(two(d_out, o0, o1, hl, slice(128 * h, 128 * h + 128)))
            line.append(two_lanes(lse, slice(h, h + 1), o0, o1, hl))
            turned = do[h].astype(F32).T[HEAD:, :]
            kept = two_lanes(ctx_t, slice(HEAD * h, HEAD * h + HEAD), o0, o1, hl)
            delta.append(jnp.sum(turned * kept, 0, keepdims=True))
        dqt[...] = jnp.zeros_like(dqt)

        @pl.loop(lo, hi)
        def _(j):
            rows = pl.ds(pl.multiple_of((2 * j + seq) * ln, ln), ln)
            keys = pl.ds(pl.multiple_of(j * ln, ln), ln)
            same = seg_col[rows, :] == sq
            for h in range(heads):
                kvh = kv[rows, 128 * h : 128 * h + 128]
                p = jnp.where(same, jnp.exp(dot_nt(kvh, q[h]) - line[h]), 0.0)
                ds = (p * (dot_nt(kvh, do[h]) - delta[h])).astype(BF)
                dkv[rows, 128 * h : 128 * h + 128] += dot_nn(ds, q[h]) + dot_nn(
                    p.astype(BF), do[h]
                )
                dqt[h] += dot_nn(kvt[seq * heads + h, :, keys], ds)

        turned = jnp.concatenate([dqt[h, :HEAD, :] for h in range(heads)], 0).T * 0.125
        d_bias[0:1, heads * 128 :] += jnp.sum(turned, 0, keepdims=True)
        low = turned.astype(BF)
        d_q[pl.ds(r0, hl), :] = low[:hl]
        d_q[pl.ds(r1, hl), :] = low[hl:]

    @pl.loop(0, 2 * nc)
    def _(c):
        rows = pl.ds(pl.multiple_of(c * ln, ln), ln)
        for h in range(heads):
            got = dkv[rows, 128 * h : 128 * h + 128]
            d_bias[0:1, 128 * h : 128 * h + 128] += jnp.sum(got, 0, keepdims=True)
            d_kv[rows, 128 * h : 128 * h + 128] = got.astype(BF)


def attend_back(info, q_ref, kv, d_out, seg_col, seg_row, lse, ctx_t, heads, ln, nc):
    rows = 3 * ln // 2 * nc
    vm = pl.BlockSpec(memory_space=pltpu.VMEM)
    return pl.pallas_call(
        functools.partial(attend_back_kernel, heads, ln, nc),
        out_shape=(
            jax.ShapeDtypeStruct((2 * nc * ln, heads * HEAD), BF),
            jax.ShapeDtypeStruct((2 * nc * ln, heads * 128), BF),
            jax.ShapeDtypeStruct((8, heads * (HEAD + 128)), F32),
        ),
        in_specs=[pl.BlockSpec(memory_space=pltpu.SMEM)] + [vm] * 7,
        out_specs=(vm, vm, vm),
        scratch_shapes=[
            pltpu.VMEM((2 * nc * ln, heads * 128), F32),
            pltpu.VMEM((2 * heads, 128, nc * ln), BF),
            pltpu.VMEM((heads, 128, ln), F32),
        ],
        compiler_params=pltpu.CompilerParams(vmem_limit_bytes=40 << 20),
        cost_estimate=pl.CostEstimate(
            flops=20 * heads * rows * nc * ln * 128,
            bytes_accessed=14 << 20,
            transcendentals=heads * rows * nc * ln,
        ),
        name="attend_back",
    )(info, q_ref, kv, d_out, seg_col, seg_row, lse, ctx_t)


MESH = pl.DeviceIdType.MESH


class Copies:
    def __init__(self, send, recv):
        self.send, self.recv, self.open = send, recv, []

    def make(self, i, src, dst, device, sent=None):
        return pltpu.make_async_remote_copy(
            src_ref=src,
            dst_ref=dst,
            send_sem=self.send.at[i if sent is None else sent],
            recv_sem=self.recv.at[i],
            device_id=device,
            device_id_type=MESH,
        )

    def start(self, i, parts, when=None, sent=None):
        number = (lambda: i) if not callable(i) else i

        def go(wait):
            copy = self.make(number(), *parts(), sent=sent)
            copy.wait_send() if wait else copy.start()

        self.run(go, when, False)
        self.open.append((go, when))

    def run(self, go, when, wait):
        if when is None:
            go(wait)
        else:

            @pl.when(when())
            def _():
                go(wait)

    def arrived(self, i, dst, device):
        self.make(i, dst, dst, device).wait_recv()

    def all_sent(self):
        for go, when in self.open:
            self.run(go, when, True)


def line_order(z, i):
    if i == 0:
        return z
    if i == 1:
        return jnp.where(z == 0, 1, z - 1)
    if i == 2:
        return jnp.where(z == 0, 2, jnp.where(z == 3, 1, z + 1))
    return jnp.where(z < 2, 3, 0)


def forward_kernel(
    heads,
    ln,
    tokens,
    segments,
    w_kinds,
    q_bias,
    v_bias,
    in_bias,
    w_o,
    w_i,
    w_b,
    ctx_all,
    xt_out,
    q_out,
    kv_out,
    wh_out,
    o_full,
    w_full,
    bu_full,
    lse,
    ctx_t,
    seg,
    x2,
    xt,
    wh,
    bh,
    q_scr,
    kv,
    s_scr,
    kvt,
    acc,
    segc,
    segr,
    context,
    w_src,
    o_src,
    seg2,
    w_head,
    b_head,
    b_unit,
    send,
    recv,
    local,
):
    d, c, z = (lax.axis_index(n) for n in ALL)
    nc = 4
    hl = ln // 2
    own = ln + hl
    half = z % 2
    wr = w_i.shape[0]
    units = w_i.shape[1]
    row = d * nc + c
    row_x, row_y, row_d = row ^ 4, row ^ 2, row ^ 6
    rc = Copies(send, recv)
    at_c = lambda k: (d, c ^ k, z)
    at_x = (1 - d, c, z)
    to_c = lambda k: (lambda: at_c(k))
    to_x = lambda: at_x
    at_z = lambda k: (d, c, z ^ k)
    across = (d, z, c)
    order = [line_order(z, i) for i in range(4)]
    number = iter(range(0, 400))
    four = lambda: [next(number) for _ in range(4)][0]
    local_number = iter(range(32))

    def copy_here(src, dst):
        copy = pltpu.make_async_copy(src, dst, local.at[next(local_number)])
        copy.start()
        return copy

    t_cols = lambda t: pl.ds(pl.multiple_of(t * units, 128), units)
    w_at = lambda r, t: w_full.at[:, r, :, t_cols(t)]
    o_at = lambda r, t: o_full.at[t, r]
    wh_at = lambda r: wh.at[pl.ds(pl.multiple_of(r * wr, wr), wr)]
    tok_at = lambda i: x2.at[pl.ds(2 * i, 2)]
    w_here = [copy_here(w_i, w_src.at[0]), copy_here(w_b, w_src.at[1]), copy_here(w_o, o_src)]
    tok_src = lambda s: tokens.at[(3 * z + 1) // 2 if s == 0 else 1 + 3 * (z // 2)]
    mine = [copy_here(tok_src(s), x2.at[2 * c + s]) for s in range(2)]
    here_sem = [local.at[next(local_number)] for _ in range(2)]
    here = [
        pltpu.make_async_copy(w_head, wh_at(row), here_sem[0]),
        pltpu.make_async_copy(b_head, bh, here_sem[1]),
    ]

    barrier = pltpu.get_barrier_semaphore()
    everyone = [at_c(k) for k in (1, 2, 3)] + [at_z(k) for k in (1, 2, 3)] + [at_x]
    for device in everyone:
        pl.semaphore_signal(barrier, inc=1, device_id=device, device_id_type=MESH)

    @pl.when(c != z)
    def _():
        pl.semaphore_signal(barrier, inc=1, device_id=across, device_id_type=MESH)

    seg2[...] = jnp.zeros_like(seg2)
    seg2[0:1, :] = segments[pl.ds((3 * z + 1) // 2, 1), :]
    seg2[1:2, :] = segments[pl.ds(1 + 3 * (z // 2), 1), :]
    wide = heads * 128
    b_head[...] = jnp.zeros_like(b_head)
    b_unit[...] = jnp.zeros_like(b_unit)
    qb = q_bias[...].reshape(1, heads * HEAD)
    vb = v_bias[...].reshape(1, heads * HEAD)
    for h in range(heads):
        cols = slice(HEAD * h, HEAD * h + HEAD)
        w_head[:, 128 * h : 128 * h + HEAD] = w_kinds[1, :, cols]
        w_head[:, 128 * h + HEAD : 128 * h + 128] = w_kinds[2, :, cols]
        b_head[0:1, 128 * h + HEAD : 128 * h + 128] = vb[:, cols]
    w_head[:, wide:] = w_kinds[0]
    b_head[0:1, wide:] = qb
    b_unit[0:1, :] = in_bias[...].reshape(1, units)
    seg_here = copy_here(seg2, seg.at[c])
    bu_here = copy_here(b_unit, bu_full.at[z])

    @pl.when(c == z)
    def _():
        for copy in here:
            copy.start()

    pl.semaphore_wait(barrier, len(everyone) + jnp.where(c != z, 1, 0))

    n_tf, n_wa, n_ba = (next(number) for _ in range(3))
    n_ty, n_tc = ([next(number) for _ in range(2)] for _ in range(2))
    not_here = lambda: c != z
    rc.start(n_wa, lambda: (w_head, wh_at(row), across), not_here)
    rc.start(n_ba, lambda: (b_head, bh, across), not_here)
    n_seg = four()
    for k in (1, 2, 3):
        rc.start(n_seg + k, lambda k=k: (seg2, seg.at[c], at_c(k)))

    class Line:
        def __init__(self, at):
            self.at = at
            self.n = [next(number) for _ in range(5)][0]

        def begin(self, src):
            rc.start(
                lambda: self.n + z,
                lambda: (src, self.at(z), (d, c, z + 1)),
                lambda: z < 3,
                self.n + 3,
            )
            rc.start(
                lambda: self.n + z,
                lambda: (src, self.at(z), (d, c, z - 1)),
                lambda: z > 0,
                self.n + 4,
            )

        def step(self, i):
            t = lambda: order[i]
            rc.arrived(self.n + t(), self.at(t()), (d, c, z))
            rc.start(
                lambda: self.n + t(),
                lambda: (
                    self.at(t()),
                    self.at(t()),
                    (d, c, jnp.where(t() < z, z + 1, z - 1)),
                ),
                lambda: jnp.where(t() < z, z < 3, z > 0),
                self.n + i - 1,
            )

    n_hz = four()
    full_at = (
        lambda r, t: w_full.at[0, r, :, t_cols(t)],
        o_at,
        lambda r, t: w_full.at[1, r, :, t_cols(t)],
    )
    sources = (w_src.at[0], o_src, w_src.at[1])
    lines = [Line(lambda t, w=w: full_at[w](row, t)) for w in range(3)]
    n_hx = four()
    n_x, n_y, n_d = ([four() for _ in range(3)] for _ in range(3))
    n_c = [[four() for _ in range(3)] for _ in range(4)]

    groups = [(0, 1), (2,)]
    over_y = ((0, 2), (1, 1), (1, 3))

    def pass_on(n, g, i, r, device, first=False):
        t = lambda: order[i]
        for w in groups[g]:
            rc.start(
                lambda w=w: n[w] + t(),
                lambda w=w: (
                    sources[w] if first and i == 0 else full_at[w](r, t()),
                    full_at[w](r, t()),
                    device(),
                ),
                None,
                n[w] + i,
            )

    def came(n, g, i, r, device):
        t = order[i]
        for w in groups[g]:
            rc.arrived(n[w] + t, full_at[w](r, t), device)

    def own_send(g):
        pass_on(n_x, g, 0, row, to_x, True)
        pass_on(n_c[0], g, 0, row, to_c(1), True)

    def line_begin(g):
        for w in groups[g]:
            lines[w].begin(sources[w])

    def y_send(g, i):
        pass_on(n_y, g, i, row, to_c(2), True)

    def line_step(g, i):
        for w in groups[g]:
            lines[w].step(i)
        pass_on(n_x, g, i, row, to_x)
        pass_on(n_c[0], g, i, row, to_c(1))

    def from_x(g, i):
        came(n_x, g, i, row_x, at_x)
        if (g, i) in over_y:
            pass_on(n_d, g, i, row_x, to_c(2))
        pass_on(n_c[1], g, i, row_x, to_c(1))

    def from_y(g, i):
        came(n_y, g, i, row_y, at_c(2))
        if (g, i) not in over_y:
            pass_on(n_d, g, i, row_y, to_x)
        pass_on(n_c[2], g, i, row_y, to_c(1))

    def from_corner(g, i):
        came(n_d, g, i, row_d, at_x)
        pass_on(n_c[3], g, i, row_d, to_c(1))

    head_at = lambda t: wh_at(d * nc + t)
    n_bu = four()
    n_ctx = four()
    ctx_at = lambda i: context.at[pl.ds(pl.multiple_of(i * own, 128), own)]

    def head_send():
        @pl.when(c != z)
        def _():
            rc.arrived(n_wa, wh_at(d * nc + z), across)
            rc.arrived(n_ba, bh, across)

        @pl.when(c == z)
        def _():
            for copy in here:
                copy.wait()

        for k in (1, 2, 3):
            rc.start(n_hz + k, lambda k=k: (head_at(z), head_at(z), at_z(k)))
        rc.start(n_hx, lambda: (head_at(z), head_at(z), at_x))
        for k in (1, 2, 3):
            rc.start(n_bu + k, lambda k=k: (b_unit, bu_full.at[z], at_z(k)))

    def head_pass(k):
        rc.arrived(n_hz + k, head_at(z ^ k), at_z(k))
        rc.start(n_hx + k, lambda: (head_at(z ^ k), head_at(z ^ k), at_x))

    def token_pass():
        for s in range(2):
            rc.arrived(n_ty[s], x2.at[2 * (c ^ 2) + s], at_c(2))
        rc.start(n_tf, lambda: (tok_at(c ^ 2), tok_at(c ^ 2), at_c(1)))

    def context_send():
        for k in (2, 3, 1):
            rc.start(n_ctx + k, lambda k=k: (ctx_at(c ^ k), ctx_all.at[c], at_c(k)))

    def segments_done():
        for k in (1, 2, 3):
            rc.arrived(n_seg + k, seg.at[c ^ k], at_c(k))
        seg_here.wait()
        for i in range(nc):
            for s in range(2):
                line = seg[i, s : s + 1, :].astype(F32)
                segr[2 * i + s, 0:1, :] = line
                segc[2 * i + s] = jnp.broadcast_to(line, (128, ln)).T

    def block(qb):
        r0, r1, o0, o1, seq = block_rows(qb, half, ln)
        b0 = jnp.where(qb < 4, qb, 2 * (qb - 4))
        b1 = jnp.where(qb < 4, qb, 2 * (qb - 4) + 1)
        s0 = pl.multiple_of(jnp.where(qb < 4, 0, hl * half), 128)
        s1 = pl.multiple_of(jnp.where(qb < 4, hl, hl * half), 128)
        sq = jnp.concatenate(
            [
                segr[2 * b0 + seq, 0:1, pl.ds(s0, hl)],
                segr[2 * b1 + seq, 0:1, pl.ds(s1, hl)],
            ],
            1,
        )
        q = [two(q_scr, r0, r1, hl, slice(128 * h, 128 * h + 128)) for h in range(heads)]

        def score(j, peaks):
            rows = pl.ds(pl.multiple_of((2 * j + seq) * ln, ln), ln)
            key_seg = segc[2 * j + seq]
            same = jnp.concatenate([key_seg, key_seg], 1) == sq
            new = []
            for h in range(heads):
                s = dot_nt(kv[rows, 128 * h : 128 * h + 128], q[h])
                s = jnp.where(same, s, NEG)
                s_scr[h, pl.ds(pl.multiple_of(j * ln, ln), ln), :] = s
                new.append(jnp.maximum(peaks[h], jnp.max(s, 0, keepdims=True)))
            return tuple(new)

        peaks = lax.fori_loop(
            0, nc, score, tuple(jnp.full((1, ln), NEG, F32) for _ in range(heads))
        )
        acc[...] = jnp.zeros_like(acc)

        def collect(j, sums):
            keys = pl.ds(pl.multiple_of(j * ln, ln), ln)
            new = []
            for h in range(heads):
                p = jnp.exp(s_scr[h, keys, :] - peaks[h])
                new.append(sums[h] + jnp.sum(p, 0, keepdims=True))
                acc[h] += dot_nn(kvt[seq * heads + h, :, keys], p.astype(BF))
            return tuple(new)

        sums = lax.fori_loop(
            0, nc, collect, tuple(jnp.zeros((1, ln), F32) for _ in range(heads))
        )
        whole = []
        for h in range(heads):
            one = acc[h, HEAD:, :] / sums[h]
            whole.append(one)
            line = peaks[h] + jnp.log(sums[h])
            for part, at in ((0, o0), (hl, o1)):
                ctx_t[HEAD * h : HEAD * h + HEAD, pl.ds(at, hl)] = one[:, part : part + hl]
                lse[h : h + 1, pl.ds(at, hl)] = line[:, part : part + hl]
        turned = jnp.concatenate(whole, 0).T.astype(BF)
        context[pl.ds(o0, hl), :] = turned[:hl]
        context[pl.ds(o1, hl), :] = turned[hl:]

    for copy in w_here:
        copy.wait()
    own_here = [
        copy_here(sources[w], full_at[w](row, z)) for w in range(3)
    ]
    q_scr[...] = jnp.zeros_like(q_scr)
    y_send(1, 0)
    own_send(0)
    line_begin(1)
    for s in range(2):
        rc.start(n_ty[s], lambda s=s: (tok_src(s), x2.at[2 * c + s], at_c(2)))
        rc.start(n_tc[s], lambda s=s: (tok_src(s), x2.at[2 * c + s], at_c(1)))
    line_begin(0)
    head_send()
    line_step(0, 1)
    y_send(0, 0)
    line_step(1, 1)
    y_send(0, 1)
    head_pass(2)
    head_pass(1)
    head_pass(3)
    line_step(0, 2)
    segments_done()
    token_pass()
    y_send(0, 2)
    own_send(1)
    line_step(1, 2)
    y_send(1, 1)
    from_y(1, 0)
    for t in range(4):
        rc.arrived(n_hx + t, wh_at((1 - d) * nc + (z ^ t)), at_x)
    for s in range(2):
        mine[s].wait()
        rc.arrived(n_tc[s], x2.at[2 * (c ^ 1) + s], at_c(1))
    rc.arrived(n_tf, tok_at(c ^ 3), at_c(1))
    wh_here = copy_here(wh, wh_out)

    @pl.loop(0, 2 * nc)
    def _(i):
        x = x2[i]
        rows = pl.ds(pl.multiple_of(i * ln, ln), ln)
        xt[:, rows] = x.T
        got = (dot_nn(x, wh[:, :wide]) + bh[0:1, :wide]).astype(BF)
        kv[rows, :] = got
        qp = ((dot_nn(x, wh[:, wide:]) + bh[0:1, wide:]).astype(BF).astype(F32) * 0.125).astype(BF)
        for h in range(heads):
            q_scr[rows, 128 * h : 128 * h + HEAD] = qp[:, HEAD * h : HEAD * h + HEAD]

    x_here = copy_here(xt, xt_out)
    q_here = copy_here(q_scr, q_out)
    kv_here = copy_here(kv, kv_out)
    y_send(1, 2)
    line_step(1, 3)
    from_x(0, 2)
    @pl.loop(0, nc)
    def _(j):
        for s in range(2):
            rows = pl.ds(pl.multiple_of((2 * j + s) * ln, ln), ln)
            for h in range(heads):
                kvt[s * heads + h, :, pl.ds(pl.multiple_of(j * ln, ln), ln)] = kv[
                    rows, 128 * h : 128 * h + 128
                ].T

    from_x(0, 1)
    line_step(0, 3)
    y_send(0, 3)
    y_send(1, 3)
    from_x(0, 0)

    @pl.loop(0, 6)
    def _(qb):
        block(qb)

        @pl.when(qb == 1)
        def _():
            from_y(0, 0)
            from_x(1, 2)
            from_x(1, 1)

        @pl.when(qb == 2)
        def _():
            from_y(0, 2)
            from_y(0, 1)

        @pl.when(qb == 3)
        def _():
            from_x(1, 3)

        @pl.when(qb == 4)
        def _():
            from_corner(0, 0)
            from_y(1, 2)

    context_send()
    ctx_here = copy_here(ctx_at(c), ctx_all.at[c])
    from_y(1, 1)
    from_x(0, 3)
    from_y(0, 3)
    from_x(1, 0)
    from_corner(0, 2)
    from_y(1, 3)
    from_corner(1, 3)
    from_corner(1, 0)
    from_corner(1, 2)
    from_corner(1, 1)
    from_corner(0, 1)
    from_corner(0, 3)
    for k in (1, 2, 3):
        rc.arrived(n_ctx + k, ctx_all.at[c ^ k], at_c(k))
    for n, r in zip(n_c, (row, row_x, row_y, row_d)):
        for i in range(4):
            for g in range(len(groups)):
                came(n, g, i, r ^ 1, at_c(1))
    for k in (1, 2, 3):
        rc.arrived(n_bu + k, bu_full.at[z ^ k], at_z(k))
    for copy in own_here + [bu_here, x_here, wh_here, q_here, kv_here, ctx_here]:
        copy.wait()
    rc.all_sent()


def forward(tokens, segments, w_kinds, q_bias, v_bias, in_bias, w_o, w_i, w_b, heads):
    ln, width = tokens.shape[1:]
    wr, units = w_i.shape
    group = w_o.shape[1]
    nc, nt, nr = 4, 4, 8
    rows = 3 * ln // 2 * nc
    hb = pl.BlockSpec(memory_space=pltpu.HBM)
    vm = pl.BlockSpec(memory_space=pltpu.VMEM)
    sds = jax.ShapeDtypeStruct
    return pl.pallas_call(
        functools.partial(forward_kernel, heads, ln),
        out_shape=(
            sds((nc, 3 * ln // 2, group), BF),
            sds((width, 2 * nc * ln), BF),
            sds((2 * nc * ln, heads * 128), BF),
            sds((2 * nc * ln, heads * 128), BF),
            sds((nr * wr, 3 * group), BF),
            sds((nt, nr, wr, group), BF),
            sds((2, nr, wr, nt * units), BF),
            sds((nt, 8, units), F32),
            sds((8, rows), F32),
            sds((group, rows), F32),
            sds((nc, 8, ln), jnp.int32),
        ),
        in_specs=[hb] + [vm] * 5 + [hb] * 3,
        out_specs=(hb,) * 8 + (vm,) * 3,
        scratch_shapes=[
            pltpu.VMEM((2 * nc, ln, width), BF),
            pltpu.VMEM((width, 2 * nc * ln), BF),
            pltpu.VMEM((nr * wr, 3 * group), BF),
            pltpu.VMEM((8, 3 * group), F32),
            pltpu.VMEM((2 * nc * ln, heads * 128), BF),
            pltpu.VMEM((2 * nc * ln, heads * 128), BF),
            pltpu.VMEM((heads, nc * ln, ln), F32),
            pltpu.VMEM((2 * heads, 128, nc * ln), BF),
            pltpu.VMEM((heads, 128, ln), F32),
            pltpu.VMEM((2 * nc, ln, 128), F32),
            pltpu.VMEM((2 * nc, 8, ln), F32),
            pltpu.VMEM((rows, group), BF),
            pltpu.VMEM((2, wr, units), BF),
            pltpu.VMEM((wr, group), BF),
            pltpu.VMEM((8, ln), jnp.int32),
            pltpu.VMEM((wr, 3 * group), BF),
            pltpu.VMEM((8, 3 * group), F32),
            pltpu.VMEM((8, units), F32),
            pltpu.SemaphoreType.DMA((140,)),
            pltpu.SemaphoreType.DMA((140,)),
            pltpu.SemaphoreType.DMA((32,)),
        ],
        compiler_params=pltpu.CompilerParams(
            vmem_limit_bytes=60 << 20, collective_id=0, has_side_effects=True
        ),
        name="forward",
    )(tokens, segments, w_kinds, q_bias, v_bias, in_bias, w_o, w_i, w_b)


def middle_kernel(
    ln,
    tokens,
    cotangent,
    ctx_all,
    w_o,
    w_ib,
    b_in,
    out_bias,
    gain_one,
    shift_one,
    back_bias,
    gain_two,
    shift_two,
    d_ctx,
    g_b,
    g_i,
    g_o,
    out_low,
    d_first,
    small,
    x_own,
    c_own,
    w_v,
    ctx_v,
    w_ov,
    n_one,
    r_one,
    normed,
    low,
    low_t,
    tmp,
    acc,
    active,
    slope,
    n_two,
    d_sec,
    d_low,
    gb_v,
    gi_v,
    w_sem,
    g_sem,
    sem,
):
    z = lax.axis_index("tp")
    hl = ln // 2
    own = ln + hl
    blocks, _, group = ctx_all.shape
    width = x_own.shape[1]
    units = w_v.shape[2] // 4
    step, thin = 128, 64
    out_bias, gain_one, shift_one, back_bias, gain_two, shift_two = (
        a[...].reshape(1, width)
        for a in (out_bias, gain_one, shift_one, back_bias, gain_two, shift_two)
    )
    half_rows = pl.ds(pl.multiple_of((z % 2) * hl, 128), hl)
    first_rows = []
    for i, (src, dst) in enumerate(((tokens, x_own), (cotangent, c_own))):
        for j, (a, b) in enumerate(
            (
                (src.at[(3 * z + 1) // 2], dst.at[pl.ds(0, ln)]),
                (src.at[1 + 3 * (z // 2), half_rows], dst.at[pl.ds(ln, hl)]),
            )
        ):
            first_rows.append(pltpu.make_async_copy(a, b, sem.at[2 * i + j]))
    first_rows.append(pltpu.make_async_copy(ctx_all, ctx_v, sem.at[4]))
    first_rows.append(pltpu.make_async_copy(w_o, w_ov, sem.at[5]))
    for copy in first_rows:
        copy.start()
    t_cols = lambda t: pl.ds(pl.multiple_of(t * units, 128), units)

    def weight(which, t):
        return pltpu.make_async_copy(
            w_ib.at[which, :, t_cols(t)], w_v.at[which, :, t_cols(t)], w_sem.at[which, t]
        )

    for t in range(4):
        for which in range(2):
            weight(which, t).start()
    for copy in first_rows:
        copy.wait()

    def chunks(body, size=step):
        @pl.loop(0, own // size)
        def _(i):
            body(pl.ds(pl.multiple_of(i * size, size), size))

    mean = lambda v: jnp.mean(v, -1, keepdims=True)
    add = lambda i, v: small.__setitem__(
        (slice(i, i + 1), slice(None)), small[i : i + 1, :] + jnp.sum(v, 0, keepdims=True)
    )
    small[...] = jnp.zeros_like(small)

    tmp[...] = dot_nt(ctx_v[0], w_ov[0])
    for g in range(1, blocks):
        tmp[...] += dot_nt(ctx_v[g], w_ov[g])

    def norm_one(r):
        value = x_own[r, :].astype(F32) + (tmp[r, :] + out_bias)
        centered = value - mean(value)
        rstd = lax.rsqrt(mean(centered * centered) + 1e-12)
        normal = centered * rstd
        n_one[r, :] = normal
        r_one[r, :] = jnp.broadcast_to(rstd, (step, 128))
        got = normal * gain_one + shift_one
        normed[r, :] = got
        low[r, :] = got.astype(BF)
        acc[r, :] = got + back_bias

    chunks(norm_one)
    low_t[...] = low[...].T

    @pl.loop(0, 4)
    def _(t):
        weight(0, t).wait()
        weight(1, t).wait()
        tmp[...] = dot_nn(low[...], w_v[0, :, t_cols(t)]) + b_in[pl.ds(t, 1), 0, :]

        def gelu(r):
            u = tmp[r, :]
            cdf = 0.5 * (1.0 + lax.erf(u * math.sqrt(0.5)))
            active[r, t_cols(t)] = (u * cdf).astype(BF)
            slope[r, t_cols(t)] = cdf + u * jnp.exp(-0.5 * u * u) * (
                1.0 / math.sqrt(2.0 * math.pi)
            )

        chunks(gelu, thin)
        acc[...] += dot_nt(active[:, t_cols(t)], w_v[1, :, t_cols(t)])

    def norm_two(r):
        value = acc[r, :]
        centered = value - mean(value)
        rstd = lax.rsqrt(mean(centered * centered) + 1e-12)
        normal = centered * rstd
        out_low[r, :] = (normal * gain_two + shift_two).astype(BF)
        grad = c_own[r, :].astype(F32)
        add(4, grad * normal)
        add(5, grad)
        scaled = grad * gain_two
        got = rstd * (scaled - mean(scaled) - normal * mean(scaled * normal))
        d_sec[r, :] = got
        add(3, got)
        d_low[r, :] = got.astype(BF)
        acc[r, :] = got

    chunks(norm_two)
    n_two[...] = d_low[...].T

    @pl.loop(0, 4)
    def _(t):
        gb_v[:, t_cols(t)] = dot_nn(n_two[...], active[:, t_cols(t)]).astype(BF)
        pltpu.make_async_copy(gb_v.at[:, t_cols(t)], g_b.at[:, t_cols(t)], g_sem.at[0, t]).start()
        tmp[...] = dot_nn(d_low[...], w_v[1, :, t_cols(t)])

        def inner_back(r):
            got = tmp[r, :] * slope[r, t_cols(t)]
            at = pl.ds(6 + t, 1)
            small[at, :] += jnp.sum(got, 0, keepdims=True)
            active[r, t_cols(t)] = got.astype(BF)

        chunks(inner_back, thin)
        gi_v[:, t_cols(t)] = dot_nn(low_t[...], active[:, t_cols(t)]).astype(BF)
        pltpu.make_async_copy(gi_v.at[:, t_cols(t)], g_i.at[:, t_cols(t)], g_sem.at[1, t]).start()
        acc[...] += dot_nt(active[:, t_cols(t)], w_v[0, :, t_cols(t)])

    def norm_one_back(r):
        grad = acc[r, :]
        normal = n_one[r, :]
        add(1, grad * normal)
        add(2, grad)
        scaled = grad * gain_one
        got = r_one[r, 0:1] * (scaled - mean(scaled) - normal * mean(scaled * normal))
        d_first[r, :] = got
        add(0, got)
        d_low[r, :] = got.astype(BF)

    chunks(norm_one_back)
    n_two[...] = d_low[...].T
    for g in range(blocks):
        d_ctx[g] = dot_nn(d_low[...], w_ov[g]).astype(BF)
        g_o[g] = dot_nn(n_two[...], ctx_v[g]).astype(BF)
    for t in range(4):
        pltpu.make_async_copy(gb_v.at[:, t_cols(t)], g_b.at[:, t_cols(t)], g_sem.at[0, t]).wait()
        pltpu.make_async_copy(gi_v.at[:, t_cols(t)], g_i.at[:, t_cols(t)], g_sem.at[1, t]).wait()


def middle(tokens, cotangent, ctx_all, w_o, w_ib, b_in, vectors):
    blocks, own, group = ctx_all.shape
    ln, width = tokens.shape[1:]
    all_units = w_ib.shape[2]
    hb = pl.BlockSpec(memory_space=pltpu.HBM)
    vm = pl.BlockSpec(memory_space=pltpu.VMEM)
    sds = jax.ShapeDtypeStruct
    v = pltpu.VMEM
    return pl.pallas_call(
        functools.partial(middle_kernel, ln),
        out_shape=(
            sds((blocks, own, group), BF),
            sds((width, all_units), BF),
            sds((width, all_units), BF),
            sds((blocks, width, group), BF),
            sds((own, width), BF),
            sds((own, width), F32),
            sds((16, width), F32),
        ),
        in_specs=[hb] * 5 + [vm] * 7,
        out_specs=(vm, hb, hb, vm, vm, vm, vm),
        scratch_shapes=[
            v((own, width), BF),
            v((own, width), BF),
            v((2, width, all_units), BF),
            v((blocks, own, group), BF),
            v((blocks, width, group), BF),
            v((own, width), F32),
            v((own, 128), F32),
            v((own, width), F32),
            v((own, width), BF),
            v((width, own), BF),
            v((own, width), F32),
            v((own, width), F32),
            v((own, all_units), BF),
            v((own, all_units), F32),
            v((width, own), BF),
            v((own, width), F32),
            v((own, width), BF),
            v((width, all_units), BF),
            v((width, all_units), BF),
            pltpu.SemaphoreType.DMA((2, 4)),
            pltpu.SemaphoreType.DMA((2, 4)),
            pltpu.SemaphoreType.DMA((6,)),
        ],
        compiler_params=pltpu.CompilerParams(vmem_limit_bytes=60 << 20),
        cost_estimate=pl.CostEstimate(
            flops=2 * own * width * (6 * all_units + 3 * width),
            bytes_accessed=24 << 20,
            transcendentals=2 * own * all_units,
        ),
        name="middle",
    )(tokens, cotangent, ctx_all, w_o, w_ib, b_in, *vectors)


def add_into(dst, other, rows):
    @pl.loop(0, rows // 16)
    def _(i):
        at = pl.ds(pl.multiple_of(i * 16, 16), 16)
        for a, b in zip(dst, other):
            a[at, :] = (a[at, :].astype(F32) + b[at, :].astype(F32)).astype(a.dtype)


def backward_kernel(
    heads,
    ln,
    d_ctx,
    g_b,
    g_i,
    g_o,
    out_low,
    d_first,
    small_in,
    q_in,
    kv_in,
    xt_in,
    wh_in,
    lse,
    ctx_t,
    seg,
    output,
    d_tokens,
    gf_b,
    gf_i,
    gf_o,
    gf_h,
    small,
    bias,
    q_scr,
    kv,
    xt,
    wh,
    d_got,
    d_o,
    kvt,
    dkv,
    dqt,
    d_proj,
    segc,
    segr,
    part,
    got_c,
    got_y,
    got_z,
    send_y,
    send_z,
    mine,
    done,
    o_b,
    o_i,
    o_o,
    r_b,
    r_i,
    r_o,
    x_b,
    x_i,
    x_o,
    y_b,
    y_i,
    y_o,
    z_b,
    z_i,
    z_o,
    acc_h,
    o_h,
    x_h,
    z_h,
    send_h,
    small_got,
    bias_sum,
    bias_got,
    h_got,
    bias_fin,
    send,
    recv,
    local,
):
    d, c, z = (lax.axis_index(n) for n in ALL)
    nc = 4
    hl = ln // 2
    own = ln + hl
    half = z % 2
    core, y = c % 2, c // 2
    wr = gf_b.shape[0]
    units = gf_b.shape[1]
    width = out_low.shape[1]
    wide = heads * 128
    rc = Copies(send, recv)
    at_c = lambda k: (d, c ^ k, z)
    at_x = (1 - d, c, z)
    at_z = lambda k: (d, c, z ^ k)
    across = (d, z, c)

    barrier = pltpu.get_barrier_semaphore()
    everyone = [at_c(k) for k in (1, 2, 3)] + [at_z(k) for k in (1, 2, 3)] + [at_x]
    for device in everyone:
        pl.semaphore_signal(barrier, inc=1, device_id=device, device_id_type=MESH)

    @pl.when(c != z)
    def _():
        pl.semaphore_signal(barrier, inc=1, device_id=across, device_id_type=MESH)

    pl.semaphore_wait(barrier, len(everyone) + jnp.where(c != z, 1, 0))

    number = iter(range(200))
    local_number = iter(range(40))

    def copy_here(src, dst):
        copy = pltpu.make_async_copy(src, dst, local.at[next(local_number)])
        copy.start()
        return copy

    flat = lambda ref: (lambda xy, h: (ref.at[xy, :, pl.ds(1536 * h, 1536)],))
    weights = []
    for own_b, got_b, x_buf, y_buf, z_buf, grad, final, is_o in (
        (o_b, r_b, x_b, y_b, z_b, g_b, gf_b, False),
        (o_i, r_i, x_i, y_i, z_i, g_i, gf_i, False),
        (o_o, r_o, x_o, y_o, z_o, g_o, gf_o, True),
    ):
        n = [next(number) for _ in range(12)]
        weights.append((own_b, got_b, x_buf, y_buf, z_buf, grad, final, is_o, n))
    half_units = 2 * units

    def of_core(w, which):
        grad, is_o = w[5], w[7]
        return grad.at[:, :, which] if is_o else grad.at[:, which]

    def part_of(w, xy, h):
        if w[7]:
            return w[0].at[pl.ds(2 * h, 2), xy]
        return w[0].at[xy, :, pl.ds(half_units * h, half_units)]

    def views(w, xy, h):
        if w[7]:
            return [w[0].at[2 * h, xy], w[0].at[2 * h + 1, xy]]
        return [w[0].at[xy, :, pl.ds(half_units * h, half_units)]]

    def buf_views(w, ref, i):
        return [ref.at[i, 0], ref.at[i, 1]] if w[7] else [ref.at[i]]

    def unit_at(w, t):
        xy = 2 * d + y
        if w[7]:
            return w[0].at[t, xy]
        return w[0].at[xy, :, pl.ds(pl.multiple_of(t * units, 128), units)]

    w_here = [copy_here(of_core(w, core), w[0]) for w in weights]
    blk = lambda x_, y_: 2 * x_ + y_

    def w_core_send(w):
        rc.start(w[8][0], lambda: (of_core(w, 1 - core), w[1], at_c(1)))

    def w_core_add(i):
        w = weights[i]
        w_here[i].wait()
        rc.arrived(w[8][0], w[1], at_c(1))

        @pl.loop(0, 4)
        def _(xy):
            if w[7]:
                add_into([w[0].at[t, xy] for t in range(4)], [w[1].at[t, xy] for t in range(4)], wr)
            else:
                add_into([w[0].at[xy]], [w[1].at[xy]], wr)

        n = w[8]
        for j in range(2):
            rc.start(n[1 + j], lambda j=j: (part_of(w, blk(1 - d, j), 0), w[2].at[j], at_x))
            rc.start(n[3 + j], lambda j=j: (part_of(w, blk(j, 1 - y), 1), w[3].at[j], at_c(2)))

    def w_plane(i):
        w = weights[i]
        n = w[8]
        for j in range(2):
            rc.arrived(n[1 + j], w[2].at[j], at_x)
        for j in range(2):
            add_into(views(w, blk(d, j), 0), buf_views(w, w[2], j), wr)
        rc.start(n[5], lambda: (part_of(w, blk(d, 1 - y), 0), w[3].at[2], at_c(2)))
        for j in range(2):
            rc.arrived(n[3 + j], w[3].at[j], at_c(2))
        for j in range(2):
            add_into(views(w, blk(j, y), 1), buf_views(w, w[3], j), wr)
        rc.start(n[6], lambda: (part_of(w, blk(1 - d, y), 1), w[2].at[2], at_x))

    def w_corner(i):
        w = weights[i]
        n = w[8]
        rc.arrived(n[5], w[3].at[2], at_c(2))
        add_into(views(w, blk(d, y), 0), buf_views(w, w[3], 2), wr)
        rc.arrived(n[6], w[2].at[2], at_x)
        add_into(views(w, blk(d, y), 1), buf_views(w, w[2], 2), wr)
        for t in (0, 1, 2):
            chain_send(w, t, 3)
        for t in (3, 2, 1):
            chain_send(w, t, 0)

    def chain_send(w, t, at):
        to = at + 1 if t > at else at - 1
        slot = 4 if to == t and t > at else t
        n = w[8]
        rc.start(
            n[7 + slot],
            lambda: (unit_at(w, t), w[4].at[slot], (d, c, to)),
            lambda: z == at,
            n[7 + t],
        )

    def chain_pass(w, t, at):
        @pl.when(z == at)
        def _():
            rc.arrived(w[8][7 + t], w[4].at[t], at_x)
            add_into([unit_at(w, t)], [w[4].at[t]], wr)

        chain_send(w, t, at)

    def w_line(i):
        w = weights[i]
        for t in (0, 1):
            chain_pass(w, t, 2)
        for t in (3, 2):
            chain_pass(w, t, 1)

    def w_next(i):
        w = weights[i]
        chain_pass(w, 3, 2)
        chain_pass(w, 0, 1)

    def w_end(i):
        w = weights[i]
        for t in range(4):

            @pl.when(z == t)
            def _():
                if t < 3:
                    rc.arrived(w[8][7 + t], w[4].at[t], at_x)
                if t > 0:
                    rc.arrived(w[8][11], w[4].at[4], at_x)

        total = unit_at(w, z)[...].astype(F32) + w[4].at[z][...].astype(F32)
        w[6][...] = total + w[4].at[4][...].astype(F32)

    whole_of = lambda t: (3 * t + 1) // 2
    shared_of = lambda t: 1 + 3 * (t // 2)

    class Line:
        def __init__(self, at):
            self.at = at
            self.left = [next(number) for _ in range(3)]
            self.right = [next(number) for _ in range(3)]

        def begin(self, src):
            rc.start(self.left[0], lambda: (src, self.at(z), (d, c, z + 1)), lambda: z < 3)
            rc.start(self.right[0], lambda: (src, self.at(z), (d, c, z - 1)), lambda: z > 0)

        def step(self, j):
            from_left, from_right = z - j, z + j

            @pl.when(z >= j)
            def _():
                rc.arrived(self.left[j - 1], self.at(from_left), (d, c, z - 1))

            if j < 3:
                rc.start(
                    self.left[j],
                    lambda: (self.at(z - j), self.at(z - j), (d, c, z + 1)),
                    lambda: (z >= j) & (z < 3),
                )

            @pl.when(z + j <= 3)
            def _():
                rc.arrived(self.right[j - 1], self.at(from_right), (d, c, z + 1))

            if j < 3:
                rc.start(
                    self.right[j],
                    lambda: (self.at(z + j), self.at(z + j), (d, c, z - 1)),
                    lambda: (z + j <= 3) & (z > 0),
                )

    whole_rows = lambda ref, a, n: (lambda t: ref.at[whole_of(t), pl.ds(a, n)])
    shared_rows = lambda ref: (
        lambda t: ref.at[shared_of(t), pl.ds(pl.multiple_of((t % 2) * hl, 128), hl)]
    )
    out_lines = [Line(whole_rows(output, 0, ln)), Line(shared_rows(output))]
    tok_lines = [
        Line(whole_rows(d_tokens, 0, hl)),
        Line(whole_rows(d_tokens, hl, hl)),
        Line(shared_rows(d_tokens)),
    ]

    n_ctx = [next(number) for _ in range(3)]
    for k in (1, 2, 3):
        rc.start(n_ctx[k - 1], lambda k=k: (d_ctx.at[c ^ k], d_got.at[c], at_c(k)))
    ctx_here = copy_here(d_ctx.at[c], d_got.at[c])
    kv_here = copy_here(kv_in, kv)
    q_here = copy_here(q_in, q_scr)
    n_small = [next(number) for _ in range(5)]
    small_to = (at_c(1), at_c(2), at_x, at_z(1), at_z(2))
    small[...] = small_in[...]

    def small_send(i):
        rc.start(n_small[i], lambda: (small_got.at[i, 1], small_got.at[i, 0], small_to[i]))

    def small_step(i):
        rc.arrived(n_small[i], small_got.at[i, 0], small_to[i])
        small[...] += small_got[i, 0]
        if i < 4:
            small_got[i + 1, 1] = small[...]
            small_send(i + 1)

    small_got[0, 1] = small_in[...]
    wh_here = copy_here(wh_in, wh)
    xt_here = copy_here(xt_in, xt)
    out_here = [
        copy_here(out_low.at[pl.ds(0, ln)], out_lines[0].at(z)),
        copy_here(out_low.at[pl.ds(ln, hl)], out_lines[1].at(z)),
    ]

    def block(qb):
        r0, r1, o0, o1, seq = block_rows(qb, half, ln)
        b0 = jnp.where(qb < 4, qb, 2 * (qb - 4))
        b1 = jnp.where(qb < 4, qb, 2 * (qb - 4) + 1)
        s0 = pl.multiple_of(jnp.where(qb < 4, 0, hl * half), 128)
        s1 = pl.multiple_of(jnp.where(qb < 4, hl, hl * half), 128)
        sq = jnp.concatenate(
            [
                segr[2 * b0 + seq, 0:1, pl.ds(s0, hl)],
                segr[2 * b1 + seq, 0:1, pl.ds(s1, hl)],
            ],
            1,
        )
        q, do, line, delta = [], [], [], []
        for h in range(heads):
            q.append(two(q_scr, r0, r1, hl, slice(128 * h, 128 * h + 128)))
            do.append(two(d_o, o0, o1, hl, slice(128 * h, 128 * h + 128)))
            line.append(two_lanes(lse, slice(h, h + 1), o0, o1, hl))
            turned = do[h].astype(F32).T[HEAD:, :]
            kept = two_lanes(ctx_t, slice(HEAD * h, HEAD * h + HEAD), o0, o1, hl)
            delta.append(jnp.sum(turned * kept, 0, keepdims=True))
        dqt[...] = jnp.zeros_like(dqt)

        @pl.loop(0, nc)
        def _(j):
            rows = pl.ds(pl.multiple_of((2 * j + seq) * ln, ln), ln)
            keys = pl.ds(pl.multiple_of(j * ln, ln), ln)
            key_seg = segc[2 * j + seq]
            same = jnp.concatenate([key_seg, key_seg], 1) == sq
            for h in range(heads):
                kvh = kv[rows, 128 * h : 128 * h + 128]
                p = jnp.where(same, jnp.exp(dot_nt(kvh, q[h]) - line[h]), 0.0)
                ds = (p * (dot_nt(kvh, do[h]) - delta[h])).astype(BF)
                dkv[rows, 128 * h : 128 * h + 128] += dot_nn(ds, q[h]) + dot_nn(
                    p.astype(BF), do[h]
                )
                dqt[h] += dot_nn(kvt[seq * heads + h, :, keys], ds)

        turned = jnp.concatenate([dqt[h, :HEAD, :] for h in range(heads)], 0).T * 0.125
        bias_sum[0:1, wide:] += jnp.sum(turned, 0, keepdims=True)
        low = turned.astype(BF)
        d_proj[pl.ds(r0, hl), wide:] = low[:hl]
        d_proj[pl.ds(r1, hl), wide:] = low[hl:]

    n_tc = [[next(number), next(number)] for _ in range(2)]
    n_ty = [[next(number), next(number)] for _ in range(2)]
    n_tz = next(number)

    def rows_of(cb, s):
        rows = pl.ds(pl.multiple_of((2 * cb + s) * ln, ln), ln)
        got = dkv[rows, :]
        bias_sum[0:1, :wide] += jnp.sum(got, 0, keepdims=True)
        d_proj[rows, :wide] = got.astype(BF)
        part[cb, s] = dot_nt(d_proj[rows, :], wh[...]).astype(BF)

    def t_partial(s):
        rows_of(c ^ 3, s)
        rc.start(n_tc[s][0], lambda: (part.at[c ^ 3, s], got_c.at[s, 0], at_c(1)))
        rows_of(c ^ 1, s)
        rc.start(n_tc[s][1], lambda: (part.at[c ^ 1, s], got_c.at[s, 1], at_c(1)))
        rows_of(c ^ 2, s)
        rows_of(c, s)

    def t_core(s):
        rc.arrived(n_tc[s][0], got_c.at[s, 0], at_c(1))
        for k in range(2):
            at = slice(k * hl, k * hl + hl)
            send_y[s, at] = (part[c ^ 2, s, at].astype(F32) + got_c[s, 0, at].astype(F32)).astype(BF)
            rc.start(
                n_ty[s][k],
                lambda k=k: (
                    send_y.at[s, pl.ds(k * hl, hl)],
                    got_y.at[s, pl.ds(k * hl, hl)],
                    at_c(2),
                ),
            )
        rc.arrived(n_tc[s][1], got_c.at[s, 1], at_c(1))
        mine[s] = part[c, s].astype(F32) + got_c[s, 1].astype(F32)

    def t_shared():
        for k in range(2):
            rc.arrived(n_ty[1][k], got_y.at[1, pl.ds(k * hl, hl)], at_c(2))
        mine[1] += got_y[1].astype(F32)
        send_z[...] = mine[1, pl.ds(pl.multiple_of((1 - half) * hl, 128), hl)].astype(BF)
        rc.start(n_tz, lambda: (send_z, got_z, at_z(1)))

    def t_shared_end():
        rc.arrived(n_tz, got_z, at_z(1))
        mine_half = mine[1, pl.ds(pl.multiple_of(half * hl, 128), hl)]
        done[ln:, :] = (mine_half + got_z[...].astype(F32) + d_first[ln:, :]).astype(BF)
        tok_lines[2].begin(done.at[pl.ds(ln, hl)])

    def t_whole(k):
        at = slice(k * hl, k * hl + hl)
        rc.arrived(n_ty[0][k], got_y.at[0, pl.ds(k * hl, hl)], at_c(2))
        done[at, :] = (mine[0, at] + got_y[0, at].astype(F32) + d_first[at, :]).astype(BF)
        tok_lines[k].begin(done.at[pl.ds(k * hl, hl)])

    n_h = [next(number) for _ in range(8)]

    def h_partial(seq):
        @pl.loop(0, nc)
        def _(i):
            rows = pl.ds(pl.multiple_of((2 * i + seq) * ln, ln), ln)
            acc_h[...] += dot_nn(xt[:, rows], d_proj[rows, :])

    def h_send():
        o_h[...] = acc_h[...].astype(BF)
        rows_x = lambda x_: pl.ds(pl.multiple_of(x_ * 4 * wr, wr), 4 * wr)
        rc.start(n_h[0], lambda: (o_h.at[rows_x(1 - d)], x_h, at_x))

    h_at = lambda t: o_h.at[pl.ds(pl.multiple_of((4 * d + t) * wr, wr), wr)]

    def h_plane():
        rc.arrived(n_h[0], x_h, at_x)
        add_into([o_h.at[pl.ds(pl.multiple_of(d * 4 * wr, wr), 4 * wr)]], [x_h], 4 * wr)
        rc.start(n_h[1], lambda: (h_at(z ^ 3), z_h.at[1], at_z(1)))
        rc.start(n_h[2], lambda: (h_at(z ^ 1), z_h.at[0], at_z(1)))

    def h_line():
        rc.arrived(n_h[1], z_h.at[1], at_z(1))
        add_into([h_at(z ^ 2)], [z_h.at[1]], wr)
        rc.start(n_h[3], lambda: (h_at(z ^ 2), z_h.at[2], at_z(2)))
        rc.arrived(n_h[2], z_h.at[0], at_z(1))
        add_into([h_at(z)], [z_h.at[0]], wr)

    def h_end():
        rc.arrived(n_h[3], z_h.at[2], at_z(2))
        send_h[...] = h_at(z)[...].astype(F32) + z_h[2].astype(F32)
        rc.start(n_h[4], lambda: (send_h, h_got, across), lambda: c != z)

        @pl.when(c == z)
        def _():
            h_got[...] = send_h[...]

    n_bias = [next(number) for _ in range(4)]
    bias_to = (at_x, at_z(1), at_z(2))

    def bias_send(i):
        bias_got[i, 1] = bias_sum[...]
        rc.start(n_bias[i], lambda: (bias_got.at[i, 1], bias_got.at[i, 0], bias_to[i]))

    def bias_step(i):
        rc.arrived(n_bias[i], bias_got.at[i, 0], bias_to[i])
        bias_sum[...] += bias_got[i, 0]
        if i < 2:
            bias_send(i + 1)
            return
        rc.start(n_bias[3], lambda: (bias_sum, bias_fin, across), lambda: c != z)

        @pl.when(c == z)
        def _():
            bias_fin[...] = bias_sum[...]

    for w in weights:

        @pl.when(z == 0)
        def _():
            w[4][4] = jnp.zeros_like(w[4][4])

        @pl.when(z == 3)
        def _():
            w[4][3] = jnp.zeros_like(w[4][3])

    def get_ctx():
        for k in (1, 2, 3):
            rc.arrived(n_ctx[k - 1], d_got.at[c ^ k], at_c(k))
        ctx_here.wait()

        @pl.loop(0, nc)
        def _(i):
            rows = pl.ds(pl.multiple_of(i * own, 128), own)
            for h in range(heads):
                d_o[rows, 128 * h + HEAD : 128 * h + 128] = d_got[
                    i, :, HEAD * h : HEAD * h + HEAD
                ]

        q_here.wait()
        wh_here.wait()
        xt_here.wait()

    def out_begin():
        out_lines[0].begin(out_low.at[pl.ds(0, ln)])
        out_lines[1].begin(out_low.at[pl.ds(ln, hl)])

    out_begin()
    w_core_send(weights[0])
    w_core_send(weights[2])
    for i in range(nc):
        for s in range(2):
            line = seg[i, s : s + 1, :].astype(F32)
            segr[2 * i + s, 0:1, :] = line
            segc[2 * i + s] = jnp.broadcast_to(line, (128, ln)).T
    dkv[...] = jnp.zeros_like(dkv)
    d_o[...] = jnp.zeros_like(d_o)
    d_proj[...] = jnp.zeros_like(d_proj)
    bias_sum[...] = jnp.zeros_like(bias_sum)
    acc_h[...] = jnp.zeros_like(acc_h)
    kv_here.wait()

    @pl.loop(0, nc)
    def _(j):
        for s in range(2):
            rows = pl.ds(pl.multiple_of((2 * j + s) * ln, ln), ln)
            for h in range(heads):
                kvt[s * heads + h, :, pl.ds(pl.multiple_of(j * ln, ln), ln)] = kv[
                    rows, 128 * h : 128 * h + 128
                ].T

    small_send(0)
    w_core_add(0)
    get_ctx()

    @pl.loop(0, 6)
    def _(i):
        block(jnp.where(i == 0, 0, jnp.where(i == 1, 1, jnp.where(i == 2, 2, jnp.where(i == 3, 3, jnp.where(i == 4, 4, 5))))))

        @pl.when(i == 0)
        def _():
            w_core_send(weights[1])
            small_step(0)
            w_core_add(2)
            out_lines[0].step(1)
            out_lines[1].step(1)

        @pl.when(i == 3)
        def _():
            t_partial(0)
            out_lines[0].step(2)
            out_lines[1].step(2)
            t_core(0)
            w_plane(2)

    t_whole(0)
    h_partial(0)
    t_whole(1)
    w_plane(0)
    t_partial(1)
    w_corner(2)
    t_core(1)
    small_step(1)
    bias_send(0)
    w_core_add(1)
    tok_lines[0].step(1)
    w_corner(0)
    w_line(2)
    small_step(2)
    bias_step(0)
    tok_lines[1].step(1)
    h_partial(1)
    out_lines[0].step(3)
    out_lines[1].step(3)
    tok_lines[0].step(2)
    t_shared()
    bias_step(1)
    h_send()
    t_shared_end()
    tok_lines[1].step(2)
    w_plane(1)
    tok_lines[0].step(3)
    w_line(0)
    h_plane()
    tok_lines[2].step(1)
    w_next(0)
    bias_step(2)
    h_line()
    small_step(3)
    w_next(2)
    w_corner(1)
    w_end(2)
    w_end(0)
    h_end()
    tok_lines[2].step(2)
    w_line(1)
    w_next(1)
    tok_lines[1].step(3)
    tok_lines[2].step(3)
    small_step(4)
    w_end(1)
    tok_here = [
        copy_here(done.at[pl.ds(0, hl)], tok_lines[0].at(z)),
        copy_here(done.at[pl.ds(hl, hl)], tok_lines[1].at(z)),
        copy_here(done.at[pl.ds(ln, hl)], tok_lines[2].at(z)),
    ]

    @pl.when(c != z)
    def _():
        rc.arrived(n_h[4], h_got, across)
        rc.arrived(n_bias[3], bias_fin, across)

    gf_h[...] = h_got[...]
    bias[...] = bias_fin[...]

    for copy in out_here + tok_here:
        copy.wait()
    rc.all_sent()


def backward(d_ctx, g_b, g_i, g_o, out_low, d_first, small, q, kv, xt, wh, lse, ctx_t, seg, heads, seqs):
    nc, own, group = d_ctx.shape
    ln = own * 2 // 3
    hl = ln // 2
    width = out_low.shape[1]
    wr, all_units = g_b.shape[2:]
    units = all_units // 4
    hb = pl.BlockSpec(memory_space=pltpu.HBM)
    vm = pl.BlockSpec(memory_space=pltpu.VMEM)
    sds = jax.ShapeDtypeStruct
    v = pltpu.VMEM
    rows = nc * own
    n2 = 2 * nc * ln
    return pl.pallas_call(
        functools.partial(backward_kernel, heads, ln),
        out_shape=(
            sds((seqs, ln, width), BF),
            sds((seqs, ln, width), BF),
            sds((wr, units), F32),
            sds((wr, units), F32),
            sds((wr, group), F32),
            sds((wr, 3 * group), F32),
            sds(small.shape, F32),
            sds((8, 3 * group), F32),
        ),
        in_specs=[hb] * 4 + [vm] * 3 + [hb] * 4 + [vm] * 3,
        out_specs=(hb, hb) + (vm,) * 6,
        scratch_shapes=[
            v((n2, heads * 128), BF),
            v((n2, heads * 128), BF),
            v((width, n2), BF),
            v((width, 3 * group), BF),
            v((nc, own, group), BF),
            v((rows, heads * 128), BF),
            v((2 * heads, 128, nc * ln), BF),
            v((n2, heads * 128), F32),
            v((heads, 128, ln), F32),
            v((n2, 3 * group), BF),
            v((2 * nc, ln, 128), F32),
            v((2 * nc, 8, ln), F32),
            v((nc, 2, ln, width), BF),
            v((2, 2, ln, width), BF),
            v((2, ln, width), BF),
            v((hl, width), BF),
            v((2, ln, width), BF),
            v((hl, width), BF),
            v((2, ln, width), F32),
            v((own, width), BF),
            v((4, wr, all_units), BF),
            v((4, wr, all_units), BF),
            v((4, 4, wr, group), BF),
            v((4, wr, all_units), BF),
            v((4, wr, all_units), BF),
            v((4, 4, wr, group), BF),
            v((3, wr, 2 * units), BF),
            v((3, wr, 2 * units), BF),
            v((3, 2, wr, group), BF),
            v((3, wr, 2 * units), BF),
            v((3, wr, 2 * units), BF),
            v((3, 2, wr, group), BF),
            v((5, wr, units), BF),
            v((5, wr, units), BF),
            v((5, wr, group), BF),
            v((width, 3 * group), F32),
            v((width, 3 * group), BF),
            v((4 * wr, 3 * group), BF),
            v((3, wr, 3 * group), BF),
            v((wr, 3 * group), F32),
            v((5, 2) + small.shape, F32),
            v((8, 3 * group), F32),
            v((3, 2, 8, 3 * group), F32),
            v((wr, 3 * group), F32),
            v((8, 3 * group), F32),
            pltpu.SemaphoreType.DMA((130,)),
            pltpu.SemaphoreType.DMA((130,)),
            pltpu.SemaphoreType.DMA((40,)),
        ],
        compiler_params=pltpu.CompilerParams(
            vmem_limit_bytes=60 << 20, collective_id=1, has_side_effects=True
        ),
        name="backward",
    )(d_ctx, g_b, g_i, g_o, out_low, d_first, small, q, kv, xt, wh, lse, ctx_t, seg)


def finish_kernel(
    heads, tok_in, out_in, g_b, g_i, g_o, g_h, small, bias,
    tok, out, gb, gi, go, gh, gq, gv, w0, w1, w2, in_b, w3, w4, w5,
):
    tok[...] = tok_in[...].astype(F32)
    out[...] = out_in[...]
    z = lax.axis_index("tp")
    wide = heads * 128

    @pl.when(pl.program_id(0) == 0)
    def _():
        gb[...] = g_b[...]
        gi[...] = g_i[...]
        go[...] = g_o[...]
        pick = lambda ref, rows, at: jnp.concatenate(
            [ref[rows, 128 * h + at : 128 * h + at + HEAD] for h in range(heads)], -1
        )
        gh[:, 0, :] = g_h[:, wide:]
        gh[:, 1, :] = pick(g_h, slice(None), 0)
        gh[:, 2, :] = pick(g_h, slice(None), HEAD)
        gq[...] = bias[0, wide:]
        gv[...] = pick(bias, 0, HEAD)
        for i, ref in ((0, w0), (1, w1), (2, w2), (3, w3), (4, w4), (5, w5)):
            ref[...] = small[i, :]
        in_b[...] = small[pl.ds(6 + z, 1), :].reshape(in_b.shape)


def finish(d_tokens, output, g_b, g_i, g_o, g_h, small, d_bias, heads):
    seqs, ln, width = d_tokens.shape
    wr, units = g_b.shape
    group = g_o.shape[1]
    one = lambda: pl.BlockSpec((1, ln, width), lambda i: (i, 0, 0))
    whole = lambda shape: pl.BlockSpec(shape, lambda i: (0,) * len(shape))
    sds = jax.ShapeDtypeStruct
    rest = [
        (wr, units), (wr, units), (wr, group), (wr, 3, group), (group,), (group,),
        (width,), (width,), (width,), (units,), (width,), (width,), (width,),
    ]
    return pl.pallas_call(
        functools.partial(finish_kernel, heads),
        grid=(seqs,),
        out_shape=[sds(d_tokens.shape, F32), sds(output.shape, BF)] + [sds(s, F32) for s in rest],
        in_specs=[one(), one()]
        + [whole(a.shape) for a in (g_b, g_i, g_o, g_h, small, d_bias)],
        out_specs=[one(), one()] + [whole(s) for s in rest],
        compiler_params=pltpu.CompilerParams(vmem_limit_bytes=60 << 20),
        name="finish",
    )(d_tokens, output, g_b, g_i, g_o, g_h, small, d_bias)


def head_order(kinds, heads):
    lead = kinds[0].shape[:-1]
    q, k, v = (a.reshape(lead + (heads, HEAD)) for a in kinds)
    kv = jnp.concatenate([k, v], -1).reshape(lead + (heads * 2 * HEAD,))
    return jnp.concatenate([kv, q.reshape(lead + (heads * HEAD,))], -1)


def forward_plain(sizes, me, tok2, seg2, w_head, b_head, b_unit, w_o, w_i, w_b, heads):
    nd, nc, nt = sizes
    d, c, z = me
    ln, width = tok2.shape[1:]
    hl = ln // 2
    half = z % 2
    group = w_o.shape[1]
    seg_all = gather_axis(seg2, "ctx", nc, c)
    x2 = gather_axis(tok2, "ctx", nc, c).reshape(2 * nc, ln, width)
    wh = gather_heads(w_head, sizes, me)
    bh = transpose_ctx_tp(b_head, nc)[0]
    b_all = gather_axis(b_unit, "tp", nt, z)
    gather = lambda w: lax.all_gather(
        lax.all_gather(w, "tp", axis=1, tiled=True), ("dp", "ctx"), axis=0, tiled=True
    )
    o_full = jnp.transpose(gather(w_o).reshape(width, nt, group), (1, 0, 2))
    proj = (jnp.dot(x2.reshape(-1, width), wh, preferred_element_type=F32) + bh).astype(BF)
    kv = proj[:, : 2 * group]
    q = (proj[:, 2 * group :].astype(F32) * 0.125).astype(BF).reshape(-1, heads, HEAD)
    q = jnp.concatenate([q, jnp.zeros_like(q)], -1).reshape(-1, heads * 128)
    info, seg_col, seg_row = key_blocks(seg_all, half, ln, nc)
    context, lse, ctx_t = attend(info, q, kv, seg_col, seg_row, heads, ln, nc)
    ctx_all = in_order(exchange_axis(context.reshape(nc, ln + hl, group), "ctx", nc, c), c)
    return (
        ctx_all,
        x2.reshape(-1, width).T,
        q,
        kv,
        wh,
        o_full,
        jnp.stack([gather(w_i), gather(w_b)]),
        b_all,
        lse,
        ctx_t,
        seg_all,
    )


def key_blocks(seg_all, half, ln, nc):
    hl = ln // 2
    seg2 = seg_all[:, :2]
    flat = jnp.transpose(seg2, (1, 0, 2)).reshape(2, nc * ln)
    first = jnp.concatenate([seg2[:, 0, 0], jnp.take(seg2[0::2, 1], half * hl, axis=1)])
    last = jnp.concatenate([seg2[:, 0, -1], jnp.take(seg2[1::2, 1], half * hl + hl - 1, axis=1)])
    of = jnp.concatenate(
        [
            jnp.broadcast_to(flat[:1], (nc, nc * ln)),
            jnp.broadcast_to(flat[1:], (nc // 2, nc * ln)),
        ],
        0,
    )
    lo = jnp.sum(of < first[:, None], 1) // ln
    hi = (jnp.sum(of <= last[:, None], 1) + ln - 1) // ln
    info = jnp.concatenate([lo, hi, half[None]]).astype(jnp.int32)
    seg_flat = seg2.reshape(2 * nc * ln)
    return info, seg_flat[:, None], seg_flat[None, :]


def backward_plain(
    sizes, me, d_ctx, low, out_low, d_first, small, q, kv, xt, wh, lse, ctx_t, seg_all, heads, seqs
):
    nd, nc, nt = sizes
    d, c, z = me
    own, group = d_ctx.shape[1:]
    ln = own * 2 // 3
    hl = ln // 2
    half = z % 2
    width = out_low.shape[1]
    units = low[0].shape[1] // nt
    nr = nd * nc
    wr = width // nr
    info, seg_col, seg_row = key_blocks(seg_all, half, ln, nc)

    def spread_rows(rows_low, dtype):
        out = jnp.zeros((seqs, ln, width), dtype)
        parts = [rows_low] + [swap_with(rows_low, "tp", nt, k) for k in range(1, nt)]
        for k, part in enumerate(parts):
            t = z ^ k
            part = part.astype(dtype)
            out = lax.dynamic_update_slice(out, part[None, :ln], ((3 * t + 1) // 2, 0, 0))
            out = lax.dynamic_update_slice(
                out, part[None, ln:], (1 + 3 * (t // 2), (t % 2) * hl, 0)
            )
        return out

    by_unit = lambda g: jnp.transpose(g.reshape(nr, wr, nt, units), (2, 0, 1, 3))
    g_back = scatter_weight(by_unit(low[0]), sizes, me)
    g_in = scatter_weight(by_unit(low[1]), sizes, me)
    g_out = scatter_weight(low[2].reshape(nt, nr, wr, group), sizes, me)
    output = spread_rows(out_low, BF)
    small = lax.psum(small, ALL)
    d_ctx = in_order(exchange_axis(d_ctx, "ctx", nc, c), c).reshape(nc * own, heads, HEAD)
    d_ctx = jnp.concatenate([jnp.zeros_like(d_ctx), d_ctx], -1).reshape(nc * own, heads * 128)
    d_q, d_kv, d_bias = attend_back(
        info, q, kv, d_ctx, seg_col, seg_row, lse, ctx_t, heads, ln, nc
    )
    d_proj = jnp.concatenate([d_kv, d_q], -1)
    part = jnp.einsum("tf,df->td", d_proj, wh, preferred_element_type=F32)
    part = lax.psum_scatter(
        part.reshape(nc, 2 * ln, width), "ctx", scatter_dimension=0, tiled=False
    ).reshape(2, ln, width)
    shared = part[1].reshape(2, hl, width)
    shared = lax.dynamic_index_in_dim(shared, half, 0, keepdims=False) + swap_with(
        lax.dynamic_index_in_dim(shared, 1 - half, 0, keepdims=False), "tp", nt, 1
    )
    d_own = (jnp.concatenate([part[0], shared], 0) + d_first).astype(BF)
    d_tokens = spread_rows(d_own, BF)
    g_h = scatter_heads(jnp.dot(xt, d_proj, preferred_element_type=F32).astype(BF), sizes, me)
    slots = jnp.zeros((nc,) + d_bias[0].shape, F32)
    slots = lax.psum(lax.dynamic_update_index_in_dim(slots, d_bias[0], c, 0), ALL)
    d_bias = lax.dynamic_index_in_dim(slots, z, 0, keepdims=False)
    d_bias = jnp.broadcast_to(d_bias[None], (8,) + d_bias.shape)
    return output, d_tokens, g_back, g_in, g_out, g_h, small, d_bias


def per_device(
    sizes,
    tokens,
    segments,
    w_qkv,
    q_bias,
    v_bias,
    w_out,
    out_bias,
    gain_one,
    shift_one,
    w_in,
    in_bias,
    w_back,
    back_bias,
    gain_two,
    shift_two,
    cotangent,
):
    nd, nc, nt = sizes
    seqs, ln, width = tokens.shape
    group = w_out.shape[1]
    heads = group // HEAD
    units = w_in.shape[1]
    wr = w_in.shape[0]
    d, c, z = (lax.axis_index(n) for n in ALL)
    me = (d, c, z)
    whole_of = lambda t: (3 * t + 1) // 2
    shared_of = lambda t: 1 + 3 * (t // 2)
    half_of = lambda t: t % 2
    sf, sh, half = whole_of(z), shared_of(z), half_of(z)

    def own_pair(a):
        return jnp.stack(
            [
                lax.dynamic_index_in_dim(a, sf, 0, keepdims=False),
                lax.dynamic_index_in_dim(a, sh, 0, keepdims=False),
            ],
            0,
        )

    w_kinds = jnp.transpose(w_qkv, (1, 0, 2))
    biases = (q_bias, v_bias, in_bias)
    weights = (w_out, w_in, w_back)
    if sizes == (2, 4, 4):
        got = forward(tokens, segments, w_kinds, *biases, *weights, heads)
    else:
        tok2 = own_pair(tokens)
        seg2 = jnp.concatenate([own_pair(segments), jnp.zeros((6, ln), jnp.int32)], 0)
        w_head = head_order(w_kinds, heads)
        b_head = head_order([q_bias, jnp.zeros_like(q_bias), v_bias], heads)
        b_head = jnp.broadcast_to(b_head[None], (8, 3 * group))
        b_unit = jnp.broadcast_to(in_bias[None], (8, units))
        got = forward_plain(sizes, me, tok2, seg2, w_head, b_head, b_unit, *weights, heads)
    ctx_all, xt, q, kv, wh, w_o, w_ib, b_in, lse, ctx_t, seg_all = got
    w_o = w_o.reshape(nt, width, group)
    w_ib = w_ib.reshape(2, width, nt * units)
    vectors = (out_bias, gain_one, shift_one, back_bias, gain_two, shift_two)
    d_ctx, g_b, g_i, g_o, out_low, d_first, small = middle(
        tokens, cotangent, ctx_all, w_o, w_ib, b_in, vectors
    )
    low = (g_b, g_i, g_o)
    if sizes == (2, 4, 4):
        output, d_tokens, g_back, g_in, g_out, g_h, small, d_bias = backward(
            d_ctx,
            low[0].reshape(4, 2, wr, nt * units),
            low[1].reshape(4, 2, wr, nt * units),
            low[2].reshape(nt, 4, 2, wr, group),
            out_low,
            d_first,
            small,
            q,
            kv,
            xt,
            wh,
            lse,
            ctx_t,
            seg_all,
            heads,
            seqs,
        )
    else:
        output, d_tokens, g_back, g_in, g_out, g_h, small, d_bias = backward_plain(
            sizes, me, d_ctx, low, out_low, d_first, small, q, kv, xt, wh, lse, ctx_t, seg_all, heads, seqs
        )
    d_tokens, output, g_b, g_i, g_o, g_h, d_qb, d_vb, w0, w1, w2, d_in, w3, w4, w5 = finish(
        d_tokens, output, g_back, g_in, g_out, g_h, small, d_bias, heads
    )
    return (output, d_tokens, g_h, d_qb, d_vb, g_o, w0, w1, w2, g_i, d_in, g_b, w3, w4, w5)


def solution(mesh):
    sizes = tuple(mesh.shape[n] for n in ALL)
    rows = P(("dp", "ctx"), "tp")
    return jax.shard_map(
        functools.partial(per_device, sizes),
        mesh=mesh,
        in_specs=(
            P("dp", "ctx", None),
            P("dp", "ctx"),
            P(("dp", "ctx"), None, "tp"),
            P("tp"),
            P("tp"),
            rows,
            P(),
            P(),
            P(),
            rows,
            P("tp"),
            rows,
            P(),
            P(),
            P(),
            P("dp", "ctx", None),
        ),
        out_specs=(
            P("dp", "ctx", None),
            P("dp", "ctx", None),
            P(("dp", "ctx"), None, "tp"),
            P("tp"),
            P("tp"),
            rows,
            P(),
            P(),
            P(),
            rows,
            P("tp"),
            rows,
            P(),
            P(),
            P(),
        ),
        check_vma=False,
    )
```

```python
import functools
import math

import jax
import jax.numpy as jnp
from jax import lax
from jax.experimental import pallas as pl
from jax.experimental.pallas import tpu as pltpu
from jax.sharding import PartitionSpec as P

HEAD = 64
NEG = -1e30
BF = jnp.bfloat16
F32 = jnp.float32
ALL = ("dp", "ctx", "tp")


def norm_parts(value):
    mean = jnp.mean(value, -1, keepdims=True)
    centered = value - mean
    rstd = lax.rsqrt(jnp.mean(centered * centered, -1, keepdims=True) + 1e-12)
    return (centered * rstd, rstd)


def norm_back(grad, normal, rstd, gain):
    d_gain = jnp.sum(grad * normal, 0)
    d_shift = jnp.sum(grad, 0)
    scaled = grad * gain
    d_value = rstd * (
        scaled
        - jnp.mean(scaled, -1, keepdims=True)
        - normal * jnp.mean(scaled * normal, -1, keepdims=True)
    )
    return (d_value, d_gain, d_shift)


def gelu_slope(inner):
    return 0.5 * (1.0 + lax.erf(inner / math.sqrt(2.0))) + inner * jnp.exp(
        -0.5 * inner * inner
    ) / math.sqrt(2.0 * math.pi)


def swap_with(value, axis, size, mask):
    return lax.ppermute(value, axis, [(i, i ^ mask) for i in range(size)])


def in_order(parts, me, axis=0):
    shape = list(parts[0].shape)
    shape.insert(axis, len(parts))
    out = jnp.zeros(tuple(shape), parts[0].dtype)
    for k, part in enumerate(parts):
        out = lax.dynamic_update_index_in_dim(out, part, me ^ k, axis)
    return out


def gather_axis(value, axis, size, me):
    parts = [value] + [swap_with(value, axis, size, k) for k in range(1, size)]
    return in_order(parts, me)


def exchange_axis(blocks, axis, size, me):
    parts = [lax.dynamic_index_in_dim(blocks, me, 0, keepdims=False)]
    for k in range(1, size):
        parts.append(
            swap_with(lax.dynamic_index_in_dim(blocks, me ^ k, 0, keepdims=False), axis, size, k)
        )
    return parts


def scatter_weight(grad, sizes, me):
    nd, nc, nt = sizes
    part = lax.psum_scatter(
        grad.astype(F32), ("dp", "ctx"), scatter_dimension=1, tiled=False
    ).astype(BF)
    parts = exchange_axis(part, "tp", nt, me[2])
    return sum(p.astype(F32) for p in parts)


def transpose_ctx_tp(value, n):
    pairs = [(a * n + b, b * n + a) for a in range(n) for b in range(n)]
    return lax.ppermute(value, ("ctx", "tp"), pairs)


def gather_heads(shard, sizes, me):
    mine = transpose_ctx_tp(shard, sizes[1])
    return lax.all_gather(mine, ("dp", "tp"), axis=0, tiled=True)


def scatter_heads(grad, sizes, me):
    nd, nc, nt = sizes
    blocks = grad.reshape((nd * nt, grad.shape[0] // (nd * nt)) + grad.shape[1:])
    total = lax.psum_scatter(
        blocks.astype(F32), ("dp", "tp"), scatter_dimension=0, tiled=False
    )
    return transpose_ctx_tp(total, nc)


def block_rows(qb, half, ln):
    hl = ln // 2
    whole = qb < 4
    b = jnp.where(whole, qb, qb - 4)
    r0 = jnp.where(whole, 2 * ln * b, (4 * b + 1) * ln + hl * half)
    r1 = jnp.where(whole, r0 + hl, r0 + 2 * ln)
    o0 = jnp.where(whole, 3 * hl * b, 6 * hl * b + ln)
    o1 = jnp.where(whole, o0 + hl, o0 + 3 * hl)
    seq = jnp.where(whole, 0, 1)
    m = lambda v: pl.multiple_of(v, 128)
    return m(r0), m(r1), m(o0), m(o1), seq


def two(ref, r0, r1, hl, cols):
    return jnp.concatenate([ref[pl.ds(r0, hl), cols], ref[pl.ds(r1, hl), cols]], 0)


def two_lanes(ref, rows, r0, r1, hl):
    return jnp.concatenate([ref[rows, pl.ds(r0, hl)], ref[rows, pl.ds(r1, hl)]], 1)


def dot_nt(a, b):
    return lax.dot_general(a, b, (((1,), (1,)), ((), ())), preferred_element_type=F32)


def dot_nn(a, b):
    return lax.dot_general(a, b, (((1,), (0,)), ((), ())), preferred_element_type=F32)


def fill_transposed(kv, kvt, ln, nc, heads):
    @pl.loop(0, nc)
    def _(j):
        for seq in range(2):
            rows = pl.ds(pl.multiple_of((2 * j + seq) * ln, ln), ln)
            for h in range(heads):
                kvt[seq * heads + h, :, pl.ds(pl.multiple_of(j * ln, ln), ln)] = kv[
                    rows, 128 * h : 128 * h + 128
                ].T


def attend_kernel(heads, ln, nc, info, q_ref, kv, seg_col, seg_row, out, lse, ctx_t, s_scr, kvt, acc):
    half = info[12]
    hl = ln // 2
    fill_transposed(kv, kvt, ln, nc, heads)

    @pl.loop(0, 6)
    def _(qb):
        r0, r1, o0, o1, seq = block_rows(qb, half, ln)
        lo, hi = info[qb], info[6 + qb]
        sq = two_lanes(seg_row, slice(0, 1), r0, r1, hl)
        q = [two(q_ref, r0, r1, hl, slice(128 * h, 128 * h + 128)) for h in range(heads)]

        def score(j, peaks):
            rows = pl.ds(pl.multiple_of((2 * j + seq) * ln, ln), ln)
            same = seg_col[rows, :] == sq
            new = []
            for h in range(heads):
                s = dot_nt(kv[rows, 128 * h : 128 * h + 128], q[h])
                s = jnp.where(same, s, NEG)
                s_scr[h, pl.ds(pl.multiple_of(j * ln, ln), ln), :] = s
                new.append(jnp.maximum(peaks[h], jnp.max(s, 0, keepdims=True)))
            return tuple(new)

        peaks = lax.fori_loop(
            lo, hi, score, tuple(jnp.full((1, ln), NEG, F32) for _ in range(heads))
        )
        acc[...] = jnp.zeros_like(acc)

        def collect(j, sums):
            keys = pl.ds(pl.multiple_of(j * ln, ln), ln)
            new = []
            for h in range(heads):
                p = jnp.exp(s_scr[h, keys, :] - peaks[h])
                new.append(sums[h] + jnp.sum(p, 0, keepdims=True))
                acc[h] += dot_nn(kvt[seq * heads + h, :, keys], p.astype(BF))
            return tuple(new)

        sums = lax.fori_loop(
            lo, hi, collect, tuple(jnp.zeros((1, ln), F32) for _ in range(heads))
        )
        whole = []
        for h in range(heads):
            one = acc[h, HEAD:, :] / sums[h]
            whole.append(one)
            line = peaks[h] + jnp.log(sums[h])
            for part, at in ((0, o0), (hl, o1)):
                ctx_t[HEAD * h : HEAD * h + HEAD, pl.ds(at, hl)] = one[:, part : part + hl]
                lse[h : h + 1, pl.ds(at, hl)] = line[:, part : part + hl]
        turned = jnp.concatenate(whole, 0).T.astype(BF)
        out[pl.ds(o0, hl), :] = turned[:hl]
        out[pl.ds(o1, hl), :] = turned[hl:]


def attend(info, q_ref, kv, seg_col, seg_row, heads, ln, nc):
    rows = 3 * ln // 2 * nc
    vm = pl.BlockSpec(memory_space=pltpu.VMEM)
    return pl.pallas_call(
        functools.partial(attend_kernel, heads, ln, nc),
        out_shape=(
            jax.ShapeDtypeStruct((rows, heads * HEAD), BF),
            jax.ShapeDtypeStruct((8, rows), F32),
            jax.ShapeDtypeStruct((heads * HEAD, rows), F32),
        ),
        in_specs=[pl.BlockSpec(memory_space=pltpu.SMEM), vm, vm, vm, vm],
        out_specs=(vm, vm, vm),
        scratch_shapes=[
            pltpu.VMEM((heads, nc * ln, ln), F32),
            pltpu.VMEM((2 * heads, 128, nc * ln), BF),
            pltpu.VMEM((heads, 128, ln), F32),
        ],
        compiler_params=pltpu.CompilerParams(vmem_limit_bytes=32 << 20),
        cost_estimate=pl.CostEstimate(
            flops=8 * heads * rows * nc * ln * 128,
            bytes_accessed=8 << 20,
            transcendentals=heads * rows * nc * ln,
        ),
        name="attend",
    )(info, q_ref, kv, seg_col, seg_row)


def attend_back_kernel(
    heads, ln, nc, info, q_ref, kv, d_out, seg_col, seg_row, lse, ctx_t, d_q, d_kv, d_bias, dkv, kvt, dqt
):
    half = info[12]
    hl = ln // 2
    fill_transposed(kv, kvt, ln, nc, heads)
    dkv[...] = jnp.zeros_like(dkv)
    d_bias[...] = jnp.zeros_like(d_bias)

    @pl.loop(0, nc)
    def _(c):
        rows = pl.ds(pl.multiple_of((2 * c + 1) * ln, ln), ln)
        d_q[rows, :] = jnp.zeros((ln, heads * HEAD), BF)

    @pl.loop(0, 6)
    def _(qb):
        r0, r1, o0, o1, seq = block_rows(qb, half, ln)
        lo, hi = info[qb], info[6 + qb]
        sq = two_lanes(seg_row, slice(0, 1), r0, r1, hl)
        q, do, line, delta = [], [], [], []
        for h in range(heads):
            q.append(two(q_ref, r0, r1, hl, slice(128 * h, 128 * h + 128)))
            do.append(two(d_out, o0, o1, hl, slice(128 * h, 128 * h + 128)))
            line.append(two_lanes(lse, slice(h, h + 1), o0, o1, hl))
            turned = do[h].astype(F32).T[HEAD:, :]
            kept = two_lanes(ctx_t, slice(HEAD * h, HEAD * h + HEAD), o0, o1, hl)
            delta.append(jnp.sum(turned * kept, 0, keepdims=True))
        dqt[...] = jnp.zeros_like(dqt)

        @pl.loop(lo, hi)
        def _(j):
            rows = pl.ds(pl.multiple_of((2 * j + seq) * ln, ln), ln)
            keys = pl.ds(pl.multiple_of(j * ln, ln), ln)
            same = seg_col[rows, :] == sq
            for h in range(heads):
                kvh = kv[rows, 128 * h : 128 * h + 128]
                p = jnp.where(same, jnp.exp(dot_nt(kvh, q[h]) - line[h]), 0.0)
                ds = (p * (dot_nt(kvh, do[h]) - delta[h])).astype(BF)
                dkv[rows, 128 * h : 128 * h + 128] += dot_nn(ds, q[h]) + dot_nn(
                    p.astype(BF), do[h]
                )
                dqt[h] += dot_nn(kvt[seq * heads + h, :, keys], ds)

        turned = jnp.concatenate([dqt[h, :HEAD, :] for h in range(heads)], 0).T * 0.125
        d_bias[0:1, heads * 128 :] += jnp.sum(turned, 0, keepdims=True)
        low = turned.astype(BF)
        d_q[pl.ds(r0, hl), :] = low[:hl]
        d_q[pl.ds(r1, hl), :] = low[hl:]

    @pl.loop(0, 2 * nc)
    def _(c):
        rows = pl.ds(pl.multiple_of(c * ln, ln), ln)
        for h in range(heads):
            got = dkv[rows, 128 * h : 128 * h + 128]
            d_bias[0:1, 128 * h : 128 * h + 128] += jnp.sum(got, 0, keepdims=True)
            d_kv[rows, 128 * h : 128 * h + 128] = got.astype(BF)


def attend_back(info, q_ref, kv, d_out, seg_col, seg_row, lse, ctx_t, heads, ln, nc):
    rows = 3 * ln // 2 * nc
    vm = pl.BlockSpec(memory_space=pltpu.VMEM)
    return pl.pallas_call(
        functools.partial(attend_back_kernel, heads, ln, nc),
        out_shape=(
            jax.ShapeDtypeStruct((2 * nc * ln, heads * HEAD), BF),
            jax.ShapeDtypeStruct((2 * nc * ln, heads * 128), BF),
            jax.ShapeDtypeStruct((8, heads * (HEAD + 128)), F32),
        ),
        in_specs=[pl.BlockSpec(memory_space=pltpu.SMEM)] + [vm] * 7,
        out_specs=(vm, vm, vm),
        scratch_shapes=[
            pltpu.VMEM((2 * nc * ln, heads * 128), F32),
            pltpu.VMEM((2 * heads, 128, nc * ln), BF),
            pltpu.VMEM((heads, 128, ln), F32),
        ],
        compiler_params=pltpu.CompilerParams(vmem_limit_bytes=40 << 20),
        cost_estimate=pl.CostEstimate(
            flops=20 * heads * rows * nc * ln * 128,
            bytes_accessed=14 << 20,
            transcendentals=heads * rows * nc * ln,
        ),
        name="attend_back",
    )(info, q_ref, kv, d_out, seg_col, seg_row, lse, ctx_t)


MESH = pl.DeviceIdType.MESH


class Copies:
    def __init__(self, send, recv):
        self.send, self.recv, self.open = send, recv, []

    def make(self, i, src, dst, device, sent=None):
        return pltpu.make_async_remote_copy(
            src_ref=src,
            dst_ref=dst,
            send_sem=self.send.at[i if sent is None else sent],
            recv_sem=self.recv.at[i],
            device_id=device,
            device_id_type=MESH,
        )

    def start(self, i, parts, when=None, sent=None):
        number = (lambda: i) if not callable(i) else i

        def go(wait):
            copy = self.make(number(), *parts(), sent=sent)
            copy.wait_send() if wait else copy.start()

        self.run(go, when, False)
        self.open.append((go, when))

    def run(self, go, when, wait):
        if when is None:
            go(wait)
        else:

            @pl.when(when())
            def _():
                go(wait)

    def arrived(self, i, dst, device):
        self.make(i, dst, dst, device).wait_recv()

    def all_sent(self):
        for go, when in self.open:
            self.run(go, when, True)


def line_order(z, i):
    if i == 0:
        return z
    if i == 1:
        return jnp.where(z == 0, 1, z - 1)
    if i == 2:
        return jnp.where(z == 0, 2, jnp.where(z == 3, 1, z + 1))
    return jnp.where(z < 2, 3, 0)


def forward_kernel(
    heads,
    ln,
    tokens,
    segments,
    w_kinds,
    q_bias,
    v_bias,
    in_bias,
    w_o,
    w_i,
    w_b,
    cotangent,
    out_bias,
    gain_one,
    shift_one,
    back_bias,
    gain_two,
    shift_two,
    xt_out,
    q_out,
    kv_out,
    wh_out,
    g_b,
    g_i,
    output,
    lse,
    ctx_t,
    seg,
    d_ctx,
    g_o,
    d_first,
    small,
    x2,
    xt,
    wh,
    bh,
    q_scr,
    kv,
    s_scr,
    kvt,
    acc,
    segc,
    segr,
    context,
    w_src,
    o_src,
    seg2,
    w_head,
    b_head,
    b_unit,
    ctx_all,
    o_full,
    w_full,
    bu_full,
    x_own,
    c_own,
    n_one,
    r_one,
    low,
    low_t,
    tmp,
    total,
    active,
    slope,
    turn,
    d_low,
    gb_v,
    gi_v,
    out_low,
    g_sem,
    send,
    recv,
    local,
):
    d, c, z = (lax.axis_index(n) for n in ALL)
    nc = 4
    hl = ln // 2
    own = ln + hl
    half = z % 2
    wr = w_i.shape[0]
    units = w_i.shape[1]
    row = d * nc + c
    row_x, row_y, row_d = row ^ 4, row ^ 2, row ^ 6
    rc = Copies(send, recv)
    at_c = lambda k: (d, c ^ k, z)
    at_x = (1 - d, c, z)
    to_c = lambda k: (lambda: at_c(k))
    to_x = lambda: at_x
    at_z = lambda k: (d, c, z ^ k)
    across = (d, z, c)
    order = [line_order(z, i) for i in range(4)]
    number = iter(range(0, 400))
    four = lambda: [next(number) for _ in range(4)][0]
    local_number = iter(range(32))

    def copy_here(src, dst):
        copy = pltpu.make_async_copy(src, dst, local.at[next(local_number)])
        copy.start()
        return copy

    t_cols = lambda t: pl.ds(pl.multiple_of(t * units, 128), units)
    w_at = lambda r, t: w_full.at[:, r, :, t_cols(t)]
    o_at = lambda r, t: o_full.at[t, r]
    wh_at = lambda r: wh.at[pl.ds(pl.multiple_of(r * wr, wr), wr)]
    tok_at = lambda i: x2.at[pl.ds(2 * i, 2)]
    w_here = [copy_here(w_i, w_src.at[0]), copy_here(w_b, w_src.at[1]), copy_here(w_o, o_src)]
    tok_src = lambda s: tokens.at[(3 * z + 1) // 2 if s == 0 else 1 + 3 * (z // 2)]
    mine = [copy_here(tok_src(s), x2.at[2 * c + s]) for s in range(2)]
    half_rows = pl.ds(pl.multiple_of(half * hl, 128), hl)
    own_rows = [
        copy_here(part, dst)
        for src, to in ((tokens, x_own), (cotangent, c_own))
        for part, dst in (
            (src.at[(3 * z + 1) // 2], to.at[pl.ds(0, ln)]),
            (src.at[1 + 3 * (z // 2), half_rows], to.at[pl.ds(ln, hl)]),
        )
    ]
    here_sem = [local.at[next(local_number)] for _ in range(2)]
    here = [
        pltpu.make_async_copy(w_head, wh_at(row), here_sem[0]),
        pltpu.make_async_copy(b_head, bh, here_sem[1]),
    ]

    barrier = pltpu.get_barrier_semaphore()
    everyone = [at_c(k) for k in (1, 2, 3)] + [at_z(k) for k in (1, 2, 3)] + [at_x]
    for device in everyone:
        pl.semaphore_signal(barrier, inc=1, device_id=device, device_id_type=MESH)

    @pl.when(c != z)
    def _():
        pl.semaphore_signal(barrier, inc=1, device_id=across, device_id_type=MESH)

    seg2[...] = jnp.zeros_like(seg2)
    seg2[0:1, :] = segments[pl.ds((3 * z + 1) // 2, 1), :]
    seg2[1:2, :] = segments[pl.ds(1 + 3 * (z // 2), 1), :]
    wide = heads * 128
    b_head[...] = jnp.zeros_like(b_head)
    b_unit[...] = jnp.zeros_like(b_unit)
    qb = q_bias[...].reshape(1, heads * HEAD)
    vb = v_bias[...].reshape(1, heads * HEAD)
    for h in range(heads):
        cols = slice(HEAD * h, HEAD * h + HEAD)
        w_head[:, 128 * h : 128 * h + HEAD] = w_kinds[1, :, cols]
        w_head[:, 128 * h + HEAD : 128 * h + 128] = w_kinds[2, :, cols]
        b_head[0:1, 128 * h + HEAD : 128 * h + 128] = vb[:, cols]
    w_head[:, wide:] = w_kinds[0]
    b_head[0:1, wide:] = qb
    b_unit[0:1, :] = in_bias[...].reshape(1, units)
    seg_here = copy_here(seg2, seg.at[c])
    bu_here = copy_here(b_unit, bu_full.at[z])

    @pl.when(c == z)
    def _():
        for copy in here:
            copy.start()

    pl.semaphore_wait(barrier, len(everyone) + jnp.where(c != z, 1, 0))

    n_tf, n_wa, n_ba = (next(number) for _ in range(3))
    n_ty, n_tc = ([next(number) for _ in range(2)] for _ in range(2))
    not_here = lambda: c != z
    rc.start(n_wa, lambda: (w_head, wh_at(row), across), not_here)
    rc.start(n_ba, lambda: (b_head, bh, across), not_here)
    n_seg = four()
    for k in (1, 2, 3):
        rc.start(n_seg + k, lambda k=k: (seg2, seg.at[c], at_c(k)))

    class Line:
        def __init__(self, at):
            self.at = at
            self.n = [next(number) for _ in range(5)][0]

        def begin(self, src):
            rc.start(
                lambda: self.n + z,
                lambda: (src, self.at(z), (d, c, z + 1)),
                lambda: z < 3,
                self.n + 3,
            )
            rc.start(
                lambda: self.n + z,
                lambda: (src, self.at(z), (d, c, z - 1)),
                lambda: z > 0,
                self.n + 4,
            )

        def step(self, i):
            t = lambda: order[i]
            rc.arrived(self.n + t(), self.at(t()), (d, c, z))
            rc.start(
                lambda: self.n + t(),
                lambda: (
                    self.at(t()),
                    self.at(t()),
                    (d, c, jnp.where(t() < z, z + 1, z - 1)),
                ),
                lambda: jnp.where(t() < z, z < 3, z > 0),
                self.n + i - 1,
            )

    n_hz = four()
    full_at = (
        lambda r, t: w_full.at[0, r, :, t_cols(t)],
        o_at,
        lambda r, t: w_full.at[1, r, :, t_cols(t)],
    )
    sources = (w_src.at[0], o_src, w_src.at[1])
    lines = [Line(lambda t, w=w: full_at[w](row, t)) for w in range(3)]
    n_hx = four()
    n_x, n_y, n_d = ([four() for _ in range(3)] for _ in range(3))
    n_c = [[four() for _ in range(3)] for _ in range(4)]

    groups = [(0, 1), (2,)]
    over_y = ((0, 1), (0, 3), (1, 1), (1, 2))

    def pass_on(n, g, i, r, device, first=False):
        t = lambda: order[i]
        for w in groups[g]:
            rc.start(
                lambda w=w: n[w] + t(),
                lambda w=w: (
                    sources[w] if first and i == 0 else full_at[w](r, t()),
                    full_at[w](r, t()),
                    device(),
                ),
                None,
                n[w] + i,
            )

    def came(n, g, i, r, device):
        t = order[i]
        for w in groups[g]:
            rc.arrived(n[w] + t, full_at[w](r, t), device)

    def own_send(g):
        pass_on(n_x, g, 0, row, to_x, True)
        pass_on(n_c[0], g, 0, row, to_c(1), True)

    def line_begin(g):
        for w in groups[g]:
            lines[w].begin(sources[w])

    def y_send(g, i):
        pass_on(n_y, g, i, row, to_c(2), True)

    def line_step(g, i):
        for w in groups[g]:
            lines[w].step(i)
        pass_on(n_x, g, i, row, to_x)
        pass_on(n_c[0], g, i, row, to_c(1))

    def from_x(g, i):
        came(n_x, g, i, row_x, at_x)
        if (g, i) in over_y:
            pass_on(n_d, g, i, row_x, to_c(2))
        pass_on(n_c[1], g, i, row_x, to_c(1))

    def from_y(g, i):
        came(n_y, g, i, row_y, at_c(2))
        if (g, i) not in over_y:
            pass_on(n_d, g, i, row_y, to_x)
        pass_on(n_c[2], g, i, row_y, to_c(1))

    def from_corner(g, i):
        came(n_d, g, i, row_d, at_x)
        pass_on(n_c[3], g, i, row_d, to_c(1))

    head_at = lambda t: wh_at(d * nc + t)
    n_bu = four()
    n_ctx = four()
    ctx_at = lambda i: context.at[pl.ds(pl.multiple_of(i * own, 128), own)]

    def head_send():
        @pl.when(c != z)
        def _():
            rc.arrived(n_wa, wh_at(d * nc + z), across)
            rc.arrived(n_ba, bh, across)

        @pl.when(c == z)
        def _():
            for copy in here:
                copy.wait()

        for k in (1, 2, 3):
            rc.start(n_hz + k, lambda k=k: (head_at(z), head_at(z), at_z(k)))
        rc.start(n_hx, lambda: (head_at(z), head_at(z), at_x))
        for k in (1, 2, 3):
            rc.start(n_bu + k, lambda k=k: (b_unit, bu_full.at[z], at_z(k)))

    def head_pass(k):
        rc.arrived(n_hz + k, head_at(z ^ k), at_z(k))
        rc.start(n_hx + k, lambda: (head_at(z ^ k), head_at(z ^ k), at_x))

    def token_pass():
        for s in range(2):
            rc.arrived(n_ty[s], x2.at[2 * (c ^ 2) + s], at_c(2))
        rc.start(n_tf, lambda: (tok_at(c ^ 2), tok_at(c ^ 2), at_c(1)))

    def context_send():
        for k in (2, 3, 1):
            rc.start(n_ctx + k, lambda k=k: (ctx_at(c ^ k), ctx_all.at[c], at_c(k)))

    def segments_done():
        for k in (1, 2, 3):
            rc.arrived(n_seg + k, seg.at[c ^ k], at_c(k))
        seg_here.wait()
        for i in range(nc):
            for s in range(2):
                line = seg[i, s : s + 1, :].astype(F32)
                segr[2 * i + s, 0:1, :] = line
                segc[2 * i + s] = jnp.broadcast_to(line, (128, ln)).T

    step, thin = 128, 64
    width = x_own.shape[1]
    w_of = lambda which, t: w_full[which, :, :, t_cols(t)].reshape(width, units)
    w_out_of = lambda g: o_full[g].reshape(width, w_o.shape[1])
    out_bias, gain_one, shift_one, back_bias, gain_two, shift_two = (
        a[...].reshape(1, width)
        for a in (out_bias, gain_one, shift_one, back_bias, gain_two, shift_two)
    )

    def chunks(body, size=step):
        @pl.loop(0, own // size)
        def _(i):
            body(pl.ds(pl.multiple_of(i * size, size), size))

    mean = lambda v: jnp.mean(v, -1, keepdims=True)
    add = lambda i, v: small.__setitem__(
        (slice(i, i + 1), slice(None)), small[i : i + 1, :] + jnp.sum(v, 0, keepdims=True)
    )
    small[...] = jnp.zeros_like(small)

    def block(qb):
        r0, r1, o0, o1, seq = block_rows(qb, half, ln)
        b0 = jnp.where(qb < 4, qb, 2 * (qb - 4))
        b1 = jnp.where(qb < 4, qb, 2 * (qb - 4) + 1)
        s0 = pl.multiple_of(jnp.where(qb < 4, 0, hl * half), 128)
        s1 = pl.multiple_of(jnp.where(qb < 4, hl, hl * half), 128)
        sq = jnp.concatenate(
            [
                segr[2 * b0 + seq, 0:1, pl.ds(s0, hl)],
                segr[2 * b1 + seq, 0:1, pl.ds(s1, hl)],
            ],
            1,
        )
        q = [two(q_scr, r0, r1, hl, slice(128 * h, 128 * h + 128)) for h in range(heads)]

        def score(j, peaks):
            rows = pl.ds(pl.multiple_of((2 * j + seq) * ln, ln), ln)
            key_seg = segc[2 * j + seq]
            same = jnp.concatenate([key_seg, key_seg], 1) == sq
            new = []
            for h in range(heads):
                s = dot_nt(kv[rows, 128 * h : 128 * h + 128], q[h])
                s = jnp.where(same, s, NEG)
                s_scr[h, pl.ds(pl.multiple_of(j * ln, ln), ln), :] = s
                new.append(jnp.maximum(peaks[h], jnp.max(s, 0, keepdims=True)))
            return tuple(new)

        peaks = lax.fori_loop(
            0, nc, score, tuple(jnp.full((1, ln), NEG, F32) for _ in range(heads))
        )
        acc[...] = jnp.zeros_like(acc)

        def collect(j, sums):
            keys = pl.ds(pl.multiple_of(j * ln, ln), ln)
            new = []
            for h in range(heads):
                p = jnp.exp(s_scr[h, keys, :] - peaks[h])
                new.append(sums[h] + jnp.sum(p, 0, keepdims=True))
                acc[h] += dot_nn(kvt[seq * heads + h, :, keys], p.astype(BF))
            return tuple(new)

        sums = lax.fori_loop(
            0, nc, collect, tuple(jnp.zeros((1, ln), F32) for _ in range(heads))
        )
        whole = []
        for h in range(heads):
            one = acc[h] / sums[h]
            whole.append(one)
            line = peaks[h] + jnp.log(sums[h])
            for part, at in ((0, o0), (hl, o1)):
                ctx_t[HEAD * h : HEAD * h + HEAD, pl.ds(at, hl)] = one[:, part : part + hl]
                lse[h : h + 1, pl.ds(at, hl)] = line[:, part : part + hl]
        turned = jnp.concatenate(whole, 0).T.astype(BF)
        context[pl.ds(o0, hl), :] = turned[:hl]
        context[pl.ds(o1, hl), :] = turned[hl:]

    for copy in w_here:
        copy.wait()
    own_here = [
        copy_here(sources[w], full_at[w](row, z)) for w in range(3)
    ]
    q_scr[...] = jnp.zeros_like(q_scr)
    line_begin(0)
    for s in range(2):
        rc.start(n_ty[s], lambda s=s: (tok_src(s), x2.at[2 * c + s], at_c(2)))
        rc.start(n_tc[s], lambda s=s: (tok_src(s), x2.at[2 * c + s], at_c(1)))
    y_send(0, 0)
    line_step(0, 1)
    line_step(0, 2)
    head_send()
    head_pass(1)
    line_begin(1)
    head_pass(3)
    y_send(1, 0)
    head_pass(2)
    segments_done()
    token_pass()
    y_send(0, 1)
    own_send(0)
    y_send(0, 2)
    line_step(0, 3)
    from_x(0, 1)
    own_send(1)
    y_send(0, 3)
    line_step(1, 1)
    y_send(1, 1)
    from_x(0, 2)
    from_y(0, 0)
    for t in range(4):
        rc.arrived(n_hx + t, wh_at((1 - d) * nc + (z ^ t)), at_x)
    for s in range(2):
        mine[s].wait()
        rc.arrived(n_tc[s], x2.at[2 * (c ^ 1) + s], at_c(1))
    rc.arrived(n_tf, tok_at(c ^ 3), at_c(1))
    wh_here = copy_here(wh, wh_out)

    @pl.loop(0, 2 * nc)
    def _(i):
        x = x2[i]
        rows = pl.ds(pl.multiple_of(i * ln, ln), ln)
        xt[:, rows] = x.T
        got = (dot_nn(x, wh[:, :wide]) + bh[0:1, :wide]).astype(BF)
        kv[rows, :] = got
        qp = ((dot_nn(x, wh[:, wide:]) + bh[0:1, wide:]).astype(BF).astype(F32) * 0.125).astype(BF)
        for h in range(heads):
            q_scr[rows, 128 * h : 128 * h + HEAD] = qp[:, HEAD * h : HEAD * h + HEAD]

    x_here = copy_here(xt, xt_out)
    q_here = copy_here(q_scr, q_out)
    kv_here = copy_here(kv, kv_out)
    line_step(1, 2)
    @pl.loop(0, nc)
    def _(j):
        for s in range(2):
            rows = pl.ds(pl.multiple_of((2 * j + s) * ln, ln), ln)
            for h in range(heads):
                kvt[s * heads + h, :, pl.ds(pl.multiple_of(j * ln, ln), ln)] = kv[
                    rows, 128 * h : 128 * h + 128
                ].T[HEAD:]

    from_x(0, 3)

    @pl.loop(0, 6)
    def _(qb):
        block(qb)

        @pl.when(qb == 0)
        def _():
            line_step(1, 3)
            y_send(1, 3)

    context_send()
    ctx_here = copy_here(ctx_at(c), ctx_all.at[c])
    y_send(1, 2)
    from_y(0, 2)
    from_x(0, 0)
    from_corner(0, 0)
    from_x(1, 1)
    from_y(0, 3)
    from_y(1, 1)
    from_y(1, 0)
    from_x(1, 3)
    from_y(0, 1)
    from_y(1, 3)
    from_corner(0, 2)
    from_corner(0, 3)
    from_corner(0, 1)
    from_x(1, 2)
    from_x(1, 0)
    for k in (1, 2, 3):
        rc.arrived(n_ctx + k, ctx_all.at[c ^ k], at_c(k))
    for n, r in zip(n_c, (row, row_x, row_y, row_d)):
        for i in range(4):
            came(n, 0, i, r ^ 1, at_c(1))
    for copy in own_here + [ctx_here, bu_here] + own_rows:
        copy.wait()
    for k in (1, 2, 3):
        rc.arrived(n_bu + k, bu_full.at[z ^ k], at_z(k))

    tmp[...] = dot_nt(ctx_all[0], w_out_of(0))
    for g in range(1, nc):
        tmp[...] += dot_nt(ctx_all[g], w_out_of(g))

    def norm_one(r):
        value = x_own[r, :].astype(F32) + (tmp[r, :] + out_bias)
        centered = value - mean(value)
        rstd = lax.rsqrt(mean(centered * centered) + 1e-12)
        normal = centered * rstd
        n_one[r, :] = normal
        r_one[r, :] = jnp.broadcast_to(rstd, (step, 128))
        got = normal * gain_one + shift_one
        low[r, :] = got.astype(BF)
        total[r, :] = got + back_bias

    chunks(norm_one)
    low_t[...] = low[...].T

    from_corner(1, 3)
    @pl.loop(0, 4)
    def _(t):
        tmp[...] = dot_nn(low[...], w_of(0, t)) + bu_full[pl.ds(t, 1), 0, :]

        def gelu(r):
            u = tmp[r, :]
            cdf = 0.5 * (1.0 + lax.erf(u * math.sqrt(0.5)))
            active[r, t_cols(t)] = (u * cdf).astype(BF)
            slope[r, t_cols(t)] = cdf + u * jnp.exp(-0.5 * u * u) * (
                1.0 / math.sqrt(2.0 * math.pi)
            )

        chunks(gelu, thin)

        @pl.when(t == 0)
        def _():
            from_corner(1, 1)
            from_y(1, 2)

        @pl.when(t == 1)
        def _():
            from_corner(1, 0)
            from_corner(1, 2)

    for n, r in zip(n_c, (row, row_x, row_y, row_d)):
        for i in range(4):
            came(n, 1, i, r ^ 1, at_c(1))

    @pl.loop(0, 4)
    def _(t):
        total[...] += dot_nt(active[:, t_cols(t)], w_of(1, t))

    def norm_two(r):
        value = total[r, :]
        centered = value - mean(value)
        rstd = lax.rsqrt(mean(centered * centered) + 1e-12)
        normal = centered * rstd
        out_low[r, :] = (normal * gain_two + shift_two).astype(BF)
        grad = c_own[r, :].astype(F32)
        add(4, grad * normal)
        add(5, grad)
        scaled = grad * gain_two
        got = rstd * (scaled - mean(scaled) - normal * mean(scaled * normal))
        add(3, got)
        d_low[r, :] = got.astype(BF)
        total[r, :] = got

    chunks(norm_two)
    whole_at = lambda t: output.at[(3 * t + 1) // 2]
    shared_at = lambda t: output.at[
        1 + 3 * (t // 2), pl.ds(pl.multiple_of((t % 2) * hl, 128), hl)
    ]
    pieces = ((whole_at, out_low.at[pl.ds(0, ln)]), (shared_at, out_low.at[pl.ds(ln, hl)]))
    n_out = four()
    out_here = [copy_here(src, at(z)) for at, src in pieces]
    for k, (at, src) in enumerate(pieces):
        rc.start(
            n_out + 2 * k,
            lambda at=at, src=src: (src, at(z), (d, c, z + 1)),
            lambda: z < 3,
        )
        rc.start(
            n_out + 2 * k + 1,
            lambda at=at, src=src: (src, at(z), (d, c, z - 1)),
            lambda: z > 0,
        )
    turn[...] = d_low[...].T

    @pl.loop(0, 4)
    def _(t):
        gb_v[:, t_cols(t)] = dot_nn(turn[...], active[:, t_cols(t)]).astype(BF)
        pltpu.make_async_copy(gb_v.at[:, t_cols(t)], g_b.at[:, t_cols(t)], g_sem.at[0, t]).start()
        tmp[...] = dot_nn(d_low[...], w_of(1, t))

        def inner_back(r):
            got = tmp[r, :] * slope[r, t_cols(t)]
            at = pl.ds(6 + t, 1)
            small[at, :] += jnp.sum(got, 0, keepdims=True)
            active[r, t_cols(t)] = got.astype(BF)

        chunks(inner_back, thin)
        gi_v[:, t_cols(t)] = dot_nn(low_t[...], active[:, t_cols(t)]).astype(BF)
        pltpu.make_async_copy(gi_v.at[:, t_cols(t)], g_i.at[:, t_cols(t)], g_sem.at[1, t]).start()
        total[...] += dot_nt(active[:, t_cols(t)], w_of(0, t))

    def norm_one_back(r):
        grad = total[r, :]
        normal = n_one[r, :]
        add(1, grad * normal)
        add(2, grad)
        scaled = grad * gain_one
        got = r_one[r, 0:1] * (scaled - mean(scaled) - normal * mean(scaled * normal))
        d_first[r, :] = got
        add(0, got)
        d_low[r, :] = got.astype(BF)

    chunks(norm_one_back)
    turn[...] = d_low[...].T
    for g in range(nc):
        d_ctx[g] = dot_nn(d_low[...], w_out_of(g)).astype(BF)
        g_o[g] = dot_nn(turn[...], ctx_all[g]).astype(BF)
    for t in range(4):
        pltpu.make_async_copy(gb_v.at[:, t_cols(t)], g_b.at[:, t_cols(t)], g_sem.at[0, t]).wait()
        pltpu.make_async_copy(gi_v.at[:, t_cols(t)], g_i.at[:, t_cols(t)], g_sem.at[1, t]).wait()
    for copy in (x_here, wh_here, q_here, kv_here):
        copy.wait()
    for copy in out_here:
        copy.wait()

    @pl.when(z > 0)
    def _():
        for k, (at, _) in enumerate(pieces):
            rc.arrived(n_out + 2 * k, at(z - 1), at_z(1))

    @pl.when(z < 3)
    def _():
        for k, (at, _) in enumerate(pieces):
            rc.arrived(n_out + 2 * k + 1, at(z + 1), at_z(1))

    rc.all_sent()


def forward(
    tokens, segments, w_kinds, q_bias, v_bias, in_bias, w_o, w_i, w_b, cotangent, vectors, heads
):
    ln, width = tokens.shape[1:]
    wr, units = w_i.shape
    group = w_o.shape[1]
    nc, nt, nr = 4, 4, 8
    own = 3 * ln // 2
    rows = own * nc
    hb = pl.BlockSpec(memory_space=pltpu.HBM)
    vm = pl.BlockSpec(memory_space=pltpu.VMEM)
    sds = jax.ShapeDtypeStruct
    return pl.pallas_call(
        functools.partial(forward_kernel, heads, ln),
        out_shape=(
            sds((width, 2 * nc * ln), BF),
            sds((2 * nc * ln, heads * 128), BF),
            sds((2 * nc * ln, heads * 128), BF),
            sds((nr * wr, 3 * group), BF),
            sds((width, nt * units), BF),
            sds((width, nt * units), BF),
            sds(tokens.shape, BF),
            sds((8, rows), F32),
            sds((group, rows), F32),
            sds((nc, 8, ln), jnp.int32),
            sds((nc, own, group), BF),
            sds((nt, width, group), BF),
            sds((own, width), F32),
            sds((16, width), F32),
        ),
        in_specs=[hb] + [vm] * 5 + [hb] * 4 + [vm] * 6,
        out_specs=(hb,) * 7 + (vm,) * 7,
        scratch_shapes=[
            pltpu.VMEM((2 * nc, ln, width), BF),
            pltpu.VMEM((width, 2 * nc * ln), BF),
            pltpu.VMEM((nr * wr, 3 * group), BF),
            pltpu.VMEM((8, 3 * group), F32),
            pltpu.VMEM((2 * nc * ln, heads * 128), BF),
            pltpu.VMEM((2 * nc * ln, heads * 128), BF),
            pltpu.VMEM((heads, nc * ln, ln), F32),
            pltpu.VMEM((2 * heads, HEAD, nc * ln), BF),
            pltpu.VMEM((heads, HEAD, ln), F32),
            pltpu.VMEM((2 * nc, ln, 128), F32),
            pltpu.VMEM((2 * nc, 8, ln), F32),
            pltpu.VMEM((rows, group), BF),
            pltpu.VMEM((2, wr, units), BF),
            pltpu.VMEM((wr, group), BF),
            pltpu.VMEM((8, ln), jnp.int32),
            pltpu.VMEM((wr, 3 * group), BF),
            pltpu.VMEM((8, 3 * group), F32),
            pltpu.VMEM((8, units), F32),
            pltpu.VMEM((nc, own, group), BF),
            pltpu.VMEM((nt, nr, wr, group), BF),
            pltpu.VMEM((2, nr, wr, nt * units), BF),
            pltpu.VMEM((nt, 8, units), F32),
            pltpu.VMEM((own, width), BF),
            pltpu.VMEM((own, width), BF),
            pltpu.VMEM((own, width), F32),
            pltpu.VMEM((own, 128), F32),
            pltpu.VMEM((own, width), BF),
            pltpu.VMEM((width, own), BF),
            pltpu.VMEM((own, width), F32),
            pltpu.VMEM((own, width), F32),
            pltpu.VMEM((own, nt * units), BF),
            pltpu.VMEM((own, nt * units), F32),
            pltpu.VMEM((width, own), BF),
            pltpu.VMEM((own, width), BF),
            pltpu.VMEM((width, nt * units), BF),
            pltpu.VMEM((width, nt * units), BF),
            pltpu.VMEM((own, width), BF),
            pltpu.SemaphoreType.DMA((2, 4)),
            pltpu.SemaphoreType.DMA((150,)),
            pltpu.SemaphoreType.DMA((150,)),
            pltpu.SemaphoreType.DMA((32,)),
        ],
        compiler_params=pltpu.CompilerParams(
            vmem_limit_bytes=60 << 20, collective_id=0, has_side_effects=True
        ),
        name="forward",
    )(tokens, segments, w_kinds, q_bias, v_bias, in_bias, w_o, w_i, w_b, cotangent, *vectors)


def middle_kernel(
    ln,
    tokens,
    cotangent,
    ctx_all,
    w_o,
    w_ib,
    b_in,
    out_bias,
    gain_one,
    shift_one,
    back_bias,
    gain_two,
    shift_two,
    d_ctx,
    g_b,
    g_i,
    g_o,
    out_low,
    d_first,
    small,
    x_own,
    c_own,
    w_v,
    ctx_v,
    w_ov,
    n_one,
    r_one,
    normed,
    low,
    low_t,
    tmp,
    acc,
    active,
    slope,
    n_two,
    d_sec,
    d_low,
    gb_v,
    gi_v,
    w_sem,
    g_sem,
    sem,
):
    z = lax.axis_index("tp")
    hl = ln // 2
    own = ln + hl
    blocks, _, group = ctx_all.shape
    width = x_own.shape[1]
    units = w_v.shape[2] // 4
    step, thin = 128, 64
    out_bias, gain_one, shift_one, back_bias, gain_two, shift_two = (
        a[...].reshape(1, width)
        for a in (out_bias, gain_one, shift_one, back_bias, gain_two, shift_two)
    )
    half_rows = pl.ds(pl.multiple_of((z % 2) * hl, 128), hl)
    first_rows = []
    for i, (src, dst) in enumerate(((tokens, x_own), (cotangent, c_own))):
        for j, (a, b) in enumerate(
            (
                (src.at[(3 * z + 1) // 2], dst.at[pl.ds(0, ln)]),
                (src.at[1 + 3 * (z // 2), half_rows], dst.at[pl.ds(ln, hl)]),
            )
        ):
            first_rows.append(pltpu.make_async_copy(a, b, sem.at[2 * i + j]))
    first_rows.append(pltpu.make_async_copy(ctx_all, ctx_v, sem.at[4]))
    first_rows.append(pltpu.make_async_copy(w_o, w_ov, sem.at[5]))
    for copy in first_rows:
        copy.start()
    t_cols = lambda t: pl.ds(pl.multiple_of(t * units, 128), units)

    def weight(which, t):
        return pltpu.make_async_copy(
            w_ib.at[which, :, t_cols(t)], w_v.at[which, :, t_cols(t)], w_sem.at[which, t]
        )

    for t in range(4):
        for which in range(2):
            weight(which, t).start()
    for copy in first_rows:
        copy.wait()

    def chunks(body, size=step):
        @pl.loop(0, own // size)
        def _(i):
            body(pl.ds(pl.multiple_of(i * size, size), size))

    mean = lambda v: jnp.mean(v, -1, keepdims=True)
    add = lambda i, v: small.__setitem__(
        (slice(i, i + 1), slice(None)), small[i : i + 1, :] + jnp.sum(v, 0, keepdims=True)
    )
    small[...] = jnp.zeros_like(small)

    tmp[...] = dot_nt(ctx_v[0], w_ov[0])
    for g in range(1, blocks):
        tmp[...] += dot_nt(ctx_v[g], w_ov[g])

    def norm_one(r):
        value = x_own[r, :].astype(F32) + (tmp[r, :] + out_bias)
        centered = value - mean(value)
        rstd = lax.rsqrt(mean(centered * centered) + 1e-12)
        normal = centered * rstd
        n_one[r, :] = normal
        r_one[r, :] = jnp.broadcast_to(rstd, (step, 128))
        got = normal * gain_one + shift_one
        normed[r, :] = got
        low[r, :] = got.astype(BF)
        acc[r, :] = got + back_bias

    chunks(norm_one)
    low_t[...] = low[...].T

    @pl.loop(0, 4)
    def _(t):
        weight(0, t).wait()
        weight(1, t).wait()
        tmp[...] = dot_nn(low[...], w_v[0, :, t_cols(t)]) + b_in[pl.ds(t, 1), 0, :]

        def gelu(r):
            u = tmp[r, :]
            cdf = 0.5 * (1.0 + lax.erf(u * math.sqrt(0.5)))
            active[r, t_cols(t)] = (u * cdf).astype(BF)
            slope[r, t_cols(t)] = cdf + u * jnp.exp(-0.5 * u * u) * (
                1.0 / math.sqrt(2.0 * math.pi)
            )

        chunks(gelu, thin)
        acc[...] += dot_nt(active[:, t_cols(t)], w_v[1, :, t_cols(t)])

    def norm_two(r):
        value = acc[r, :]
        centered = value - mean(value)
        rstd = lax.rsqrt(mean(centered * centered) + 1e-12)
        normal = centered * rstd
        out_low[r, :] = (normal * gain_two + shift_two).astype(BF)
        grad = c_own[r, :].astype(F32)
        add(4, grad * normal)
        add(5, grad)
        scaled = grad * gain_two
        got = rstd * (scaled - mean(scaled) - normal * mean(scaled * normal))
        d_sec[r, :] = got
        add(3, got)
        d_low[r, :] = got.astype(BF)
        acc[r, :] = got

    chunks(norm_two)
    n_two[...] = d_low[...].T

    @pl.loop(0, 4)
    def _(t):
        gb_v[:, t_cols(t)] = dot_nn(n_two[...], active[:, t_cols(t)]).astype(BF)
        pltpu.make_async_copy(gb_v.at[:, t_cols(t)], g_b.at[:, t_cols(t)], g_sem.at[0, t]).start()
        tmp[...] = dot_nn(d_low[...], w_v[1, :, t_cols(t)])

        def inner_back(r):
            got = tmp[r, :] * slope[r, t_cols(t)]
            at = pl.ds(6 + t, 1)
            small[at, :] += jnp.sum(got, 0, keepdims=True)
            active[r, t_cols(t)] = got.astype(BF)

        chunks(inner_back, thin)
        gi_v[:, t_cols(t)] = dot_nn(low_t[...], active[:, t_cols(t)]).astype(BF)
        pltpu.make_async_copy(gi_v.at[:, t_cols(t)], g_i.at[:, t_cols(t)], g_sem.at[1, t]).start()
        acc[...] += dot_nt(active[:, t_cols(t)], w_v[0, :, t_cols(t)])

    def norm_one_back(r):
        grad = acc[r, :]
        normal = n_one[r, :]
        add(1, grad * normal)
        add(2, grad)
        scaled = grad * gain_one
        got = r_one[r, 0:1] * (scaled - mean(scaled) - normal * mean(scaled * normal))
        d_first[r, :] = got
        add(0, got)
        d_low[r, :] = got.astype(BF)

    chunks(norm_one_back)
    n_two[...] = d_low[...].T
    for g in range(blocks):
        d_ctx[g] = dot_nn(d_low[...], w_ov[g]).astype(BF)
        g_o[g] = dot_nn(n_two[...], ctx_v[g]).astype(BF)
    for t in range(4):
        pltpu.make_async_copy(gb_v.at[:, t_cols(t)], g_b.at[:, t_cols(t)], g_sem.at[0, t]).wait()
        pltpu.make_async_copy(gi_v.at[:, t_cols(t)], g_i.at[:, t_cols(t)], g_sem.at[1, t]).wait()


def middle(tokens, cotangent, ctx_all, w_o, w_ib, b_in, vectors):
    blocks, own, group = ctx_all.shape
    ln, width = tokens.shape[1:]
    all_units = w_ib.shape[2]
    hb = pl.BlockSpec(memory_space=pltpu.HBM)
    vm = pl.BlockSpec(memory_space=pltpu.VMEM)
    sds = jax.ShapeDtypeStruct
    v = pltpu.VMEM
    return pl.pallas_call(
        functools.partial(middle_kernel, ln),
        out_shape=(
            sds((blocks, own, group), BF),
            sds((width, all_units), BF),
            sds((width, all_units), BF),
            sds((blocks, width, group), BF),
            sds((own, width), BF),
            sds((own, width), F32),
            sds((16, width), F32),
        ),
        in_specs=[hb] * 5 + [vm] * 7,
        out_specs=(vm, hb, hb, vm, vm, vm, vm),
        scratch_shapes=[
            v((own, width), BF),
            v((own, width), BF),
            v((2, width, all_units), BF),
            v((blocks, own, group), BF),
            v((blocks, width, group), BF),
            v((own, width), F32),
            v((own, 128), F32),
            v((own, width), F32),
            v((own, width), BF),
            v((width, own), BF),
            v((own, width), F32),
            v((own, width), F32),
            v((own, all_units), BF),
            v((own, all_units), F32),
            v((width, own), BF),
            v((own, width), F32),
            v((own, width), BF),
            v((width, all_units), BF),
            v((width, all_units), BF),
            pltpu.SemaphoreType.DMA((2, 4)),
            pltpu.SemaphoreType.DMA((2, 4)),
            pltpu.SemaphoreType.DMA((6,)),
        ],
        compiler_params=pltpu.CompilerParams(vmem_limit_bytes=60 << 20),
        cost_estimate=pl.CostEstimate(
            flops=2 * own * width * (6 * all_units + 3 * width),
            bytes_accessed=24 << 20,
            transcendentals=2 * own * all_units,
        ),
        name="middle",
    )(tokens, cotangent, ctx_all, w_o, w_ib, b_in, *vectors)


def add_into(dst, other, rows):
    @pl.loop(0, rows // 16)
    def _(i):
        at = pl.ds(pl.multiple_of(i * 16, 16), 16)
        for a, b in zip(dst, other):
            a[at, :] = (a[at, :].astype(F32) + b[at, :].astype(F32)).astype(a.dtype)


def backward_kernel(
    heads,
    ln,
    d_ctx,
    g_b,
    g_i,
    g_o,
    out_in,
    d_first,
    small_in,
    q_in,
    kv_in,
    xt_in,
    wh_in,
    lse,
    ctx_t,
    seg,
    output,
    d_tokens,
    gf_b,
    gf_i,
    gf_o,
    gf_h,
    small,
    bias,
    q_scr,
    kv,
    xt,
    wh,
    d_got,
    d_o,
    kvt,
    dkv,
    dqt,
    d_proj,
    segc,
    segr,
    part,
    got_c,
    got_y,
    got_z,
    send_y,
    send_z,
    mine,
    done,
    o_b,
    o_i,
    o_o,
    r_b,
    r_i,
    r_o,
    x_b,
    x_i,
    x_o,
    y_b,
    y_i,
    y_o,
    z_b,
    z_i,
    z_o,
    acc_h,
    o_h,
    x_h,
    z_h,
    send_h,
    small_got,
    bias_sum,
    bias_got,
    h_got,
    bias_fin,
    send,
    recv,
    local,
):
    d, c, z = (lax.axis_index(n) for n in ALL)
    nc = 4
    hl = ln // 2
    own = ln + hl
    half = z % 2
    core, y = c % 2, c // 2
    wr = gf_b.shape[0]
    units = gf_b.shape[1]
    width = d_first.shape[1]
    wide = heads * 128
    rc = Copies(send, recv)
    at_c = lambda k: (d, c ^ k, z)
    at_x = (1 - d, c, z)
    at_z = lambda k: (d, c, z ^ k)
    across = (d, z, c)

    barrier = pltpu.get_barrier_semaphore()
    everyone = [at_c(k) for k in (1, 2, 3)] + [at_z(k) for k in (1, 2, 3)] + [at_x]
    for device in everyone:
        pl.semaphore_signal(barrier, inc=1, device_id=device, device_id_type=MESH)

    @pl.when(c != z)
    def _():
        pl.semaphore_signal(barrier, inc=1, device_id=across, device_id_type=MESH)

    pl.semaphore_wait(barrier, len(everyone) + jnp.where(c != z, 1, 0))

    number = iter(range(200))
    local_number = iter(range(40))

    def copy_here(src, dst):
        copy = pltpu.make_async_copy(src, dst, local.at[next(local_number)])
        copy.start()
        return copy

    flat = lambda ref: (lambda xy, h: (ref.at[xy, :, pl.ds(1536 * h, 1536)],))
    weights = []
    for own_b, got_b, x_buf, y_buf, z_buf, grad, final, is_o in (
        (o_b, r_b, x_b, y_b, z_b, g_b, gf_b, False),
        (o_i, r_i, x_i, y_i, z_i, g_i, gf_i, False),
        (o_o, r_o, x_o, y_o, z_o, g_o, gf_o, True),
    ):
        n = [next(number) for _ in range(12)]
        weights.append((own_b, got_b, x_buf, y_buf, z_buf, grad, final, is_o, n))
    half_units = 2 * units

    def of_core(w, which):
        grad, is_o = w[5], w[7]
        return grad.at[:, :, which] if is_o else grad.at[:, which]

    def part_of(w, xy, h):
        if w[7]:
            return w[0].at[pl.ds(2 * h, 2), xy]
        return w[0].at[xy, :, pl.ds(half_units * h, half_units)]

    def views(w, xy, h):
        if w[7]:
            return [w[0].at[2 * h, xy], w[0].at[2 * h + 1, xy]]
        return [w[0].at[xy, :, pl.ds(half_units * h, half_units)]]

    def buf_views(w, ref, i):
        return [ref.at[i, 0], ref.at[i, 1]] if w[7] else [ref.at[i]]

    def unit_at(w, t):
        xy = 2 * d + y
        if w[7]:
            return w[0].at[t, xy]
        return w[0].at[xy, :, pl.ds(pl.multiple_of(t * units, 128), units)]

    w_here = [copy_here(of_core(w, core), w[0]) for w in weights]
    blk = lambda x_, y_: 2 * x_ + y_

    def w_core_send(w):
        rc.start(w[8][0], lambda: (of_core(w, 1 - core), w[1], at_c(1)))

    def w_core_add(i):
        w = weights[i]
        w_here[i].wait()
        rc.arrived(w[8][0], w[1], at_c(1))

        @pl.loop(0, 4)
        def _(xy):
            if w[7]:
                add_into([w[0].at[t, xy] for t in range(4)], [w[1].at[t, xy] for t in range(4)], wr)
            else:
                add_into([w[0].at[xy]], [w[1].at[xy]], wr)

        n = w[8]
        for j in range(2):
            rc.start(n[1 + j], lambda j=j: (part_of(w, blk(1 - d, j), 0), w[2].at[j], at_x))
            rc.start(n[3 + j], lambda j=j: (part_of(w, blk(j, 1 - y), 1), w[3].at[j], at_c(2)))

    def w_plane(i):
        w = weights[i]
        n = w[8]
        for j in range(2):
            rc.arrived(n[1 + j], w[2].at[j], at_x)
        for j in range(2):
            add_into(views(w, blk(d, j), 0), buf_views(w, w[2], j), wr)
        rc.start(n[5], lambda: (part_of(w, blk(d, 1 - y), 0), w[3].at[2], at_c(2)))
        for j in range(2):
            rc.arrived(n[3 + j], w[3].at[j], at_c(2))
        for j in range(2):
            add_into(views(w, blk(j, y), 1), buf_views(w, w[3], j), wr)
        rc.start(n[6], lambda: (part_of(w, blk(1 - d, y), 1), w[2].at[2], at_x))

    def w_corner(i):
        w = weights[i]
        n = w[8]
        rc.arrived(n[5], w[3].at[2], at_c(2))
        add_into(views(w, blk(d, y), 0), buf_views(w, w[3], 2), wr)
        rc.arrived(n[6], w[2].at[2], at_x)
        add_into(views(w, blk(d, y), 1), buf_views(w, w[2], 2), wr)
        for t in (0, 1, 2):
            chain_send(w, t, 3)
        for t in (3, 2, 1):
            chain_send(w, t, 0)

    def chain_send(w, t, at):
        to = at + 1 if t > at else at - 1
        slot = 4 if to == t and t > at else t
        n = w[8]
        rc.start(
            n[7 + slot],
            lambda: (unit_at(w, t), w[4].at[slot], (d, c, to)),
            lambda: z == at,
            n[7 + t],
        )

    def chain_pass(w, t, at):
        @pl.when(z == at)
        def _():
            rc.arrived(w[8][7 + t], w[4].at[t], at_x)
            add_into([unit_at(w, t)], [w[4].at[t]], wr)

        chain_send(w, t, at)

    def w_line(i):
        w = weights[i]
        for t in (0, 1):
            chain_pass(w, t, 2)
        for t in (3, 2):
            chain_pass(w, t, 1)

    def w_next(i):
        w = weights[i]
        chain_pass(w, 3, 2)
        chain_pass(w, 0, 1)

    def w_end(i):
        w = weights[i]
        for t in range(4):

            @pl.when(z == t)
            def _():
                if t < 3:
                    rc.arrived(w[8][7 + t], w[4].at[t], at_x)
                if t > 0:
                    rc.arrived(w[8][11], w[4].at[4], at_x)

        total = unit_at(w, z)[...].astype(F32) + w[4].at[z][...].astype(F32)
        w[6][...] = total + w[4].at[4][...].astype(F32)

    whole_of = lambda t: (3 * t + 1) // 2
    shared_of = lambda t: 1 + 3 * (t // 2)

    class Line:
        def __init__(self, at):
            self.at = at
            self.left = [next(number) for _ in range(3)]
            self.right = [next(number) for _ in range(3)]

        def begin(self, src):
            rc.start(self.left[0], lambda: (src, self.at(z), (d, c, z + 1)), lambda: z < 3)
            rc.start(self.right[0], lambda: (src, self.at(z), (d, c, z - 1)), lambda: z > 0)

        def step(self, j, wait=True):
            from_left, from_right = z - j, z + j

            if wait:

                @pl.when(z >= j)
                def _():
                    rc.arrived(self.left[j - 1], self.at(from_left), (d, c, z - 1))

            if j < 3:
                rc.start(
                    self.left[j],
                    lambda: (self.at(z - j), self.at(z - j), (d, c, z + 1)),
                    lambda: (z >= j) & (z < 3),
                )

            if wait:

                @pl.when(z + j <= 3)
                def _():
                    rc.arrived(self.right[j - 1], self.at(from_right), (d, c, z + 1))

            if j < 3:
                rc.start(
                    self.right[j],
                    lambda: (self.at(z + j), self.at(z + j), (d, c, z - 1)),
                    lambda: (z + j <= 3) & (z > 0),
                )

    whole_rows = lambda ref, a, n: (lambda t: ref.at[whole_of(t), pl.ds(a, n)])
    shared_rows = lambda ref: (
        lambda t: ref.at[shared_of(t), pl.ds(pl.multiple_of((t % 2) * hl, 128), hl)]
    )
    out_lines = [Line(whole_rows(output, 0, ln)), Line(shared_rows(output))]
    tok_lines = [
        Line(whole_rows(d_tokens, 0, hl)),
        Line(whole_rows(d_tokens, hl, hl)),
        Line(shared_rows(d_tokens)),
    ]

    n_ctx = [next(number) for _ in range(3)]
    for k in (1, 2, 3):
        rc.start(n_ctx[k - 1], lambda k=k: (d_ctx.at[c ^ k], d_got.at[c], at_c(k)))
    ctx_here = copy_here(d_ctx.at[c], d_got.at[c])
    kv_here = copy_here(kv_in, kv)
    q_here = copy_here(q_in, q_scr)
    n_small = [next(number) for _ in range(5)]
    small_to = (at_c(1), at_c(2), at_x, at_z(1), at_z(2))
    small[...] = small_in[...]

    def small_send(i):
        rc.start(n_small[i], lambda: (small_got.at[i, 1], small_got.at[i, 0], small_to[i]))

    def small_step(i):
        rc.arrived(n_small[i], small_got.at[i, 0], small_to[i])
        small[...] += small_got[i, 0]
        if i < 4:
            small_got[i + 1, 1] = small[...]
            small_send(i + 1)

    small_got[0, 1] = small_in[...]
    wh_here = copy_here(wh_in, wh)
    xt_here = copy_here(xt_in, xt)

    def block(qb):
        r0, r1, o0, o1, seq = block_rows(qb, half, ln)
        b0 = jnp.where(qb < 4, qb, 2 * (qb - 4))
        b1 = jnp.where(qb < 4, qb, 2 * (qb - 4) + 1)
        s0 = pl.multiple_of(jnp.where(qb < 4, 0, hl * half), 128)
        s1 = pl.multiple_of(jnp.where(qb < 4, hl, hl * half), 128)
        sq = jnp.concatenate(
            [
                segr[2 * b0 + seq, 0:1, pl.ds(s0, hl)],
                segr[2 * b1 + seq, 0:1, pl.ds(s1, hl)],
            ],
            1,
        )
        q, do, line, delta = [], [], [], []
        for h in range(heads):
            q.append(two(q_scr, r0, r1, hl, slice(128 * h, 128 * h + 128)))
            do.append(two(d_o, o0, o1, hl, slice(128 * h, 128 * h + 128)))
            line.append(two_lanes(lse, slice(h, h + 1), o0, o1, hl))
            turned = do[h].astype(F32).T[HEAD:, :]
            kept = two_lanes(ctx_t, slice(HEAD * h, HEAD * h + HEAD), o0, o1, hl)
            delta.append(jnp.sum(turned * kept, 0, keepdims=True))
        q_do = [jnp.concatenate([q[h], do[h]], 0) for h in range(heads)]
        dqt[...] = jnp.zeros_like(dqt)

        @pl.loop(0, nc)
        def _(j):
            rows = pl.ds(pl.multiple_of((2 * j + seq) * ln, ln), ln)
            keys = pl.ds(pl.multiple_of(j * ln, ln), ln)
            key_seg = segc[2 * j + seq]
            same = jnp.concatenate([key_seg, key_seg], 1) == sq
            for h in range(heads):
                kvh = kv[rows, 128 * h : 128 * h + 128]
                p = jnp.where(same, jnp.exp(dot_nt(kvh, q[h]) - line[h]), 0.0)
                ds = (p * (dot_nt(kvh, do[h]) - delta[h])).astype(BF)
                both = jnp.concatenate([ds, p.astype(BF)], 1)
                dkv[rows, 128 * h : 128 * h + 128] += dot_nn(both, q_do[h])
                dqt[h] += dot_nn(kvt[seq * heads + h, :, keys], ds)

        turned = jnp.concatenate([dqt[h] for h in range(heads)], 0).T * 0.125
        bias_sum[0:1, wide:] += jnp.sum(turned, 0, keepdims=True)
        low = turned.astype(BF)
        d_proj[pl.ds(r0, hl), wide:] = low[:hl]
        d_proj[pl.ds(r1, hl), wide:] = low[hl:]

    n_tc = [[next(number), next(number)] for _ in range(2)]
    n_ty = [[next(number), next(number)] for _ in range(2)]
    n_tz = next(number)

    def rows_of(cb, s):
        rows = pl.ds(pl.multiple_of((2 * cb + s) * ln, ln), ln)
        got = dkv[rows, :]
        bias_sum[0:1, :wide] += jnp.sum(got, 0, keepdims=True)
        d_proj[rows, :wide] = got.astype(BF)
        part[cb, s] = dot_nt(d_proj[rows, :], wh[...]).astype(BF)

    def t_partial(s):
        rows_of(c ^ 3, s)
        rc.start(n_tc[s][0], lambda: (part.at[c ^ 3, s], got_c.at[s, 0], at_c(1)))
        rows_of(c ^ 1, s)
        rc.start(n_tc[s][1], lambda: (part.at[c ^ 1, s], got_c.at[s, 1], at_c(1)))
        rows_of(c ^ 2, s)
        rows_of(c, s)

    def t_core(s):
        rc.arrived(n_tc[s][0], got_c.at[s, 0], at_c(1))
        for k in range(2):
            at = slice(k * hl, k * hl + hl)
            send_y[s, at] = (part[c ^ 2, s, at].astype(F32) + got_c[s, 0, at].astype(F32)).astype(BF)
            rc.start(
                n_ty[s][k],
                lambda k=k: (
                    send_y.at[s, pl.ds(k * hl, hl)],
                    got_y.at[s, pl.ds(k * hl, hl)],
                    at_c(2),
                ),
            )
        rc.arrived(n_tc[s][1], got_c.at[s, 1], at_c(1))
        mine[s] = part[c, s].astype(F32) + got_c[s, 1].astype(F32)

    def t_shared():
        for k in range(2):
            rc.arrived(n_ty[1][k], got_y.at[1, pl.ds(k * hl, hl)], at_c(2))
        mine[1] += got_y[1].astype(F32)
        send_z[...] = mine[1, pl.ds(pl.multiple_of((1 - half) * hl, 128), hl)].astype(BF)
        rc.start(n_tz, lambda: (send_z, got_z, at_z(1)))

    def t_shared_end():
        rc.arrived(n_tz, got_z, at_z(1))
        mine_half = mine[1, pl.ds(pl.multiple_of(half * hl, 128), hl)]
        done[ln:, :] = (mine_half + got_z[...].astype(F32) + d_first[ln:, :]).astype(BF)
        tok_lines[2].begin(done.at[pl.ds(ln, hl)])

    def t_whole(k):
        at = slice(k * hl, k * hl + hl)
        rc.arrived(n_ty[0][k], got_y.at[0, pl.ds(k * hl, hl)], at_c(2))
        done[at, :] = (mine[0, at] + got_y[0, at].astype(F32) + d_first[at, :]).astype(BF)
        tok_lines[k].begin(done.at[pl.ds(k * hl, hl)])

    n_h = [next(number) for _ in range(8)]

    def h_partial(seq):
        @pl.loop(0, nc)
        def _(i):
            rows = pl.ds(pl.multiple_of((2 * i + seq) * ln, ln), ln)
            acc_h[...] += dot_nn(xt[:, rows], d_proj[rows, :])

    def h_send():
        o_h[...] = acc_h[...].astype(BF)
        rows_x = lambda x_: pl.ds(pl.multiple_of(x_ * 4 * wr, wr), 4 * wr)
        rc.start(n_h[0], lambda: (o_h.at[rows_x(1 - d)], x_h, at_x))

    h_at = lambda t: o_h.at[pl.ds(pl.multiple_of((4 * d + t) * wr, wr), wr)]

    def h_plane():
        rc.arrived(n_h[0], x_h, at_x)
        add_into([o_h.at[pl.ds(pl.multiple_of(d * 4 * wr, wr), 4 * wr)]], [x_h], 4 * wr)
        rc.start(n_h[1], lambda: (h_at(z ^ 3), z_h.at[1], at_z(1)))
        rc.start(n_h[2], lambda: (h_at(z ^ 1), z_h.at[0], at_z(1)))

    def h_line():
        rc.arrived(n_h[1], z_h.at[1], at_z(1))
        add_into([h_at(z ^ 2)], [z_h.at[1]], wr)
        rc.start(n_h[3], lambda: (h_at(z ^ 2), z_h.at[2], at_z(2)))
        rc.arrived(n_h[2], z_h.at[0], at_z(1))
        add_into([h_at(z)], [z_h.at[0]], wr)

    def h_end():
        rc.arrived(n_h[3], z_h.at[2], at_z(2))
        send_h[...] = h_at(z)[...].astype(F32) + z_h[2].astype(F32)
        rc.start(n_h[4], lambda: (send_h, h_got, across), lambda: c != z)

        @pl.when(c == z)
        def _():
            h_got[...] = send_h[...]

    n_bias = [next(number) for _ in range(4)]
    bias_to = (at_x, at_z(1), at_z(2))

    def bias_send(i):
        bias_got[i, 1] = bias_sum[...]
        rc.start(n_bias[i], lambda: (bias_got.at[i, 1], bias_got.at[i, 0], bias_to[i]))

    def bias_step(i):
        rc.arrived(n_bias[i], bias_got.at[i, 0], bias_to[i])
        bias_sum[...] += bias_got[i, 0]
        if i < 2:
            bias_send(i + 1)
            return
        rc.start(n_bias[3], lambda: (bias_sum, bias_fin, across), lambda: c != z)

        @pl.when(c == z)
        def _():
            bias_fin[...] = bias_sum[...]

    for w in weights:

        @pl.when(z == 0)
        def _():
            w[4][4] = jnp.zeros_like(w[4][4])

        @pl.when(z == 3)
        def _():
            w[4][3] = jnp.zeros_like(w[4][3])

    def get_ctx():
        for k in (1, 2, 3):
            rc.arrived(n_ctx[k - 1], d_got.at[c ^ k], at_c(k))
        ctx_here.wait()

        @pl.loop(0, nc)
        def _(i):
            rows = pl.ds(pl.multiple_of(i * own, 128), own)
            for h in range(heads):
                d_o[rows, 128 * h + HEAD : 128 * h + 128] = d_got[
                    i, :, HEAD * h : HEAD * h + HEAD
                ]

        q_here.wait()
        wh_here.wait()
        xt_here.wait()

    def out_begin():
        for line in out_lines:
            line.step(1, False)

    w_core_send(weights[0])
    out_begin()
    small_send(0)
    for i in range(nc):
        for s in range(2):
            line = seg[i, s : s + 1, :].astype(F32)
            segr[2 * i + s, 0:1, :] = line
            segc[2 * i + s] = jnp.broadcast_to(line, (128, ln)).T
    dkv[...] = jnp.zeros_like(dkv)
    d_o[...] = jnp.zeros_like(d_o)
    d_proj[...] = jnp.zeros_like(d_proj)
    bias_sum[...] = jnp.zeros_like(bias_sum)
    acc_h[...] = jnp.zeros_like(acc_h)
    kv_here.wait()

    @pl.loop(0, nc)
    def _(j):
        for s in range(2):
            rows = pl.ds(pl.multiple_of((2 * j + s) * ln, ln), ln)
            for h in range(heads):
                kvt[s * heads + h, :, pl.ds(pl.multiple_of(j * ln, ln), ln)] = kv[
                    rows, 128 * h : 128 * h + 128
                ].T[:HEAD]

    small_step(0)
    w_core_send(weights[2])
    w_core_add(0)
    w_core_send(weights[1])
    get_ctx()

    @pl.loop(0, 6)
    def _(i):
        block(jnp.where(i == 0, 0, jnp.where(i == 1, 1, jnp.where(i == 2, 2, jnp.where(i == 3, 3, jnp.where(i == 4, 4, 5))))))

        @pl.when(i == 1)
        def _():
            w_core_add(2)
            out_lines[0].step(2)
            out_lines[1].step(2)

        @pl.when(i == 3)
        def _():
            t_partial(0)
            t_core(0)

    t_whole(0)
    w_plane(0)
    t_partial(1)
    t_whole(1)
    h_partial(1)
    w_plane(2)
    bias_send(0)
    tok_lines[0].step(1)
    small_step(1)
    h_partial(0)
    w_corner(0)
    h_send()
    bias_step(0)
    t_core(1)
    tok_lines[1].step(1)
    w_core_add(1)
    w_corner(2)
    tok_lines[0].step(2)
    w_line(0)
    tok_lines[1].step(2)
    small_step(2)
    t_shared()
    w_line(2)
    small_step(3)
    h_plane()
    bias_step(1)
    tok_lines[0].step(3)
    t_shared_end()
    w_plane(1)
    h_line()
    out_lines[0].step(3)
    out_lines[1].step(3)
    tok_lines[2].step(1)
    w_corner(1)
    w_next(2)
    h_end()
    w_next(0)
    tok_lines[2].step(2)
    w_end(0)
    bias_step(2)
    w_end(2)
    small_step(4)
    w_line(1)
    tok_lines[1].step(3)
    w_next(1)
    w_end(1)
    tok_lines[2].step(3)
    tok_here = [
        copy_here(done.at[pl.ds(0, hl)], tok_lines[0].at(z)),
        copy_here(done.at[pl.ds(hl, hl)], tok_lines[1].at(z)),
        copy_here(done.at[pl.ds(ln, hl)], tok_lines[2].at(z)),
    ]

    @pl.when(c != z)
    def _():
        rc.arrived(n_h[4], h_got, across)
        rc.arrived(n_bias[3], bias_fin, across)

    gf_h[...] = h_got[...]
    bias[...] = bias_fin[...]

    for copy in tok_here:
        copy.wait()
    rc.all_sent()


def backward(d_ctx, g_b, g_i, g_o, out_in, d_first, small, q, kv, xt, wh, lse, ctx_t, seg, heads, seqs):
    nc, own, group = d_ctx.shape
    ln = own * 2 // 3
    hl = ln // 2
    width = out_in.shape[2]
    wr, all_units = g_b.shape[2:]
    units = all_units // 4
    hb = pl.BlockSpec(memory_space=pltpu.HBM)
    vm = pl.BlockSpec(memory_space=pltpu.VMEM)
    sds = jax.ShapeDtypeStruct
    v = pltpu.VMEM
    rows = nc * own
    n2 = 2 * nc * ln
    return pl.pallas_call(
        functools.partial(backward_kernel, heads, ln),
        out_shape=(
            sds((seqs, ln, width), BF),
            sds((seqs, ln, width), BF),
            sds((wr, units), F32),
            sds((wr, units), F32),
            sds((wr, group), F32),
            sds((wr, 3 * group), F32),
            sds(small.shape, F32),
            sds((8, 3 * group), F32),
        ),
        in_specs=[hb] * 5 + [vm] * 2 + [hb] * 4 + [vm] * 3,
        out_specs=(hb, hb) + (vm,) * 6,
        scratch_shapes=[
            v((n2, heads * 128), BF),
            v((n2, heads * 128), BF),
            v((width, n2), BF),
            v((width, 3 * group), BF),
            v((nc, own, group), BF),
            v((rows, heads * 128), BF),
            v((2 * heads, HEAD, nc * ln), BF),
            v((n2, heads * 128), F32),
            v((heads, HEAD, ln), F32),
            v((n2, 3 * group), BF),
            v((2 * nc, ln, 128), F32),
            v((2 * nc, 8, ln), F32),
            v((nc, 2, ln, width), BF),
            v((2, 2, ln, width), BF),
            v((2, ln, width), BF),
            v((hl, width), BF),
            v((2, ln, width), BF),
            v((hl, width), BF),
            v((2, ln, width), F32),
            v((own, width), BF),
            v((4, wr, all_units), BF),
            v((4, wr, all_units), BF),
            v((4, 4, wr, group), BF),
            v((4, wr, all_units), BF),
            v((4, wr, all_units), BF),
            v((4, 4, wr, group), BF),
            v((3, wr, 2 * units), BF),
            v((3, wr, 2 * units), BF),
            v((3, 2, wr, group), BF),
            v((3, wr, 2 * units), BF),
            v((3, wr, 2 * units), BF),
            v((3, 2, wr, group), BF),
            v((5, wr, units), BF),
            v((5, wr, units), BF),
            v((5, wr, group), BF),
            v((width, 3 * group), F32),
            v((width, 3 * group), BF),
            v((4 * wr, 3 * group), BF),
            v((3, wr, 3 * group), BF),
            v((wr, 3 * group), F32),
            v((5, 2) + small.shape, F32),
            v((8, 3 * group), F32),
            v((3, 2, 8, 3 * group), F32),
            v((wr, 3 * group), F32),
            v((8, 3 * group), F32),
            pltpu.SemaphoreType.DMA((130,)),
            pltpu.SemaphoreType.DMA((130,)),
            pltpu.SemaphoreType.DMA((40,)),
        ],
        compiler_params=pltpu.CompilerParams(
            vmem_limit_bytes=60 << 20, collective_id=1, has_side_effects=True
        ),
        input_output_aliases={4: 0},
        name="backward",
    )(d_ctx, g_b, g_i, g_o, out_in, d_first, small, q, kv, xt, wh, lse, ctx_t, seg)


def finish_kernel(
    heads, tok_in, out_in, g_b, g_i, g_o, g_h, small, bias,
    tok, out, gb, gi, go, gh, gq, gv, w0, w1, w2, in_b, w3, w4, w5,
):
    tok[...] = tok_in[...].astype(F32)
    out[...] = out_in[...]
    z = lax.axis_index("tp")
    wide = heads * 128

    @pl.when(pl.program_id(0) == 0)
    def _():
        gb[...] = g_b[...]
        gi[...] = g_i[...]
        go[...] = g_o[...]
        pick = lambda ref, rows, at: jnp.concatenate(
            [ref[rows, 128 * h + at : 128 * h + at + HEAD] for h in range(heads)], -1
        )
        gh[:, 0, :] = g_h[:, wide:]
        gh[:, 1, :] = pick(g_h, slice(None), 0)
        gh[:, 2, :] = pick(g_h, slice(None), HEAD)
        gq[...] = bias[0, wide:]
        gv[...] = pick(bias, 0, HEAD)
        for i, ref in ((0, w0), (1, w1), (2, w2), (3, w3), (4, w4), (5, w5)):
            ref[...] = small[i, :]
        in_b[...] = small[pl.ds(6 + z, 1), :].reshape(in_b.shape)


def finish(d_tokens, output, g_b, g_i, g_o, g_h, small, d_bias, heads):
    seqs, ln, width = d_tokens.shape
    wr, units = g_b.shape
    group = g_o.shape[1]
    one = lambda: pl.BlockSpec((1, ln, width), lambda i: (i, 0, 0))
    whole = lambda shape: pl.BlockSpec(shape, lambda i: (0,) * len(shape))
    sds = jax.ShapeDtypeStruct
    rest = [
        (wr, units), (wr, units), (wr, group), (wr, 3, group), (group,), (group,),
        (width,), (width,), (width,), (units,), (width,), (width,), (width,),
    ]
    return pl.pallas_call(
        functools.partial(finish_kernel, heads),
        grid=(seqs,),
        out_shape=[sds(d_tokens.shape, F32), sds(output.shape, BF)] + [sds(s, F32) for s in rest],
        in_specs=[one(), one()]
        + [whole(a.shape) for a in (g_b, g_i, g_o, g_h, small, d_bias)],
        out_specs=[one(), one()] + [whole(s) for s in rest],
        compiler_params=pltpu.CompilerParams(vmem_limit_bytes=60 << 20),
        name="finish",
    )(d_tokens, output, g_b, g_i, g_o, g_h, small, d_bias)


def head_order(kinds, heads):
    lead = kinds[0].shape[:-1]
    q, k, v = (a.reshape(lead + (heads, HEAD)) for a in kinds)
    kv = jnp.concatenate([k, v], -1).reshape(lead + (heads * 2 * HEAD,))
    return jnp.concatenate([kv, q.reshape(lead + (heads * HEAD,))], -1)


def forward_plain(sizes, me, tok2, seg2, w_head, b_head, b_unit, w_o, w_i, w_b, heads):
    nd, nc, nt = sizes
    d, c, z = me
    ln, width = tok2.shape[1:]
    hl = ln // 2
    half = z % 2
    group = w_o.shape[1]
    seg_all = gather_axis(seg2, "ctx", nc, c)
    x2 = gather_axis(tok2, "ctx", nc, c).reshape(2 * nc, ln, width)
    wh = gather_heads(w_head, sizes, me)
    bh = transpose_ctx_tp(b_head, nc)[0]
    b_all = gather_axis(b_unit, "tp", nt, z)
    gather = lambda w: lax.all_gather(
        lax.all_gather(w, "tp", axis=1, tiled=True), ("dp", "ctx"), axis=0, tiled=True
    )
    o_full = jnp.transpose(gather(w_o).reshape(width, nt, group), (1, 0, 2))
    proj = (jnp.dot(x2.reshape(-1, width), wh, preferred_element_type=F32) + bh).astype(BF)
    kv = proj[:, : 2 * group]
    q = (proj[:, 2 * group :].astype(F32) * 0.125).astype(BF).reshape(-1, heads, HEAD)
    q = jnp.concatenate([q, jnp.zeros_like(q)], -1).reshape(-1, heads * 128)
    info, seg_col, seg_row = key_blocks(seg_all, half, ln, nc)
    context, lse, ctx_t = attend(info, q, kv, seg_col, seg_row, heads, ln, nc)
    ctx_all = in_order(exchange_axis(context.reshape(nc, ln + hl, group), "ctx", nc, c), c)
    return (
        ctx_all,
        x2.reshape(-1, width).T,
        q,
        kv,
        wh,
        o_full,
        jnp.stack([gather(w_i), gather(w_b)]),
        b_all,
        lse,
        ctx_t,
        seg_all,
    )


def key_blocks(seg_all, half, ln, nc):
    hl = ln // 2
    seg2 = seg_all[:, :2]
    flat = jnp.transpose(seg2, (1, 0, 2)).reshape(2, nc * ln)
    first = jnp.concatenate([seg2[:, 0, 0], jnp.take(seg2[0::2, 1], half * hl, axis=1)])
    last = jnp.concatenate([seg2[:, 0, -1], jnp.take(seg2[1::2, 1], half * hl + hl - 1, axis=1)])
    of = jnp.concatenate(
        [
            jnp.broadcast_to(flat[:1], (nc, nc * ln)),
            jnp.broadcast_to(flat[1:], (nc // 2, nc * ln)),
        ],
        0,
    )
    lo = jnp.sum(of < first[:, None], 1) // ln
    hi = (jnp.sum(of <= last[:, None], 1) + ln - 1) // ln
    info = jnp.concatenate([lo, hi, half[None]]).astype(jnp.int32)
    seg_flat = seg2.reshape(2 * nc * ln)
    return info, seg_flat[:, None], seg_flat[None, :]


def backward_plain(
    sizes, me, d_ctx, low, out_low, d_first, small, q, kv, xt, wh, lse, ctx_t, seg_all, heads, seqs
):
    nd, nc, nt = sizes
    d, c, z = me
    own, group = d_ctx.shape[1:]
    ln = own * 2 // 3
    hl = ln // 2
    half = z % 2
    width = out_low.shape[1]
    units = low[0].shape[1] // nt
    nr = nd * nc
    wr = width // nr
    info, seg_col, seg_row = key_blocks(seg_all, half, ln, nc)

    def spread_rows(rows_low, dtype):
        out = jnp.zeros((seqs, ln, width), dtype)
        parts = [rows_low] + [swap_with(rows_low, "tp", nt, k) for k in range(1, nt)]
        for k, part in enumerate(parts):
            t = z ^ k
            part = part.astype(dtype)
            out = lax.dynamic_update_slice(out, part[None, :ln], ((3 * t + 1) // 2, 0, 0))
            out = lax.dynamic_update_slice(
                out, part[None, ln:], (1 + 3 * (t // 2), (t % 2) * hl, 0)
            )
        return out

    by_unit = lambda g: jnp.transpose(g.reshape(nr, wr, nt, units), (2, 0, 1, 3))
    g_back = scatter_weight(by_unit(low[0]), sizes, me)
    g_in = scatter_weight(by_unit(low[1]), sizes, me)
    g_out = scatter_weight(low[2].reshape(nt, nr, wr, group), sizes, me)
    output = spread_rows(out_low, BF)
    small = lax.psum(small, ALL)
    d_ctx = in_order(exchange_axis(d_ctx, "ctx", nc, c), c).reshape(nc * own, heads, HEAD)
    d_ctx = jnp.concatenate([jnp.zeros_like(d_ctx), d_ctx], -1).reshape(nc * own, heads * 128)
    d_q, d_kv, d_bias = attend_back(
        info, q, kv, d_ctx, seg_col, seg_row, lse, ctx_t, heads, ln, nc
    )
    d_proj = jnp.concatenate([d_kv, d_q], -1)
    part = jnp.einsum("tf,df->td", d_proj, wh, preferred_element_type=F32)
    part = lax.psum_scatter(
        part.reshape(nc, 2 * ln, width), "ctx", scatter_dimension=0, tiled=False
    ).reshape(2, ln, width)
    shared = part[1].reshape(2, hl, width)
    shared = lax.dynamic_index_in_dim(shared, half, 0, keepdims=False) + swap_with(
        lax.dynamic_index_in_dim(shared, 1 - half, 0, keepdims=False), "tp", nt, 1
    )
    d_own = (jnp.concatenate([part[0], shared], 0) + d_first).astype(BF)
    d_tokens = spread_rows(d_own, BF)
    g_h = scatter_heads(jnp.dot(xt, d_proj, preferred_element_type=F32).astype(BF), sizes, me)
    slots = jnp.zeros((nc,) + d_bias[0].shape, F32)
    slots = lax.psum(lax.dynamic_update_index_in_dim(slots, d_bias[0], c, 0), ALL)
    d_bias = lax.dynamic_index_in_dim(slots, z, 0, keepdims=False)
    d_bias = jnp.broadcast_to(d_bias[None], (8,) + d_bias.shape)
    return output, d_tokens, g_back, g_in, g_out, g_h, small, d_bias


def per_device(
    sizes,
    tokens,
    segments,
    w_qkv,
    q_bias,
    v_bias,
    w_out,
    out_bias,
    gain_one,
    shift_one,
    w_in,
    in_bias,
    w_back,
    back_bias,
    gain_two,
    shift_two,
    cotangent,
):
    nd, nc, nt = sizes
    seqs, ln, width = tokens.shape
    group = w_out.shape[1]
    heads = group // HEAD
    units = w_in.shape[1]
    wr = w_in.shape[0]
    d, c, z = (lax.axis_index(n) for n in ALL)
    me = (d, c, z)
    whole_of = lambda t: (3 * t + 1) // 2
    shared_of = lambda t: 1 + 3 * (t // 2)
    half_of = lambda t: t % 2
    sf, sh, half = whole_of(z), shared_of(z), half_of(z)

    def own_pair(a):
        return jnp.stack(
            [
                lax.dynamic_index_in_dim(a, sf, 0, keepdims=False),
                lax.dynamic_index_in_dim(a, sh, 0, keepdims=False),
            ],
            0,
        )

    w_kinds = jnp.transpose(w_qkv, (1, 0, 2))
    biases = (q_bias, v_bias, in_bias)
    weights = (w_out, w_in, w_back)
    vectors = (out_bias, gain_one, shift_one, back_bias, gain_two, shift_two)
    if sizes == (2, 4, 4):
        xt, q, kv, wh, g_b, g_i, out_low, lse, ctx_t, seg_all, d_ctx, g_o, d_first, small = forward(
            tokens, segments, w_kinds, *biases, *weights, cotangent, vectors, heads
        )
    else:
        tok2 = own_pair(tokens)
        seg2 = jnp.concatenate([own_pair(segments), jnp.zeros((6, ln), jnp.int32)], 0)
        w_head = head_order(w_kinds, heads)
        b_head = head_order([q_bias, jnp.zeros_like(q_bias), v_bias], heads)
        b_head = jnp.broadcast_to(b_head[None], (8, 3 * group))
        b_unit = jnp.broadcast_to(in_bias[None], (8, units))
        got = forward_plain(sizes, me, tok2, seg2, w_head, b_head, b_unit, *weights, heads)
        ctx_all, xt, q, kv, wh, w_o, w_ib, b_in, lse, ctx_t, seg_all = got
        d_ctx, g_b, g_i, g_o, out_low, d_first, small = middle(
            tokens,
            cotangent,
            ctx_all,
            w_o.reshape(nt, width, group),
            w_ib.reshape(2, width, nt * units),
            b_in,
            vectors,
        )
    low = (g_b, g_i, g_o)
    if sizes == (2, 4, 4):
        output, d_tokens, g_back, g_in, g_out, g_h, small, d_bias = backward(
            d_ctx,
            low[0].reshape(4, 2, wr, nt * units),
            low[1].reshape(4, 2, wr, nt * units),
            low[2].reshape(nt, 4, 2, wr, group),
            out_low,
            d_first,
            small,
            q,
            kv,
            xt,
            wh,
            lse,
            ctx_t,
            seg_all,
            heads,
            seqs,
        )
    else:
        output, d_tokens, g_back, g_in, g_out, g_h, small, d_bias = backward_plain(
            sizes, me, d_ctx, low, out_low, d_first, small, q, kv, xt, wh, lse, ctx_t, seg_all, heads, seqs
        )
    d_tokens, output, g_b, g_i, g_o, g_h, d_qb, d_vb, w0, w1, w2, d_in, w3, w4, w5 = finish(
        d_tokens, output, g_back, g_in, g_out, g_h, small, d_bias, heads
    )
    return (output, d_tokens, g_h, d_qb, d_vb, g_o, w0, w1, w2, g_i, d_in, g_b, w3, w4, w5)


def solution(mesh):
    sizes = tuple(mesh.shape[n] for n in ALL)
    rows = P(("dp", "ctx"), "tp")
    return jax.shard_map(
        functools.partial(per_device, sizes),
        mesh=mesh,
        in_specs=(
            P("dp", "ctx", None),
            P("dp", "ctx"),
            P(("dp", "ctx"), None, "tp"),
            P("tp"),
            P("tp"),
            rows,
            P(),
            P(),
            P(),
            rows,
            P("tp"),
            rows,
            P(),
            P(),
            P(),
            P("dp", "ctx", None),
        ),
        out_specs=(
            P("dp", "ctx", None),
            P("dp", "ctx", None),
            P(("dp", "ctx"), None, "tp"),
            P("tp"),
            P("tp"),
            rows,
            P(),
            P(),
            P(),
            rows,
            P("tp"),
            rows,
            P(),
            P(),
            P(),
        ),
        check_vma=False,
    )
```

```python
import functools
import math

import jax
import jax.numpy as jnp
from jax import lax
from jax.experimental import pallas as pl
from jax.experimental.pallas import tpu as pltpu
from jax.sharding import PartitionSpec as P

HEAD = 64
NEG = -1e30
BF = jnp.bfloat16
F32 = jnp.float32
ALL = ("dp", "ctx", "tp")


def norm_parts(value):
    mean = jnp.mean(value, -1, keepdims=True)
    centered = value - mean
    rstd = lax.rsqrt(jnp.mean(centered * centered, -1, keepdims=True) + 1e-12)
    return (centered * rstd, rstd)


def norm_back(grad, normal, rstd, gain):
    d_gain = jnp.sum(grad * normal, 0)
    d_shift = jnp.sum(grad, 0)
    scaled = grad * gain
    d_value = rstd * (
        scaled
        - jnp.mean(scaled, -1, keepdims=True)
        - normal * jnp.mean(scaled * normal, -1, keepdims=True)
    )
    return (d_value, d_gain, d_shift)


def gelu_slope(inner):
    return 0.5 * (1.0 + lax.erf(inner / math.sqrt(2.0))) + inner * jnp.exp(
        -0.5 * inner * inner
    ) / math.sqrt(2.0 * math.pi)


def swap_with(value, axis, size, mask):
    return lax.ppermute(value, axis, [(i, i ^ mask) for i in range(size)])


def in_order(parts, me, axis=0):
    shape = list(parts[0].shape)
    shape.insert(axis, len(parts))
    out = jnp.zeros(tuple(shape), parts[0].dtype)
    for k, part in enumerate(parts):
        out = lax.dynamic_update_index_in_dim(out, part, me ^ k, axis)
    return out


def gather_axis(value, axis, size, me):
    parts = [value] + [swap_with(value, axis, size, k) for k in range(1, size)]
    return in_order(parts, me)


def exchange_axis(blocks, axis, size, me):
    parts = [lax.dynamic_index_in_dim(blocks, me, 0, keepdims=False)]
    for k in range(1, size):
        parts.append(
            swap_with(lax.dynamic_index_in_dim(blocks, me ^ k, 0, keepdims=False), axis, size, k)
        )
    return parts


def scatter_weight(grad, sizes, me):
    nd, nc, nt = sizes
    part = lax.psum_scatter(
        grad.astype(F32), ("dp", "ctx"), scatter_dimension=1, tiled=False
    ).astype(BF)
    parts = exchange_axis(part, "tp", nt, me[2])
    return sum(p.astype(F32) for p in parts)


def transpose_ctx_tp(value, n):
    pairs = [(a * n + b, b * n + a) for a in range(n) for b in range(n)]
    return lax.ppermute(value, ("ctx", "tp"), pairs)


def gather_heads(shard, sizes, me):
    mine = transpose_ctx_tp(shard, sizes[1])
    return lax.all_gather(mine, ("dp", "tp"), axis=0, tiled=True)


def scatter_heads(grad, sizes, me):
    nd, nc, nt = sizes
    blocks = grad.reshape((nd * nt, grad.shape[0] // (nd * nt)) + grad.shape[1:])
    total = lax.psum_scatter(
        blocks.astype(F32), ("dp", "tp"), scatter_dimension=0, tiled=False
    )
    return transpose_ctx_tp(total, nc)


def block_rows(qb, half, ln):
    hl = ln // 2
    whole = qb < 4
    b = jnp.where(whole, qb, qb - 4)
    r0 = jnp.where(whole, 2 * ln * b, (4 * b + 1) * ln + hl * half)
    r1 = jnp.where(whole, r0 + hl, r0 + 2 * ln)
    o0 = jnp.where(whole, 3 * hl * b, 6 * hl * b + ln)
    o1 = jnp.where(whole, o0 + hl, o0 + 3 * hl)
    seq = jnp.where(whole, 0, 1)
    m = lambda v: pl.multiple_of(v, 128)
    return m(r0), m(r1), m(o0), m(o1), seq


def two(ref, r0, r1, hl, cols):
    return jnp.concatenate([ref[pl.ds(r0, hl), cols], ref[pl.ds(r1, hl), cols]], 0)


def two_lanes(ref, rows, r0, r1, hl):
    return jnp.concatenate([ref[rows, pl.ds(r0, hl)], ref[rows, pl.ds(r1, hl)]], 1)


def dot_nt(a, b):
    return lax.dot_general(a, b, (((1,), (1,)), ((), ())), preferred_element_type=F32)


def dot_nn(a, b):
    return lax.dot_general(a, b, (((1,), (0,)), ((), ())), preferred_element_type=F32)


def fill_transposed(kv, kvt, ln, nc, heads):
    @pl.loop(0, nc)
    def _(j):
        for seq in range(2):
            rows = pl.ds(pl.multiple_of((2 * j + seq) * ln, ln), ln)
            for h in range(heads):
                kvt[seq * heads + h, :, pl.ds(pl.multiple_of(j * ln, ln), ln)] = kv[
                    rows, 128 * h : 128 * h + 128
                ].T


def attend_kernel(heads, ln, nc, info, q_ref, kv, seg_col, seg_row, out, lse, ctx_t, s_scr, kvt, acc):
    half = info[12]
    hl = ln // 2
    fill_transposed(kv, kvt, ln, nc, heads)

    @pl.loop(0, 6)
    def _(qb):
        r0, r1, o0, o1, seq = block_rows(qb, half, ln)
        lo, hi = info[qb], info[6 + qb]
        sq = two_lanes(seg_row, slice(0, 1), r0, r1, hl)
        q = [two(q_ref, r0, r1, hl, slice(128 * h, 128 * h + 128)) for h in range(heads)]

        def score(j, peaks):
            rows = pl.ds(pl.multiple_of((2 * j + seq) * ln, ln), ln)
            same = seg_col[rows, :] == sq
            new = []
            for h in range(heads):
                s = dot_nt(kv[rows, 128 * h : 128 * h + 128], q[h])
                s = jnp.where(same, s, NEG)
                s_scr[h, pl.ds(pl.multiple_of(j * ln, ln), ln), :] = s
                new.append(jnp.maximum(peaks[h], jnp.max(s, 0, keepdims=True)))
            return tuple(new)

        peaks = lax.fori_loop(
            lo, hi, score, tuple(jnp.full((1, ln), NEG, F32) for _ in range(heads))
        )
        acc[...] = jnp.zeros_like(acc)

        def collect(j, sums):
            keys = pl.ds(pl.multiple_of(j * ln, ln), ln)
            new = []
            for h in range(heads):
                p = jnp.exp(s_scr[h, keys, :] - peaks[h])
                new.append(sums[h] + jnp.sum(p, 0, keepdims=True))
                acc[h] += dot_nn(kvt[seq * heads + h, :, keys], p.astype(BF))
            return tuple(new)

        sums = lax.fori_loop(
            lo, hi, collect, tuple(jnp.zeros((1, ln), F32) for _ in range(heads))
        )
        whole = []
        for h in range(heads):
            one = acc[h, HEAD:, :] / sums[h]
            whole.append(one)
            line = peaks[h] + jnp.log(sums[h])
            for part, at in ((0, o0), (hl, o1)):
                ctx_t[HEAD * h : HEAD * h + HEAD, pl.ds(at, hl)] = one[:, part : part + hl]
                lse[h : h + 1, pl.ds(at, hl)] = line[:, part : part + hl]
        turned = jnp.concatenate(whole, 0).T.astype(BF)
        out[pl.ds(o0, hl), :] = turned[:hl]
        out[pl.ds(o1, hl), :] = turned[hl:]


def attend(info, q_ref, kv, seg_col, seg_row, heads, ln, nc):
    rows = 3 * ln // 2 * nc
    vm = pl.BlockSpec(memory_space=pltpu.VMEM)
    return pl.pallas_call(
        functools.partial(attend_kernel, heads, ln, nc),
        out_shape=(
            jax.ShapeDtypeStruct((rows, heads * HEAD), BF),
            jax.ShapeDtypeStruct((8, rows), F32),
            jax.ShapeDtypeStruct((heads * HEAD, rows), F32),
        ),
        in_specs=[pl.BlockSpec(memory_space=pltpu.SMEM), vm, vm, vm, vm],
        out_specs=(vm, vm, vm),
        scratch_shapes=[
            pltpu.VMEM((heads, nc * ln, ln), F32),
            pltpu.VMEM((2 * heads, 128, nc * ln), BF),
            pltpu.VMEM((heads, 128, ln), F32),
        ],
        compiler_params=pltpu.CompilerParams(vmem_limit_bytes=32 << 20),
        cost_estimate=pl.CostEstimate(
            flops=8 * heads * rows * nc * ln * 128,
            bytes_accessed=8 << 20,
            transcendentals=heads * rows * nc * ln,
        ),
        name="attend",
    )(info, q_ref, kv, seg_col, seg_row)


def attend_back_kernel(
    heads, ln, nc, info, q_ref, kv, d_out, seg_col, seg_row, lse, ctx_t, d_q, d_kv, d_bias, dkv, kvt, dqt
):
    half = info[12]
    hl = ln // 2
    fill_transposed(kv, kvt, ln, nc, heads)
    dkv[...] = jnp.zeros_like(dkv)
    d_bias[...] = jnp.zeros_like(d_bias)

    @pl.loop(0, nc)
    def _(c):
        rows = pl.ds(pl.multiple_of((2 * c + 1) * ln, ln), ln)
        d_q[rows, :] = jnp.zeros((ln, heads * HEAD), BF)

    @pl.loop(0, 6)
    def _(qb):
        r0, r1, o0, o1, seq = block_rows(qb, half, ln)
        lo, hi = info[qb], info[6 + qb]
        sq = two_lanes(seg_row, slice(0, 1), r0, r1, hl)
        q, do, line, delta = [], [], [], []
        for h in range(heads):
            q.append(two(q_ref, r0, r1, hl, slice(128 * h, 128 * h + 128)))
            do.append(two(d_out, o0, o1, hl, slice(128 * h, 128 * h + 128)))
            line.append(two_lanes(lse, slice(h, h + 1), o0, o1, hl))
            turned = do[h].astype(F32).T[HEAD:, :]
            kept = two_lanes(ctx_t, slice(HEAD * h, HEAD * h + HEAD), o0, o1, hl)
            delta.append(jnp.sum(turned * kept, 0, keepdims=True))
        dqt[...] = jnp.zeros_like(dqt)

        @pl.loop(lo, hi)
        def _(j):
            rows = pl.ds(pl.multiple_of((2 * j + seq) * ln, ln), ln)
            keys = pl.ds(pl.multiple_of(j * ln, ln), ln)
            same = seg_col[rows, :] == sq
            for h in range(heads):
                kvh = kv[rows, 128 * h : 128 * h + 128]
                p = jnp.where(same, jnp.exp(dot_nt(kvh, q[h]) - line[h]), 0.0)
                ds = (p * (dot_nt(kvh, do[h]) - delta[h])).astype(BF)
                dkv[rows, 128 * h : 128 * h + 128] += dot_nn(ds, q[h]) + dot_nn(
                    p.astype(BF), do[h]
                )
                dqt[h] += dot_nn(kvt[seq * heads + h, :, keys], ds)

        turned = jnp.concatenate([dqt[h, :HEAD, :] for h in range(heads)], 0).T * 0.125
        d_bias[0:1, heads * 128 :] += jnp.sum(turned, 0, keepdims=True)
        low = turned.astype(BF)
        d_q[pl.ds(r0, hl), :] = low[:hl]
        d_q[pl.ds(r1, hl), :] = low[hl:]

    @pl.loop(0, 2 * nc)
    def _(c):
        rows = pl.ds(pl.multiple_of(c * ln, ln), ln)
        for h in range(heads):
            got = dkv[rows, 128 * h : 128 * h + 128]
            d_bias[0:1, 128 * h : 128 * h + 128] += jnp.sum(got, 0, keepdims=True)
            d_kv[rows, 128 * h : 128 * h + 128] = got.astype(BF)


def attend_back(info, q_ref, kv, d_out, seg_col, seg_row, lse, ctx_t, heads, ln, nc):
    rows = 3 * ln // 2 * nc
    vm = pl.BlockSpec(memory_space=pltpu.VMEM)
    return pl.pallas_call(
        functools.partial(attend_back_kernel, heads, ln, nc),
        out_shape=(
            jax.ShapeDtypeStruct((2 * nc * ln, heads * HEAD), BF),
            jax.ShapeDtypeStruct((2 * nc * ln, heads * 128), BF),
            jax.ShapeDtypeStruct((8, heads * (HEAD + 128)), F32),
        ),
        in_specs=[pl.BlockSpec(memory_space=pltpu.SMEM)] + [vm] * 7,
        out_specs=(vm, vm, vm),
        scratch_shapes=[
            pltpu.VMEM((2 * nc * ln, heads * 128), F32),
            pltpu.VMEM((2 * heads, 128, nc * ln), BF),
            pltpu.VMEM((heads, 128, ln), F32),
        ],
        compiler_params=pltpu.CompilerParams(vmem_limit_bytes=40 << 20),
        cost_estimate=pl.CostEstimate(
            flops=20 * heads * rows * nc * ln * 128,
            bytes_accessed=14 << 20,
            transcendentals=heads * rows * nc * ln,
        ),
        name="attend_back",
    )(info, q_ref, kv, d_out, seg_col, seg_row, lse, ctx_t)


MESH = pl.DeviceIdType.MESH


class Copies:
    def __init__(self, send, recv):
        self.send, self.recv, self.open = send, recv, []

    def make(self, i, src, dst, device, sent=None):
        return pltpu.make_async_remote_copy(
            src_ref=src,
            dst_ref=dst,
            send_sem=self.send.at[i if sent is None else sent],
            recv_sem=self.recv.at[i],
            device_id=device,
            device_id_type=MESH,
        )

    def start(self, i, parts, when=None, sent=None):
        number = (lambda: i) if not callable(i) else i

        def go(wait):
            copy = self.make(number(), *parts(), sent=sent)
            copy.wait_send() if wait else copy.start()

        self.run(go, when, False)
        self.open.append((go, when))

    def run(self, go, when, wait):
        if when is None:
            go(wait)
        else:

            @pl.when(when())
            def _():
                go(wait)

    def arrived(self, i, dst, device):
        self.make(i, dst, dst, device).wait_recv()

    def all_sent(self):
        for go, when in self.open:
            self.run(go, when, True)


def line_order(z, i):
    if i == 0:
        return z
    if i == 1:
        return jnp.where(z == 0, 1, z - 1)
    if i == 2:
        return jnp.where(z == 0, 2, jnp.where(z == 3, 1, z + 1))
    return jnp.where(z < 2, 3, 0)


def forward_kernel(
    heads,
    ln,
    tokens,
    segments,
    w_kinds,
    q_bias,
    v_bias,
    in_bias,
    w_o,
    w_i,
    w_b,
    cotangent,
    out_bias,
    gain_one,
    shift_one,
    back_bias,
    gain_two,
    shift_two,
    xt_out,
    q_out,
    kv_out,
    wh_out,
    g_b,
    g_i,
    output,
    lse,
    ctx_t,
    seg,
    d_ctx,
    g_o,
    d_first,
    small,
    x2,
    xt,
    wh,
    bh,
    q_scr,
    kv,
    s_scr,
    kvt,
    acc,
    segc,
    segr,
    context,
    w_src,
    o_src,
    seg2,
    w_head,
    b_head,
    b_unit,
    ctx_all,
    o_full,
    w_full,
    bu_full,
    x_own,
    c_own,
    n_one,
    r_one,
    low,
    low_t,
    tmp,
    total,
    active,
    slope,
    turn,
    d_low,
    gb_v,
    gi_v,
    out_low,
    g_sem,
    send,
    recv,
    local,
):
    d, c, z = (lax.axis_index(n) for n in ALL)
    nc = 4
    hl = ln // 2
    own = ln + hl
    half = z % 2
    wr = w_i.shape[0]
    units = w_i.shape[1]
    row = d * nc + c
    row_x, row_y, row_d = row ^ 4, row ^ 2, row ^ 6
    rc = Copies(send, recv)
    at_c = lambda k: (d, c ^ k, z)
    at_x = (1 - d, c, z)
    to_c = lambda k: (lambda: at_c(k))
    to_x = lambda: at_x
    at_z = lambda k: (d, c, z ^ k)
    across = (d, z, c)
    order = [line_order(z, i) for i in range(4)]
    number = iter(range(0, 400))
    four = lambda: [next(number) for _ in range(4)][0]
    local_number = iter(range(32))

    def copy_here(src, dst):
        copy = pltpu.make_async_copy(src, dst, local.at[next(local_number)])
        copy.start()
        return copy

    t_cols = lambda t: pl.ds(pl.multiple_of(t * units, 128), units)
    w_at = lambda r, t: w_full.at[:, r, :, t_cols(t)]
    o_at = lambda r, t: o_full.at[t, r]
    wh_at = lambda r: wh.at[pl.ds(pl.multiple_of(r * wr, wr), wr)]
    tok_at = lambda i: x2.at[pl.ds(2 * i, 2)]
    w_here = [copy_here(w_i, w_src.at[0]), copy_here(w_b, w_src.at[1]), copy_here(w_o, o_src)]
    tok_src = lambda s: tokens.at[(3 * z + 1) // 2 if s == 0 else 1 + 3 * (z // 2)]
    mine = [copy_here(tok_src(s), x2.at[2 * c + s]) for s in range(2)]
    half_rows = pl.ds(pl.multiple_of(half * hl, 128), hl)
    own_rows = [
        copy_here(part, dst)
        for src, to in ((tokens, x_own), (cotangent, c_own))
        for part, dst in (
            (src.at[(3 * z + 1) // 2], to.at[pl.ds(0, ln)]),
            (src.at[1 + 3 * (z // 2), half_rows], to.at[pl.ds(ln, hl)]),
        )
    ]
    here_sem = [local.at[next(local_number)] for _ in range(2)]
    here = [
        pltpu.make_async_copy(w_head, wh_at(row), here_sem[0]),
        pltpu.make_async_copy(b_head, bh, here_sem[1]),
    ]

    barrier = pltpu.get_barrier_semaphore()
    everyone = [at_c(k) for k in (1, 2, 3)] + [at_z(k) for k in (1, 2, 3)] + [at_x]
    for device in everyone:
        pl.semaphore_signal(barrier, inc=1, device_id=device, device_id_type=MESH)

    @pl.when(c != z)
    def _():
        pl.semaphore_signal(barrier, inc=1, device_id=across, device_id_type=MESH)

    seg2[...] = jnp.zeros_like(seg2)
    seg2[0:1, :] = segments[pl.ds((3 * z + 1) // 2, 1), :]
    seg2[1:2, :] = segments[pl.ds(1 + 3 * (z // 2), 1), :]
    wide = heads * 128
    b_head[...] = jnp.zeros_like(b_head)
    b_unit[...] = jnp.zeros_like(b_unit)
    qb = q_bias[...].reshape(1, heads * HEAD)
    vb = v_bias[...].reshape(1, heads * HEAD)
    for h in range(heads):
        cols = slice(HEAD * h, HEAD * h + HEAD)
        w_head[:, 128 * h : 128 * h + HEAD] = w_kinds[1, :, cols]
        w_head[:, 128 * h + HEAD : 128 * h + 128] = w_kinds[2, :, cols]
        b_head[0:1, 128 * h + HEAD : 128 * h + 128] = vb[:, cols]
    w_head[:, wide:] = w_kinds[0]
    b_head[0:1, wide:] = qb
    b_unit[0:1, :] = in_bias[...].reshape(1, units)
    seg_here = copy_here(seg2, seg.at[c])
    bu_here = copy_here(b_unit, bu_full.at[z])

    @pl.when(c == z)
    def _():
        for copy in here:
            copy.start()

    pl.semaphore_wait(barrier, len(everyone) + jnp.where(c != z, 1, 0))

    n_tf, n_wa, n_ba = (next(number) for _ in range(3))
    n_ty, n_tc = ([next(number) for _ in range(2)] for _ in range(2))
    not_here = lambda: c != z
    rc.start(n_wa, lambda: (w_head, wh_at(row), across), not_here)
    rc.start(n_ba, lambda: (b_head, bh, across), not_here)
    n_seg = four()
    for k in (1, 2, 3):
        rc.start(n_seg + k, lambda k=k: (seg2, seg.at[c], at_c(k)))

    class Line:
        def __init__(self, at):
            self.at = at
            self.n = [next(number) for _ in range(5)][0]

        def begin(self, src):
            rc.start(
                lambda: self.n + z,
                lambda: (src, self.at(z), (d, c, z + 1)),
                lambda: z < 3,
                self.n + 3,
            )
            rc.start(
                lambda: self.n + z,
                lambda: (src, self.at(z), (d, c, z - 1)),
                lambda: z > 0,
                self.n + 4,
            )

        def step(self, i):
            t = lambda: order[i]
            rc.arrived(self.n + t(), self.at(t()), (d, c, z))
            rc.start(
                lambda: self.n + t(),
                lambda: (
                    self.at(t()),
                    self.at(t()),
                    (d, c, jnp.where(t() < z, z + 1, z - 1)),
                ),
                lambda: jnp.where(t() < z, z < 3, z > 0),
                self.n + i - 1,
            )

    n_hz = four()
    full_at = (
        lambda r, t: w_full.at[0, r, :, t_cols(t)],
        o_at,
        lambda r, t: w_full.at[1, r, :, t_cols(t)],
    )
    sources = (w_src.at[0], o_src, w_src.at[1])
    lines = [Line(lambda t, w=w: full_at[w](row, t)) for w in range(3)]
    n_hx = four()
    n_x, n_y, n_d = ([four() for _ in range(3)] for _ in range(3))
    n_c = [[four() for _ in range(3)] for _ in range(4)]

    groups = [(0, 1), (2,)]
    over_y = ((0, 2), (1, 0))

    def pass_on(n, g, i, r, device, first=False):
        t = lambda: order[i]
        for w in groups[g]:
            rc.start(
                lambda w=w: n[w] + t(),
                lambda w=w: (
                    sources[w] if first and i == 0 else full_at[w](r, t()),
                    full_at[w](r, t()),
                    device(),
                ),
                None,
                n[w] + i,
            )

    def came(n, g, i, r, device):
        t = order[i]
        for w in groups[g]:
            rc.arrived(n[w] + t, full_at[w](r, t), device)

    def own_send(g):
        pass_on(n_x, g, 0, row, to_x, True)
        pass_on(n_c[0], g, 0, row, to_c(1), True)

    def line_begin(g):
        for w in groups[g]:
            lines[w].begin(sources[w])

    def y_send(g, i):
        pass_on(n_y, g, i, row, to_c(2), True)

    def line_step(g, i):
        for w in groups[g]:
            lines[w].step(i)
        pass_on(n_x, g, i, row, to_x)
        pass_on(n_c[0], g, i, row, to_c(1))

    def from_x(g, i):
        came(n_x, g, i, row_x, at_x)
        if (g, i) in over_y:
            pass_on(n_d, g, i, row_x, to_c(2))
        pass_on(n_c[1], g, i, row_x, to_c(1))

    def from_y(g, i):
        came(n_y, g, i, row_y, at_c(2))
        if (g, i) not in over_y:
            pass_on(n_d, g, i, row_y, to_x)
        pass_on(n_c[2], g, i, row_y, to_c(1))

    def from_corner(g, i):
        came(n_d, g, i, row_d, at_x)
        pass_on(n_c[3], g, i, row_d, to_c(1))

    head_at = lambda t: wh_at(d * nc + t)
    n_bu = four()
    n_ctx = four()
    ctx_at = lambda i: context.at[pl.ds(pl.multiple_of(i * own, 128), own)]

    def head_send():
        @pl.when(c != z)
        def _():
            rc.arrived(n_wa, wh_at(d * nc + z), across)
            rc.arrived(n_ba, bh, across)

        @pl.when(c == z)
        def _():
            for copy in here:
                copy.wait()

        for k in (1, 2, 3):
            rc.start(n_hz + k, lambda k=k: (head_at(z), head_at(z), at_z(k)))
        rc.start(n_hx, lambda: (head_at(z), head_at(z), at_x))
        for k in (1, 2, 3):
            rc.start(n_bu + k, lambda k=k: (b_unit, bu_full.at[z], at_z(k)))

    def head_pass(k):
        rc.arrived(n_hz + k, head_at(z ^ k), at_z(k))
        rc.start(n_hx + k, lambda: (head_at(z ^ k), head_at(z ^ k), at_x))

    def token_pass():
        for s in range(2):
            rc.arrived(n_ty[s], x2.at[2 * (c ^ 2) + s], at_c(2))
        rc.start(n_tf, lambda: (tok_at(c ^ 2), tok_at(c ^ 2), at_c(1)))

    def context_send():
        for k in (2, 3, 1):
            rc.start(n_ctx + k, lambda k=k: (ctx_at(c ^ k), ctx_all.at[c], at_c(k)))

    def segments_done():
        for k in (1, 2, 3):
            rc.arrived(n_seg + k, seg.at[c ^ k], at_c(k))
        seg_here.wait()
        for i in range(nc):
            for s in range(2):
                line = seg[i, s : s + 1, :].astype(F32)
                segr[2 * i + s, 0:1, :] = line
                segc[2 * i + s] = jnp.broadcast_to(line, (128, ln)).T

    step, thin = 128, 64
    width = x_own.shape[1]
    w_of = lambda which, t: w_full[which, :, :, t_cols(t)].reshape(width, units)
    w_out_of = lambda g: o_full[g].reshape(width, w_o.shape[1])
    out_bias, gain_one, shift_one, back_bias, gain_two, shift_two = (
        a[...].reshape(1, width)
        for a in (out_bias, gain_one, shift_one, back_bias, gain_two, shift_two)
    )

    def chunks(body, size=step):
        @pl.loop(0, own // size)
        def _(i):
            body(pl.ds(pl.multiple_of(i * size, size), size))

    mean = lambda v: jnp.mean(v, -1, keepdims=True)
    add = lambda i, v: small.__setitem__(
        (slice(i, i + 1), slice(None)), small[i : i + 1, :] + jnp.sum(v, 0, keepdims=True)
    )
    small[...] = jnp.zeros_like(small)

    def block(qb):
        r0, r1, o0, o1, seq = block_rows(qb, half, ln)
        b0 = jnp.where(qb < 4, qb, 2 * (qb - 4))
        b1 = jnp.where(qb < 4, qb, 2 * (qb - 4) + 1)
        s0 = pl.multiple_of(jnp.where(qb < 4, 0, hl * half), 128)
        s1 = pl.multiple_of(jnp.where(qb < 4, hl, hl * half), 128)
        sq = jnp.concatenate(
            [
                segr[2 * b0 + seq, 0:1, pl.ds(s0, hl)],
                segr[2 * b1 + seq, 0:1, pl.ds(s1, hl)],
            ],
            1,
        )
        q = [two(q_scr, r0, r1, hl, slice(128 * h, 128 * h + 128)) for h in range(heads)]

        def score(j, peaks):
            rows = pl.ds(pl.multiple_of((2 * j + seq) * ln, ln), ln)
            key_seg = segc[2 * j + seq]
            same = jnp.concatenate([key_seg, key_seg], 1) == sq
            new = []
            for h in range(heads):
                s = dot_nt(kv[rows, 128 * h : 128 * h + 128], q[h])
                s = jnp.where(same, s, NEG)
                s_scr[h, pl.ds(pl.multiple_of(j * ln, ln), ln), :] = s
                new.append(jnp.maximum(peaks[h], jnp.max(s, 0, keepdims=True)))
            return tuple(new)

        peaks = lax.fori_loop(
            0, nc, score, tuple(jnp.full((1, ln), NEG, F32) for _ in range(heads))
        )
        acc[...] = jnp.zeros_like(acc)

        def collect(j, sums):
            keys = pl.ds(pl.multiple_of(j * ln, ln), ln)
            new = []
            for h in range(heads):
                p = jnp.exp(s_scr[h, keys, :] - peaks[h])
                new.append(sums[h] + jnp.sum(p, 0, keepdims=True))
                acc[h] += dot_nn(kvt[seq * heads + h, :, keys], p.astype(BF))
            return tuple(new)

        sums = lax.fori_loop(
            0, nc, collect, tuple(jnp.zeros((1, ln), F32) for _ in range(heads))
        )
        whole = []
        for h in range(heads):
            one = acc[h] / sums[h]
            whole.append(one)
            line = peaks[h] + jnp.log(sums[h])
            for part, at in ((0, o0), (hl, o1)):
                ctx_t[HEAD * h : HEAD * h + HEAD, pl.ds(at, hl)] = one[:, part : part + hl]
                lse[h : h + 1, pl.ds(at, hl)] = line[:, part : part + hl]
        turned = jnp.concatenate(whole, 0).T.astype(BF)
        context[pl.ds(o0, hl), :] = turned[:hl]
        context[pl.ds(o1, hl), :] = turned[hl:]

    for copy in w_here:
        copy.wait()
    own_here = [
        copy_here(sources[w], full_at[w](row, z)) for w in range(3)
    ]
    q_scr[...] = jnp.zeros_like(q_scr)
    line_begin(0)
    for s in range(2):
        rc.start(n_ty[s], lambda s=s: (tok_src(s), x2.at[2 * c + s], at_c(2)))
        rc.start(n_tc[s], lambda s=s: (tok_src(s), x2.at[2 * c + s], at_c(1)))
    own_send(0)
    line_begin(1)
    head_send()
    line_step(0, 1)
    y_send(0, 0)
    y_send(0, 1)
    line_step(1, 1)
    head_pass(2)
    head_pass(1)
    line_step(0, 2)
    head_pass(3)
    y_send(1, 1)
    from_x(0, 1)
    segments_done()
    token_pass()
    line_step(1, 2)
    from_y(0, 0)
    y_send(1, 2)
    own_send(1)
    from_x(0, 0)
    line_step(0, 3)
    y_send(0, 2)
    y_send(0, 3)
    from_x(0, 2)
    y_send(1, 0)
    from_y(0, 1)
    for t in range(4):
        rc.arrived(n_hx + t, wh_at((1 - d) * nc + (z ^ t)), at_x)
    for s in range(2):
        mine[s].wait()
        rc.arrived(n_tc[s], x2.at[2 * (c ^ 1) + s], at_c(1))
    rc.arrived(n_tf, tok_at(c ^ 3), at_c(1))
    wh_here = copy_here(wh, wh_out)

    @pl.loop(0, 2 * nc)
    def _(i):
        x = x2[i]
        rows = pl.ds(pl.multiple_of(i * ln, ln), ln)
        xt[:, rows] = x.T
        got = (dot_nn(x, wh[:, :wide]) + bh[0:1, :wide]).astype(BF)
        kv[rows, :] = got
        qp = ((dot_nn(x, wh[:, wide:]) + bh[0:1, wide:]).astype(BF).astype(F32) * 0.125).astype(BF)
        for h in range(heads):
            q_scr[rows, 128 * h : 128 * h + HEAD] = qp[:, HEAD * h : HEAD * h + HEAD]

    x_here = copy_here(xt, xt_out)
    q_here = copy_here(q_scr, q_out)
    kv_here = copy_here(kv, kv_out)
    @pl.loop(0, nc)
    def _(j):
        for s in range(2):
            rows = pl.ds(pl.multiple_of((2 * j + s) * ln, ln), ln)
            for h in range(heads):
                kvt[s * heads + h, :, pl.ds(pl.multiple_of(j * ln, ln), ln)] = kv[
                    rows, 128 * h : 128 * h + 128
                ].T[HEAD:]


    @pl.loop(0, 6)
    def _(qb):
        block(qb)

        @pl.when(qb == 2)
        def _():
            from_y(1, 2)
            line_step(1, 3)

        @pl.when(qb == 3)
        def _():
            y_send(1, 3)

    context_send()
    ctx_here = copy_here(ctx_at(c), ctx_all.at[c])
    from_x(1, 2)
    from_x(1, 0)
    from_y(0, 2)
    from_y(0, 3)
    from_corner(0, 2)
    from_x(1, 1)
    from_y(1, 0)
    from_x(0, 3)
    from_x(1, 3)
    from_y(1, 3)
    from_corner(1, 2)
    from_corner(0, 0)
    from_corner(0, 1)
    from_y(1, 1)
    from_corner(0, 3)
    for k in (1, 2, 3):
        rc.arrived(n_ctx + k, ctx_all.at[c ^ k], at_c(k))
    for n, r in zip(n_c, (row, row_x, row_y, row_d)):
        for i in range(4):
            came(n, 0, i, r ^ 1, at_c(1))
    for copy in own_here + [ctx_here, bu_here] + own_rows:
        copy.wait()
    for k in (1, 2, 3):
        rc.arrived(n_bu + k, bu_full.at[z ^ k], at_z(k))

    tmp[...] = dot_nt(ctx_all[0], w_out_of(0))
    for g in range(1, nc):
        tmp[...] += dot_nt(ctx_all[g], w_out_of(g))

    def norm_one(r):
        value = x_own[r, :].astype(F32) + (tmp[r, :] + out_bias)
        centered = value - mean(value)
        rstd = lax.rsqrt(mean(centered * centered) + 1e-12)
        normal = centered * rstd
        n_one[r, :] = normal
        r_one[r, :] = jnp.broadcast_to(rstd, (step, 128))
        got = normal * gain_one + shift_one
        low[r, :] = got.astype(BF)
        total[r, :] = got + back_bias

    chunks(norm_one)
    low_t[...] = low[...].T

    from_corner(1, 3)
    @pl.loop(0, 4)
    def _(t):
        tmp[...] = dot_nn(low[...], w_of(0, t)) + bu_full[pl.ds(t, 1), 0, :]

        def gelu(r):
            u = tmp[r, :]
            cdf = 0.5 * (1.0 + lax.erf(u * math.sqrt(0.5)))
            active[r, t_cols(t)] = (u * cdf).astype(BF)
            slope[r, t_cols(t)] = cdf + u * jnp.exp(-0.5 * u * u) * (
                1.0 / math.sqrt(2.0 * math.pi)
            )

        chunks(gelu, thin)

        @pl.when(t == 1)
        def _():
            from_corner(1, 1)
            from_corner(1, 0)

    for n, r in zip(n_c, (row, row_x, row_y, row_d)):
        for i in range(4):
            came(n, 1, i, r ^ 1, at_c(1))

    @pl.loop(0, 4)
    def _(t):
        total[...] += dot_nt(active[:, t_cols(t)], w_of(1, t))

    def norm_two(r):
        value = total[r, :]
        centered = value - mean(value)
        rstd = lax.rsqrt(mean(centered * centered) + 1e-12)
        normal = centered * rstd
        out_low[r, :] = (normal * gain_two + shift_two).astype(BF)
        grad = c_own[r, :].astype(F32)
        add(4, grad * normal)
        add(5, grad)
        scaled = grad * gain_two
        got = rstd * (scaled - mean(scaled) - normal * mean(scaled * normal))
        add(3, got)
        d_low[r, :] = got.astype(BF)
        total[r, :] = got

    chunks(norm_two)
    whole_at = lambda t: output.at[(3 * t + 1) // 2]
    shared_at = lambda t: output.at[
        1 + 3 * (t // 2), pl.ds(pl.multiple_of((t % 2) * hl, 128), hl)
    ]
    pieces = ((whole_at, out_low.at[pl.ds(0, ln)]), (shared_at, out_low.at[pl.ds(ln, hl)]))
    n_out = four()
    out_here = [copy_here(src, at(z)) for at, src in pieces]
    for k, (at, src) in enumerate(pieces):
        rc.start(
            n_out + 2 * k,
            lambda at=at, src=src: (src, at(z), (d, c, z + 1)),
            lambda: z < 3,
        )
        rc.start(
            n_out + 2 * k + 1,
            lambda at=at, src=src: (src, at(z), (d, c, z - 1)),
            lambda: z > 0,
        )
    turn[...] = d_low[...].T

    @pl.loop(0, 4)
    def _(t):
        gb_v[:, t_cols(t)] = dot_nn(turn[...], active[:, t_cols(t)]).astype(BF)
        pltpu.make_async_copy(gb_v.at[:, t_cols(t)], g_b.at[:, t_cols(t)], g_sem.at[0, t]).start()
        tmp[...] = dot_nn(d_low[...], w_of(1, t))

        def inner_back(r):
            got = tmp[r, :] * slope[r, t_cols(t)]
            at = pl.ds(6 + t, 1)
            small[at, :] += jnp.sum(got, 0, keepdims=True)
            active[r, t_cols(t)] = got.astype(BF)

        chunks(inner_back, thin)
        gi_v[:, t_cols(t)] = dot_nn(low_t[...], active[:, t_cols(t)]).astype(BF)
        pltpu.make_async_copy(gi_v.at[:, t_cols(t)], g_i.at[:, t_cols(t)], g_sem.at[1, t]).start()
        total[...] += dot_nt(active[:, t_cols(t)], w_of(0, t))

    def norm_one_back(r):
        grad = total[r, :]
        normal = n_one[r, :]
        add(1, grad * normal)
        add(2, grad)
        scaled = grad * gain_one
        got = r_one[r, 0:1] * (scaled - mean(scaled) - normal * mean(scaled * normal))
        d_first[r, :] = got
        add(0, got)
        d_low[r, :] = got.astype(BF)

    chunks(norm_one_back)
    turn[...] = d_low[...].T
    for g in range(nc):
        d_ctx[g] = dot_nn(d_low[...], w_out_of(g)).astype(BF)
        g_o[g] = dot_nn(turn[...], ctx_all[g]).astype(BF)
    for t in range(4):
        pltpu.make_async_copy(gb_v.at[:, t_cols(t)], g_b.at[:, t_cols(t)], g_sem.at[0, t]).wait()
        pltpu.make_async_copy(gi_v.at[:, t_cols(t)], g_i.at[:, t_cols(t)], g_sem.at[1, t]).wait()
    for copy in (x_here, wh_here, q_here, kv_here):
        copy.wait()
    for copy in out_here:
        copy.wait()

    @pl.when(z > 0)
    def _():
        for k, (at, _) in enumerate(pieces):
            rc.arrived(n_out + 2 * k, at(z - 1), at_z(1))

    @pl.when(z < 3)
    def _():
        for k, (at, _) in enumerate(pieces):
            rc.arrived(n_out + 2 * k + 1, at(z + 1), at_z(1))

    rc.all_sent()


def forward(
    tokens, segments, w_kinds, q_bias, v_bias, in_bias, w_o, w_i, w_b, cotangent, vectors, heads
):
    ln, width = tokens.shape[1:]
    wr, units = w_i.shape
    group = w_o.shape[1]
    nc, nt, nr = 4, 4, 8
    own = 3 * ln // 2
    rows = own * nc
    hb = pl.BlockSpec(memory_space=pltpu.HBM)
    vm = pl.BlockSpec(memory_space=pltpu.VMEM)
    sds = jax.ShapeDtypeStruct
    return pl.pallas_call(
        functools.partial(forward_kernel, heads, ln),
        out_shape=(
            sds((width, 2 * nc * ln), BF),
            sds((2 * nc * ln, heads * 128), BF),
            sds((2 * nc * ln, heads * 128), BF),
            sds((nr * wr, 3 * group), BF),
            sds((width, nt * units), BF),
            sds((width, nt * units), BF),
            sds(tokens.shape, BF),
            sds((8, rows), F32),
            sds((group, rows), F32),
            sds((nc, 8, ln), jnp.int32),
            sds((nc, own, group), BF),
            sds((nt, width, group), BF),
            sds((own, width), F32),
            sds((16, width), F32),
        ),
        in_specs=[hb] + [vm] * 5 + [hb] * 4 + [vm] * 6,
        out_specs=(hb,) * 7 + (vm,) * 7,
        scratch_shapes=[
            pltpu.VMEM((2 * nc, ln, width), BF),
            pltpu.VMEM((width, 2 * nc * ln), BF),
            pltpu.VMEM((nr * wr, 3 * group), BF),
            pltpu.VMEM((8, 3 * group), F32),
            pltpu.VMEM((2 * nc * ln, heads * 128), BF),
            pltpu.VMEM((2 * nc * ln, heads * 128), BF),
            pltpu.VMEM((heads, nc * ln, ln), F32),
            pltpu.VMEM((2 * heads, HEAD, nc * ln), BF),
            pltpu.VMEM((heads, HEAD, ln), F32),
            pltpu.VMEM((2 * nc, ln, 128), F32),
            pltpu.VMEM((2 * nc, 8, ln), F32),
            pltpu.VMEM((rows, group), BF),
            pltpu.VMEM((2, wr, units), BF),
            pltpu.VMEM((wr, group), BF),
            pltpu.VMEM((8, ln), jnp.int32),
            pltpu.VMEM((wr, 3 * group), BF),
            pltpu.VMEM((8, 3 * group), F32),
            pltpu.VMEM((8, units), F32),
            pltpu.VMEM((nc, own, group), BF),
            pltpu.VMEM((nt, nr, wr, group), BF),
            pltpu.VMEM((2, nr, wr, nt * units), BF),
            pltpu.VMEM((nt, 8, units), F32),
            pltpu.VMEM((own, width), BF),
            pltpu.VMEM((own, width), BF),
            pltpu.VMEM((own, width), F32),
            pltpu.VMEM((own, 128), F32),
            pltpu.VMEM((own, width), BF),
            pltpu.VMEM((width, own), BF),
            pltpu.VMEM((own, width), F32),
            pltpu.VMEM((own, width), F32),
            pltpu.VMEM((own, nt * units), BF),
            pltpu.VMEM((own, nt * units), F32),
            pltpu.VMEM((width, own), BF),
            pltpu.VMEM((own, width), BF),
            pltpu.VMEM((width, nt * units), BF),
            pltpu.VMEM((width, nt * units), BF),
            pltpu.VMEM((own, width), BF),
            pltpu.SemaphoreType.DMA((2, 4)),
            pltpu.SemaphoreType.DMA((150,)),
            pltpu.SemaphoreType.DMA((150,)),
            pltpu.SemaphoreType.DMA((32,)),
        ],
        compiler_params=pltpu.CompilerParams(
            vmem_limit_bytes=60 << 20, collective_id=0, has_side_effects=True
        ),
        name="forward",
    )(tokens, segments, w_kinds, q_bias, v_bias, in_bias, w_o, w_i, w_b, cotangent, *vectors)


def middle_kernel(
    ln,
    tokens,
    cotangent,
    ctx_all,
    w_o,
    w_ib,
    b_in,
    out_bias,
    gain_one,
    shift_one,
    back_bias,
    gain_two,
    shift_two,
    d_ctx,
    g_b,
    g_i,
    g_o,
    out_low,
    d_first,
    small,
    x_own,
    c_own,
    w_v,
    ctx_v,
    w_ov,
    n_one,
    r_one,
    normed,
    low,
    low_t,
    tmp,
    acc,
    active,
    slope,
    n_two,
    d_sec,
    d_low,
    gb_v,
    gi_v,
    w_sem,
    g_sem,
    sem,
):
    z = lax.axis_index("tp")
    hl = ln // 2
    own = ln + hl
    blocks, _, group = ctx_all.shape
    width = x_own.shape[1]
    units = w_v.shape[2] // 4
    step, thin = 128, 64
    out_bias, gain_one, shift_one, back_bias, gain_two, shift_two = (
        a[...].reshape(1, width)
        for a in (out_bias, gain_one, shift_one, back_bias, gain_two, shift_two)
    )
    half_rows = pl.ds(pl.multiple_of((z % 2) * hl, 128), hl)
    first_rows = []
    for i, (src, dst) in enumerate(((tokens, x_own), (cotangent, c_own))):
        for j, (a, b) in enumerate(
            (
                (src.at[(3 * z + 1) // 2], dst.at[pl.ds(0, ln)]),
                (src.at[1 + 3 * (z // 2), half_rows], dst.at[pl.ds(ln, hl)]),
            )
        ):
            first_rows.append(pltpu.make_async_copy(a, b, sem.at[2 * i + j]))
    first_rows.append(pltpu.make_async_copy(ctx_all, ctx_v, sem.at[4]))
    first_rows.append(pltpu.make_async_copy(w_o, w_ov, sem.at[5]))
    for copy in first_rows:
        copy.start()
    t_cols = lambda t: pl.ds(pl.multiple_of(t * units, 128), units)

    def weight(which, t):
        return pltpu.make_async_copy(
            w_ib.at[which, :, t_cols(t)], w_v.at[which, :, t_cols(t)], w_sem.at[which, t]
        )

    for t in range(4):
        for which in range(2):
            weight(which, t).start()
    for copy in first_rows:
        copy.wait()

    def chunks(body, size=step):
        @pl.loop(0, own // size)
        def _(i):
            body(pl.ds(pl.multiple_of(i * size, size), size))

    mean = lambda v: jnp.mean(v, -1, keepdims=True)
    add = lambda i, v: small.__setitem__(
        (slice(i, i + 1), slice(None)), small[i : i + 1, :] + jnp.sum(v, 0, keepdims=True)
    )
    small[...] = jnp.zeros_like(small)

    tmp[...] = dot_nt(ctx_v[0], w_ov[0])
    for g in range(1, blocks):
        tmp[...] += dot_nt(ctx_v[g], w_ov[g])

    def norm_one(r):
        value = x_own[r, :].astype(F32) + (tmp[r, :] + out_bias)
        centered = value - mean(value)
        rstd = lax.rsqrt(mean(centered * centered) + 1e-12)
        normal = centered * rstd
        n_one[r, :] = normal
        r_one[r, :] = jnp.broadcast_to(rstd, (step, 128))
        got = normal * gain_one + shift_one
        normed[r, :] = got
        low[r, :] = got.astype(BF)
        acc[r, :] = got + back_bias

    chunks(norm_one)
    low_t[...] = low[...].T

    @pl.loop(0, 4)
    def _(t):
        weight(0, t).wait()
        weight(1, t).wait()
        tmp[...] = dot_nn(low[...], w_v[0, :, t_cols(t)]) + b_in[pl.ds(t, 1), 0, :]

        def gelu(r):
            u = tmp[r, :]
            cdf = 0.5 * (1.0 + lax.erf(u * math.sqrt(0.5)))
            active[r, t_cols(t)] = (u * cdf).astype(BF)
            slope[r, t_cols(t)] = cdf + u * jnp.exp(-0.5 * u * u) * (
                1.0 / math.sqrt(2.0 * math.pi)
            )

        chunks(gelu, thin)
        acc[...] += dot_nt(active[:, t_cols(t)], w_v[1, :, t_cols(t)])

    def norm_two(r):
        value = acc[r, :]
        centered = value - mean(value)
        rstd = lax.rsqrt(mean(centered * centered) + 1e-12)
        normal = centered * rstd
        out_low[r, :] = (normal * gain_two + shift_two).astype(BF)
        grad = c_own[r, :].astype(F32)
        add(4, grad * normal)
        add(5, grad)
        scaled = grad * gain_two
        got = rstd * (scaled - mean(scaled) - normal * mean(scaled * normal))
        d_sec[r, :] = got
        add(3, got)
        d_low[r, :] = got.astype(BF)
        acc[r, :] = got

    chunks(norm_two)
    n_two[...] = d_low[...].T

    @pl.loop(0, 4)
    def _(t):
        gb_v[:, t_cols(t)] = dot_nn(n_two[...], active[:, t_cols(t)]).astype(BF)
        pltpu.make_async_copy(gb_v.at[:, t_cols(t)], g_b.at[:, t_cols(t)], g_sem.at[0, t]).start()
        tmp[...] = dot_nn(d_low[...], w_v[1, :, t_cols(t)])

        def inner_back(r):
            got = tmp[r, :] * slope[r, t_cols(t)]
            at = pl.ds(6 + t, 1)
            small[at, :] += jnp.sum(got, 0, keepdims=True)
            active[r, t_cols(t)] = got.astype(BF)

        chunks(inner_back, thin)
        gi_v[:, t_cols(t)] = dot_nn(low_t[...], active[:, t_cols(t)]).astype(BF)
        pltpu.make_async_copy(gi_v.at[:, t_cols(t)], g_i.at[:, t_cols(t)], g_sem.at[1, t]).start()
        acc[...] += dot_nt(active[:, t_cols(t)], w_v[0, :, t_cols(t)])

    def norm_one_back(r):
        grad = acc[r, :]
        normal = n_one[r, :]
        add(1, grad * normal)
        add(2, grad)
        scaled = grad * gain_one
        got = r_one[r, 0:1] * (scaled - mean(scaled) - normal * mean(scaled * normal))
        d_first[r, :] = got
        add(0, got)
        d_low[r, :] = got.astype(BF)

    chunks(norm_one_back)
    n_two[...] = d_low[...].T
    for g in range(blocks):
        d_ctx[g] = dot_nn(d_low[...], w_ov[g]).astype(BF)
        g_o[g] = dot_nn(n_two[...], ctx_v[g]).astype(BF)
    for t in range(4):
        pltpu.make_async_copy(gb_v.at[:, t_cols(t)], g_b.at[:, t_cols(t)], g_sem.at[0, t]).wait()
        pltpu.make_async_copy(gi_v.at[:, t_cols(t)], g_i.at[:, t_cols(t)], g_sem.at[1, t]).wait()


def middle(tokens, cotangent, ctx_all, w_o, w_ib, b_in, vectors):
    blocks, own, group = ctx_all.shape
    ln, width = tokens.shape[1:]
    all_units = w_ib.shape[2]
    hb = pl.BlockSpec(memory_space=pltpu.HBM)
    vm = pl.BlockSpec(memory_space=pltpu.VMEM)
    sds = jax.ShapeDtypeStruct
    v = pltpu.VMEM
    return pl.pallas_call(
        functools.partial(middle_kernel, ln),
        out_shape=(
            sds((blocks, own, group), BF),
            sds((width, all_units), BF),
            sds((width, all_units), BF),
            sds((blocks, width, group), BF),
            sds((own, width), BF),
            sds((own, width), F32),
            sds((16, width), F32),
        ),
        in_specs=[hb] * 5 + [vm] * 7,
        out_specs=(vm, hb, hb, vm, vm, vm, vm),
        scratch_shapes=[
            v((own, width), BF),
            v((own, width), BF),
            v((2, width, all_units), BF),
            v((blocks, own, group), BF),
            v((blocks, width, group), BF),
            v((own, width), F32),
            v((own, 128), F32),
            v((own, width), F32),
            v((own, width), BF),
            v((width, own), BF),
            v((own, width), F32),
            v((own, width), F32),
            v((own, all_units), BF),
            v((own, all_units), F32),
            v((width, own), BF),
            v((own, width), F32),
            v((own, width), BF),
            v((width, all_units), BF),
            v((width, all_units), BF),
            pltpu.SemaphoreType.DMA((2, 4)),
            pltpu.SemaphoreType.DMA((2, 4)),
            pltpu.SemaphoreType.DMA((6,)),
        ],
        compiler_params=pltpu.CompilerParams(vmem_limit_bytes=60 << 20),
        cost_estimate=pl.CostEstimate(
            flops=2 * own * width * (6 * all_units + 3 * width),
            bytes_accessed=24 << 20,
            transcendentals=2 * own * all_units,
        ),
        name="middle",
    )(tokens, cotangent, ctx_all, w_o, w_ib, b_in, *vectors)


def add_into(dst, other, rows):
    @pl.loop(0, rows // 16)
    def _(i):
        at = pl.ds(pl.multiple_of(i * 16, 16), 16)
        for a, b in zip(dst, other):
            a[at, :] = (a[at, :].astype(F32) + b[at, :].astype(F32)).astype(a.dtype)


def backward_kernel(
    heads,
    ln,
    d_ctx,
    g_b,
    g_i,
    g_o,
    out_in,
    d_first,
    small_in,
    q_in,
    kv_in,
    xt_in,
    wh_in,
    lse,
    ctx_t,
    seg,
    output,
    d_tokens,
    gf_b,
    gf_i,
    gf_o,
    gf_h,
    small,
    bias,
    q_scr,
    kv,
    xt,
    wh,
    d_got,
    d_o,
    kvt,
    dkv,
    dqt,
    d_proj,
    segc,
    segr,
    part,
    got_c,
    got_y,
    got_z,
    send_y,
    send_z,
    mine,
    done,
    o_b,
    o_i,
    o_o,
    r_b,
    r_i,
    r_o,
    x_b,
    x_i,
    x_o,
    y_b,
    y_i,
    y_o,
    z_b,
    z_i,
    z_o,
    acc_h,
    o_h,
    x_h,
    z_h,
    send_h,
    small_got,
    bias_sum,
    bias_got,
    h_got,
    bias_fin,
    send,
    recv,
    local,
):
    d, c, z = (lax.axis_index(n) for n in ALL)
    nc = 4
    hl = ln // 2
    own = ln + hl
    half = z % 2
    core, y = c % 2, c // 2
    wr = gf_b.shape[0]
    units = gf_b.shape[1]
    width = d_first.shape[1]
    wide = heads * 128
    rc = Copies(send, recv)
    at_c = lambda k: (d, c ^ k, z)
    at_x = (1 - d, c, z)
    at_z = lambda k: (d, c, z ^ k)
    across = (d, z, c)

    barrier = pltpu.get_barrier_semaphore()
    everyone = [at_c(k) for k in (1, 2, 3)] + [at_z(k) for k in (1, 2, 3)] + [at_x]
    for device in everyone:
        pl.semaphore_signal(barrier, inc=1, device_id=device, device_id_type=MESH)

    @pl.when(c != z)
    def _():
        pl.semaphore_signal(barrier, inc=1, device_id=across, device_id_type=MESH)

    pl.semaphore_wait(barrier, len(everyone) + jnp.where(c != z, 1, 0))

    number = iter(range(200))
    local_number = iter(range(40))

    def copy_here(src, dst):
        copy = pltpu.make_async_copy(src, dst, local.at[next(local_number)])
        copy.start()
        return copy

    flat = lambda ref: (lambda xy, h: (ref.at[xy, :, pl.ds(1536 * h, 1536)],))
    weights = []
    for own_b, got_b, x_buf, y_buf, z_buf, grad, final, is_o in (
        (o_b, r_b, x_b, y_b, z_b, g_b, gf_b, False),
        (o_i, r_i, x_i, y_i, z_i, g_i, gf_i, False),
        (o_o, r_o, x_o, y_o, z_o, g_o, gf_o, True),
    ):
        n = [next(number) for _ in range(12)]
        weights.append((own_b, got_b, x_buf, y_buf, z_buf, grad, final, is_o, n))
    half_units = 2 * units

    def of_core(w, which):
        grad, is_o = w[5], w[7]
        return grad.at[:, :, which] if is_o else grad.at[:, which]

    def part_of(w, xy, h):
        if w[7]:
            return w[0].at[pl.ds(2 * h, 2), xy]
        return w[0].at[xy, :, pl.ds(half_units * h, half_units)]

    def views(w, xy, h):
        if w[7]:
            return [w[0].at[2 * h, xy], w[0].at[2 * h + 1, xy]]
        return [w[0].at[xy, :, pl.ds(half_units * h, half_units)]]

    def buf_views(w, ref, i):
        return [ref.at[i, 0], ref.at[i, 1]] if w[7] else [ref.at[i]]

    def unit_at(w, t):
        xy = 2 * d + y
        if w[7]:
            return w[0].at[t, xy]
        return w[0].at[xy, :, pl.ds(pl.multiple_of(t * units, 128), units)]

    w_here = [copy_here(of_core(w, core), w[0]) for w in weights]
    blk = lambda x_, y_: 2 * x_ + y_

    def w_core_send(w):
        rc.start(w[8][0], lambda: (of_core(w, 1 - core), w[1], at_c(1)))

    def w_core_add(i):
        w = weights[i]
        w_here[i].wait()
        rc.arrived(w[8][0], w[1], at_c(1))

        @pl.loop(0, 4)
        def _(xy):
            if w[7]:
                add_into([w[0].at[t, xy] for t in range(4)], [w[1].at[t, xy] for t in range(4)], wr)
            else:
                add_into([w[0].at[xy]], [w[1].at[xy]], wr)

        n = w[8]
        for j in range(2):
            rc.start(n[1 + j], lambda j=j: (part_of(w, blk(1 - d, j), 0), w[2].at[j], at_x))
            rc.start(n[3 + j], lambda j=j: (part_of(w, blk(j, 1 - y), 1), w[3].at[j], at_c(2)))

    def w_plane(i):
        w = weights[i]
        n = w[8]
        for j in range(2):
            rc.arrived(n[1 + j], w[2].at[j], at_x)
        for j in range(2):
            add_into(views(w, blk(d, j), 0), buf_views(w, w[2], j), wr)
        rc.start(n[5], lambda: (part_of(w, blk(d, 1 - y), 0), w[3].at[2], at_c(2)))
        for j in range(2):
            rc.arrived(n[3 + j], w[3].at[j], at_c(2))
        for j in range(2):
            add_into(views(w, blk(j, y), 1), buf_views(w, w[3], j), wr)
        rc.start(n[6], lambda: (part_of(w, blk(1 - d, y), 1), w[2].at[2], at_x))

    def w_corner(i):
        w = weights[i]
        n = w[8]
        rc.arrived(n[5], w[3].at[2], at_c(2))
        add_into(views(w, blk(d, y), 0), buf_views(w, w[3], 2), wr)
        rc.arrived(n[6], w[2].at[2], at_x)
        add_into(views(w, blk(d, y), 1), buf_views(w, w[2], 2), wr)
        for t in (0, 1, 2):
            chain_send(w, t, 3)
        for t in (3, 2, 1):
            chain_send(w, t, 0)

    def chain_send(w, t, at):
        to = at + 1 if t > at else at - 1
        slot = 4 if to == t and t > at else t
        n = w[8]
        rc.start(
            n[7 + slot],
            lambda: (unit_at(w, t), w[4].at[slot], (d, c, to)),
            lambda: z == at,
            n[7 + t],
        )

    def chain_pass(w, t, at):
        @pl.when(z == at)
        def _():
            rc.arrived(w[8][7 + t], w[4].at[t], at_x)
            add_into([unit_at(w, t)], [w[4].at[t]], wr)

        chain_send(w, t, at)

    def w_line(i):
        w = weights[i]
        for t in (0, 1):
            chain_pass(w, t, 2)
        for t in (3, 2):
            chain_pass(w, t, 1)

    def w_next(i):
        w = weights[i]
        chain_pass(w, 3, 2)
        chain_pass(w, 0, 1)

    def w_end(i):
        w = weights[i]
        for t in range(4):

            @pl.when(z == t)
            def _():
                if t < 3:
                    rc.arrived(w[8][7 + t], w[4].at[t], at_x)
                if t > 0:
                    rc.arrived(w[8][11], w[4].at[4], at_x)

        total = unit_at(w, z)[...].astype(F32) + w[4].at[z][...].astype(F32)
        w[6][...] = total + w[4].at[4][...].astype(F32)

    whole_of = lambda t: (3 * t + 1) // 2
    shared_of = lambda t: 1 + 3 * (t // 2)

    class Line:
        def __init__(self, at):
            self.at = at
            self.left = [next(number) for _ in range(3)]
            self.right = [next(number) for _ in range(3)]

        def begin(self, src):
            rc.start(self.left[0], lambda: (src, self.at(z), (d, c, z + 1)), lambda: z < 3)
            rc.start(self.right[0], lambda: (src, self.at(z), (d, c, z - 1)), lambda: z > 0)

        def step(self, j, wait=True):
            from_left, from_right = z - j, z + j

            if wait:

                @pl.when(z >= j)
                def _():
                    rc.arrived(self.left[j - 1], self.at(from_left), (d, c, z - 1))

            if j < 3:
                rc.start(
                    self.left[j],
                    lambda: (self.at(z - j), self.at(z - j), (d, c, z + 1)),
                    lambda: (z >= j) & (z < 3),
                )

            if wait:

                @pl.when(z + j <= 3)
                def _():
                    rc.arrived(self.right[j - 1], self.at(from_right), (d, c, z + 1))

            if j < 3:
                rc.start(
                    self.right[j],
                    lambda: (self.at(z + j), self.at(z + j), (d, c, z - 1)),
                    lambda: (z + j <= 3) & (z > 0),
                )

    whole_rows = lambda ref, a, n: (lambda t: ref.at[whole_of(t), pl.ds(a, n)])
    shared_rows = lambda ref: (
        lambda t: ref.at[shared_of(t), pl.ds(pl.multiple_of((t % 2) * hl, 128), hl)]
    )
    out_lines = [Line(whole_rows(output, 0, ln)), Line(shared_rows(output))]
    tok_lines = [
        Line(whole_rows(d_tokens, 0, hl)),
        Line(whole_rows(d_tokens, hl, hl)),
        Line(shared_rows(d_tokens)),
    ]

    n_ctx = [next(number) for _ in range(3)]
    for k in (1, 2, 3):
        rc.start(n_ctx[k - 1], lambda k=k: (d_ctx.at[c ^ k], d_got.at[c], at_c(k)))
    ctx_here = copy_here(d_ctx.at[c], d_got.at[c])
    kv_here = copy_here(kv_in, kv)
    q_here = copy_here(q_in, q_scr)
    n_small = [next(number) for _ in range(5)]
    small_to = (at_c(1), at_c(2), at_x, at_z(1), at_z(2))
    small[...] = small_in[...]

    def small_send(i):
        rc.start(n_small[i], lambda: (small_got.at[i, 1], small_got.at[i, 0], small_to[i]))

    def small_step(i):
        rc.arrived(n_small[i], small_got.at[i, 0], small_to[i])
        small[...] += small_got[i, 0]
        if i < 4:
            small_got[i + 1, 1] = small[...]
            small_send(i + 1)

    small_got[0, 1] = small_in[...]
    wh_here = copy_here(wh_in, wh)
    xt_here = copy_here(xt_in, xt)

    def block(qb):
        r0, r1, o0, o1, seq = block_rows(qb, half, ln)
        b0 = jnp.where(qb < 4, qb, 2 * (qb - 4))
        b1 = jnp.where(qb < 4, qb, 2 * (qb - 4) + 1)
        s0 = pl.multiple_of(jnp.where(qb < 4, 0, hl * half), 128)
        s1 = pl.multiple_of(jnp.where(qb < 4, hl, hl * half), 128)
        sq = jnp.concatenate(
            [
                segr[2 * b0 + seq, 0:1, pl.ds(s0, hl)],
                segr[2 * b1 + seq, 0:1, pl.ds(s1, hl)],
            ],
            1,
        )
        q, do, line, delta = [], [], [], []
        for h in range(heads):
            q.append(two(q_scr, r0, r1, hl, slice(128 * h, 128 * h + 128)))
            do.append(two(d_o, o0, o1, hl, slice(128 * h, 128 * h + 128)))
            line.append(two_lanes(lse, slice(h, h + 1), o0, o1, hl))
            turned = do[h].astype(F32).T[HEAD:, :]
            kept = two_lanes(ctx_t, slice(HEAD * h, HEAD * h + HEAD), o0, o1, hl)
            delta.append(jnp.sum(turned * kept, 0, keepdims=True))
        q_do = [jnp.concatenate([q[h], do[h]], 0) for h in range(heads)]
        dqt[...] = jnp.zeros_like(dqt)

        @pl.loop(0, nc)
        def _(j):
            rows = pl.ds(pl.multiple_of((2 * j + seq) * ln, ln), ln)
            keys = pl.ds(pl.multiple_of(j * ln, ln), ln)
            key_seg = segc[2 * j + seq]
            same = jnp.concatenate([key_seg, key_seg], 1) == sq
            for h in range(heads):
                kvh = kv[rows, 128 * h : 128 * h + 128]
                p = jnp.where(same, jnp.exp(dot_nt(kvh, q[h]) - line[h]), 0.0)
                ds = (p * (dot_nt(kvh, do[h]) - delta[h])).astype(BF)
                both = jnp.concatenate([ds, p.astype(BF)], 1)
                dkv[rows, 128 * h : 128 * h + 128] += dot_nn(both, q_do[h])
                dqt[h] += dot_nn(kvt[seq * heads + h, :, keys], ds)

        turned = jnp.concatenate([dqt[h] for h in range(heads)], 0).T * 0.125
        bias_sum[0:1, wide:] += jnp.sum(turned, 0, keepdims=True)
        low = turned.astype(BF)
        d_proj[pl.ds(r0, hl), wide:] = low[:hl]
        d_proj[pl.ds(r1, hl), wide:] = low[hl:]

    n_tc = [[next(number), next(number)] for _ in range(2)]
    n_ty = [[next(number), next(number)] for _ in range(2)]
    n_tz = next(number)

    def rows_of(cb, s):
        rows = pl.ds(pl.multiple_of((2 * cb + s) * ln, ln), ln)
        got = dkv[rows, :]
        bias_sum[0:1, :wide] += jnp.sum(got, 0, keepdims=True)
        d_proj[rows, :wide] = got.astype(BF)
        part[cb, s] = dot_nt(d_proj[rows, :], wh[...]).astype(BF)

    def t_partial(s):
        rows_of(c ^ 3, s)
        rc.start(n_tc[s][0], lambda: (part.at[c ^ 3, s], got_c.at[s, 0], at_c(1)))
        rows_of(c ^ 1, s)
        rc.start(n_tc[s][1], lambda: (part.at[c ^ 1, s], got_c.at[s, 1], at_c(1)))
        rows_of(c ^ 2, s)
        rows_of(c, s)

    def t_core(s):
        rc.arrived(n_tc[s][0], got_c.at[s, 0], at_c(1))
        for k in range(2):
            at = slice(k * hl, k * hl + hl)
            send_y[s, at] = (part[c ^ 2, s, at].astype(F32) + got_c[s, 0, at].astype(F32)).astype(BF)
            rc.start(
                n_ty[s][k],
                lambda k=k: (
                    send_y.at[s, pl.ds(k * hl, hl)],
                    got_y.at[s, pl.ds(k * hl, hl)],
                    at_c(2),
                ),
            )
        rc.arrived(n_tc[s][1], got_c.at[s, 1], at_c(1))
        mine[s] = part[c, s].astype(F32) + got_c[s, 1].astype(F32)

    def t_shared():
        for k in range(2):
            rc.arrived(n_ty[1][k], got_y.at[1, pl.ds(k * hl, hl)], at_c(2))
        mine[1] += got_y[1].astype(F32)
        send_z[...] = mine[1, pl.ds(pl.multiple_of((1 - half) * hl, 128), hl)].astype(BF)
        rc.start(n_tz, lambda: (send_z, got_z, at_z(1)))

    def t_shared_end():
        rc.arrived(n_tz, got_z, at_z(1))
        mine_half = mine[1, pl.ds(pl.multiple_of(half * hl, 128), hl)]
        done[ln:, :] = (mine_half + got_z[...].astype(F32) + d_first[ln:, :]).astype(BF)
        tok_lines[2].begin(done.at[pl.ds(ln, hl)])

    def t_whole(k):
        at = slice(k * hl, k * hl + hl)
        rc.arrived(n_ty[0][k], got_y.at[0, pl.ds(k * hl, hl)], at_c(2))
        done[at, :] = (mine[0, at] + got_y[0, at].astype(F32) + d_first[at, :]).astype(BF)
        tok_lines[k].begin(done.at[pl.ds(k * hl, hl)])

    n_h = [next(number) for _ in range(8)]

    def h_partial(seq):
        @pl.loop(0, nc)
        def _(i):
            rows = pl.ds(pl.multiple_of((2 * i + seq) * ln, ln), ln)
            acc_h[...] += dot_nn(xt[:, rows], d_proj[rows, :])

    def h_send():
        o_h[...] = acc_h[...].astype(BF)
        rows_x = lambda x_: pl.ds(pl.multiple_of(x_ * 4 * wr, wr), 4 * wr)
        rc.start(n_h[0], lambda: (o_h.at[rows_x(1 - d)], x_h, at_x))

    h_at = lambda t: o_h.at[pl.ds(pl.multiple_of((4 * d + t) * wr, wr), wr)]

    def h_plane():
        rc.arrived(n_h[0], x_h, at_x)
        add_into([o_h.at[pl.ds(pl.multiple_of(d * 4 * wr, wr), 4 * wr)]], [x_h], 4 * wr)
        rc.start(n_h[1], lambda: (h_at(z ^ 3), z_h.at[1], at_z(1)))
        rc.start(n_h[2], lambda: (h_at(z ^ 1), z_h.at[0], at_z(1)))

    def h_line():
        rc.arrived(n_h[1], z_h.at[1], at_z(1))
        add_into([h_at(z ^ 2)], [z_h.at[1]], wr)
        rc.start(n_h[3], lambda: (h_at(z ^ 2), z_h.at[2], at_z(2)))
        rc.arrived(n_h[2], z_h.at[0], at_z(1))
        add_into([h_at(z)], [z_h.at[0]], wr)

    def h_end():
        rc.arrived(n_h[3], z_h.at[2], at_z(2))
        send_h[...] = h_at(z)[...].astype(F32) + z_h[2].astype(F32)
        rc.start(n_h[4], lambda: (send_h, h_got, across), lambda: c != z)

        @pl.when(c == z)
        def _():
            h_got[...] = send_h[...]

    n_bias = [next(number) for _ in range(4)]
    bias_to = (at_x, at_z(1), at_z(2))

    def bias_send(i):
        bias_got[i, 1] = bias_sum[...]
        rc.start(n_bias[i], lambda: (bias_got.at[i, 1], bias_got.at[i, 0], bias_to[i]))

    def bias_step(i):
        rc.arrived(n_bias[i], bias_got.at[i, 0], bias_to[i])
        bias_sum[...] += bias_got[i, 0]
        if i < 2:
            bias_send(i + 1)
            return
        rc.start(n_bias[3], lambda: (bias_sum, bias_fin, across), lambda: c != z)

        @pl.when(c == z)
        def _():
            bias_fin[...] = bias_sum[...]

    for w in weights:

        @pl.when(z == 0)
        def _():
            w[4][4] = jnp.zeros_like(w[4][4])

        @pl.when(z == 3)
        def _():
            w[4][3] = jnp.zeros_like(w[4][3])

    def get_ctx():
        for k in (1, 2, 3):
            rc.arrived(n_ctx[k - 1], d_got.at[c ^ k], at_c(k))
        ctx_here.wait()

        @pl.loop(0, nc)
        def _(i):
            rows = pl.ds(pl.multiple_of(i * own, 128), own)
            for h in range(heads):
                d_o[rows, 128 * h + HEAD : 128 * h + 128] = d_got[
                    i, :, HEAD * h : HEAD * h + HEAD
                ]

        q_here.wait()
        wh_here.wait()
        xt_here.wait()

    def out_begin():
        for line in out_lines:
            line.step(1, False)

    w_core_send(weights[0])
    w_core_send(weights[2])
    out_begin()
    small_send(0)
    w_core_add(0)
    for i in range(nc):
        for s in range(2):
            line = seg[i, s : s + 1, :].astype(F32)
            segr[2 * i + s, 0:1, :] = line
            segc[2 * i + s] = jnp.broadcast_to(line, (128, ln)).T
    dkv[...] = jnp.zeros_like(dkv)
    d_o[...] = jnp.zeros_like(d_o)
    d_proj[...] = jnp.zeros_like(d_proj)
    bias_sum[...] = jnp.zeros_like(bias_sum)
    acc_h[...] = jnp.zeros_like(acc_h)
    kv_here.wait()

    @pl.loop(0, nc)
    def _(j):
        for s in range(2):
            rows = pl.ds(pl.multiple_of((2 * j + s) * ln, ln), ln)
            for h in range(heads):
                kvt[s * heads + h, :, pl.ds(pl.multiple_of(j * ln, ln), ln)] = kv[
                    rows, 128 * h : 128 * h + 128
                ].T[:HEAD]

    w_core_add(2)
    get_ctx()

    @pl.loop(0, 6)
    def _(i):
        block(jnp.where(i == 0, 0, jnp.where(i == 1, 1, jnp.where(i == 2, 2, jnp.where(i == 3, 3, jnp.where(i == 4, 4, 5))))))

        @pl.when(i == 1)
        def _():
            out_lines[0].step(2)
            out_lines[1].step(2)

        @pl.when(i == 3)
        def _():
            small_step(0)
            w_plane(2)
            t_partial(0)
            t_core(0)
            w_core_send(weights[1])
            small_step(1)

        @pl.when(i == 4)
        def _():
            w_plane(0)
            t_whole(0)

    t_whole(1)
    t_partial(1)
    small_step(2)
    tok_lines[0].step(1)
    t_core(1)
    bias_send(0)
    w_corner(2)
    w_corner(0)
    tok_lines[1].step(1)
    w_core_add(1)
    h_partial(1)
    bias_step(0)
    w_line(2)
    h_partial(0)
    tok_lines[1].step(2)
    w_next(2)
    t_shared()
    h_send()
    w_line(0)
    t_shared_end()
    tok_lines[0].step(2)
    w_plane(1)
    small_step(3)
    h_plane()
    tok_lines[2].step(1)
    h_line()
    bias_step(1)
    w_end(2)
    tok_lines[1].step(3)
    w_next(0)
    w_corner(1)
    bias_step(2)
    tok_lines[0].step(3)
    h_end()
    tok_lines[2].step(2)
    w_end(0)
    w_line(1)
    w_next(1)
    small_step(4)
    w_end(1)
    tok_lines[2].step(3)
    out_lines[0].step(3)
    out_lines[1].step(3)
    tok_here = [
        copy_here(done.at[pl.ds(0, hl)], tok_lines[0].at(z)),
        copy_here(done.at[pl.ds(hl, hl)], tok_lines[1].at(z)),
        copy_here(done.at[pl.ds(ln, hl)], tok_lines[2].at(z)),
    ]

    @pl.when(c != z)
    def _():
        rc.arrived(n_h[4], h_got, across)
        rc.arrived(n_bias[3], bias_fin, across)

    gf_h[...] = h_got[...]
    bias[...] = bias_fin[...]

    for copy in tok_here:
        copy.wait()
    rc.all_sent()


def backward(d_ctx, g_b, g_i, g_o, out_in, d_first, small, q, kv, xt, wh, lse, ctx_t, seg, heads, seqs):
    nc, own, group = d_ctx.shape
    ln = own * 2 // 3
    hl = ln // 2
    width = out_in.shape[2]
    wr, all_units = g_b.shape[2:]
    units = all_units // 4
    hb = pl.BlockSpec(memory_space=pltpu.HBM)
    vm = pl.BlockSpec(memory_space=pltpu.VMEM)
    sds = jax.ShapeDtypeStruct
    v = pltpu.VMEM
    rows = nc * own
    n2 = 2 * nc * ln
    return pl.pallas_call(
        functools.partial(backward_kernel, heads, ln),
        out_shape=(
            sds((seqs, ln, width), BF),
            sds((seqs, ln, width), BF),
            sds((wr, units), F32),
            sds((wr, units), F32),
            sds((wr, group), F32),
            sds((wr, 3 * group), F32),
            sds(small.shape, F32),
            sds((8, 3 * group), F32),
        ),
        in_specs=[hb] * 5 + [vm] * 2 + [hb] * 4 + [vm] * 3,
        out_specs=(hb, hb) + (vm,) * 6,
        scratch_shapes=[
            v((n2, heads * 128), BF),
            v((n2, heads * 128), BF),
            v((width, n2), BF),
            v((width, 3 * group), BF),
            v((nc, own, group), BF),
            v((rows, heads * 128), BF),
            v((2 * heads, HEAD, nc * ln), BF),
            v((n2, heads * 128), F32),
            v((heads, HEAD, ln), F32),
            v((n2, 3 * group), BF),
            v((2 * nc, ln, 128), F32),
            v((2 * nc, 8, ln), F32),
            v((nc, 2, ln, width), BF),
            v((2, 2, ln, width), BF),
            v((2, ln, width), BF),
            v((hl, width), BF),
            v((2, ln, width), BF),
            v((hl, width), BF),
            v((2, ln, width), F32),
            v((own, width), BF),
            v((4, wr, all_units), BF),
            v((4, wr, all_units), BF),
            v((4, 4, wr, group), BF),
            v((4, wr, all_units), BF),
            v((4, wr, all_units), BF),
            v((4, 4, wr, group), BF),
            v((3, wr, 2 * units), BF),
            v((3, wr, 2 * units), BF),
            v((3, 2, wr, group), BF),
            v((3, wr, 2 * units), BF),
            v((3, wr, 2 * units), BF),
            v((3, 2, wr, group), BF),
            v((5, wr, units), BF),
            v((5, wr, units), BF),
            v((5, wr, group), BF),
            v((width, 3 * group), F32),
            v((width, 3 * group), BF),
            v((4 * wr, 3 * group), BF),
            v((3, wr, 3 * group), BF),
            v((wr, 3 * group), F32),
            v((5, 2) + small.shape, F32),
            v((8, 3 * group), F32),
            v((3, 2, 8, 3 * group), F32),
            v((wr, 3 * group), F32),
            v((8, 3 * group), F32),
            pltpu.SemaphoreType.DMA((130,)),
            pltpu.SemaphoreType.DMA((130,)),
            pltpu.SemaphoreType.DMA((40,)),
        ],
        compiler_params=pltpu.CompilerParams(
            vmem_limit_bytes=60 << 20, collective_id=1, has_side_effects=True
        ),
        input_output_aliases={4: 0},
        name="backward",
    )(d_ctx, g_b, g_i, g_o, out_in, d_first, small, q, kv, xt, wh, lse, ctx_t, seg)


def finish_kernel(
    heads, tok_in, out_in, g_b, g_i, g_o, g_h, small, bias,
    tok, out, gb, gi, go, gh, gq, gv, w0, w1, w2, in_b, w3, w4, w5,
):
    tok[...] = tok_in[...].astype(F32)
    out[...] = out_in[...]
    z = lax.axis_index("tp")
    wide = heads * 128

    @pl.when(pl.program_id(0) == 0)
    def _():
        gb[...] = g_b[...]
        gi[...] = g_i[...]
        go[...] = g_o[...]
        pick = lambda ref, rows, at: jnp.concatenate(
            [ref[rows, 128 * h + at : 128 * h + at + HEAD] for h in range(heads)], -1
        )
        gh[0] = g_h[:, wide:]
        gh[1] = pick(g_h, slice(None), 0)
        gh[2] = pick(g_h, slice(None), HEAD)
        gq[...] = bias[0, wide:]
        gv[...] = pick(bias, 0, HEAD)
        for i, ref in ((0, w0), (1, w1), (2, w2), (3, w3), (4, w4), (5, w5)):
            ref[...] = small[i, :]
        in_b[...] = small[pl.ds(6 + z, 1), :].reshape(in_b.shape)


def finish(d_tokens, output, g_b, g_i, g_o, g_h, small, d_bias, heads):
    seqs, ln, width = d_tokens.shape
    wr, units = g_b.shape
    group = g_o.shape[1]
    one = lambda: pl.BlockSpec((seqs // 3, ln, width), lambda i: (i, 0, 0))
    whole = lambda shape: pl.BlockSpec(shape, lambda i: (0,) * len(shape))
    sds = jax.ShapeDtypeStruct
    rest = [
        (wr, units), (wr, units), (wr, group), (3, wr, group), (group,), (group,),
        (width,), (width,), (width,), (units,), (width,), (width,), (width,),
    ]
    return pl.pallas_call(
        functools.partial(finish_kernel, heads),
        grid=(3,),
        out_shape=[sds(d_tokens.shape, F32), sds(output.shape, BF)] + [sds(s, F32) for s in rest],
        in_specs=[one(), one()]
        + [whole(a.shape) for a in (g_b, g_i, g_o, g_h, small, d_bias)],
        out_specs=[one(), one()] + [whole(s) for s in rest],
        compiler_params=pltpu.CompilerParams(vmem_limit_bytes=60 << 20),
        name="finish",
    )(d_tokens, output, g_b, g_i, g_o, g_h, small, d_bias)


def head_order(kinds, heads):
    lead = kinds[0].shape[:-1]
    q, k, v = (a.reshape(lead + (heads, HEAD)) for a in kinds)
    kv = jnp.concatenate([k, v], -1).reshape(lead + (heads * 2 * HEAD,))
    return jnp.concatenate([kv, q.reshape(lead + (heads * HEAD,))], -1)


def forward_plain(sizes, me, tok2, seg2, w_head, b_head, b_unit, w_o, w_i, w_b, heads):
    nd, nc, nt = sizes
    d, c, z = me
    ln, width = tok2.shape[1:]
    hl = ln // 2
    half = z % 2
    group = w_o.shape[1]
    seg_all = gather_axis(seg2, "ctx", nc, c)
    x2 = gather_axis(tok2, "ctx", nc, c).reshape(2 * nc, ln, width)
    wh = gather_heads(w_head, sizes, me)
    bh = transpose_ctx_tp(b_head, nc)[0]
    b_all = gather_axis(b_unit, "tp", nt, z)
    gather = lambda w: lax.all_gather(
        lax.all_gather(w, "tp", axis=1, tiled=True), ("dp", "ctx"), axis=0, tiled=True
    )
    o_full = jnp.transpose(gather(w_o).reshape(width, nt, group), (1, 0, 2))
    proj = (jnp.dot(x2.reshape(-1, width), wh, preferred_element_type=F32) + bh).astype(BF)
    kv = proj[:, : 2 * group]
    q = (proj[:, 2 * group :].astype(F32) * 0.125).astype(BF).reshape(-1, heads, HEAD)
    q = jnp.concatenate([q, jnp.zeros_like(q)], -1).reshape(-1, heads * 128)
    info, seg_col, seg_row = key_blocks(seg_all, half, ln, nc)
    context, lse, ctx_t = attend(info, q, kv, seg_col, seg_row, heads, ln, nc)
    ctx_all = in_order(exchange_axis(context.reshape(nc, ln + hl, group), "ctx", nc, c), c)
    return (
        ctx_all,
        x2.reshape(-1, width).T,
        q,
        kv,
        wh,
        o_full,
        jnp.stack([gather(w_i), gather(w_b)]),
        b_all,
        lse,
        ctx_t,
        seg_all,
    )


def key_blocks(seg_all, half, ln, nc):
    hl = ln // 2
    seg2 = seg_all[:, :2]
    flat = jnp.transpose(seg2, (1, 0, 2)).reshape(2, nc * ln)
    first = jnp.concatenate([seg2[:, 0, 0], jnp.take(seg2[0::2, 1], half * hl, axis=1)])
    last = jnp.concatenate([seg2[:, 0, -1], jnp.take(seg2[1::2, 1], half * hl + hl - 1, axis=1)])
    of = jnp.concatenate(
        [
            jnp.broadcast_to(flat[:1], (nc, nc * ln)),
            jnp.broadcast_to(flat[1:], (nc // 2, nc * ln)),
        ],
        0,
    )
    lo = jnp.sum(of < first[:, None], 1) // ln
    hi = (jnp.sum(of <= last[:, None], 1) + ln - 1) // ln
    info = jnp.concatenate([lo, hi, half[None]]).astype(jnp.int32)
    seg_flat = seg2.reshape(2 * nc * ln)
    return info, seg_flat[:, None], seg_flat[None, :]


def backward_plain(
    sizes, me, d_ctx, low, out_low, d_first, small, q, kv, xt, wh, lse, ctx_t, seg_all, heads, seqs
):
    nd, nc, nt = sizes
    d, c, z = me
    own, group = d_ctx.shape[1:]
    ln = own * 2 // 3
    hl = ln // 2
    half = z % 2
    width = out_low.shape[1]
    units = low[0].shape[1] // nt
    nr = nd * nc
    wr = width // nr
    info, seg_col, seg_row = key_blocks(seg_all, half, ln, nc)

    def spread_rows(rows_low, dtype):
        out = jnp.zeros((seqs, ln, width), dtype)
        parts = [rows_low] + [swap_with(rows_low, "tp", nt, k) for k in range(1, nt)]
        for k, part in enumerate(parts):
            t = z ^ k
            part = part.astype(dtype)
            out = lax.dynamic_update_slice(out, part[None, :ln], ((3 * t + 1) // 2, 0, 0))
            out = lax.dynamic_update_slice(
                out, part[None, ln:], (1 + 3 * (t // 2), (t % 2) * hl, 0)
            )
        return out

    by_unit = lambda g: jnp.transpose(g.reshape(nr, wr, nt, units), (2, 0, 1, 3))
    g_back = scatter_weight(by_unit(low[0]), sizes, me)
    g_in = scatter_weight(by_unit(low[1]), sizes, me)
    g_out = scatter_weight(low[2].reshape(nt, nr, wr, group), sizes, me)
    output = spread_rows(out_low, BF)
    small = lax.psum(small, ALL)
    d_ctx = in_order(exchange_axis(d_ctx, "ctx", nc, c), c).reshape(nc * own, heads, HEAD)
    d_ctx = jnp.concatenate([jnp.zeros_like(d_ctx), d_ctx], -1).reshape(nc * own, heads * 128)
    d_q, d_kv, d_bias = attend_back(
        info, q, kv, d_ctx, seg_col, seg_row, lse, ctx_t, heads, ln, nc
    )
    d_proj = jnp.concatenate([d_kv, d_q], -1)
    part = jnp.einsum("tf,df->td", d_proj, wh, preferred_element_type=F32)
    part = lax.psum_scatter(
        part.reshape(nc, 2 * ln, width), "ctx", scatter_dimension=0, tiled=False
    ).reshape(2, ln, width)
    shared = part[1].reshape(2, hl, width)
    shared = lax.dynamic_index_in_dim(shared, half, 0, keepdims=False) + swap_with(
        lax.dynamic_index_in_dim(shared, 1 - half, 0, keepdims=False), "tp", nt, 1
    )
    d_own = (jnp.concatenate([part[0], shared], 0) + d_first).astype(BF)
    d_tokens = spread_rows(d_own, BF)
    g_h = scatter_heads(jnp.dot(xt, d_proj, preferred_element_type=F32).astype(BF), sizes, me)
    slots = jnp.zeros((nc,) + d_bias[0].shape, F32)
    slots = lax.psum(lax.dynamic_update_index_in_dim(slots, d_bias[0], c, 0), ALL)
    d_bias = lax.dynamic_index_in_dim(slots, z, 0, keepdims=False)
    d_bias = jnp.broadcast_to(d_bias[None], (8,) + d_bias.shape)
    return output, d_tokens, g_back, g_in, g_out, g_h, small, d_bias


def per_device(
    sizes,
    tokens,
    segments,
    w_qkv,
    q_bias,
    v_bias,
    w_out,
    out_bias,
    gain_one,
    shift_one,
    w_in,
    in_bias,
    w_back,
    back_bias,
    gain_two,
    shift_two,
    cotangent,
):
    nd, nc, nt = sizes
    seqs, ln, width = tokens.shape
    group = w_out.shape[1]
    heads = group // HEAD
    units = w_in.shape[1]
    wr = w_in.shape[0]
    d, c, z = (lax.axis_index(n) for n in ALL)
    me = (d, c, z)
    whole_of = lambda t: (3 * t + 1) // 2
    shared_of = lambda t: 1 + 3 * (t // 2)
    half_of = lambda t: t % 2
    sf, sh, half = whole_of(z), shared_of(z), half_of(z)

    def own_pair(a):
        return jnp.stack(
            [
                lax.dynamic_index_in_dim(a, sf, 0, keepdims=False),
                lax.dynamic_index_in_dim(a, sh, 0, keepdims=False),
            ],
            0,
        )

    w_kinds = jnp.transpose(w_qkv, (1, 0, 2))
    biases = (q_bias, v_bias, in_bias)
    weights = (w_out, w_in, w_back)
    vectors = (out_bias, gain_one, shift_one, back_bias, gain_two, shift_two)
    if sizes == (2, 4, 4):
        xt, q, kv, wh, g_b, g_i, out_low, lse, ctx_t, seg_all, d_ctx, g_o, d_first, small = forward(
            tokens, segments, w_kinds, *biases, *weights, cotangent, vectors, heads
        )
    else:
        tok2 = own_pair(tokens)
        seg2 = jnp.concatenate([own_pair(segments), jnp.zeros((6, ln), jnp.int32)], 0)
        w_head = head_order(w_kinds, heads)
        b_head = head_order([q_bias, jnp.zeros_like(q_bias), v_bias], heads)
        b_head = jnp.broadcast_to(b_head[None], (8, 3 * group))
        b_unit = jnp.broadcast_to(in_bias[None], (8, units))
        got = forward_plain(sizes, me, tok2, seg2, w_head, b_head, b_unit, *weights, heads)
        ctx_all, xt, q, kv, wh, w_o, w_ib, b_in, lse, ctx_t, seg_all = got
        d_ctx, g_b, g_i, g_o, out_low, d_first, small = middle(
            tokens,
            cotangent,
            ctx_all,
            w_o.reshape(nt, width, group),
            w_ib.reshape(2, width, nt * units),
            b_in,
            vectors,
        )
    low = (g_b, g_i, g_o)
    if sizes == (2, 4, 4):
        output, d_tokens, g_back, g_in, g_out, g_h, small, d_bias = backward(
            d_ctx,
            low[0].reshape(4, 2, wr, nt * units),
            low[1].reshape(4, 2, wr, nt * units),
            low[2].reshape(nt, 4, 2, wr, group),
            out_low,
            d_first,
            small,
            q,
            kv,
            xt,
            wh,
            lse,
            ctx_t,
            seg_all,
            heads,
            seqs,
        )
    else:
        output, d_tokens, g_back, g_in, g_out, g_h, small, d_bias = backward_plain(
            sizes, me, d_ctx, low, out_low, d_first, small, q, kv, xt, wh, lse, ctx_t, seg_all, heads, seqs
        )
    d_tokens, output, g_b, g_i, g_o, g_h, d_qb, d_vb, w0, w1, w2, d_in, w3, w4, w5 = finish(
        d_tokens, output, g_back, g_in, g_out, g_h, small, d_bias, heads
    )
    g_h = jnp.transpose(g_h, (1, 0, 2))
    return (output, d_tokens, g_h, d_qb, d_vb, g_o, w0, w1, w2, g_i, d_in, g_b, w3, w4, w5)


def solution(mesh):
    sizes = tuple(mesh.shape[n] for n in ALL)
    rows = P(("dp", "ctx"), "tp")
    return jax.shard_map(
        functools.partial(per_device, sizes),
        mesh=mesh,
        in_specs=(
            P("dp", "ctx", None),
            P("dp", "ctx"),
            P(("dp", "ctx"), None, "tp"),
            P("tp"),
            P("tp"),
            rows,
            P(),
            P(),
            P(),
            rows,
            P("tp"),
            rows,
            P(),
            P(),
            P(),
            P("dp", "ctx", None),
        ),
        out_specs=(
            P("dp", "ctx", None),
            P("dp", "ctx", None),
            P(("dp", "ctx"), None, "tp"),
            P("tp"),
            P("tp"),
            rows,
            P(),
            P(),
            P(),
            rows,
            P("tp"),
            rows,
            P(),
            P(),
            P(),
        ),
        check_vma=False,
    )
```

```python
import functools
import math

import jax
import jax.numpy as jnp
from jax import lax
from jax.experimental import pallas as pl
from jax.experimental.pallas import tpu as pltpu
from jax.sharding import PartitionSpec as P

HEAD = 64
NEG = -1e30
BF = jnp.bfloat16
F32 = jnp.float32
ALL = ("dp", "ctx", "tp")


def norm_parts(value):
    mean = jnp.mean(value, -1, keepdims=True)
    centered = value - mean
    rstd = lax.rsqrt(jnp.mean(centered * centered, -1, keepdims=True) + 1e-12)
    return (centered * rstd, rstd)


def norm_back(grad, normal, rstd, gain):
    d_gain = jnp.sum(grad * normal, 0)
    d_shift = jnp.sum(grad, 0)
    scaled = grad * gain
    d_value = rstd * (
        scaled
        - jnp.mean(scaled, -1, keepdims=True)
        - normal * jnp.mean(scaled * normal, -1, keepdims=True)
    )
    return (d_value, d_gain, d_shift)


def gelu_slope(inner):
    return 0.5 * (1.0 + lax.erf(inner / math.sqrt(2.0))) + inner * jnp.exp(
        -0.5 * inner * inner
    ) / math.sqrt(2.0 * math.pi)


def swap_with(value, axis, size, mask):
    return lax.ppermute(value, axis, [(i, i ^ mask) for i in range(size)])


def in_order(parts, me, axis=0):
    shape = list(parts[0].shape)
    shape.insert(axis, len(parts))
    out = jnp.zeros(tuple(shape), parts[0].dtype)
    for k, part in enumerate(parts):
        out = lax.dynamic_update_index_in_dim(out, part, me ^ k, axis)
    return out


def gather_axis(value, axis, size, me):
    parts = [value] + [swap_with(value, axis, size, k) for k in range(1, size)]
    return in_order(parts, me)


def exchange_axis(blocks, axis, size, me):
    parts = [lax.dynamic_index_in_dim(blocks, me, 0, keepdims=False)]
    for k in range(1, size):
        parts.append(
            swap_with(lax.dynamic_index_in_dim(blocks, me ^ k, 0, keepdims=False), axis, size, k)
        )
    return parts


def scatter_weight(grad, sizes, me):
    nd, nc, nt = sizes
    part = lax.psum_scatter(
        grad.astype(F32), ("dp", "ctx"), scatter_dimension=1, tiled=False
    ).astype(BF)
    parts = exchange_axis(part, "tp", nt, me[2])
    return sum(p.astype(F32) for p in parts)


def transpose_ctx_tp(value, n):
    pairs = [(a * n + b, b * n + a) for a in range(n) for b in range(n)]
    return lax.ppermute(value, ("ctx", "tp"), pairs)


def gather_heads(shard, sizes, me):
    mine = transpose_ctx_tp(shard, sizes[1])
    return lax.all_gather(mine, ("dp", "tp"), axis=0, tiled=True)


def scatter_heads(grad, sizes, me):
    nd, nc, nt = sizes
    blocks = grad.reshape((nd * nt, grad.shape[0] // (nd * nt)) + grad.shape[1:])
    total = lax.psum_scatter(
        blocks.astype(F32), ("dp", "tp"), scatter_dimension=0, tiled=False
    )
    return transpose_ctx_tp(total, nc)


def block_rows(qb, half, ln):
    hl = ln // 2
    whole = qb < 4
    b = jnp.where(whole, qb, qb - 4)
    r0 = jnp.where(whole, 2 * ln * b, (4 * b + 1) * ln + hl * half)
    r1 = jnp.where(whole, r0 + hl, r0 + 2 * ln)
    o0 = jnp.where(whole, 3 * hl * b, 6 * hl * b + ln)
    o1 = jnp.where(whole, o0 + hl, o0 + 3 * hl)
    seq = jnp.where(whole, 0, 1)
    m = lambda v: pl.multiple_of(v, 128)
    return m(r0), m(r1), m(o0), m(o1), seq


def two(ref, r0, r1, hl, cols):
    return jnp.concatenate([ref[pl.ds(r0, hl), cols], ref[pl.ds(r1, hl), cols]], 0)


def two_lanes(ref, rows, r0, r1, hl):
    return jnp.concatenate([ref[rows, pl.ds(r0, hl)], ref[rows, pl.ds(r1, hl)]], 1)


def dot_nt(a, b):
    return lax.dot_general(a, b, (((1,), (1,)), ((), ())), preferred_element_type=F32)


def dot_nn(a, b):
    return lax.dot_general(a, b, (((1,), (0,)), ((), ())), preferred_element_type=F32)


def fill_transposed(kv, kvt, ln, nc, heads):
    @pl.loop(0, nc)
    def _(j):
        for seq in range(2):
            rows = pl.ds(pl.multiple_of((2 * j + seq) * ln, ln), ln)
            for h in range(heads):
                kvt[seq * heads + h, :, pl.ds(pl.multiple_of(j * ln, ln), ln)] = kv[
                    rows, 128 * h : 128 * h + 128
                ].T


def attend_kernel(heads, ln, nc, info, q_ref, kv, seg_col, seg_row, out, lse, ctx_t, s_scr, kvt, acc):
    half = info[12]
    hl = ln // 2
    fill_transposed(kv, kvt, ln, nc, heads)

    @pl.loop(0, 6)
    def _(qb):
        r0, r1, o0, o1, seq = block_rows(qb, half, ln)
        lo, hi = info[qb], info[6 + qb]
        sq = two_lanes(seg_row, slice(0, 1), r0, r1, hl)
        q = [two(q_ref, r0, r1, hl, slice(128 * h, 128 * h + 128)) for h in range(heads)]

        def score(j, peaks):
            rows = pl.ds(pl.multiple_of((2 * j + seq) * ln, ln), ln)
            same = seg_col[rows, :] == sq
            new = []
            for h in range(heads):
                s = dot_nt(kv[rows, 128 * h : 128 * h + 128], q[h])
                s = jnp.where(same, s, NEG)
                s_scr[h, pl.ds(pl.multiple_of(j * ln, ln), ln), :] = s
                new.append(jnp.maximum(peaks[h], jnp.max(s, 0, keepdims=True)))
            return tuple(new)

        peaks = lax.fori_loop(
            lo, hi, score, tuple(jnp.full((1, ln), NEG, F32) for _ in range(heads))
        )
        acc[...] = jnp.zeros_like(acc)

        def collect(j, sums):
            keys = pl.ds(pl.multiple_of(j * ln, ln), ln)
            new = []
            for h in range(heads):
                p = jnp.exp(s_scr[h, keys, :] - peaks[h])
                new.append(sums[h] + jnp.sum(p, 0, keepdims=True))
                acc[h] += dot_nn(kvt[seq * heads + h, :, keys], p.astype(BF))
            return tuple(new)

        sums = lax.fori_loop(
            lo, hi, collect, tuple(jnp.zeros((1, ln), F32) for _ in range(heads))
        )
        whole = []
        for h in range(heads):
            one = acc[h, HEAD:, :] / sums[h]
            whole.append(one)
            line = peaks[h] + jnp.log(sums[h])
            for part, at in ((0, o0), (hl, o1)):
                ctx_t[HEAD * h : HEAD * h + HEAD, pl.ds(at, hl)] = one[:, part : part + hl]
                lse[h : h + 1, pl.ds(at, hl)] = line[:, part : part + hl]
        turned = jnp.concatenate(whole, 0).T.astype(BF)
        out[pl.ds(o0, hl), :] = turned[:hl]
        out[pl.ds(o1, hl), :] = turned[hl:]


def attend(info, q_ref, kv, seg_col, seg_row, heads, ln, nc):
    rows = 3 * ln // 2 * nc
    vm = pl.BlockSpec(memory_space=pltpu.VMEM)
    return pl.pallas_call(
        functools.partial(attend_kernel, heads, ln, nc),
        out_shape=(
            jax.ShapeDtypeStruct((rows, heads * HEAD), BF),
            jax.ShapeDtypeStruct((8, rows), F32),
            jax.ShapeDtypeStruct((heads * HEAD, rows), F32),
        ),
        in_specs=[pl.BlockSpec(memory_space=pltpu.SMEM), vm, vm, vm, vm],
        out_specs=(vm, vm, vm),
        scratch_shapes=[
            pltpu.VMEM((heads, nc * ln, ln), F32),
            pltpu.VMEM((2 * heads, 128, nc * ln), BF),
            pltpu.VMEM((heads, 128, ln), F32),
        ],
        compiler_params=pltpu.CompilerParams(vmem_limit_bytes=32 << 20),
        cost_estimate=pl.CostEstimate(
            flops=8 * heads * rows * nc * ln * 128,
            bytes_accessed=8 << 20,
            transcendentals=heads * rows * nc * ln,
        ),
        name="attend",
    )(info, q_ref, kv, seg_col, seg_row)


def attend_back_kernel(
    heads, ln, nc, info, q_ref, kv, d_out, seg_col, seg_row, lse, ctx_t, d_q, d_kv, d_bias, dkv, kvt, dqt
):
    half = info[12]
    hl = ln // 2
    fill_transposed(kv, kvt, ln, nc, heads)
    dkv[...] = jnp.zeros_like(dkv)
    d_bias[...] = jnp.zeros_like(d_bias)

    @pl.loop(0, nc)
    def _(c):
        rows = pl.ds(pl.multiple_of((2 * c + 1) * ln, ln), ln)
        d_q[rows, :] = jnp.zeros((ln, heads * HEAD), BF)

    @pl.loop(0, 6)
    def _(qb):
        r0, r1, o0, o1, seq = block_rows(qb, half, ln)
        lo, hi = info[qb], info[6 + qb]
        sq = two_lanes(seg_row, slice(0, 1), r0, r1, hl)
        q, do, line, delta = [], [], [], []
        for h in range(heads):
            q.append(two(q_ref, r0, r1, hl, slice(128 * h, 128 * h + 128)))
            do.append(two(d_out, o0, o1, hl, slice(128 * h, 128 * h + 128)))
            line.append(two_lanes(lse, slice(h, h + 1), o0, o1, hl))
            turned = do[h].astype(F32).T[HEAD:, :]
            kept = two_lanes(ctx_t, slice(HEAD * h, HEAD * h + HEAD), o0, o1, hl)
            delta.append(jnp.sum(turned * kept, 0, keepdims=True))
        dqt[...] = jnp.zeros_like(dqt)

        @pl.loop(lo, hi)
        def _(j):
            rows = pl.ds(pl.multiple_of((2 * j + seq) * ln, ln), ln)
            keys = pl.ds(pl.multiple_of(j * ln, ln), ln)
            same = seg_col[rows, :] == sq
            for h in range(heads):
                kvh = kv[rows, 128 * h : 128 * h + 128]
                p = jnp.where(same, jnp.exp(dot_nt(kvh, q[h]) - line[h]), 0.0)
                ds = (p * (dot_nt(kvh, do[h]) - delta[h])).astype(BF)
                dkv[rows, 128 * h : 128 * h + 128] += dot_nn(ds, q[h]) + dot_nn(
                    p.astype(BF), do[h]
                )
                dqt[h] += dot_nn(kvt[seq * heads + h, :, keys], ds)

        turned = jnp.concatenate([dqt[h, :HEAD, :] for h in range(heads)], 0).T * 0.125
        d_bias[0:1, heads * 128 :] += jnp.sum(turned, 0, keepdims=True)
        low = turned.astype(BF)
        d_q[pl.ds(r0, hl), :] = low[:hl]
        d_q[pl.ds(r1, hl), :] = low[hl:]

    @pl.loop(0, 2 * nc)
    def _(c):
        rows = pl.ds(pl.multiple_of(c * ln, ln), ln)
        for h in range(heads):
            got = dkv[rows, 128 * h : 128 * h + 128]
            d_bias[0:1, 128 * h : 128 * h + 128] += jnp.sum(got, 0, keepdims=True)
            d_kv[rows, 128 * h : 128 * h + 128] = got.astype(BF)


def attend_back(info, q_ref, kv, d_out, seg_col, seg_row, lse, ctx_t, heads, ln, nc):
    rows = 3 * ln // 2 * nc
    vm = pl.BlockSpec(memory_space=pltpu.VMEM)
    return pl.pallas_call(
        functools.partial(attend_back_kernel, heads, ln, nc),
        out_shape=(
            jax.ShapeDtypeStruct((2 * nc * ln, heads * HEAD), BF),
            jax.ShapeDtypeStruct((2 * nc * ln, heads * 128), BF),
            jax.ShapeDtypeStruct((8, heads * (HEAD + 128)), F32),
        ),
        in_specs=[pl.BlockSpec(memory_space=pltpu.SMEM)] + [vm] * 7,
        out_specs=(vm, vm, vm),
        scratch_shapes=[
            pltpu.VMEM((2 * nc * ln, heads * 128), F32),
            pltpu.VMEM((2 * heads, 128, nc * ln), BF),
            pltpu.VMEM((heads, 128, ln), F32),
        ],
        compiler_params=pltpu.CompilerParams(vmem_limit_bytes=40 << 20),
        cost_estimate=pl.CostEstimate(
            flops=20 * heads * rows * nc * ln * 128,
            bytes_accessed=14 << 20,
            transcendentals=heads * rows * nc * ln,
        ),
        name="attend_back",
    )(info, q_ref, kv, d_out, seg_col, seg_row, lse, ctx_t)


MESH = pl.DeviceIdType.MESH


class Copies:
    def __init__(self, send, recv):
        self.send, self.recv, self.open = send, recv, []

    def make(self, i, src, dst, device, sent=None):
        return pltpu.make_async_remote_copy(
            src_ref=src,
            dst_ref=dst,
            send_sem=self.send.at[i if sent is None else sent],
            recv_sem=self.recv.at[i],
            device_id=device,
            device_id_type=MESH,
        )

    def start(self, i, parts, when=None, sent=None):
        number = (lambda: i) if not callable(i) else i

        def go(wait):
            copy = self.make(number(), *parts(), sent=sent)
            copy.wait_send() if wait else copy.start()

        self.run(go, when, False)
        self.open.append((go, when))

    def run(self, go, when, wait):
        if when is None:
            go(wait)
        else:

            @pl.when(when())
            def _():
                go(wait)

    def arrived(self, i, dst, device):
        self.make(i, dst, dst, device).wait_recv()

    def all_sent(self):
        for go, when in self.open:
            self.run(go, when, True)


def line_order(z, i):
    if i == 0:
        return z
    if i == 1:
        return jnp.where(z == 0, 1, z - 1)
    if i == 2:
        return jnp.where(z == 0, 2, jnp.where(z == 3, 1, z + 1))
    return jnp.where(z < 2, 3, 0)


def forward_kernel(
    heads,
    ln,
    tokens,
    segments,
    w_kinds,
    q_bias,
    v_bias,
    in_bias,
    w_o,
    w_i,
    w_b,
    cotangent,
    out_bias,
    gain_one,
    shift_one,
    back_bias,
    gain_two,
    shift_two,
    xt_out,
    q_out,
    kv_out,
    wh_out,
    g_b,
    g_i,
    output,
    lse,
    ctx_t,
    seg,
    d_ctx,
    g_o,
    d_first,
    small,
    x2,
    xt,
    wh,
    bh,
    q_scr,
    kv,
    s_scr,
    kvt,
    acc,
    segc,
    segr,
    context,
    w_src,
    o_src,
    seg2,
    w_head,
    b_head,
    b_unit,
    ctx_all,
    o_full,
    w_full,
    bu_full,
    x_own,
    c_own,
    n_one,
    r_one,
    low,
    low_t,
    tmp,
    total,
    active,
    slope,
    turn,
    d_low,
    gb_v,
    gi_v,
    out_low,
    g_sem,
    send,
    recv,
    local,
):
    d, c, z = (lax.axis_index(n) for n in ALL)
    nc = 4
    hl = ln // 2
    own = ln + hl
    half = z % 2
    wr = w_i.shape[0]
    units = w_i.shape[1]
    row = d * nc + c
    row_x, row_y, row_d = row ^ 4, row ^ 2, row ^ 6
    rc = Copies(send, recv)
    at_c = lambda k: (d, c ^ k, z)
    at_x = (1 - d, c, z)
    to_c = lambda k: (lambda: at_c(k))
    to_x = lambda: at_x
    at_z = lambda k: (d, c, z ^ k)
    across = (d, z, c)
    order = [line_order(z, i) for i in range(4)]
    number = iter(range(0, 400))
    four = lambda: [next(number) for _ in range(4)][0]
    local_number = iter(range(32))

    def copy_here(src, dst):
        copy = pltpu.make_async_copy(src, dst, local.at[next(local_number)])
        copy.start()
        return copy

    t_cols = lambda t: pl.ds(pl.multiple_of(t * units, 128), units)
    w_at = lambda r, t: w_full.at[:, r, :, t_cols(t)]
    o_at = lambda r, t: o_full.at[t, r]
    wh_at = lambda r: wh.at[pl.ds(pl.multiple_of(r * wr, wr), wr)]
    tok_at = lambda i: x2.at[pl.ds(2 * i, 2)]
    w_here = [copy_here(w_i, w_src.at[0]), copy_here(w_b, w_src.at[1]), copy_here(w_o, o_src)]
    tok_src = lambda s: tokens.at[(3 * z + 1) // 2 if s == 0 else 1 + 3 * (z // 2)]
    mine = [copy_here(tok_src(s), x2.at[2 * c + s]) for s in range(2)]
    half_rows = pl.ds(pl.multiple_of(half * hl, 128), hl)
    own_rows = [
        copy_here(part, dst)
        for src, to in ((tokens, x_own), (cotangent, c_own))
        for part, dst in (
            (src.at[(3 * z + 1) // 2], to.at[pl.ds(0, ln)]),
            (src.at[1 + 3 * (z // 2), half_rows], to.at[pl.ds(ln, hl)]),
        )
    ]
    here_sem = [local.at[next(local_number)] for _ in range(2)]
    here = [
        pltpu.make_async_copy(w_head, wh_at(row), here_sem[0]),
        pltpu.make_async_copy(b_head, bh, here_sem[1]),
    ]

    barrier = pltpu.get_barrier_semaphore()
    everyone = [at_c(k) for k in (1, 2, 3)] + [at_z(k) for k in (1, 2, 3)] + [at_x]
    for device in everyone:
        pl.semaphore_signal(barrier, inc=1, device_id=device, device_id_type=MESH)

    @pl.when(c != z)
    def _():
        pl.semaphore_signal(barrier, inc=1, device_id=across, device_id_type=MESH)

    seg2[...] = jnp.zeros_like(seg2)
    seg2[0:1, :] = segments[pl.ds((3 * z + 1) // 2, 1), :]
    seg2[1:2, :] = segments[pl.ds(1 + 3 * (z // 2), 1), :]
    wide = heads * 128
    b_head[...] = jnp.zeros_like(b_head)
    b_unit[...] = jnp.zeros_like(b_unit)
    qb = q_bias[...].reshape(1, heads * HEAD)
    vb = v_bias[...].reshape(1, heads * HEAD)
    for h in range(heads):
        cols = slice(HEAD * h, HEAD * h + HEAD)
        w_head[:, 128 * h : 128 * h + HEAD] = w_kinds[1, :, cols]
        w_head[:, 128 * h + HEAD : 128 * h + 128] = w_kinds[2, :, cols]
        b_head[0:1, 128 * h + HEAD : 128 * h + 128] = vb[:, cols]
    w_head[:, wide:] = w_kinds[0]
    b_head[0:1, wide:] = qb
    b_unit[0:1, :] = in_bias[...].reshape(1, units)
    seg_here = copy_here(seg2, seg.at[c])
    bu_here = copy_here(b_unit, bu_full.at[z])

    @pl.when(c == z)
    def _():
        for copy in here:
            copy.start()

    pl.semaphore_wait(barrier, len(everyone) + jnp.where(c != z, 1, 0))

    n_tf, n_wa, n_ba = (next(number) for _ in range(3))
    n_ty, n_tc = ([next(number) for _ in range(2)] for _ in range(2))
    not_here = lambda: c != z
    rc.start(n_wa, lambda: (w_head, wh_at(row), across), not_here)
    rc.start(n_ba, lambda: (b_head, bh, across), not_here)
    n_seg = four()
    for k in (1, 2, 3):
        rc.start(n_seg + k, lambda k=k: (seg2, seg.at[c], at_c(k)))

    class Line:
        def __init__(self, at):
            self.at = at
            self.n = [next(number) for _ in range(5)][0]

        def begin(self, src):
            rc.start(
                lambda: self.n + z,
                lambda: (src, self.at(z), (d, c, z + 1)),
                lambda: z < 3,
                self.n + 3,
            )
            rc.start(
                lambda: self.n + z,
                lambda: (src, self.at(z), (d, c, z - 1)),
                lambda: z > 0,
                self.n + 4,
            )

        def step(self, i):
            t = lambda: order[i]
            rc.arrived(self.n + t(), self.at(t()), (d, c, z))
            rc.start(
                lambda: self.n + t(),
                lambda: (
                    self.at(t()),
                    self.at(t()),
                    (d, c, jnp.where(t() < z, z + 1, z - 1)),
                ),
                lambda: jnp.where(t() < z, z < 3, z > 0),
                self.n + i - 1,
            )

    n_hz = four()
    full_at = (
        lambda r, t: w_full.at[0, r, :, t_cols(t)],
        o_at,
        lambda r, t: w_full.at[1, r, :, t_cols(t)],
    )
    sources = (w_src.at[0], o_src, w_src.at[1])
    lines = [Line(lambda t, w=w: full_at[w](row, t)) for w in range(3)]
    n_hx = four()
    n_x, n_y, n_d = ([four() for _ in range(3)] for _ in range(3))
    n_c = [[four() for _ in range(3)] for _ in range(4)]

    groups = [(0, 1), (2,)]
    over_y = ((0, 2), (1, 0))

    def pass_on(n, g, i, r, device, first=False):
        t = lambda: order[i]
        for w in groups[g]:
            rc.start(
                lambda w=w: n[w] + t(),
                lambda w=w: (
                    sources[w] if first and i == 0 else full_at[w](r, t()),
                    full_at[w](r, t()),
                    device(),
                ),
                None,
                n[w] + i,
            )

    def came(n, g, i, r, device):
        t = order[i]
        for w in groups[g]:
            rc.arrived(n[w] + t, full_at[w](r, t), device)

    def own_send(g):
        pass_on(n_x, g, 0, row, to_x, True)
        pass_on(n_c[0], g, 0, row, to_c(1), True)

    def line_begin(g):
        for w in groups[g]:
            lines[w].begin(sources[w])

    def y_send(g, i):
        pass_on(n_y, g, i, row, to_c(2), True)

    def line_step(g, i):
        for w in groups[g]:
            lines[w].step(i)
        pass_on(n_x, g, i, row, to_x)
        pass_on(n_c[0], g, i, row, to_c(1))

    def from_x(g, i):
        came(n_x, g, i, row_x, at_x)
        if (g, i) in over_y:
            pass_on(n_d, g, i, row_x, to_c(2))
        pass_on(n_c[1], g, i, row_x, to_c(1))

    def from_y(g, i):
        came(n_y, g, i, row_y, at_c(2))
        if (g, i) not in over_y:
            pass_on(n_d, g, i, row_y, to_x)
        pass_on(n_c[2], g, i, row_y, to_c(1))

    def from_corner(g, i):
        came(n_d, g, i, row_d, at_x)
        pass_on(n_c[3], g, i, row_d, to_c(1))

    head_at = lambda t: wh_at(d * nc + t)
    n_bu = four()
    n_ctx = four()
    ctx_at = lambda i: context.at[pl.ds(pl.multiple_of(i * own, 128), own)]

    def head_send():
        @pl.when(c != z)
        def _():
            rc.arrived(n_wa, wh_at(d * nc + z), across)
            rc.arrived(n_ba, bh, across)

        @pl.when(c == z)
        def _():
            for copy in here:
                copy.wait()

        for k in (1, 2, 3):
            rc.start(n_hz + k, lambda k=k: (head_at(z), head_at(z), at_z(k)))
        rc.start(n_hx, lambda: (head_at(z), head_at(z), at_x))
        for k in (1, 2, 3):
            rc.start(n_bu + k, lambda k=k: (b_unit, bu_full.at[z], at_z(k)))

    def head_pass(k):
        rc.arrived(n_hz + k, head_at(z ^ k), at_z(k))
        rc.start(n_hx + k, lambda: (head_at(z ^ k), head_at(z ^ k), at_x))

    def token_pass():
        for s in range(2):
            rc.arrived(n_ty[s], x2.at[2 * (c ^ 2) + s], at_c(2))
        rc.start(n_tf, lambda: (tok_at(c ^ 2), tok_at(c ^ 2), at_c(1)))

    def context_send():
        for k in (2, 3, 1):
            rc.start(n_ctx + k, lambda k=k: (ctx_at(c ^ k), ctx_all.at[c], at_c(k)))

    def segments_done():
        for k in (1, 2, 3):
            rc.arrived(n_seg + k, seg.at[c ^ k], at_c(k))
        seg_here.wait()
        for i in range(nc):
            for s in range(2):
                line = seg[i, s : s + 1, :].astype(F32)
                segr[2 * i + s, 0:1, :] = line
                segc[2 * i + s] = jnp.broadcast_to(line, (128, ln)).T

    step, thin = 128, 64
    width = x_own.shape[1]
    w_of = lambda which, t: w_full[which, :, :, t_cols(t)].reshape(width, units)
    w_out_of = lambda g: o_full[g].reshape(width, w_o.shape[1])
    out_bias, gain_one, shift_one, back_bias, gain_two, shift_two = (
        a[...].reshape(1, width)
        for a in (out_bias, gain_one, shift_one, back_bias, gain_two, shift_two)
    )

    def chunks(body, size=step):
        @pl.loop(0, own // size)
        def _(i):
            body(pl.ds(pl.multiple_of(i * size, size), size))

    mean = lambda v: jnp.mean(v, -1, keepdims=True)
    add = lambda i, v: small.__setitem__(
        (slice(i, i + 1), slice(None)), small[i : i + 1, :] + jnp.sum(v, 0, keepdims=True)
    )
    small[...] = jnp.zeros_like(small)

    def block(qb):
        r0, r1, o0, o1, seq = block_rows(qb, half, ln)
        b0 = jnp.where(qb < 4, qb, 2 * (qb - 4))
        b1 = jnp.where(qb < 4, qb, 2 * (qb - 4) + 1)
        s0 = pl.multiple_of(jnp.where(qb < 4, 0, hl * half), 128)
        s1 = pl.multiple_of(jnp.where(qb < 4, hl, hl * half), 128)
        sq = jnp.concatenate(
            [
                segr[2 * b0 + seq, 0:1, pl.ds(s0, hl)],
                segr[2 * b1 + seq, 0:1, pl.ds(s1, hl)],
            ],
            1,
        )
        q = [two(q_scr, r0, r1, hl, slice(128 * h, 128 * h + 128)) for h in range(heads)]

        def score(j, peaks):
            rows = pl.ds(pl.multiple_of((2 * j + seq) * ln, ln), ln)
            key_seg = segc[2 * j + seq]
            same = jnp.concatenate([key_seg, key_seg], 1) == sq
            new = []
            for h in range(heads):
                s = dot_nt(kv[rows, 128 * h : 128 * h + 128], q[h])
                s = jnp.where(same, s, NEG)
                s_scr[h, pl.ds(pl.multiple_of(j * ln, ln), ln), :] = s
                new.append(jnp.maximum(peaks[h], jnp.max(s, 0, keepdims=True)))
            return tuple(new)

        peaks = lax.fori_loop(
            0, nc, score, tuple(jnp.full((1, ln), NEG, F32) for _ in range(heads))
        )
        acc[...] = jnp.zeros_like(acc)

        def collect(j, sums):
            keys = pl.ds(pl.multiple_of(j * ln, ln), ln)
            new = []
            for h in range(heads):
                p = jnp.exp(s_scr[h, keys, :] - peaks[h])
                new.append(sums[h] + jnp.sum(p, 0, keepdims=True))
                acc[h] += dot_nn(kvt[seq * heads + h, :, keys], p.astype(BF))
            return tuple(new)

        sums = lax.fori_loop(
            0, nc, collect, tuple(jnp.zeros((1, ln), F32) for _ in range(heads))
        )
        whole = []
        for h in range(heads):
            one = acc[h] / sums[h]
            whole.append(one)
            line = peaks[h] + jnp.log(sums[h])
            for part, at in ((0, o0), (hl, o1)):
                ctx_t[HEAD * h : HEAD * h + HEAD, pl.ds(at, hl)] = one[:, part : part + hl]
                lse[h : h + 1, pl.ds(at, hl)] = line[:, part : part + hl]
        turned = jnp.concatenate(whole, 0).T.astype(BF)
        context[pl.ds(o0, hl), :] = turned[:hl]
        context[pl.ds(o1, hl), :] = turned[hl:]

    for copy in w_here:
        copy.wait()
    own_here = [
        copy_here(sources[w], full_at[w](row, z)) for w in range(3)
    ]
    q_scr[...] = jnp.zeros_like(q_scr)
    line_begin(0)
    for s in range(2):
        rc.start(n_ty[s], lambda s=s: (tok_src(s), x2.at[2 * c + s], at_c(2)))
        rc.start(n_tc[s], lambda s=s: (tok_src(s), x2.at[2 * c + s], at_c(1)))
    own_send(0)
    line_begin(1)
    head_send()
    line_step(0, 1)
    y_send(0, 0)
    y_send(0, 1)
    line_step(1, 1)
    head_pass(2)
    head_pass(1)
    line_step(0, 2)
    head_pass(3)
    y_send(1, 1)
    from_x(0, 1)
    segments_done()
    token_pass()
    line_step(1, 2)
    from_y(0, 0)
    y_send(1, 2)
    own_send(1)
    from_x(0, 0)
    line_step(0, 3)
    y_send(0, 2)
    y_send(0, 3)
    from_x(0, 2)
    y_send(1, 0)
    from_y(0, 1)
    for t in range(4):
        rc.arrived(n_hx + t, wh_at((1 - d) * nc + (z ^ t)), at_x)
    for s in range(2):
        mine[s].wait()
        rc.arrived(n_tc[s], x2.at[2 * (c ^ 1) + s], at_c(1))
    rc.arrived(n_tf, tok_at(c ^ 3), at_c(1))
    wh_here = copy_here(wh, wh_out)

    @pl.loop(0, 2 * nc)
    def _(i):
        x = x2[i]
        rows = pl.ds(pl.multiple_of(i * ln, ln), ln)
        xt[:, rows] = x.T
        got = (dot_nn(x, wh[:, :wide]) + bh[0:1, :wide]).astype(BF)
        kv[rows, :] = got
        qp = ((dot_nn(x, wh[:, wide:]) + bh[0:1, wide:]).astype(BF).astype(F32) * 0.125).astype(BF)
        for h in range(heads):
            q_scr[rows, 128 * h : 128 * h + HEAD] = qp[:, HEAD * h : HEAD * h + HEAD]

    x_here = copy_here(xt, xt_out)
    q_here = copy_here(q_scr, q_out)
    kv_here = copy_here(kv, kv_out)
    @pl.loop(0, nc)
    def _(j):
        for s in range(2):
            rows = pl.ds(pl.multiple_of((2 * j + s) * ln, ln), ln)
            for h in range(heads):
                kvt[s * heads + h, :, pl.ds(pl.multiple_of(j * ln, ln), ln)] = kv[
                    rows, 128 * h : 128 * h + 128
                ].T[HEAD:]


    @pl.loop(0, 6)
    def _(qb):
        block(qb)

        @pl.when(qb == 2)
        def _():
            from_y(1, 2)
            line_step(1, 3)

        @pl.when(qb == 3)
        def _():
            y_send(1, 3)

    context_send()
    ctx_here = copy_here(ctx_at(c), ctx_all.at[c])
    from_x(1, 2)
    from_x(1, 0)
    from_y(0, 2)
    from_y(0, 3)
    from_corner(0, 2)
    from_x(1, 1)
    from_y(1, 0)
    from_x(0, 3)
    from_x(1, 3)
    from_y(1, 3)
    from_corner(1, 2)
    from_corner(0, 0)
    from_corner(0, 1)
    from_y(1, 1)
    from_corner(0, 3)
    for k in (1, 2, 3):
        rc.arrived(n_ctx + k, ctx_all.at[c ^ k], at_c(k))
    for n, r in zip(n_c, (row, row_x, row_y, row_d)):
        for i in range(4):
            came(n, 0, i, r ^ 1, at_c(1))
    for copy in own_here + [ctx_here, bu_here] + own_rows:
        copy.wait()
    for k in (1, 2, 3):
        rc.arrived(n_bu + k, bu_full.at[z ^ k], at_z(k))

    tmp[...] = dot_nt(ctx_all[0], w_out_of(0))
    for g in range(1, nc):
        tmp[...] += dot_nt(ctx_all[g], w_out_of(g))

    def norm_one(r):
        value = x_own[r, :].astype(F32) + (tmp[r, :] + out_bias)
        centered = value - mean(value)
        rstd = lax.rsqrt(mean(centered * centered) + 1e-12)
        normal = centered * rstd
        n_one[r, :] = normal
        r_one[r, :] = jnp.broadcast_to(rstd, (step, 128))
        got = normal * gain_one + shift_one
        low[r, :] = got.astype(BF)
        total[r, :] = got + back_bias

    chunks(norm_one)
    low_t[...] = low[...].T

    from_corner(1, 3)
    @pl.loop(0, 4)
    def _(t):
        tmp[...] = dot_nn(low[...], w_of(0, t)) + bu_full[pl.ds(t, 1), 0, :]

        def gelu(r):
            u = tmp[r, :]
            cdf = 0.5 * (1.0 + lax.erf(u * math.sqrt(0.5)))
            active[r, t_cols(t)] = (u * cdf).astype(BF)
            slope[r, t_cols(t)] = cdf + u * jnp.exp(-0.5 * u * u) * (
                1.0 / math.sqrt(2.0 * math.pi)
            )

        chunks(gelu, thin)

        @pl.when(t == 1)
        def _():
            from_corner(1, 1)
            from_corner(1, 0)

    for n, r in zip(n_c, (row, row_x, row_y, row_d)):
        for i in range(4):
            came(n, 1, i, r ^ 1, at_c(1))

    @pl.loop(0, 4)
    def _(t):
        total[...] += dot_nt(active[:, t_cols(t)], w_of(1, t))

    def norm_two(r):
        value = total[r, :]
        centered = value - mean(value)
        rstd = lax.rsqrt(mean(centered * centered) + 1e-12)
        normal = centered * rstd
        out_low[r, :] = (normal * gain_two + shift_two).astype(BF)
        grad = c_own[r, :].astype(F32)
        add(4, grad * normal)
        add(5, grad)
        scaled = grad * gain_two
        got = rstd * (scaled - mean(scaled) - normal * mean(scaled * normal))
        add(3, got)
        d_low[r, :] = got.astype(BF)
        total[r, :] = got

    chunks(norm_two)
    whole_at = lambda t: output.at[(3 * t + 1) // 2]
    shared_at = lambda t: output.at[
        1 + 3 * (t // 2), pl.ds(pl.multiple_of((t % 2) * hl, 128), hl)
    ]
    pieces = ((whole_at, out_low.at[pl.ds(0, ln)]), (shared_at, out_low.at[pl.ds(ln, hl)]))
    n_out = four()
    out_here = [copy_here(src, at(z)) for at, src in pieces]
    for k, (at, src) in enumerate(pieces):
        rc.start(
            n_out + 2 * k,
            lambda at=at, src=src: (src, at(z), (d, c, z + 1)),
            lambda: z < 3,
        )
        rc.start(
            n_out + 2 * k + 1,
            lambda at=at, src=src: (src, at(z), (d, c, z - 1)),
            lambda: z > 0,
        )
    turn[...] = d_low[...].T

    @pl.loop(0, 4)
    def _(t):
        gb_v[:, t_cols(t)] = dot_nn(turn[...], active[:, t_cols(t)]).astype(BF)
        pltpu.make_async_copy(gb_v.at[:, t_cols(t)], g_b.at[:, t_cols(t)], g_sem.at[0, t]).start()
        tmp[...] = dot_nn(d_low[...], w_of(1, t))

        def inner_back(r):
            got = tmp[r, :] * slope[r, t_cols(t)]
            at = pl.ds(6 + t, 1)
            small[at, :] += jnp.sum(got, 0, keepdims=True)
            active[r, t_cols(t)] = got.astype(BF)

        chunks(inner_back, thin)
        gi_v[:, t_cols(t)] = dot_nn(low_t[...], active[:, t_cols(t)]).astype(BF)
        pltpu.make_async_copy(gi_v.at[:, t_cols(t)], g_i.at[:, t_cols(t)], g_sem.at[1, t]).start()
        total[...] += dot_nt(active[:, t_cols(t)], w_of(0, t))

    def norm_one_back(r):
        grad = total[r, :]
        normal = n_one[r, :]
        add(1, grad * normal)
        add(2, grad)
        scaled = grad * gain_one
        got = r_one[r, 0:1] * (scaled - mean(scaled) - normal * mean(scaled * normal))
        d_first[r, :] = got
        add(0, got)
        d_low[r, :] = got.astype(BF)

    chunks(norm_one_back)
    turn[...] = d_low[...].T
    for g in range(nc):
        d_ctx[g] = dot_nn(d_low[...], w_out_of(g)).astype(BF)
        g_o[g] = dot_nn(turn[...], ctx_all[g]).astype(BF)
    for t in range(4):
        pltpu.make_async_copy(gb_v.at[:, t_cols(t)], g_b.at[:, t_cols(t)], g_sem.at[0, t]).wait()
        pltpu.make_async_copy(gi_v.at[:, t_cols(t)], g_i.at[:, t_cols(t)], g_sem.at[1, t]).wait()
    for copy in (x_here, wh_here, q_here, kv_here):
        copy.wait()
    for copy in out_here:
        copy.wait()

    @pl.when(z > 0)
    def _():
        for k, (at, _) in enumerate(pieces):
            rc.arrived(n_out + 2 * k, at(z - 1), at_z(1))

    @pl.when(z < 3)
    def _():
        for k, (at, _) in enumerate(pieces):
            rc.arrived(n_out + 2 * k + 1, at(z + 1), at_z(1))

    rc.all_sent()


def forward(
    tokens, segments, w_kinds, q_bias, v_bias, in_bias, w_o, w_i, w_b, cotangent, vectors, heads
):
    ln, width = tokens.shape[1:]
    wr, units = w_i.shape
    group = w_o.shape[1]
    nc, nt, nr = 4, 4, 8
    own = 3 * ln // 2
    rows = own * nc
    hb = pl.BlockSpec(memory_space=pltpu.HBM)
    vm = pl.BlockSpec(memory_space=pltpu.VMEM)
    sds = jax.ShapeDtypeStruct
    return pl.pallas_call(
        functools.partial(forward_kernel, heads, ln),
        out_shape=(
            sds((width, 2 * nc * ln), BF),
            sds((2 * nc * ln, heads * 128), BF),
            sds((2 * nc * ln, heads * 128), BF),
            sds((nr * wr, 3 * group), BF),
            sds((width, nt * units), BF),
            sds((width, nt * units), BF),
            sds(tokens.shape, BF),
            sds((8, rows), F32),
            sds((group, rows), F32),
            sds((nc, 8, ln), jnp.int32),
            sds((nc, own, group), BF),
            sds((nt, width, group), BF),
            sds((own, width), F32),
            sds((16, width), F32),
        ),
        in_specs=[hb] + [vm] * 5 + [hb] * 4 + [vm] * 6,
        out_specs=(hb,) * 7 + (vm,) * 7,
        scratch_shapes=[
            pltpu.VMEM((2 * nc, ln, width), BF),
            pltpu.VMEM((width, 2 * nc * ln), BF),
            pltpu.VMEM((nr * wr, 3 * group), BF),
            pltpu.VMEM((8, 3 * group), F32),
            pltpu.VMEM((2 * nc * ln, heads * 128), BF),
            pltpu.VMEM((2 * nc * ln, heads * 128), BF),
            pltpu.VMEM((heads, nc * ln, ln), F32),
            pltpu.VMEM((2 * heads, HEAD, nc * ln), BF),
            pltpu.VMEM((heads, HEAD, ln), F32),
            pltpu.VMEM((2 * nc, ln, 128), F32),
            pltpu.VMEM((2 * nc, 8, ln), F32),
            pltpu.VMEM((rows, group), BF),
            pltpu.VMEM((2, wr, units), BF),
            pltpu.VMEM((wr, group), BF),
            pltpu.VMEM((8, ln), jnp.int32),
            pltpu.VMEM((wr, 3 * group), BF),
            pltpu.VMEM((8, 3 * group), F32),
            pltpu.VMEM((8, units), F32),
            pltpu.VMEM((nc, own, group), BF),
            pltpu.VMEM((nt, nr, wr, group), BF),
            pltpu.VMEM((2, nr, wr, nt * units), BF),
            pltpu.VMEM((nt, 8, units), F32),
            pltpu.VMEM((own, width), BF),
            pltpu.VMEM((own, width), BF),
            pltpu.VMEM((own, width), F32),
            pltpu.VMEM((own, 128), F32),
            pltpu.VMEM((own, width), BF),
            pltpu.VMEM((width, own), BF),
            pltpu.VMEM((own, width), F32),
            pltpu.VMEM((own, width), F32),
            pltpu.VMEM((own, nt * units), BF),
            pltpu.VMEM((own, nt * units), F32),
            pltpu.VMEM((width, own), BF),
            pltpu.VMEM((own, width), BF),
            pltpu.VMEM((width, nt * units), BF),
            pltpu.VMEM((width, nt * units), BF),
            pltpu.VMEM((own, width), BF),
            pltpu.SemaphoreType.DMA((2, 4)),
            pltpu.SemaphoreType.DMA((150,)),
            pltpu.SemaphoreType.DMA((150,)),
            pltpu.SemaphoreType.DMA((32,)),
        ],
        compiler_params=pltpu.CompilerParams(
            vmem_limit_bytes=60 << 20, collective_id=0, has_side_effects=True
        ),
        name="forward",
    )(tokens, segments, w_kinds, q_bias, v_bias, in_bias, w_o, w_i, w_b, cotangent, *vectors)


def middle_kernel(
    ln,
    tokens,
    cotangent,
    ctx_all,
    w_o,
    w_ib,
    b_in,
    out_bias,
    gain_one,
    shift_one,
    back_bias,
    gain_two,
    shift_two,
    d_ctx,
    g_b,
    g_i,
    g_o,
    out_low,
    d_first,
    small,
    x_own,
    c_own,
    w_v,
    ctx_v,
    w_ov,
    n_one,
    r_one,
    normed,
    low,
    low_t,
    tmp,
    acc,
    active,
    slope,
    n_two,
    d_sec,
    d_low,
    gb_v,
    gi_v,
    w_sem,
    g_sem,
    sem,
):
    z = lax.axis_index("tp")
    hl = ln // 2
    own = ln + hl
    blocks, _, group = ctx_all.shape
    width = x_own.shape[1]
    units = w_v.shape[2] // 4
    step, thin = 128, 64
    out_bias, gain_one, shift_one, back_bias, gain_two, shift_two = (
        a[...].reshape(1, width)
        for a in (out_bias, gain_one, shift_one, back_bias, gain_two, shift_two)
    )
    half_rows = pl.ds(pl.multiple_of((z % 2) * hl, 128), hl)
    first_rows = []
    for i, (src, dst) in enumerate(((tokens, x_own), (cotangent, c_own))):
        for j, (a, b) in enumerate(
            (
                (src.at[(3 * z + 1) // 2], dst.at[pl.ds(0, ln)]),
                (src.at[1 + 3 * (z // 2), half_rows], dst.at[pl.ds(ln, hl)]),
            )
        ):
            first_rows.append(pltpu.make_async_copy(a, b, sem.at[2 * i + j]))
    first_rows.append(pltpu.make_async_copy(ctx_all, ctx_v, sem.at[4]))
    first_rows.append(pltpu.make_async_copy(w_o, w_ov, sem.at[5]))
    for copy in first_rows:
        copy.start()
    t_cols = lambda t: pl.ds(pl.multiple_of(t * units, 128), units)

    def weight(which, t):
        return pltpu.make_async_copy(
            w_ib.at[which, :, t_cols(t)], w_v.at[which, :, t_cols(t)], w_sem.at[which, t]
        )

    for t in range(4):
        for which in range(2):
            weight(which, t).start()
    for copy in first_rows:
        copy.wait()

    def chunks(body, size=step):
        @pl.loop(0, own // size)
        def _(i):
            body(pl.ds(pl.multiple_of(i * size, size), size))

    mean = lambda v: jnp.mean(v, -1, keepdims=True)
    add = lambda i, v: small.__setitem__(
        (slice(i, i + 1), slice(None)), small[i : i + 1, :] + jnp.sum(v, 0, keepdims=True)
    )
    small[...] = jnp.zeros_like(small)

    tmp[...] = dot_nt(ctx_v[0], w_ov[0])
    for g in range(1, blocks):
        tmp[...] += dot_nt(ctx_v[g], w_ov[g])

    def norm_one(r):
        value = x_own[r, :].astype(F32) + (tmp[r, :] + out_bias)
        centered = value - mean(value)
        rstd = lax.rsqrt(mean(centered * centered) + 1e-12)
        normal = centered * rstd
        n_one[r, :] = normal
        r_one[r, :] = jnp.broadcast_to(rstd, (step, 128))
        got = normal * gain_one + shift_one
        normed[r, :] = got
        low[r, :] = got.astype(BF)
        acc[r, :] = got + back_bias

    chunks(norm_one)
    low_t[...] = low[...].T

    @pl.loop(0, 4)
    def _(t):
        weight(0, t).wait()
        weight(1, t).wait()
        tmp[...] = dot_nn(low[...], w_v[0, :, t_cols(t)]) + b_in[pl.ds(t, 1), 0, :]

        def gelu(r):
            u = tmp[r, :]
            cdf = 0.5 * (1.0 + lax.erf(u * math.sqrt(0.5)))
            active[r, t_cols(t)] = (u * cdf).astype(BF)
            slope[r, t_cols(t)] = cdf + u * jnp.exp(-0.5 * u * u) * (
                1.0 / math.sqrt(2.0 * math.pi)
            )

        chunks(gelu, thin)
        acc[...] += dot_nt(active[:, t_cols(t)], w_v[1, :, t_cols(t)])

    def norm_two(r):
        value = acc[r, :]
        centered = value - mean(value)
        rstd = lax.rsqrt(mean(centered * centered) + 1e-12)
        normal = centered * rstd
        out_low[r, :] = (normal * gain_two + shift_two).astype(BF)
        grad = c_own[r, :].astype(F32)
        add(4, grad * normal)
        add(5, grad)
        scaled = grad * gain_two
        got = rstd * (scaled - mean(scaled) - normal * mean(scaled * normal))
        d_sec[r, :] = got
        add(3, got)
        d_low[r, :] = got.astype(BF)
        acc[r, :] = got

    chunks(norm_two)
    n_two[...] = d_low[...].T

    @pl.loop(0, 4)
    def _(t):
        gb_v[:, t_cols(t)] = dot_nn(n_two[...], active[:, t_cols(t)]).astype(BF)
        pltpu.make_async_copy(gb_v.at[:, t_cols(t)], g_b.at[:, t_cols(t)], g_sem.at[0, t]).start()
        tmp[...] = dot_nn(d_low[...], w_v[1, :, t_cols(t)])

        def inner_back(r):
            got = tmp[r, :] * slope[r, t_cols(t)]
            at = pl.ds(6 + t, 1)
            small[at, :] += jnp.sum(got, 0, keepdims=True)
            active[r, t_cols(t)] = got.astype(BF)

        chunks(inner_back, thin)
        gi_v[:, t_cols(t)] = dot_nn(low_t[...], active[:, t_cols(t)]).astype(BF)
        pltpu.make_async_copy(gi_v.at[:, t_cols(t)], g_i.at[:, t_cols(t)], g_sem.at[1, t]).start()
        acc[...] += dot_nt(active[:, t_cols(t)], w_v[0, :, t_cols(t)])

    def norm_one_back(r):
        grad = acc[r, :]
        normal = n_one[r, :]
        add(1, grad * normal)
        add(2, grad)
        scaled = grad * gain_one
        got = r_one[r, 0:1] * (scaled - mean(scaled) - normal * mean(scaled * normal))
        d_first[r, :] = got
        add(0, got)
        d_low[r, :] = got.astype(BF)

    chunks(norm_one_back)
    n_two[...] = d_low[...].T
    for g in range(blocks):
        d_ctx[g] = dot_nn(d_low[...], w_ov[g]).astype(BF)
        g_o[g] = dot_nn(n_two[...], ctx_v[g]).astype(BF)
    for t in range(4):
        pltpu.make_async_copy(gb_v.at[:, t_cols(t)], g_b.at[:, t_cols(t)], g_sem.at[0, t]).wait()
        pltpu.make_async_copy(gi_v.at[:, t_cols(t)], g_i.at[:, t_cols(t)], g_sem.at[1, t]).wait()


def middle(tokens, cotangent, ctx_all, w_o, w_ib, b_in, vectors):
    blocks, own, group = ctx_all.shape
    ln, width = tokens.shape[1:]
    all_units = w_ib.shape[2]
    hb = pl.BlockSpec(memory_space=pltpu.HBM)
    vm = pl.BlockSpec(memory_space=pltpu.VMEM)
    sds = jax.ShapeDtypeStruct
    v = pltpu.VMEM
    return pl.pallas_call(
        functools.partial(middle_kernel, ln),
        out_shape=(
            sds((blocks, own, group), BF),
            sds((width, all_units), BF),
            sds((width, all_units), BF),
            sds((blocks, width, group), BF),
            sds((own, width), BF),
            sds((own, width), F32),
            sds((16, width), F32),
        ),
        in_specs=[hb] * 5 + [vm] * 7,
        out_specs=(vm, hb, hb, vm, vm, vm, vm),
        scratch_shapes=[
            v((own, width), BF),
            v((own, width), BF),
            v((2, width, all_units), BF),
            v((blocks, own, group), BF),
            v((blocks, width, group), BF),
            v((own, width), F32),
            v((own, 128), F32),
            v((own, width), F32),
            v((own, width), BF),
            v((width, own), BF),
            v((own, width), F32),
            v((own, width), F32),
            v((own, all_units), BF),
            v((own, all_units), F32),
            v((width, own), BF),
            v((own, width), F32),
            v((own, width), BF),
            v((width, all_units), BF),
            v((width, all_units), BF),
            pltpu.SemaphoreType.DMA((2, 4)),
            pltpu.SemaphoreType.DMA((2, 4)),
            pltpu.SemaphoreType.DMA((6,)),
        ],
        compiler_params=pltpu.CompilerParams(vmem_limit_bytes=60 << 20),
        cost_estimate=pl.CostEstimate(
            flops=2 * own * width * (6 * all_units + 3 * width),
            bytes_accessed=24 << 20,
            transcendentals=2 * own * all_units,
        ),
        name="middle",
    )(tokens, cotangent, ctx_all, w_o, w_ib, b_in, *vectors)


def add_into(dst, other, rows):
    @pl.loop(0, rows // 16)
    def _(i):
        at = pl.ds(pl.multiple_of(i * 16, 16), 16)
        for a, b in zip(dst, other):
            a[at, :] = (a[at, :].astype(F32) + b[at, :].astype(F32)).astype(a.dtype)


def backward_kernel(
    heads,
    ln,
    d_ctx,
    g_b,
    g_i,
    g_o,
    out_in,
    d_first,
    small_in,
    q_in,
    kv_in,
    xt_in,
    wh_in,
    lse,
    ctx_t,
    seg,
    output,
    d_tokens,
    gf_b,
    gf_i,
    gf_o,
    gf_h,
    small,
    bias,
    q_scr,
    kv,
    xt,
    wh,
    d_got,
    d_o,
    kvt,
    dkv,
    dqt,
    d_proj,
    segc,
    segr,
    part,
    got_c,
    got_y,
    got_z,
    send_y,
    send_z,
    mine,
    done,
    o_b,
    o_i,
    o_o,
    r_b,
    r_i,
    r_o,
    x_b,
    x_i,
    x_o,
    y_b,
    y_i,
    y_o,
    z_b,
    z_i,
    z_o,
    acc_h,
    o_h,
    x_h,
    z_h,
    send_h,
    small_got,
    bias_sum,
    bias_got,
    h_got,
    bias_fin,
    send,
    recv,
    local,
):
    d, c, z = (lax.axis_index(n) for n in ALL)
    nc = 4
    hl = ln // 2
    own = ln + hl
    half = z % 2
    core, y = c % 2, c // 2
    wr = gf_b.shape[0]
    units = gf_b.shape[1]
    width = d_first.shape[1]
    wide = heads * 128
    rc = Copies(send, recv)
    at_c = lambda k: (d, c ^ k, z)
    at_x = (1 - d, c, z)
    at_z = lambda k: (d, c, z ^ k)
    across = (d, z, c)

    barrier = pltpu.get_barrier_semaphore()
    everyone = [at_c(k) for k in (1, 2, 3)] + [at_z(k) for k in (1, 2, 3)] + [at_x]
    for device in everyone:
        pl.semaphore_signal(barrier, inc=1, device_id=device, device_id_type=MESH)

    @pl.when(c != z)
    def _():
        pl.semaphore_signal(barrier, inc=1, device_id=across, device_id_type=MESH)

    pl.semaphore_wait(barrier, len(everyone) + jnp.where(c != z, 1, 0))

    number = iter(range(200))
    local_number = iter(range(40))

    def copy_here(src, dst):
        copy = pltpu.make_async_copy(src, dst, local.at[next(local_number)])
        copy.start()
        return copy

    flat = lambda ref: (lambda xy, h: (ref.at[xy, :, pl.ds(1536 * h, 1536)],))
    weights = []
    for own_b, got_b, x_buf, y_buf, z_buf, grad, final, is_o in (
        (o_b, r_b, x_b, y_b, z_b, g_b, gf_b, False),
        (o_i, r_i, x_i, y_i, z_i, g_i, gf_i, False),
        (o_o, r_o, x_o, y_o, z_o, g_o, gf_o, True),
    ):
        n = [next(number) for _ in range(12)]
        weights.append((own_b, got_b, x_buf, y_buf, z_buf, grad, final, is_o, n))
    half_units = 2 * units

    def of_core(w, which):
        grad, is_o = w[5], w[7]
        return grad.at[:, :, which] if is_o else grad.at[:, which]

    def part_of(w, xy, h):
        if w[7]:
            return w[0].at[pl.ds(2 * h, 2), xy]
        return w[0].at[xy, :, pl.ds(half_units * h, half_units)]

    def views(w, xy, h):
        if w[7]:
            return [w[0].at[2 * h, xy], w[0].at[2 * h + 1, xy]]
        return [w[0].at[xy, :, pl.ds(half_units * h, half_units)]]

    def buf_views(w, ref, i):
        return [ref.at[i, 0], ref.at[i, 1]] if w[7] else [ref.at[i]]

    def unit_at(w, t):
        xy = 2 * d + y
        if w[7]:
            return w[0].at[t, xy]
        return w[0].at[xy, :, pl.ds(pl.multiple_of(t * units, 128), units)]

    w_here = [copy_here(of_core(w, core), w[0]) for w in weights]
    blk = lambda x_, y_: 2 * x_ + y_

    def w_core_send(w):
        rc.start(w[8][0], lambda: (of_core(w, 1 - core), w[1], at_c(1)))

    def w_core_add(i):
        w = weights[i]
        w_here[i].wait()
        rc.arrived(w[8][0], w[1], at_c(1))

        @pl.loop(0, 4)
        def _(xy):
            if w[7]:
                add_into([w[0].at[t, xy] for t in range(4)], [w[1].at[t, xy] for t in range(4)], wr)
            else:
                add_into([w[0].at[xy]], [w[1].at[xy]], wr)

        n = w[8]
        for j in range(2):
            rc.start(n[1 + j], lambda j=j: (part_of(w, blk(1 - d, j), 0), w[2].at[j], at_x))
            rc.start(n[3 + j], lambda j=j: (part_of(w, blk(j, 1 - y), 1), w[3].at[j], at_c(2)))

    def w_plane(i):
        w = weights[i]
        n = w[8]
        for j in range(2):
            rc.arrived(n[1 + j], w[2].at[j], at_x)
        for j in range(2):
            add_into(views(w, blk(d, j), 0), buf_views(w, w[2], j), wr)
        rc.start(n[5], lambda: (part_of(w, blk(d, 1 - y), 0), w[3].at[2], at_c(2)))
        for j in range(2):
            rc.arrived(n[3 + j], w[3].at[j], at_c(2))
        for j in range(2):
            add_into(views(w, blk(j, y), 1), buf_views(w, w[3], j), wr)
        rc.start(n[6], lambda: (part_of(w, blk(1 - d, y), 1), w[2].at[2], at_x))

    def w_corner(i):
        w = weights[i]
        n = w[8]
        rc.arrived(n[5], w[3].at[2], at_c(2))
        add_into(views(w, blk(d, y), 0), buf_views(w, w[3], 2), wr)
        rc.arrived(n[6], w[2].at[2], at_x)
        add_into(views(w, blk(d, y), 1), buf_views(w, w[2], 2), wr)
        for t in (0, 1, 2):
            chain_send(w, t, 3)
        for t in (3, 2, 1):
            chain_send(w, t, 0)

    def chain_send(w, t, at):
        to = at + 1 if t > at else at - 1
        slot = 4 if to == t and t > at else t
        n = w[8]
        rc.start(
            n[7 + slot],
            lambda: (unit_at(w, t), w[4].at[slot], (d, c, to)),
            lambda: z == at,
            n[7 + t],
        )

    def chain_pass(w, t, at):
        @pl.when(z == at)
        def _():
            rc.arrived(w[8][7 + t], w[4].at[t], at_x)
            add_into([unit_at(w, t)], [w[4].at[t]], wr)

        chain_send(w, t, at)

    def w_line(i):
        w = weights[i]
        for t in (0, 1):
            chain_pass(w, t, 2)
        for t in (3, 2):
            chain_pass(w, t, 1)

    def w_next(i):
        w = weights[i]
        chain_pass(w, 3, 2)
        chain_pass(w, 0, 1)

    def w_end(i):
        w = weights[i]
        for t in range(4):

            @pl.when(z == t)
            def _():
                if t < 3:
                    rc.arrived(w[8][7 + t], w[4].at[t], at_x)
                if t > 0:
                    rc.arrived(w[8][11], w[4].at[4], at_x)

        total = unit_at(w, z)[...].astype(F32) + w[4].at[z][...].astype(F32)
        w[6][...] = total + w[4].at[4][...].astype(F32)

    whole_of = lambda t: (3 * t + 1) // 2
    shared_of = lambda t: 1 + 3 * (t // 2)

    class Line:
        def __init__(self, at):
            self.at = at
            self.left = [next(number) for _ in range(3)]
            self.right = [next(number) for _ in range(3)]

        def begin(self, src):
            rc.start(self.left[0], lambda: (src, self.at(z), (d, c, z + 1)), lambda: z < 3)
            rc.start(self.right[0], lambda: (src, self.at(z), (d, c, z - 1)), lambda: z > 0)

        def step(self, j, wait=True):
            from_left, from_right = z - j, z + j

            if wait:

                @pl.when(z >= j)
                def _():
                    rc.arrived(self.left[j - 1], self.at(from_left), (d, c, z - 1))

            if j < 3:
                rc.start(
                    self.left[j],
                    lambda: (self.at(z - j), self.at(z - j), (d, c, z + 1)),
                    lambda: (z >= j) & (z < 3),
                )

            if wait:

                @pl.when(z + j <= 3)
                def _():
                    rc.arrived(self.right[j - 1], self.at(from_right), (d, c, z + 1))

            if j < 3:
                rc.start(
                    self.right[j],
                    lambda: (self.at(z + j), self.at(z + j), (d, c, z - 1)),
                    lambda: (z + j <= 3) & (z > 0),
                )

    whole_rows = lambda ref, a, n: (lambda t: ref.at[whole_of(t), pl.ds(a, n)])
    shared_rows = lambda ref: (
        lambda t: ref.at[shared_of(t), pl.ds(pl.multiple_of((t % 2) * hl, 128), hl)]
    )
    out_lines = [Line(whole_rows(output, 0, ln)), Line(shared_rows(output))]
    tok_lines = [
        Line(whole_rows(d_tokens, 0, hl)),
        Line(whole_rows(d_tokens, hl, hl)),
        Line(shared_rows(d_tokens)),
    ]

    n_ctx = [next(number) for _ in range(3)]
    for k in (1, 2, 3):
        rc.start(n_ctx[k - 1], lambda k=k: (d_ctx.at[c ^ k], d_got.at[c], at_c(k)))
    ctx_here = copy_here(d_ctx.at[c], d_got.at[c])
    kv_here = copy_here(kv_in, kv)
    q_here = copy_here(q_in, q_scr)
    n_small = [next(number) for _ in range(5)]
    small_to = (at_c(1), at_c(2), at_x, at_z(1), at_z(2))
    small[...] = small_in[...]

    def small_send(i):
        rc.start(n_small[i], lambda: (small_got.at[i, 1], small_got.at[i, 0], small_to[i]))

    def small_step(i):
        rc.arrived(n_small[i], small_got.at[i, 0], small_to[i])
        small[...] += small_got[i, 0]
        if i < 4:
            small_got[i + 1, 1] = small[...]
            small_send(i + 1)

    small_got[0, 1] = small_in[...]
    wh_here = copy_here(wh_in, wh)
    xt_here = copy_here(xt_in, xt)

    def block(qb):
        r0, r1, o0, o1, seq = block_rows(qb, half, ln)
        b0 = jnp.where(qb < 4, qb, 2 * (qb - 4))
        b1 = jnp.where(qb < 4, qb, 2 * (qb - 4) + 1)
        s0 = pl.multiple_of(jnp.where(qb < 4, 0, hl * half), 128)
        s1 = pl.multiple_of(jnp.where(qb < 4, hl, hl * half), 128)
        sq = jnp.concatenate(
            [
                segr[2 * b0 + seq, 0:1, pl.ds(s0, hl)],
                segr[2 * b1 + seq, 0:1, pl.ds(s1, hl)],
            ],
            1,
        )
        q, do, line, delta = [], [], [], []
        for h in range(heads):
            q.append(two(q_scr, r0, r1, hl, slice(128 * h, 128 * h + 128)))
            do.append(two(d_o, o0, o1, hl, slice(128 * h, 128 * h + 128)))
            line.append(two_lanes(lse, slice(h, h + 1), o0, o1, hl))
            turned = do[h].astype(F32).T[HEAD:, :]
            kept = two_lanes(ctx_t, slice(HEAD * h, HEAD * h + HEAD), o0, o1, hl)
            delta.append(jnp.sum(turned * kept, 0, keepdims=True))
        q_do = [jnp.concatenate([q[h], do[h]], 0) for h in range(heads)]
        dqt[...] = jnp.zeros_like(dqt)

        @pl.loop(0, nc)
        def _(j):
            rows = pl.ds(pl.multiple_of((2 * j + seq) * ln, ln), ln)
            keys = pl.ds(pl.multiple_of(j * ln, ln), ln)
            key_seg = segc[2 * j + seq]
            same = jnp.concatenate([key_seg, key_seg], 1) == sq
            for h in range(heads):
                kvh = kv[rows, 128 * h : 128 * h + 128]
                p = jnp.where(same, jnp.exp(dot_nt(kvh, q[h]) - line[h]), 0.0)
                ds = (p * (dot_nt(kvh, do[h]) - delta[h])).astype(BF)
                both = jnp.concatenate([ds, p.astype(BF)], 1)
                dkv[rows, 128 * h : 128 * h + 128] += dot_nn(both, q_do[h])
                dqt[h] += dot_nn(kvt[seq * heads + h, :, keys], ds)

        turned = jnp.concatenate([dqt[h] for h in range(heads)], 0).T * 0.125
        bias_sum[0:1, wide:] += jnp.sum(turned, 0, keepdims=True)
        low = turned.astype(BF)
        d_proj[pl.ds(r0, hl), wide:] = low[:hl]
        d_proj[pl.ds(r1, hl), wide:] = low[hl:]

    n_tc = [[next(number), next(number)] for _ in range(2)]
    n_ty = [[next(number), next(number)] for _ in range(2)]
    n_tz = next(number)

    def rows_of(cb, s):
        rows = pl.ds(pl.multiple_of((2 * cb + s) * ln, ln), ln)
        got = dkv[rows, :]
        bias_sum[0:1, :wide] += jnp.sum(got, 0, keepdims=True)
        d_proj[rows, :wide] = got.astype(BF)
        part[cb, s] = dot_nt(d_proj[rows, :], wh[...]).astype(BF)

    def t_partial(s):
        rows_of(c ^ 3, s)
        rc.start(n_tc[s][0], lambda: (part.at[c ^ 3, s], got_c.at[s, 0], at_c(1)))
        rows_of(c ^ 1, s)
        rc.start(n_tc[s][1], lambda: (part.at[c ^ 1, s], got_c.at[s, 1], at_c(1)))
        rows_of(c ^ 2, s)
        rows_of(c, s)

    def t_core(s):
        rc.arrived(n_tc[s][0], got_c.at[s, 0], at_c(1))
        for k in range(2):
            at = slice(k * hl, k * hl + hl)
            send_y[s, at] = (part[c ^ 2, s, at].astype(F32) + got_c[s, 0, at].astype(F32)).astype(BF)
            rc.start(
                n_ty[s][k],
                lambda k=k: (
                    send_y.at[s, pl.ds(k * hl, hl)],
                    got_y.at[s, pl.ds(k * hl, hl)],
                    at_c(2),
                ),
            )
        rc.arrived(n_tc[s][1], got_c.at[s, 1], at_c(1))
        mine[s] = part[c, s].astype(F32) + got_c[s, 1].astype(F32)

    def t_shared():
        for k in range(2):
            rc.arrived(n_ty[1][k], got_y.at[1, pl.ds(k * hl, hl)], at_c(2))
        mine[1] += got_y[1].astype(F32)
        send_z[...] = mine[1, pl.ds(pl.multiple_of((1 - half) * hl, 128), hl)].astype(BF)
        rc.start(n_tz, lambda: (send_z, got_z, at_z(1)))

    def t_shared_end():
        rc.arrived(n_tz, got_z, at_z(1))
        mine_half = mine[1, pl.ds(pl.multiple_of(half * hl, 128), hl)]
        done[ln:, :] = (mine_half + got_z[...].astype(F32) + d_first[ln:, :]).astype(BF)
        tok_lines[2].begin(done.at[pl.ds(ln, hl)])

    def t_whole(k):
        at = slice(k * hl, k * hl + hl)
        rc.arrived(n_ty[0][k], got_y.at[0, pl.ds(k * hl, hl)], at_c(2))
        done[at, :] = (mine[0, at] + got_y[0, at].astype(F32) + d_first[at, :]).astype(BF)
        tok_lines[k].begin(done.at[pl.ds(k * hl, hl)])

    n_h = [next(number) for _ in range(8)]

    def h_partial(seq):
        @pl.loop(0, nc)
        def _(i):
            rows = pl.ds(pl.multiple_of((2 * i + seq) * ln, ln), ln)
            acc_h[...] += dot_nn(xt[:, rows], d_proj[rows, :])

    def h_send():
        o_h[...] = acc_h[...].astype(BF)
        rows_x = lambda x_: pl.ds(pl.multiple_of(x_ * 4 * wr, wr), 4 * wr)
        rc.start(n_h[0], lambda: (o_h.at[rows_x(1 - d)], x_h, at_x))

    h_at = lambda t: o_h.at[pl.ds(pl.multiple_of((4 * d + t) * wr, wr), wr)]

    def h_plane():
        rc.arrived(n_h[0], x_h, at_x)
        add_into([o_h.at[pl.ds(pl.multiple_of(d * 4 * wr, wr), 4 * wr)]], [x_h], 4 * wr)
        rc.start(n_h[1], lambda: (h_at(z ^ 3), z_h.at[1], at_z(1)))
        rc.start(n_h[2], lambda: (h_at(z ^ 1), z_h.at[0], at_z(1)))

    def h_line():
        rc.arrived(n_h[1], z_h.at[1], at_z(1))
        add_into([h_at(z ^ 2)], [z_h.at[1]], wr)
        rc.start(n_h[3], lambda: (h_at(z ^ 2), z_h.at[2], at_z(2)))
        rc.arrived(n_h[2], z_h.at[0], at_z(1))
        add_into([h_at(z)], [z_h.at[0]], wr)

    def h_end():
        rc.arrived(n_h[3], z_h.at[2], at_z(2))
        send_h[...] = h_at(z)[...].astype(F32) + z_h[2].astype(F32)
        rc.start(n_h[4], lambda: (send_h, h_got, across), lambda: c != z)

        @pl.when(c == z)
        def _():
            h_got[...] = send_h[...]

    n_bias = [next(number) for _ in range(4)]
    bias_to = (at_x, at_z(1), at_z(2))

    def bias_send(i):
        bias_got[i, 1] = bias_sum[...]
        rc.start(n_bias[i], lambda: (bias_got.at[i, 1], bias_got.at[i, 0], bias_to[i]))

    def bias_step(i):
        rc.arrived(n_bias[i], bias_got.at[i, 0], bias_to[i])
        bias_sum[...] += bias_got[i, 0]
        if i < 2:
            bias_send(i + 1)
            return
        rc.start(n_bias[3], lambda: (bias_sum, bias_fin, across), lambda: c != z)

        @pl.when(c == z)
        def _():
            bias_fin[...] = bias_sum[...]

    for w in weights:

        @pl.when(z == 0)
        def _():
            w[4][4] = jnp.zeros_like(w[4][4])

        @pl.when(z == 3)
        def _():
            w[4][3] = jnp.zeros_like(w[4][3])

    def get_ctx():
        for k in (1, 2, 3):
            rc.arrived(n_ctx[k - 1], d_got.at[c ^ k], at_c(k))
        ctx_here.wait()

        @pl.loop(0, nc)
        def _(i):
            rows = pl.ds(pl.multiple_of(i * own, 128), own)
            for h in range(heads):
                d_o[rows, 128 * h + HEAD : 128 * h + 128] = d_got[
                    i, :, HEAD * h : HEAD * h + HEAD
                ]

        q_here.wait()
        wh_here.wait()
        xt_here.wait()

    def out_begin():
        for line in out_lines:
            line.step(1, False)

    out_begin()
    small_send(0)
    w_core_send(weights[0])
    w_core_add(0)
    w_core_send(weights[2])
    for i in range(nc):
        for s in range(2):
            line = seg[i, s : s + 1, :].astype(F32)
            segr[2 * i + s, 0:1, :] = line
            segc[2 * i + s] = jnp.broadcast_to(line, (128, ln)).T
    dkv[...] = jnp.zeros_like(dkv)
    d_o[...] = jnp.zeros_like(d_o)
    d_proj[...] = jnp.zeros_like(d_proj)
    bias_sum[...] = jnp.zeros_like(bias_sum)
    acc_h[...] = jnp.zeros_like(acc_h)
    kv_here.wait()

    @pl.loop(0, nc)
    def _(j):
        for s in range(2):
            rows = pl.ds(pl.multiple_of((2 * j + s) * ln, ln), ln)
            for h in range(heads):
                kvt[s * heads + h, :, pl.ds(pl.multiple_of(j * ln, ln), ln)] = kv[
                    rows, 128 * h : 128 * h + 128
                ].T[:HEAD]

    get_ctx()

    @pl.loop(0, 6)
    def _(i):
        block(jnp.where(i == 0, 4, jnp.where(i == 1, 5, jnp.where(i == 2, 0, jnp.where(i == 3, 1, jnp.where(i == 4, 2, 3))))))

        @pl.when(i == 1)
        def _():
            out_lines[0].step(2)
            out_lines[1].step(2)
            t_partial(1)
            t_core(1)

        @pl.when(i == 2)
        def _():
            small_step(0)
            w_plane(0)
            w_core_send(weights[1])
            w_core_add(2)

        @pl.when(i == 3)
        def _():
            t_shared()

        @pl.when(i == 4)
        def _():
            small_step(1)

    small_step(2)
    t_shared_end()
    t_partial(0)
    small_step(3)
    t_core(0)
    bias_send(0)
    w_plane(2)
    tok_lines[2].step(1)
    w_core_add(1)
    t_whole(0)
    bias_step(0)
    t_whole(1)
    h_partial(1)
    bias_step(1)
    w_corner(0)
    small_step(4)
    tok_lines[2].step(2)
    h_partial(0)
    h_send()
    tok_lines[1].step(1)
    tok_lines[0].step(1)
    bias_step(2)
    w_plane(1)
    w_corner(2)
    tok_lines[2].step(3)
    w_line(0)
    h_plane()
    w_line(2)
    w_next(0)
    tok_lines[0].step(2)
    h_line()
    w_corner(1)
    tok_lines[1].step(2)
    w_end(0)
    h_end()
    tok_lines[1].step(3)
    w_next(2)
    w_line(1)
    w_end(2)
    w_next(1)
    out_lines[0].step(3)
    out_lines[1].step(3)
    tok_lines[0].step(3)
    w_end(1)
    tok_here = [
        copy_here(done.at[pl.ds(0, hl)], tok_lines[0].at(z)),
        copy_here(done.at[pl.ds(hl, hl)], tok_lines[1].at(z)),
        copy_here(done.at[pl.ds(ln, hl)], tok_lines[2].at(z)),
    ]

    @pl.when(c != z)
    def _():
        rc.arrived(n_h[4], h_got, across)
        rc.arrived(n_bias[3], bias_fin, across)

    gf_h[...] = h_got[...]
    bias[...] = bias_fin[...]

    for copy in tok_here:
        copy.wait()
    rc.all_sent()


def backward(d_ctx, g_b, g_i, g_o, out_in, d_first, small, q, kv, xt, wh, lse, ctx_t, seg, heads, seqs):
    nc, own, group = d_ctx.shape
    ln = own * 2 // 3
    hl = ln // 2
    width = out_in.shape[2]
    wr, all_units = g_b.shape[2:]
    units = all_units // 4
    hb = pl.BlockSpec(memory_space=pltpu.HBM)
    vm = pl.BlockSpec(memory_space=pltpu.VMEM)
    sds = jax.ShapeDtypeStruct
    v = pltpu.VMEM
    rows = nc * own
    n2 = 2 * nc * ln
    return pl.pallas_call(
        functools.partial(backward_kernel, heads, ln),
        out_shape=(
            sds((seqs, ln, width), BF),
            sds((seqs, ln, width), BF),
            sds((wr, units), F32),
            sds((wr, units), F32),
            sds((wr, group), F32),
            sds((wr, 3 * group), F32),
            sds(small.shape, F32),
            sds((8, 3 * group), F32),
        ),
        in_specs=[hb] * 5 + [vm] * 2 + [hb] * 4 + [vm] * 3,
        out_specs=(hb, hb) + (vm,) * 6,
        scratch_shapes=[
            v((n2, heads * 128), BF),
            v((n2, heads * 128), BF),
            v((width, n2), BF),
            v((width, 3 * group), BF),
            v((nc, own, group), BF),
            v((rows, heads * 128), BF),
            v((2 * heads, HEAD, nc * ln), BF),
            v((n2, heads * 128), F32),
            v((heads, HEAD, ln), F32),
            v((n2, 3 * group), BF),
            v((2 * nc, ln, 128), F32),
            v((2 * nc, 8, ln), F32),
            v((nc, 2, ln, width), BF),
            v((2, 2, ln, width), BF),
            v((2, ln, width), BF),
            v((hl, width), BF),
            v((2, ln, width), BF),
            v((hl, width), BF),
            v((2, ln, width), F32),
            v((own, width), BF),
            v((4, wr, all_units), BF),
            v((4, wr, all_units), BF),
            v((4, 4, wr, group), BF),
            v((4, wr, all_units), BF),
            v((4, wr, all_units), BF),
            v((4, 4, wr, group), BF),
            v((3, wr, 2 * units), BF),
            v((3, wr, 2 * units), BF),
            v((3, 2, wr, group), BF),
            v((3, wr, 2 * units), BF),
            v((3, wr, 2 * units), BF),
            v((3, 2, wr, group), BF),
            v((5, wr, units), BF),
            v((5, wr, units), BF),
            v((5, wr, group), BF),
            v((width, 3 * group), F32),
            v((width, 3 * group), BF),
            v((4 * wr, 3 * group), BF),
            v((3, wr, 3 * group), BF),
            v((wr, 3 * group), F32),
            v((5, 2) + small.shape, F32),
            v((8, 3 * group), F32),
            v((3, 2, 8, 3 * group), F32),
            v((wr, 3 * group), F32),
            v((8, 3 * group), F32),
            pltpu.SemaphoreType.DMA((130,)),
            pltpu.SemaphoreType.DMA((130,)),
            pltpu.SemaphoreType.DMA((40,)),
        ],
        compiler_params=pltpu.CompilerParams(
            vmem_limit_bytes=60 << 20, collective_id=1, has_side_effects=True
        ),
        input_output_aliases={4: 0},
        name="backward",
    )(d_ctx, g_b, g_i, g_o, out_in, d_first, small, q, kv, xt, wh, lse, ctx_t, seg)


def finish_kernel(
    heads, tok_in, out_in, g_b, g_i, g_o, g_h, small, bias,
    tok, out, gb, gi, go, gh, gq, gv, w0, w1, w2, in_b, w3, w4, w5,
):
    tok[...] = tok_in[...].astype(F32)
    out[...] = out_in[...]
    z = lax.axis_index("tp")
    wide = heads * 128

    @pl.when(pl.program_id(0) == 0)
    def _():
        gb[...] = g_b[...]
        gi[...] = g_i[...]
        go[...] = g_o[...]
        pick = lambda ref, rows, at: jnp.concatenate(
            [ref[rows, 128 * h + at : 128 * h + at + HEAD] for h in range(heads)], -1
        )
        gh[0] = g_h[:, wide:]
        gh[1] = pick(g_h, slice(None), 0)
        gh[2] = pick(g_h, slice(None), HEAD)
        gq[...] = bias[0, wide:]
        gv[...] = pick(bias, 0, HEAD)
        for i, ref in ((0, w0), (1, w1), (2, w2), (3, w3), (4, w4), (5, w5)):
            ref[...] = small[i, :]
        in_b[...] = small[pl.ds(6 + z, 1), :].reshape(in_b.shape)


def finish(d_tokens, output, g_b, g_i, g_o, g_h, small, d_bias, heads):
    seqs, ln, width = d_tokens.shape
    wr, units = g_b.shape
    group = g_o.shape[1]
    one = lambda: pl.BlockSpec((seqs // 2, ln, width), lambda i: (i, 0, 0))
    whole = lambda shape: pl.BlockSpec(shape, lambda i: (0,) * len(shape))
    sds = jax.ShapeDtypeStruct
    rest = [
        (wr, units), (wr, units), (wr, group), (3, wr, group), (group,), (group,),
        (width,), (width,), (width,), (units,), (width,), (width,), (width,),
    ]
    return pl.pallas_call(
        functools.partial(finish_kernel, heads),
        grid=(2,),
        out_shape=[sds(d_tokens.shape, F32), sds(output.shape, BF)] + [sds(s, F32) for s in rest],
        in_specs=[one(), one()]
        + [whole(a.shape) for a in (g_b, g_i, g_o, g_h, small, d_bias)],
        out_specs=[one(), one()] + [whole(s) for s in rest],
        compiler_params=pltpu.CompilerParams(vmem_limit_bytes=60 << 20),
        name="finish",
    )(d_tokens, output, g_b, g_i, g_o, g_h, small, d_bias)


def head_order(kinds, heads):
    lead = kinds[0].shape[:-1]
    q, k, v = (a.reshape(lead + (heads, HEAD)) for a in kinds)
    kv = jnp.concatenate([k, v], -1).reshape(lead + (heads * 2 * HEAD,))
    return jnp.concatenate([kv, q.reshape(lead + (heads * HEAD,))], -1)


def forward_plain(sizes, me, tok2, seg2, w_head, b_head, b_unit, w_o, w_i, w_b, heads):
    nd, nc, nt = sizes
    d, c, z = me
    ln, width = tok2.shape[1:]
    hl = ln // 2
    half = z % 2
    group = w_o.shape[1]
    seg_all = gather_axis(seg2, "ctx", nc, c)
    x2 = gather_axis(tok2, "ctx", nc, c).reshape(2 * nc, ln, width)
    wh = gather_heads(w_head, sizes, me)
    bh = transpose_ctx_tp(b_head, nc)[0]
    b_all = gather_axis(b_unit, "tp", nt, z)
    gather = lambda w: lax.all_gather(
        lax.all_gather(w, "tp", axis=1, tiled=True), ("dp", "ctx"), axis=0, tiled=True
    )
    o_full = jnp.transpose(gather(w_o).reshape(width, nt, group), (1, 0, 2))
    proj = (jnp.dot(x2.reshape(-1, width), wh, preferred_element_type=F32) + bh).astype(BF)
    kv = proj[:, : 2 * group]
    q = (proj[:, 2 * group :].astype(F32) * 0.125).astype(BF).reshape(-1, heads, HEAD)
    q = jnp.concatenate([q, jnp.zeros_like(q)], -1).reshape(-1, heads * 128)
    info, seg_col, seg_row = key_blocks(seg_all, half, ln, nc)
    context, lse, ctx_t = attend(info, q, kv, seg_col, seg_row, heads, ln, nc)
    ctx_all = in_order(exchange_axis(context.reshape(nc, ln + hl, group), "ctx", nc, c), c)
    return (
        ctx_all,
        x2.reshape(-1, width).T,
        q,
        kv,
        wh,
        o_full,
        jnp.stack([gather(w_i), gather(w_b)]),
        b_all,
        lse,
        ctx_t,
        seg_all,
    )


def key_blocks(seg_all, half, ln, nc):
    hl = ln // 2
    seg2 = seg_all[:, :2]
    flat = jnp.transpose(seg2, (1, 0, 2)).reshape(2, nc * ln)
    first = jnp.concatenate([seg2[:, 0, 0], jnp.take(seg2[0::2, 1], half * hl, axis=1)])
    last = jnp.concatenate([seg2[:, 0, -1], jnp.take(seg2[1::2, 1], half * hl + hl - 1, axis=1)])
    of = jnp.concatenate(
        [
            jnp.broadcast_to(flat[:1], (nc, nc * ln)),
            jnp.broadcast_to(flat[1:], (nc // 2, nc * ln)),
        ],
        0,
    )
    lo = jnp.sum(of < first[:, None], 1) // ln
    hi = (jnp.sum(of <= last[:, None], 1) + ln - 1) // ln
    info = jnp.concatenate([lo, hi, half[None]]).astype(jnp.int32)
    seg_flat = seg2.reshape(2 * nc * ln)
    return info, seg_flat[:, None], seg_flat[None, :]


def backward_plain(
    sizes, me, d_ctx, low, out_low, d_first, small, q, kv, xt, wh, lse, ctx_t, seg_all, heads, seqs
):
    nd, nc, nt = sizes
    d, c, z = me
    own, group = d_ctx.shape[1:]
    ln = own * 2 // 3
    hl = ln // 2
    half = z % 2
    width = out_low.shape[1]
    units = low[0].shape[1] // nt
    nr = nd * nc
    wr = width // nr
    info, seg_col, seg_row = key_blocks(seg_all, half, ln, nc)

    def spread_rows(rows_low, dtype):
        out = jnp.zeros((seqs, ln, width), dtype)
        parts = [rows_low] + [swap_with(rows_low, "tp", nt, k) for k in range(1, nt)]
        for k, part in enumerate(parts):
            t = z ^ k
            part = part.astype(dtype)
            out = lax.dynamic_update_slice(out, part[None, :ln], ((3 * t + 1) // 2, 0, 0))
            out = lax.dynamic_update_slice(
                out, part[None, ln:], (1 + 3 * (t // 2), (t % 2) * hl, 0)
            )
        return out

    by_unit = lambda g: jnp.transpose(g.reshape(nr, wr, nt, units), (2, 0, 1, 3))
    g_back = scatter_weight(by_unit(low[0]), sizes, me)
    g_in = scatter_weight(by_unit(low[1]), sizes, me)
    g_out = scatter_weight(low[2].reshape(nt, nr, wr, group), sizes, me)
    output = spread_rows(out_low, BF)
    small = lax.psum(small, ALL)
    d_ctx = in_order(exchange_axis(d_ctx, "ctx", nc, c), c).reshape(nc * own, heads, HEAD)
    d_ctx = jnp.concatenate([jnp.zeros_like(d_ctx), d_ctx], -1).reshape(nc * own, heads * 128)
    d_q, d_kv, d_bias = attend_back(
        info, q, kv, d_ctx, seg_col, seg_row, lse, ctx_t, heads, ln, nc
    )
    d_proj = jnp.concatenate([d_kv, d_q], -1)
    part = jnp.einsum("tf,df->td", d_proj, wh, preferred_element_type=F32)
    part = lax.psum_scatter(
        part.reshape(nc, 2 * ln, width), "ctx", scatter_dimension=0, tiled=False
    ).reshape(2, ln, width)
    shared = part[1].reshape(2, hl, width)
    shared = lax.dynamic_index_in_dim(shared, half, 0, keepdims=False) + swap_with(
        lax.dynamic_index_in_dim(shared, 1 - half, 0, keepdims=False), "tp", nt, 1
    )
    d_own = (jnp.concatenate([part[0], shared], 0) + d_first).astype(BF)
    d_tokens = spread_rows(d_own, BF)
    g_h = scatter_heads(jnp.dot(xt, d_proj, preferred_element_type=F32).astype(BF), sizes, me)
    slots = jnp.zeros((nc,) + d_bias[0].shape, F32)
    slots = lax.psum(lax.dynamic_update_index_in_dim(slots, d_bias[0], c, 0), ALL)
    d_bias = lax.dynamic_index_in_dim(slots, z, 0, keepdims=False)
    d_bias = jnp.broadcast_to(d_bias[None], (8,) + d_bias.shape)
    return output, d_tokens, g_back, g_in, g_out, g_h, small, d_bias


def per_device(
    sizes,
    tokens,
    segments,
    w_qkv,
    q_bias,
    v_bias,
    w_out,
    out_bias,
    gain_one,
    shift_one,
    w_in,
    in_bias,
    w_back,
    back_bias,
    gain_two,
    shift_two,
    cotangent,
):
    nd, nc, nt = sizes
    seqs, ln, width = tokens.shape
    group = w_out.shape[1]
    heads = group // HEAD
    units = w_in.shape[1]
    wr = w_in.shape[0]
    d, c, z = (lax.axis_index(n) for n in ALL)
    me = (d, c, z)
    whole_of = lambda t: (3 * t + 1) // 2
    shared_of = lambda t: 1 + 3 * (t // 2)
    half_of = lambda t: t % 2
    sf, sh, half = whole_of(z), shared_of(z), half_of(z)

    def own_pair(a):
        return jnp.stack(
            [
                lax.dynamic_index_in_dim(a, sf, 0, keepdims=False),
                lax.dynamic_index_in_dim(a, sh, 0, keepdims=False),
            ],
            0,
        )

    w_kinds = jnp.transpose(w_qkv, (1, 0, 2))
    biases = (q_bias, v_bias, in_bias)
    weights = (w_out, w_in, w_back)
    vectors = (out_bias, gain_one, shift_one, back_bias, gain_two, shift_two)
    if sizes == (2, 4, 4):
        xt, q, kv, wh, g_b, g_i, out_low, lse, ctx_t, seg_all, d_ctx, g_o, d_first, small = forward(
            tokens, segments, w_kinds, *biases, *weights, cotangent, vectors, heads
        )
    else:
        tok2 = own_pair(tokens)
        seg2 = jnp.concatenate([own_pair(segments), jnp.zeros((6, ln), jnp.int32)], 0)
        w_head = head_order(w_kinds, heads)
        b_head = head_order([q_bias, jnp.zeros_like(q_bias), v_bias], heads)
        b_head = jnp.broadcast_to(b_head[None], (8, 3 * group))
        b_unit = jnp.broadcast_to(in_bias[None], (8, units))
        got = forward_plain(sizes, me, tok2, seg2, w_head, b_head, b_unit, *weights, heads)
        ctx_all, xt, q, kv, wh, w_o, w_ib, b_in, lse, ctx_t, seg_all = got
        d_ctx, g_b, g_i, g_o, out_low, d_first, small = middle(
            tokens,
            cotangent,
            ctx_all,
            w_o.reshape(nt, width, group),
            w_ib.reshape(2, width, nt * units),
            b_in,
            vectors,
        )
    low = (g_b, g_i, g_o)
    if sizes == (2, 4, 4):
        output, d_tokens, g_back, g_in, g_out, g_h, small, d_bias = backward(
            d_ctx,
            low[0].reshape(4, 2, wr, nt * units),
            low[1].reshape(4, 2, wr, nt * units),
            low[2].reshape(nt, 4, 2, wr, group),
            out_low,
            d_first,
            small,
            q,
            kv,
            xt,
            wh,
            lse,
            ctx_t,
            seg_all,
            heads,
            seqs,
        )
    else:
        output, d_tokens, g_back, g_in, g_out, g_h, small, d_bias = backward_plain(
            sizes, me, d_ctx, low, out_low, d_first, small, q, kv, xt, wh, lse, ctx_t, seg_all, heads, seqs
        )
    d_tokens, output, g_b, g_i, g_o, g_h, d_qb, d_vb, w0, w1, w2, d_in, w3, w4, w5 = finish(
        d_tokens, output, g_back, g_in, g_out, g_h, small, d_bias, heads
    )
    g_h = jnp.transpose(g_h, (1, 0, 2))
    return (output, d_tokens, g_h, d_qb, d_vb, g_o, w0, w1, w2, g_i, d_in, g_b, w3, w4, w5)


def solution(mesh):
    sizes = tuple(mesh.shape[n] for n in ALL)
    rows = P(("dp", "ctx"), "tp")
    return jax.shard_map(
        functools.partial(per_device, sizes),
        mesh=mesh,
        in_specs=(
            P("dp", "ctx", None),
            P("dp", "ctx"),
            P(("dp", "ctx"), None, "tp"),
            P("tp"),
            P("tp"),
            rows,
            P(),
            P(),
            P(),
            rows,
            P("tp"),
            rows,
            P(),
            P(),
            P(),
            P("dp", "ctx", None),
        ),
        out_specs=(
            P("dp", "ctx", None),
            P("dp", "ctx", None),
            P(("dp", "ctx"), None, "tp"),
            P("tp"),
            P("tp"),
            rows,
            P(),
            P(),
            P(),
            rows,
            P("tp"),
            rows,
            P(),
            P(),
            P(),
        ),
        check_vma=False,
    )
```
